32 devices in a mesh: dp: 8 (over y, x, core), ffn: 4 (over z).
Axes of the slice: x: 2, y: 2, z: 4, core: 2. Of those that a mesh axis runs over, the one named last changes fastest.
Arguments:
- layer_activations: bfloat16 [64, 512, 768], P(('dp', 'ffn')), may hold values from -6 to 6
- token_counts_each: int32 [64], P(('dp', 'ffn')), may hold values from 64 to 512, as said below
- attention_triple_matrix: bfloat16 [768, 2304], P('dp', 'ffn'), may hold values from -0.21875 to 0.21875
- attention_final_matrix: bfloat16 [768, 768], P('dp', 'ffn'), may hold values from -1.75 to 1.75
- feedfwd_expand_matrix: bfloat16 [768, 3072], P('dp', 'ffn'), may hold values from -0.21875 to 0.21875
- feedfwd_expand_offset: bfloat16 [3072], P('ffn'), may hold values from -3 to 3
- feedfwd_contract_matrix: bfloat16 [3072, 768], P('ffn', 'dp'), may hold values from -0.109375 to 0.109375
- layernorm_scales: bfloat16 [2, 768], P(None, 'dp'), may hold values from 0.25 to 1.75
- offset_vectors: bfloat16 [6, 768], P(None, 'dp'), may hold values from -2 to 2
- learned_gate_scores: bfloat16 [512, 512], P('dp', 'ffn'), may hold values from -5 to 5
- fixed_jitter_matrix: bfloat16 [512, 512], P('dp', 'ffn'), may hold values from -1 to 1
- relaxation_heat: float32 [1], replicated, may hold values from 0.67 to 1
- loss_grad_result: bfloat16 [64, 512, 768], P(('dp', 'ffn')), may hold values from -6 to 6
Outputs:
- outputs: bfloat16 [64, 512, 768], P(('dp', 'ffn'))
- grad_inputs: float32 [64, 512, 768], P(('dp', 'ffn'))
- grad_w_qkv: float32 [768, 2304], P('dp', 'ffn')
- grad_w_out: float32 [768, 768], P('dp', 'ffn')
- grad_w_up: float32 [768, 3072], P('dp', 'ffn')
- grad_b_up: float32 [3072], P('ffn')
- grad_w_down: float32 [3072, 768], P('ffn', 'dp')
- grad_gains: float32 [2, 768], P(None, 'dp')
- grad_shifts: float32 [6, 768], P(None, 'dp')
- grad_logits: float32 [512, 512], P('dp', 'ffn')
The draws below stay inside these ranges and needn't reach their ends.
Inputs may be any that keep to these rules, and one draw needn't show every extreme that they name: `token_counts_each`: number of real tokens of a sequence; the other positions of its 512 are padding, and only key positions are masked; some sequence has exactly 512 and some exactly 64.
All inputs are finite; a program needn't handle non-finite values.
Results may differ from the reference program's by a relative error of at most 0.012.
The reference program's roundings to bfloat16 on the way count: a program that leaves them out, or rounds other values in their place, can miss the bound.
Values may be sent and summed in bfloat16 or wider, within the bound.
A program may use at most 192 MiB of HBM per device.

```python
import math
import jax
import jax.numpy as jnp
from jax import lax

D = 768
HEADS = 12
HEAD_DIM = 64
FF = 3072
SEQ_LEN = 512
MIN_LEN = 64
SEQS = 64


def draw_token_counts_each(key, part):
    drawn = jax.random.randint(key, (SEQS,), MIN_LEN, SEQ_LEN + 1, dtype=jnp.int32)
    drawn = drawn.at[0].set(SEQ_LEN)
    return drawn.at[SEQS - 1].set(MIN_LEN)


def spiked(values, stream_key, source, target, blocks, factor):
    def block_of(position):
        return (jnp.arange(values.shape[position]) // (values.shape[position] // blocks)).reshape((-1,) + (1,) * (values.ndim - 1 - position))

    near = jax.random.permutation(stream_key, blocks)[block_of(target)]
    second = (block_of(target) + blocks // 2) % blocks
    return jnp.where((block_of(source) == near) | (block_of(source) == second), factor * values, values)


def steps_of(key, extent, split, low, largest):
    factor_of, own = 1.0, jax.random.fold_in(key, 6)
    for axis_at, blocks in split:
        steps = jnp.exp(jax.random.uniform(jax.random.fold_in(own, axis_at), (blocks,), jnp.float32, low / len(split), largest / len(split)))
        factor_of = factor_of * jnp.repeat(steps, extent[axis_at] // blocks).reshape([-1 if axis == axis_at else 1 for axis in range(len(extent))])
    return factor_of


def scatter_about(key, dims, scale, reach, pieces=(), kind=jnp.bfloat16):
    values = jax.random.normal(key, dims, jnp.float32) * scale
    if len(pieces) > 0:
        values = steps_of(key, dims, pieces, -0.22, 0.18) * values
    return jnp.clip(values, min=-reach, max=reach).astype(kind)


def gaussian_with(key, extent, deviation, most, cuts, heavy, held_as=jnp.bfloat16):
    values = deviation * jax.random.normal(key, extent, jnp.float32)
    if cuts:
        values = values * steps_of(key, extent, cuts, -0.22, 0.18)
    return jnp.clip(spiked(values, jax.random.fold_in(key, 3), *heavy), -most, most).astype(held_as)


def setup_inputs(seed: int = 0) -> dict:
    seeds = jax.random.split(jax.random.key(seed), 14)
    layer_activations = gaussian_with(seeds[0], (SEQS, SEQ_LEN, D), 1.0, 6.0, ((0, 32),), (0, 2, 32, 2.75))
    token_counts_each = draw_token_counts_each(jax.random.fold_in(seeds[13], 71), 0)
    attention_triple_matrix = scatter_about(seeds[2], (D, 3 * D), D ** -0.5, 0.21875, ((0, 8), (1, 4)))
    attention_final_matrix = scatter_about(seeds[3], (D, D), (max(D // 64, 1)) ** -0.5, 1.75, ((0, 8), (1, 4)))
    feedfwd_expand_matrix = scatter_about(seeds[4], (D, FF), D ** -0.5, 0.21875, ((0, 8), (1, 4)))
    feedfwd_expand_offset = scatter_about(seeds[5], (FF,), 0.5, 3.0, ((0, 4),))
    feedfwd_contract_matrix = scatter_about(seeds[6], (FF, D), FF ** -0.5, 0.109375, ((0, 4), (1, 8)))
    layernorm_scales = jnp.clip(1.0 + 0.15 * jax.random.normal(seeds[7], (2, D), jnp.float32), 0.25, 1.75).astype(jnp.bfloat16)
    offset_vectors = scatter_about(seeds[8], (6, D), 0.3, 2.0, ((1, 8),))
    learned_gate_scores = scatter_about(seeds[9], (SEQ_LEN, SEQ_LEN), 1.0, 5.0, ((0, 8), (1, 4)))
    fixed_jitter_matrix = jnp.clip(jax.random.uniform(seeds[10], (SEQ_LEN, SEQ_LEN), jnp.float32, -1.0, 1.0) * steps_of(seeds[10], (SEQ_LEN, SEQ_LEN), ((0, 8), (1, 4)), -0.4, 0.0), -1.0, 1.0).astype(jnp.bfloat16)
    relaxation_heat = jnp.clip(jax.random.uniform(seeds[11], (1,), jnp.float32, 0.67, 1.0), 0.67, 1.0)
    loss_grad_result = gaussian_with(seeds[12], (SEQS, SEQ_LEN, D), 1.0, 6.0, ((0, 32),), (0, 2, 32, 2.75))
    return dict(layer_activations=layer_activations, token_counts_each=token_counts_each, attention_triple_matrix=attention_triple_matrix, attention_final_matrix=attention_final_matrix, feedfwd_expand_matrix=feedfwd_expand_matrix, feedfwd_expand_offset=feedfwd_expand_offset, feedfwd_contract_matrix=feedfwd_contract_matrix, layernorm_scales=layernorm_scales, offset_vectors=offset_vectors, learned_gate_scores=learned_gate_scores, fixed_jitter_matrix=fixed_jitter_matrix, relaxation_heat=relaxation_heat, loss_grad_result=loss_grad_result)


norm_eps = 1e-06

@jax.custom_vjp
def low(v):
    return lax.optimization_barrier(v.astype(jnp.bfloat16)).astype(jnp.float32)

@jax.custom_vjp
def low_back(v):
    return v

def low_keep(v):
    return (low(v), None)

def low_pass(kept, grad):
    return (grad,)

def back_keep(v):
    return (v, None)

def back_low(kept, grad):
    return (low(grad),)
low.defvjp(low_keep, low_pass)
low_back.defvjp(back_keep, back_low)

def exact_dot(left, right):
    return jnp.dot(left, right, precision=lax.Precision.HIGHEST)

def normalize(values, gain, shift):
    mean_row = lax.optimization_barrier(jnp.mean(values, axis=-1, keepdims=True))
    centered = values - mean_row
    inv_std = lax.rsqrt(lax.optimization_barrier(jnp.mean(centered * centered, axis=-1, keepdims=True)) + norm_eps)
    return centered * inv_std * gain + shift

def evaluate_layer(batch_activations_slice, batch_token_counts, attention_triple_matrix, attention_final_matrix, feedfwd_expand_matrix, feedfwd_expand_offset, feedfwd_contract_matrix, layernorm_scales, offset_vectors, learned_gate_scores, fixed_jitter_matrix, relaxation_heat):
    seq_count = batch_activations_slice.shape[0]
    row_count = seq_count * SEQ_LEN
    flat_in = batch_activations_slice.reshape(row_count, D)
    natural_log_gate = jax.nn.log_sigmoid((learned_gate_scores + fixed_jitter_matrix) / relaxation_heat[0])
    qkv_bias = jnp.concatenate([offset_vectors[0], jnp.zeros((D,), jnp.float32), offset_vectors[1]])
    projected = exact_dot(flat_in, attention_triple_matrix) + qkv_bias
    head_shape = (seq_count, SEQ_LEN, HEADS, HEAD_DIM)
    queries = low_back(low(projected[:, :D])).reshape(head_shape)
    keys_all = low_back(low(projected[:, D:2 * D])).reshape(head_shape)
    values_all = low_back(low(projected[:, 2 * D:])).reshape(head_shape)
    score_scale = HEAD_DIM ** (-0.5)

    def one_sequence(packed):
        seq_queries, seq_keys, seq_values, seq_length = packed
        scores = jnp.einsum('qhd,khd->hqk', seq_queries, seq_keys, precision=lax.Precision.HIGHEST) * score_scale
        scores = low_back(scores) + natural_log_gate
        live = jnp.arange(SEQ_LEN, dtype=jnp.int32) < seq_length
        scores = jnp.where(live[None, None, :], scores, -1e+30)
        probs = low(jax.nn.softmax(scores, axis=-1))
        return jnp.einsum('hqk,khd->qhd', probs, seq_values, precision=lax.Precision.HIGHEST)
    context = lax.map(jax.checkpoint(one_sequence), (queries, keys_all, values_all, batch_token_counts))
    context = low_back(low(context.reshape(row_count, D)))
    first_sum = flat_in + low_back(exact_dot(context, attention_final_matrix)) + offset_vectors[2]
    hidden = normalize(first_sum, layernorm_scales[0], offset_vectors[4])
    hidden_low = low(hidden)
    pre_act = low_back(exact_dot(hidden_low, feedfwd_expand_matrix) + feedfwd_expand_offset)
    act = low(jax.nn.gelu(pre_act, approximate=False))
    ffn_out = low_back(exact_dot(act, feedfwd_contract_matrix))
    second_sum = hidden + ffn_out + offset_vectors[3]
    result = normalize(second_sum, layernorm_scales[1], offset_vectors[5])
    return result.reshape(seq_count, SEQ_LEN, D)

def reference(layer_activations, token_counts_each, attention_triple_matrix, attention_final_matrix, feedfwd_expand_matrix, feedfwd_expand_offset, feedfwd_contract_matrix, layernorm_scales, offset_vectors, learned_gate_scores, fixed_jitter_matrix, relaxation_heat, loss_grad_result):
    params = tuple((item.astype(jnp.float32) for item in (attention_triple_matrix, attention_final_matrix, feedfwd_expand_matrix, feedfwd_expand_offset, feedfwd_contract_matrix, layernorm_scales, offset_vectors, learned_gate_scores)))
    jitter_single_float = fixed_jitter_matrix.astype(jnp.float32)
    relaxation_heat_float = relaxation_heat.astype(jnp.float32)
    seq_total = layer_activations.shape[0]
    group_size = math.gcd(seq_total, max(1, 4096 // SEQ_LEN))
    group_count = seq_total // group_size
    grouped = (layer_activations.reshape(group_count, group_size, SEQ_LEN, D), token_counts_each.reshape(group_count, group_size), loss_grad_result.reshape(group_count, group_size, SEQ_LEN, D))

    def step(carry, packed):
        batch_activations_slice, batch_token_counts, group_cot = packed

        def closed(incoming_entries, *parameter_matrices):
            return evaluate_layer(incoming_entries, batch_token_counts, *parameter_matrices, jitter_single_float, relaxation_heat_float)
        result, pullback = jax.vjp(closed, batch_activations_slice.astype(jnp.float32), *params)
        grads = pullback(group_cot.astype(jnp.float32))
        new_carry = tuple((total + piece for total, piece in zip(carry, grads[1:])))
        return (new_carry, (result.astype(jnp.bfloat16), grads[0]))
    initial = tuple((jnp.zeros_like(item) for item in params))
    totals, stacked = lax.scan(step, initial, grouped)
    results, grad_in = stacked
    return (results.reshape(layer_activations.shape), grad_in.reshape(layer_activations.shape), totals[0], totals[1], totals[2], totals[3], totals[4], totals[5], totals[6], totals[7])
```

```python
import jax
import jax.numpy as jnp
from jax import lax
from jax.sharding import PartitionSpec as P

D = 768
HEADS = 12
HEAD_DIM = 64
SEQ_LEN = 512
AXES = ("dp", "ffn")
norm_eps = 1e-06
f32 = jnp.float32
bf16 = jnp.bfloat16


def dot_first(left, right):
    return lax.dot_general(left, right, (((0,), (0,)), ((), ())), preferred_element_type=f32)


def dot_last(left, right):
    return lax.dot_general(left, right, (((1,), (1,)), ((), ())), preferred_element_type=f32)


def dot(left, right):
    return jnp.dot(left, right, preferred_element_type=f32)


def layer_norm(values, gain, shift):
    mean_row = jnp.mean(values, axis=-1, keepdims=True)
    centered = values - mean_row
    inv_std = lax.rsqrt(jnp.mean(centered * centered, axis=-1, keepdims=True) + norm_eps)
    normed = centered * inv_std
    return (normed * gain + shift, normed, inv_std)


def norm_back(grad_out, normed, inv_std, gain):
    grad_normed = grad_out * gain
    grad_in = inv_std * (
        grad_normed
        - jnp.mean(grad_normed, axis=-1, keepdims=True)
        - normed * jnp.mean(grad_normed * normed, axis=-1, keepdims=True)
    )
    return (grad_in, jnp.sum(grad_out * normed, axis=0), jnp.sum(grad_out, axis=0))


def gelu_slope(values):
    return (
        0.5 * (1.0 + lax.erf(values * 0.7071067811865476))
        + values * jnp.exp(-0.5 * values * values) * 0.3989422804014327
    )


def score_block(queries, keys_low, natural_log_gate, live):
    scores = (
        jnp.einsum("qhd,khd->hqk", queries, keys_low, preferred_element_type=f32)
        * HEAD_DIM ** (-0.5)
        + natural_log_gate
    )
    return jnp.where(live[None, None, :], scores, -1e30)


def attend(queries, keys_low, values_low, natural_log_gate, live):
    scores = score_block(queries, keys_low, natural_log_gate, live)
    peak = jnp.max(scores, axis=-1, keepdims=True)
    shifted_exp = jnp.exp(scores - peak)
    total_exp = jnp.sum(shifted_exp, axis=-1, keepdims=True)
    probs_low = (shifted_exp / total_exp).astype(bf16)
    context = jnp.einsum("hqk,khd->qhd", probs_low, values_low, preferred_element_type=f32)
    return (context, peak + jnp.log(total_exp))


def attend_back(queries, keys_low, values_low, natural_log_gate, live, log_total, grad_context):
    scores = score_block(queries, keys_low, natural_log_gate, live)
    probs = jnp.exp(scores - log_total)
    grad_probs = jnp.einsum("qhd,khd->hqk", grad_context, values_low, preferred_element_type=f32)
    grad_values = jnp.einsum(
        "hqk,qhd->khd", probs.astype(bf16), grad_context, preferred_element_type=f32
    )
    grad_scores = probs * (grad_probs - jnp.sum(probs * grad_probs, axis=-1, keepdims=True))
    grad_mask = jnp.sum(grad_scores, axis=0)
    grad_scores_low = grad_scores.astype(bf16)
    grad_queries = jnp.einsum(
        "hqk,khd->qhd", grad_scores_low, keys_low, preferred_element_type=f32
    ) * HEAD_DIM ** (-0.5)
    grad_keys = jnp.einsum(
        "hqk,qhd->khd", grad_scores_low, queries, preferred_element_type=f32
    ) * HEAD_DIM ** (-0.5)
    return (grad_queries, grad_keys, grad_values, grad_mask)


def gather_weights(pack, small):
    rows_dp = lax.axis_size("dp")
    cols_ffn = lax.axis_size("ffn")
    full = lax.all_gather(pack[None], AXES, axis=0, tiled=True)
    full = full.reshape(rows_dp, cols_ffn, *pack.shape)
    small_full = lax.all_gather(small[None], AXES, axis=0, tiled=True)
    return full, small_full.reshape(rows_dp, cols_ffn, *small.shape)


def columns(blocks):
    rows_dp, cols_ffn, rows, cols = blocks.shape
    return blocks.transpose(0, 2, 1, 3).reshape(rows_dp * rows, cols_ffn * cols)


def blocks_of(full, rows_dp, cols_ffn):
    rows, cols = full.shape
    return full.reshape(rows_dp, rows // rows_dp, cols_ffn, cols // cols_ffn).transpose(0, 2, 1, 3)


def on_device(
    layer_activations,
    token_counts_each,
    attention_triple_matrix,
    attention_final_matrix,
    feedfwd_expand_matrix,
    feedfwd_expand_offset,
    feedfwd_contract_matrix,
    layernorm_scales,
    offset_vectors,
    learned_gate_scores,
    fixed_jitter_matrix,
    relaxation_heat,
    loss_grad_result,
):
    rows_dp = lax.axis_size("dp")
    cols_ffn = lax.axis_size("ffn")
    seq_count = layer_activations.shape[0]
    row_count = seq_count * SEQ_LEN
    shard_rows = attention_triple_matrix.shape[0]
    qkv_cols = attention_triple_matrix.shape[1]
    out_cols = attention_final_matrix.shape[1]
    ff_cols = feedfwd_expand_matrix.shape[1]

    pack = jnp.concatenate(
        [
            attention_triple_matrix,
            attention_final_matrix,
            feedfwd_expand_matrix,
            feedfwd_contract_matrix.T,
        ],
        axis=1,
    )
    mask_cols = learned_gate_scores.shape[1]
    vectors = jnp.concatenate([layernorm_scales, offset_vectors], axis=0)
    small = jnp.concatenate(
        [
            learned_gate_scores,
            fixed_jitter_matrix,
            jnp.pad(vectors, ((0, 0), (0, mask_cols - vectors.shape[1]))),
            feedfwd_expand_offset.reshape(-1, mask_cols),
        ],
        axis=0,
    )
    full, small_full = gather_weights(pack, small)
    full_qkv = columns(full[..., :qkv_cols])
    full_out = columns(full[..., qkv_cols : qkv_cols + out_cols])
    full_up = columns(full[..., qkv_cols + out_cols : qkv_cols + out_cols + ff_cols])
    full_down_t = columns(full[..., qkv_cols + out_cols + ff_cols :])
    mask_rows = learned_gate_scores.shape[0]
    logits_sum = columns(small_full[:, :, :mask_rows]).astype(f32) + columns(
        small_full[:, :, mask_rows : 2 * mask_rows]
    ).astype(f32)
    natural_log_gate = jax.nn.log_sigmoid(logits_sum / relaxation_heat[0])
    vectors_full = (
        small_full[:, 0, 2 * mask_rows : 2 * mask_rows + 8, :shard_rows]
        .transpose(1, 0, 2)
        .reshape(8, D)
        .astype(f32)
    )
    gains_full = vectors_full[:2]
    shifts_full = vectors_full[2:]
    bias_up = small_full[0, :, 2 * mask_rows + 8 :].reshape(1, -1).astype(f32)

    flat_in = layer_activations.reshape(row_count, D)
    qkv_bias = jnp.concatenate([shifts_full[0], jnp.zeros((D,), f32), shifts_full[1]])
    proj_low = (dot(flat_in, full_qkv) + qkv_bias).astype(bf16)
    head_shape = (seq_count, SEQ_LEN, HEADS, HEAD_DIM)
    queries = proj_low[:, :D].reshape(head_shape)
    keys_low = proj_low[:, D : 2 * D].reshape(head_shape)
    values_low = proj_low[:, 2 * D :].reshape(head_shape)
    live = lax.broadcasted_iota(jnp.int32, (seq_count, SEQ_LEN), 1) < token_counts_each[:, None]
    attended = [
        attend(queries[s], keys_low[s], values_low[s], natural_log_gate, live[s])
        for s in range(seq_count)
    ]
    context_low = jnp.concatenate(
        [item[0].reshape(SEQ_LEN, D).astype(bf16) for item in attended], axis=0
    )
    first_sum = flat_in.astype(f32) + dot(context_low, full_out) + shifts_full[2]
    hidden, normed_one, inv_one = layer_norm(first_sum, gains_full[0], shifts_full[4])
    hidden_low = hidden.astype(bf16)
    pre_act = dot(hidden_low, full_up) + bias_up
    act_low = jax.nn.gelu(pre_act, approximate=False).astype(bf16)
    second_sum = hidden + dot_last(act_low, full_down_t) + shifts_full[3]
    result, normed_two, inv_two = layer_norm(second_sum, gains_full[1], shifts_full[5])
    cot_flat = loss_grad_result.reshape(row_count, D).astype(f32)
    grad_second, grad_gain_two, grad_shift_two = norm_back(
        cot_flat, normed_two, inv_two, gains_full[1]
    )
    grad_second_low = grad_second.astype(bf16)
    grad_w_down_t = dot_first(grad_second_low, act_low)
    grad_act = dot(grad_second_low, full_down_t)
    grad_pre = (grad_act * gelu_slope(pre_act)).astype(bf16)
    grad_bias_up = jnp.sum(grad_pre, axis=0, dtype=f32)
    grad_w_up = dot_first(hidden_low, grad_pre)
    grad_hidden = grad_second + dot_last(grad_pre, full_up)
    grad_first, grad_gain_one, grad_shift_one = norm_back(
        grad_hidden, normed_one, inv_one, gains_full[0]
    )
    grad_first_low = grad_first.astype(bf16)
    grad_w_out = dot_first(context_low, grad_first_low)
    grad_context = dot_last(grad_first_low, full_out).astype(bf16).reshape(head_shape)
    back = [
        attend_back(
            queries[s],
            keys_low[s],
            values_low[s],
            natural_log_gate,
            live[s],
            attended[s][1],
            grad_context[s],
        )
        for s in range(seq_count)
    ]
    grad_mask = sum(item[3] for item in back)
    grad_projected = jnp.concatenate(
        [
            jnp.concatenate(
                [item[part].reshape(SEQ_LEN, D).astype(bf16) for item in back], axis=0
            )
            for part in range(3)
        ],
        axis=1,
    )
    grad_w_qkv = dot_first(flat_in, grad_projected)
    grad_inputs = grad_first + dot_last(grad_projected, full_qkv)
    grad_vectors = jnp.stack(
        [
            grad_gain_one,
            grad_gain_two,
            jnp.sum(grad_projected[:, :D], axis=0, dtype=f32),
            jnp.sum(grad_projected[:, 2 * D :], axis=0, dtype=f32),
            jnp.sum(grad_first, axis=0),
            jnp.sum(grad_second, axis=0),
            grad_shift_one,
            grad_shift_two,
        ]
    )
    big = jnp.concatenate(
        [
            blocks_of(item, rows_dp, cols_ffn)
            for item in (grad_w_qkv, grad_w_out, grad_w_up, grad_w_down_t)
        ],
        axis=-1,
    ).reshape(rows_dp * cols_ffn, shard_rows, -1)
    vector_blocks = jnp.broadcast_to(
        grad_vectors.reshape(8, rows_dp, 1, shard_rows).transpose(1, 2, 0, 3),
        (rows_dp, cols_ffn, 8, shard_rows),
    )
    bias_blocks = jnp.broadcast_to(
        grad_bias_up.reshape(1, cols_ffn, -1, mask_cols),
        (rows_dp, cols_ffn, ff_cols // mask_cols, mask_cols),
    )
    little = jnp.concatenate(
        [
            blocks_of(grad_mask, rows_dp, cols_ffn),
            jnp.pad(vector_blocks, ((0, 0), (0, 0), (0, 0), (0, mask_cols - shard_rows))),
            bias_blocks,
        ],
        axis=2,
    ).reshape(rows_dp * cols_ffn, -1, mask_cols)
    big = lax.psum_scatter(big, AXES, scatter_dimension=0, tiled=True)[0]
    little = lax.psum_scatter(little, AXES, scatter_dimension=0, tiled=True)[0]

    own_mixed = (
        learned_gate_scores.astype(f32) + fixed_jitter_matrix.astype(f32)
    ) / relaxation_heat[0]
    grad_logits = little[:mask_rows] * (jax.nn.sigmoid(-own_mixed) / relaxation_heat[0])
    return (
        result.astype(bf16).reshape(layer_activations.shape),
        grad_inputs.reshape(layer_activations.shape),
        big[:, :qkv_cols],
        big[:, qkv_cols : qkv_cols + out_cols],
        big[:, qkv_cols + out_cols : qkv_cols + out_cols + ff_cols],
        little[mask_rows + 8 :].reshape(-1),
        big[:, qkv_cols + out_cols + ff_cols :].T,
        little[mask_rows : mask_rows + 2, :shard_rows],
        little[mask_rows + 2 : mask_rows + 8, :shard_rows],
        grad_logits,
    )


def solution(mesh):
    in_specs = (
        P(AXES, None, None),
        P(AXES),
        P("dp", "ffn"),
        P("dp", "ffn"),
        P("dp", "ffn"),
        P("ffn"),
        P("ffn", "dp"),
        P(None, "dp"),
        P(None, "dp"),
        P("dp", "ffn"),
        P("dp", "ffn"),
        P(),
        P(AXES, None, None),
    )
    out_specs = (
        P(AXES, None, None),
        P(AXES, None, None),
        P("dp", "ffn"),
        P("dp", "ffn"),
        P("dp", "ffn"),
        P("ffn"),
        P("ffn", "dp"),
        P(None, "dp"),
        P(None, "dp"),
        P("dp", "ffn"),
    )
    return jax.shard_map(
        on_device, mesh=mesh, in_specs=in_specs, out_specs=out_specs, check_vma=False
    )
```

```python
import jax
import jax.numpy as jnp
from jax import lax
from jax.experimental import pallas as pl
from jax.experimental.pallas import tpu as pltpu
from jax.sharding import PartitionSpec as P

D = 768
HEADS = 12
HEAD_DIM = 64
SEQ_LEN = 512
AXES = ("dp", "ffn")
norm_eps = 1e-06
f32 = jnp.float32
bf16 = jnp.bfloat16
MESH = pl.DeviceIdType.MESH


def dot_first(left, right):
    return lax.dot_general(left, right, (((0,), (0,)), ((), ())), preferred_element_type=f32)


def dot_last(left, right):
    return lax.dot_general(left, right, (((1,), (1,)), ((), ())), preferred_element_type=f32)


def dot(left, right):
    return jnp.dot(left, right, preferred_element_type=f32)


def layer_norm(values, gain, shift):
    mean_row = jnp.mean(values, axis=-1, keepdims=True)
    centered = values - mean_row
    inv_std = lax.rsqrt(jnp.mean(centered * centered, axis=-1, keepdims=True) + norm_eps)
    normed = centered * inv_std
    return (normed * gain + shift, normed, inv_std)


def norm_back(grad_out, normed, inv_std, gain):
    grad_normed = grad_out * gain
    grad_in = inv_std * (
        grad_normed
        - jnp.mean(grad_normed, axis=-1, keepdims=True)
        - normed * jnp.mean(grad_normed * normed, axis=-1, keepdims=True)
    )
    return (grad_in, jnp.sum(grad_out * normed, axis=0), jnp.sum(grad_out, axis=0))


def gelu_slope(values):
    return (
        0.5 * (1.0 + lax.erf(values * 0.7071067811865476))
        + values * jnp.exp(-0.5 * values * values) * 0.3989422804014327
    )


def score_block(queries, keys_low, natural_log_gate, live):
    scores = (
        jnp.einsum("qhd,khd->hqk", queries, keys_low, preferred_element_type=f32)
        * HEAD_DIM ** (-0.5)
        + natural_log_gate
    )
    return jnp.where(live[None, None, :], scores, -1e30)


def attend(queries, keys_low, values_low, natural_log_gate, live):
    scores = score_block(queries, keys_low, natural_log_gate, live)
    peak = jnp.max(scores, axis=-1, keepdims=True)
    shifted_exp = jnp.exp(scores - peak)
    total_exp = jnp.sum(shifted_exp, axis=-1, keepdims=True)
    probs_low = (shifted_exp / total_exp).astype(bf16)
    context = jnp.einsum("hqk,khd->qhd", probs_low, values_low, preferred_element_type=f32)
    return (context, peak + jnp.log(total_exp))


def attend_back(queries, keys_low, values_low, natural_log_gate, live, log_total, grad_context):
    scores = score_block(queries, keys_low, natural_log_gate, live)
    probs = jnp.exp(scores - log_total)
    grad_probs = jnp.einsum("qhd,khd->hqk", grad_context, values_low, preferred_element_type=f32)
    grad_values = jnp.einsum(
        "hqk,qhd->khd", probs.astype(bf16), grad_context, preferred_element_type=f32
    )
    grad_scores = probs * (grad_probs - jnp.sum(probs * grad_probs, axis=-1, keepdims=True))
    grad_mask = jnp.sum(grad_scores, axis=0)
    grad_scores_low = grad_scores.astype(bf16)
    grad_queries = jnp.einsum(
        "hqk,khd->qhd", grad_scores_low, keys_low, preferred_element_type=f32
    ) * HEAD_DIM ** (-0.5)
    grad_keys = jnp.einsum(
        "hqk,qhd->khd", grad_scores_low, queries, preferred_element_type=f32
    ) * HEAD_DIM ** (-0.5)
    return (grad_queries, grad_keys, grad_values, grad_mask)


def partners():
    i = lax.axis_index("dp"); f = lax.axis_index("ffn")
    c = i % 2
    x = (i // 2) % 2
    core = i + 1 - 2 * c
    ix = i + 2 - 4 * x
    iy = (i + 4) % 8
    idg = (ix + 4) % 8
    return i, f, core, ix, iy, idg

class Gather:
    NS = 19
    def __init__(self, src, dst, ssem, rsem, lsem):
        self.src, self.dst, self.ssem, self.rsem, self.lsem = src, dst, ssem, rsem, lsem
        self.rows = src.shape[0]
        self.me = partners()
        self.pending = []
    def piece(self, i, p):
        return self.dst.at[p, pl.ds(i * self.rows, self.rows)]
    def block(self, i):
        return self.dst.at[:, pl.ds(i * self.rows, self.rows)]
    def remote(self, src, dst, n, to):
        return pltpu.make_async_remote_copy(src_ref=src, dst_ref=dst, send_sem=self.ssem.at[n], recv_sem=self.rsem.at[n], device_id=to, device_id_type=MESH)
    def send(self, src, dst, n, to):
        cp = self.remote(src, dst, n, to)
        cp.start()
        self.pending.append(cp)
    def recv(self, ref, n):
        i, f, *_ = self.me
        self.remote(ref, ref, n, (i, f)).wait_recv()
    def s0(self):
        i, f, core, ix, iy, idg = self.me
        own = self.piece(i, f)
        cp = pltpu.make_async_copy(self.src, own, self.lsem)
        cp.start()
        self.local = cp
        for k in (1, 2, 3):
            self.send(self.src, own, 3 - k, (i, (f + k) % 4))
        self.send(self.src, own, 3, (ix, f))
        self.send(self.src, own, 7, (iy, f))
    def s1(self):
        i, f, core, ix, iy, idg = self.me
        for k in (1, 2, 3):
            p = (f + k) % 4
            ref = self.piece(i, p)
            self.recv(ref, k - 1)
            self.send(ref, ref, 3 + k, (ix, f))
            self.send(ref, ref, 7 + k, (iy, f))
        self.local.wait()
        blk = self.block(i)
        self.send(blk, blk, 15, (core, f))
    def s2(self):
        i, f, core, ix, iy, idg = self.me
        for k in range(4):
            p = (f + k) % 4
            rx = self.piece(ix, p); ry = self.piece(iy, p)
            self.recv(rx, 3 + k)
            if k % 2: self.send(rx, rx, 11 + k, (iy, f))
            self.recv(ry, 7 + k)
            if k % 2 == 0: self.send(ry, ry, 11 + k, (ix, f))
        bx = self.block(ix); by = self.block(iy)
        self.send(bx, bx, 16, (core, f))
        self.send(by, by, 17, (core, f))
    def s3(self):
        i, f, core, ix, iy, idg = self.me
        for k in range(4):
            self.recv(self.piece(idg, (f + k) % 4), 11 + k)
        b = self.block(idg)
        self.send(b, b, 18, (core, f))
    def s4(self):
        i, f, core, ix, iy, idg = self.me
        co = lambda v: v + 1 - 2 * (i % 2)
        for n, b in ((15, i), (16, ix), (17, iy), (18, idg)):
            self.recv(self.block(co(b)), n)
    def finish(self):
        for cp in self.pending:
            cp.wait_send()

def barrier():
    i, f, core, ix, iy, idg = partners()
    b = pltpu.get_barrier_semaphore()
    for to in ((i, (f + 1) % 4), (i, (f + 2) % 4), (i, (f + 3) % 4), (core, f), (ix, f), (iy, f)):
        pl.semaphore_signal(b, inc=1, device_id=to, device_id_type=MESH)
    pl.semaphore_wait(b, 6)

def ag_kernel(pack, small, wfull, sfull, ssem, rsem, lsem):
    barrier()
    gs = [Gather(small, sfull, ssem.at[0], rsem.at[0], lsem.at[0])]
    for g in range(3):
        gs.append(Gather(pack.at[g], wfull.at[g], ssem.at[1 + g], rsem.at[1 + g], lsem.at[1 + g]))
    S, A, U, Dn = gs
    S.s0(); A.s0()
    S.s1(); A.s1(); U.s0()
    S.s2(); A.s2(); U.s1(); Dn.s0()
    S.s3(); A.s3(); U.s2(); Dn.s1()
    S.s4(); A.s4()
    U.s3(); Dn.s2(); U.s4(); Dn.s3(); Dn.s4()
    for g in gs: g.finish()

def ag_call(pack, small):
    _, rows, cols = pack.shape
    srows, scols = small.shape
    any_ = pl.BlockSpec(memory_space=pl.ANY)
    return pl.pallas_call(
        ag_kernel,
        out_shape=(jax.ShapeDtypeStruct((3, 4, rows * 8, cols), bf16), jax.ShapeDtypeStruct((4, 8 * srows, scols), bf16)),
        in_specs=[any_] * 2, out_specs=(any_, any_),
        scratch_shapes=[pltpu.SemaphoreType.DMA((4, 19)), pltpu.SemaphoreType.DMA((4, 19)), pltpu.SemaphoreType.DMA((4,))],
        compiler_params=pltpu.CompilerParams(collective_id=0, has_side_effects=True),
        name="gather_weights",
    )(pack, small)

class Scatter:
    NS = 19
    def __init__(self, part, rc, rq, rx, ry, rz, out, ssem, rsem):
        self.part, self.rc, self.rq, self.rx, self.ry, self.rz, self.out = part, rc, rq, rx, ry, rz, out
        self.ssem, self.rsem = ssem, rsem
        self.rows = part.shape[1] // 8
        self.me = partners()
        self.pending = []
    def piece(self, i, p):
        return self.part.at[p, pl.ds(pl.multiple_of(i * self.rows, self.rows), self.rows)]
    def block(self, i):
        return self.part.at[:, pl.ds(pl.multiple_of(i * self.rows, self.rows), self.rows)]
    def send(self, src, dst, n, to):
        cp = pltpu.make_async_remote_copy(src_ref=src, dst_ref=dst, send_sem=self.ssem.at[n], recv_sem=self.rsem.at[n], device_id=to, device_id_type=MESH)
        cp.start()
        self.pending.append(cp)
    def recv(self, ref, n):
        i, f, *_ = self.me
        pltpu.make_async_remote_copy(src_ref=ref, dst_ref=ref, send_sem=self.ssem.at[n], recv_sem=self.rsem.at[n], device_id=(i, f), device_id_type=MESH).wait_recv()
    def r0(self):
        i, f, core, ix, iy, idg = self.me
        d = core - i
        for n, b in ((3, idg), (1, ix), (2, iy), (0, i)):
            self.send(self.block(b + d), self.rc.at[n], n, (core, f))
    def add_core(self, n, b, ks=(0, 1, 2, 3)):
        f = self.me[1]
        for k in ks:
            p = (f + k) % 4
            ref = self.piece(b, p)
            ref[...] = (ref[...].astype(f32) + self.rc[n, p].astype(f32)).astype(ref.dtype)
    def r1(self):
        i, f, core, ix, iy, idg = self.me
        self.recv(self.rc.at[3], 3)
        self.add_core(3, idg)
        for k in range(4):
            self.send(self.piece(idg, (f + k) % 4), self.rq.at[k], 4 + k, (iy if k % 2 else ix, f))
        self.recv(self.rc.at[1], 1)
        self.add_core(1, ix)
        for k in (0, 2):
            self.send(self.piece(ix, (f + k) % 4), self.rx.at[k], 8 + k, (ix, f))
        self.recv(self.rc.at[2], 2)
        self.add_core(2, iy)
        for k in (1, 3):
            self.send(self.piece(iy, (f + k) % 4), self.ry.at[k], 12 + k, (iy, f))
        self.recv(self.rc.at[0], 0)
        self.add_core(0, i)
    def r2(self):
        i, f, core, ix, iy, idg = self.me
        for k in range(4):
            self.recv(self.rq.at[k], 4 + k)
            b = ix if k % 2 else iy
            ref = self.piece(b, (f + k) % 4)
            ref[...] = (ref[...].astype(f32) + self.rq[k].astype(f32)).astype(ref.dtype)
            if k % 2:
                self.send(ref, self.rx.at[k], 8 + k, (ix, f))
            else:
                self.send(ref, self.ry.at[k], 12 + k, (iy, f))
    def r3(self):
        i, f, core, ix, iy, idg = self.me
        for k in (1, 2, 3, 0):
            self.recv(self.rx.at[k], 8 + k)
            self.recv(self.ry.at[k], 12 + k)
            ref = self.piece(i, (f + k) % 4)
            total = ref[...].astype(f32) + self.rx[k].astype(f32) + self.ry[k].astype(f32)
            if k:
                ref[...] = total.astype(ref.dtype)
                self.send(ref, self.rz.at[3 - k], 19 - k, (i, (f + k) % 4))
            else:
                self.out[...] = total
    def r4(self):
        for k in range(3):
            self.recv(self.rz.at[k], 16 + k)
        self.out[...] = self.out[...] + self.rz[0].astype(f32) + self.rz[1].astype(f32) + self.rz[2].astype(f32)
    def finish(self):
        for cp in self.pending:
            cp.wait_send()

def scatter_scratch(rows, cols, dt):
    return [pltpu.VMEM((4, 4, rows, cols), dt), pltpu.VMEM((4, rows, cols), dt), pltpu.VMEM((4, rows, cols), dt), pltpu.VMEM((4, rows, cols), dt), pltpu.VMEM((3, rows, cols), dt)]

def rs_kernel(big, little, obig, olit, part, lpart, rc, rq, rx, ry, rz, lrc, lrq, lrx, lry, lrz, ssem, rsem, lsem):
    cps = []
    for g, (s, d) in enumerate(((big.at[0], part.at[0]), (big.at[1], part.at[1]), (big.at[2], part.at[2]), (little, lpart))):
        cp = pltpu.make_async_copy(s, d, lsem.at[g]); cp.start(); cps.append(cp)
    barrier()
    G = [Scatter(part.at[g], rc.at[g], rq.at[g], rx.at[g], ry.at[g], rz.at[g], obig.at[g], ssem.at[g], rsem.at[g]) for g in range(3)]
    L = Scatter(lpart, lrc, lrq, lrx, lry, lrz, olit, ssem.at[3], rsem.at[3])
    G.append(L)
    for n in range(4 + 4):
        for g in range(4):
            st = n - g
            if st == 0: cps[g].wait()
            if 0 <= st <= 4: (G[g].r0, G[g].r1, G[g].r2, G[g].r3, G[g].r4)[st]()
    for g in G: g.finish()

def rs_call(big, little):
    _, _, r8, cols = big.shape
    rows = r8 // 8
    lrows, lcols = little.shape[1] // 8, little.shape[2]
    vm = pl.BlockSpec(memory_space=pltpu.VMEM)
    any_ = pl.BlockSpec(memory_space=pl.ANY)
    v3 = [pltpu.VMEM((3,) + s.shape, s.dtype) for s in [pltpu.VMEM((4, 4, rows, cols), bf16), pltpu.VMEM((4, rows, cols), bf16), pltpu.VMEM((4, rows, cols), bf16), pltpu.VMEM((4, rows, cols), bf16), pltpu.VMEM((3, rows, cols), bf16)]]
    return pl.pallas_call(
        rs_kernel,
        out_shape=(jax.ShapeDtypeStruct((3, rows, cols), f32), jax.ShapeDtypeStruct((lrows, lcols), f32)),
        in_specs=[any_, any_], out_specs=(vm, vm),
        scratch_shapes=[pltpu.VMEM(big.shape, bf16), pltpu.VMEM(little.shape, f32)] + v3 + scatter_scratch(lrows, lcols, f32)
            + [pltpu.SemaphoreType.DMA((4, 19)), pltpu.SemaphoreType.DMA((4, 19)), pltpu.SemaphoreType.DMA((4,))],
        compiler_params=pltpu.CompilerParams(collective_id=1, has_side_effects=True, vmem_limit_bytes=60 << 20),
        name="reduce_gradients",
    )(big, little)


def gather_weights(pack, small):
    rows_dp = lax.axis_size("dp")
    cols_ffn = lax.axis_size("ffn")
    if (rows_dp, cols_ffn) == (8, 4):
        rows, cols = pack.shape
        packs = pack.reshape(rows, 3, cols // 3).transpose(1, 0, 2)
        fill = -small.shape[0] % 16
        full, small_full = ag_call(packs, jnp.pad(small, ((0, fill), (0, 0))))
        full = full.reshape(3, 4, 8, rows, cols // 3).transpose(2, 1, 3, 0, 4)
        small_full = small_full.reshape(4, 8, -1, small.shape[1]).transpose(1, 0, 2, 3)
        return full.reshape(8, 4, rows, cols), small_full[:, :, : small.shape[0]]
    full = lax.all_gather(pack[None], AXES, axis=0, tiled=True)
    full = full.reshape(rows_dp, cols_ffn, *pack.shape)
    small_full = lax.all_gather(small[None], AXES, axis=0, tiled=True)
    return full, small_full.reshape(rows_dp, cols_ffn, *small.shape)


def columns(blocks):
    rows_dp, cols_ffn, rows, cols = blocks.shape
    return blocks.transpose(0, 2, 1, 3).reshape(rows_dp * rows, cols_ffn * cols)


def blocks_of(full, rows_dp, cols_ffn):
    rows, cols = full.shape
    return full.reshape(rows_dp, rows // rows_dp, cols_ffn, cols // cols_ffn).transpose(0, 2, 1, 3)


def reduce_gradients(big, little, rows_dp, cols_ffn):
    if (rows_dp, cols_ffn) == (8, 4):
        rows, cols = big.shape[1:]
        parts = big.astype(bf16).reshape(8, 4, rows, 3, cols // 3).transpose(3, 1, 0, 2, 4)
        little_rows = little.shape[1]
        little = jnp.pad(little, ((0, 0), (0, -little_rows % 8), (0, 0)))
        little_parts = little.reshape(8, 4, *little.shape[1:]).transpose(1, 0, 2, 3)
        big, little = rs_call(
            parts.reshape(3, 4, 8 * rows, cols // 3),
            little_parts.reshape(4, -1, little.shape[2]),
        )
        return big.transpose(1, 0, 2).reshape(rows, cols), little[:little_rows]
    return (
        lax.psum_scatter(big, AXES, scatter_dimension=0, tiled=True)[0],
        lax.psum_scatter(little, AXES, scatter_dimension=0, tiled=True)[0],
    )


def on_device(
    layer_activations,
    token_counts_each,
    attention_triple_matrix,
    attention_final_matrix,
    feedfwd_expand_matrix,
    feedfwd_expand_offset,
    feedfwd_contract_matrix,
    layernorm_scales,
    offset_vectors,
    learned_gate_scores,
    fixed_jitter_matrix,
    relaxation_heat,
    loss_grad_result,
):
    rows_dp = lax.axis_size("dp")
    cols_ffn = lax.axis_size("ffn")
    seq_count = layer_activations.shape[0]
    row_count = seq_count * SEQ_LEN
    shard_rows = attention_triple_matrix.shape[0]
    qkv_cols = attention_triple_matrix.shape[1]
    out_cols = attention_final_matrix.shape[1]
    ff_cols = feedfwd_expand_matrix.shape[1]

    pack = jnp.concatenate(
        [
            attention_triple_matrix,
            attention_final_matrix,
            feedfwd_expand_matrix,
            feedfwd_contract_matrix.T,
        ],
        axis=1,
    )
    mask_cols = learned_gate_scores.shape[1]
    vectors = jnp.concatenate([layernorm_scales, offset_vectors], axis=0)
    small = jnp.concatenate(
        [
            learned_gate_scores,
            fixed_jitter_matrix,
            jnp.pad(vectors, ((0, 0), (0, mask_cols - vectors.shape[1]))),
            feedfwd_expand_offset.reshape(-1, mask_cols),
        ],
        axis=0,
    )
    full, small_full = gather_weights(pack, small)
    full_qkv = columns(full[..., :qkv_cols])
    full_out = columns(full[..., qkv_cols : qkv_cols + out_cols])
    full_up = columns(full[..., qkv_cols + out_cols : qkv_cols + out_cols + ff_cols])
    full_down_t = columns(full[..., qkv_cols + out_cols + ff_cols :])
    mask_rows = learned_gate_scores.shape[0]
    logits_sum = columns(small_full[:, :, :mask_rows]).astype(f32) + columns(
        small_full[:, :, mask_rows : 2 * mask_rows]
    ).astype(f32)
    natural_log_gate = jax.nn.log_sigmoid(logits_sum / relaxation_heat[0])
    vectors_full = (
        small_full[:, 0, 2 * mask_rows : 2 * mask_rows + 8, :shard_rows]
        .transpose(1, 0, 2)
        .reshape(8, D)
        .astype(f32)
    )
    gains_full = vectors_full[:2]
    shifts_full = vectors_full[2:]
    bias_up = small_full[0, :, 2 * mask_rows + 8 :].reshape(1, -1).astype(f32)

    flat_in = layer_activations.reshape(row_count, D)
    qkv_bias = jnp.concatenate([shifts_full[0], jnp.zeros((D,), f32), shifts_full[1]])
    proj_low = (dot(flat_in, full_qkv) + qkv_bias).astype(bf16)
    head_shape = (seq_count, SEQ_LEN, HEADS, HEAD_DIM)
    queries = proj_low[:, :D].reshape(head_shape)
    keys_low = proj_low[:, D : 2 * D].reshape(head_shape)
    values_low = proj_low[:, 2 * D :].reshape(head_shape)
    live = lax.broadcasted_iota(jnp.int32, (seq_count, SEQ_LEN), 1) < token_counts_each[:, None]
    attended = [
        attend(queries[s], keys_low[s], values_low[s], natural_log_gate, live[s])
        for s in range(seq_count)
    ]
    context_low = jnp.concatenate(
        [item[0].reshape(SEQ_LEN, D).astype(bf16) for item in attended], axis=0
    )
    first_sum = flat_in.astype(f32) + dot(context_low, full_out) + shifts_full[2]
    hidden, normed_one, inv_one = layer_norm(first_sum, gains_full[0], shifts_full[4])
    hidden_low = hidden.astype(bf16)
    pre_act = dot(hidden_low, full_up) + bias_up
    act_low = jax.nn.gelu(pre_act, approximate=False).astype(bf16)
    second_sum = hidden + dot_last(act_low, full_down_t) + shifts_full[3]
    result, normed_two, inv_two = layer_norm(second_sum, gains_full[1], shifts_full[5])
    cot_flat = loss_grad_result.reshape(row_count, D).astype(f32)
    grad_second, grad_gain_two, grad_shift_two = norm_back(
        cot_flat, normed_two, inv_two, gains_full[1]
    )
    grad_second_low = grad_second.astype(bf16)
    grad_w_down_t = dot_first(grad_second_low, act_low)
    grad_act = dot(grad_second_low, full_down_t)
    grad_pre = (grad_act * gelu_slope(pre_act)).astype(bf16)
    grad_bias_up = jnp.sum(grad_pre, axis=0, dtype=f32)
    grad_w_up = dot_first(hidden_low, grad_pre)
    grad_hidden = grad_second + dot_last(grad_pre, full_up)
    grad_first, grad_gain_one, grad_shift_one = norm_back(
        grad_hidden, normed_one, inv_one, gains_full[0]
    )
    grad_first_low = grad_first.astype(bf16)
    grad_w_out = dot_first(context_low, grad_first_low)
    grad_context = dot_last(grad_first_low, full_out).astype(bf16).reshape(head_shape)
    back = [
        attend_back(
            queries[s],
            keys_low[s],
            values_low[s],
            natural_log_gate,
            live[s],
            attended[s][1],
            grad_context[s],
        )
        for s in range(seq_count)
    ]
    grad_mask = sum(item[3] for item in back)
    grad_projected = jnp.concatenate(
        [
            jnp.concatenate(
                [item[part].reshape(SEQ_LEN, D).astype(bf16) for item in back], axis=0
            )
            for part in range(3)
        ],
        axis=1,
    )
    grad_w_qkv = dot_first(flat_in, grad_projected)
    grad_inputs = grad_first + dot_last(grad_projected, full_qkv)
    grad_vectors = jnp.stack(
        [
            grad_gain_one,
            grad_gain_two,
            jnp.sum(grad_projected[:, :D], axis=0, dtype=f32),
            jnp.sum(grad_projected[:, 2 * D :], axis=0, dtype=f32),
            jnp.sum(grad_first, axis=0),
            jnp.sum(grad_second, axis=0),
            grad_shift_one,
            grad_shift_two,
        ]
    )
    big = jnp.concatenate(
        [
            blocks_of(item, rows_dp, cols_ffn)
            for item in (grad_w_qkv, grad_w_out, grad_w_up, grad_w_down_t)
        ],
        axis=-1,
    ).reshape(rows_dp * cols_ffn, shard_rows, -1)
    vector_blocks = jnp.broadcast_to(
        grad_vectors.reshape(8, rows_dp, 1, shard_rows).transpose(1, 2, 0, 3),
        (rows_dp, cols_ffn, 8, shard_rows),
    )
    bias_blocks = jnp.broadcast_to(
        grad_bias_up.reshape(1, cols_ffn, -1, mask_cols),
        (rows_dp, cols_ffn, ff_cols // mask_cols, mask_cols),
    )
    little = jnp.concatenate(
        [
            blocks_of(grad_mask, rows_dp, cols_ffn),
            jnp.pad(vector_blocks, ((0, 0), (0, 0), (0, 0), (0, mask_cols - shard_rows))),
            bias_blocks,
        ],
        axis=2,
    ).reshape(rows_dp * cols_ffn, -1, mask_cols)
    big, little = reduce_gradients(big, little, rows_dp, cols_ffn)

    own_mixed = (
        learned_gate_scores.astype(f32) + fixed_jitter_matrix.astype(f32)
    ) / relaxation_heat[0]
    grad_logits = little[:mask_rows] * (jax.nn.sigmoid(-own_mixed) / relaxation_heat[0])
    return (
        result.astype(bf16).reshape(layer_activations.shape),
        grad_inputs.reshape(layer_activations.shape),
        big[:, :qkv_cols],
        big[:, qkv_cols : qkv_cols + out_cols],
        big[:, qkv_cols + out_cols : qkv_cols + out_cols + ff_cols],
        little[mask_rows + 8 :].reshape(-1),
        big[:, qkv_cols + out_cols + ff_cols :].T,
        little[mask_rows : mask_rows + 2, :shard_rows],
        little[mask_rows + 2 : mask_rows + 8, :shard_rows],
        grad_logits,
    )


def solution(mesh):
    in_specs = (
        P(AXES, None, None),
        P(AXES),
        P("dp", "ffn"),
        P("dp", "ffn"),
        P("dp", "ffn"),
        P("ffn"),
        P("ffn", "dp"),
        P(None, "dp"),
        P(None, "dp"),
        P("dp", "ffn"),
        P("dp", "ffn"),
        P(),
        P(AXES, None, None),
    )
    out_specs = (
        P(AXES, None, None),
        P(AXES, None, None),
        P("dp", "ffn"),
        P("dp", "ffn"),
        P("dp", "ffn"),
        P("ffn"),
        P("ffn", "dp"),
        P(None, "dp"),
        P(None, "dp"),
        P("dp", "ffn"),
    )
    return jax.shard_map(
        on_device, mesh=mesh, in_specs=in_specs, out_specs=out_specs, check_vma=False
    )
```

```python
import jax
import jax.numpy as jnp
from jax import lax
from jax.experimental import pallas as pl
from jax.experimental.pallas import tpu as pltpu
from jax.sharding import PartitionSpec as P

D = 768
HEADS = 12
HEAD_DIM = 64
SEQ_LEN = 512
AXES = ("dp", "ffn")
norm_eps = 1e-06
f32 = jnp.float32
bf16 = jnp.bfloat16
MESH = pl.DeviceIdType.MESH


def dot_first(left, right):
    return lax.dot_general(left, right, (((0,), (0,)), ((), ())), preferred_element_type=f32)


def dot_last(left, right):
    return lax.dot_general(left, right, (((1,), (1,)), ((), ())), preferred_element_type=f32)


def dot(left, right):
    return jnp.dot(left, right, preferred_element_type=f32)


def layer_norm(values, gain, shift):
    mean_row = jnp.mean(values, axis=-1, keepdims=True)
    centered = values - mean_row
    inv_std = lax.rsqrt(jnp.mean(centered * centered, axis=-1, keepdims=True) + norm_eps)
    normed = centered * inv_std
    return (normed * gain + shift, normed, inv_std)


def norm_back(grad_out, normed, inv_std, gain):
    grad_normed = grad_out * gain
    grad_in = inv_std * (
        grad_normed
        - jnp.mean(grad_normed, axis=-1, keepdims=True)
        - normed * jnp.mean(grad_normed * normed, axis=-1, keepdims=True)
    )
    return (grad_in, jnp.sum(grad_out * normed, axis=0), jnp.sum(grad_out, axis=0))


def gelu_slope(values):
    return (
        0.5 * (1.0 + lax.erf(values * 0.7071067811865476))
        + values * jnp.exp(-0.5 * values * values) * 0.3989422804014327
    )


def score_block(queries, keys_low, natural_log_gate, live):
    scores = (
        jnp.einsum("qhd,khd->hqk", queries, keys_low, preferred_element_type=f32)
        * HEAD_DIM ** (-0.5)
        + natural_log_gate
    )
    return jnp.where(live[None, None, :], scores, -1e30)


def attend(queries, keys_low, values_low, natural_log_gate, live):
    scores = score_block(queries, keys_low, natural_log_gate, live)
    peak = jnp.max(scores, axis=-1, keepdims=True)
    shifted_exp = jnp.exp(scores - peak)
    total_exp = jnp.sum(shifted_exp, axis=-1, keepdims=True)
    probs_low = (shifted_exp / total_exp).astype(bf16)
    context = jnp.einsum("hqk,khd->qhd", probs_low, values_low, preferred_element_type=f32)
    return (context, peak + jnp.log(total_exp))


def attend_back(queries, keys_low, values_low, natural_log_gate, live, log_total, grad_context):
    scores = score_block(queries, keys_low, natural_log_gate, live)
    probs = jnp.exp(scores - log_total)
    grad_probs = jnp.einsum("qhd,khd->hqk", grad_context, values_low, preferred_element_type=f32)
    grad_values = jnp.einsum(
        "hqk,qhd->khd", probs.astype(bf16), grad_context, preferred_element_type=f32
    )
    grad_scores = probs * (grad_probs - jnp.sum(probs * grad_probs, axis=-1, keepdims=True))
    grad_mask = jnp.sum(grad_scores, axis=0)
    grad_scores_low = grad_scores.astype(bf16)
    grad_queries = jnp.einsum(
        "hqk,khd->qhd", grad_scores_low, keys_low, preferred_element_type=f32
    ) * HEAD_DIM ** (-0.5)
    grad_keys = jnp.einsum(
        "hqk,qhd->khd", grad_scores_low, queries, preferred_element_type=f32
    ) * HEAD_DIM ** (-0.5)
    return (grad_queries, grad_keys, grad_values, grad_mask)


def gather_weights(pack, small):
    rows_dp = lax.axis_size("dp")
    cols_ffn = lax.axis_size("ffn")
    full = lax.all_gather(pack[None], AXES, axis=0, tiled=True)
    full = full.reshape(rows_dp, cols_ffn, *pack.shape)
    small_full = lax.all_gather(small[None], AXES, axis=0, tiled=True)
    return full, small_full.reshape(rows_dp, cols_ffn, *small.shape)


def columns(blocks):
    rows_dp, cols_ffn, rows, cols = blocks.shape
    return blocks.transpose(0, 2, 1, 3).reshape(rows_dp * rows, cols_ffn * cols)


def blocks_of(full, rows_dp, cols_ffn):
    rows, cols = full.shape
    return full.reshape(rows_dp, rows // rows_dp, cols_ffn, cols // cols_ffn).transpose(0, 2, 1, 3)


def general_device(
    layer_activations,
    token_counts_each,
    attention_triple_matrix,
    attention_final_matrix,
    feedfwd_expand_matrix,
    feedfwd_expand_offset,
    feedfwd_contract_matrix,
    layernorm_scales,
    offset_vectors,
    learned_gate_scores,
    fixed_jitter_matrix,
    relaxation_heat,
    loss_grad_result,
):
    rows_dp = lax.axis_size("dp")
    cols_ffn = lax.axis_size("ffn")
    seq_count = layer_activations.shape[0]
    row_count = seq_count * SEQ_LEN
    shard_rows = attention_triple_matrix.shape[0]
    qkv_cols = attention_triple_matrix.shape[1]
    out_cols = attention_final_matrix.shape[1]
    ff_cols = feedfwd_expand_matrix.shape[1]

    pack = jnp.concatenate(
        [
            attention_triple_matrix,
            attention_final_matrix,
            feedfwd_expand_matrix,
            feedfwd_contract_matrix.T,
        ],
        axis=1,
    )
    mask_cols = learned_gate_scores.shape[1]
    vectors = jnp.concatenate([layernorm_scales, offset_vectors], axis=0)
    small = jnp.concatenate(
        [
            learned_gate_scores,
            fixed_jitter_matrix,
            jnp.pad(vectors, ((0, 0), (0, mask_cols - vectors.shape[1]))),
            feedfwd_expand_offset.reshape(-1, mask_cols),
        ],
        axis=0,
    )
    full, small_full = gather_weights(pack, small)
    full_qkv = columns(full[..., :qkv_cols])
    full_out = columns(full[..., qkv_cols : qkv_cols + out_cols])
    full_up = columns(full[..., qkv_cols + out_cols : qkv_cols + out_cols + ff_cols])
    full_down_t = columns(full[..., qkv_cols + out_cols + ff_cols :])
    mask_rows = learned_gate_scores.shape[0]
    logits_sum = columns(small_full[:, :, :mask_rows]).astype(f32) + columns(
        small_full[:, :, mask_rows : 2 * mask_rows]
    ).astype(f32)
    natural_log_gate = jax.nn.log_sigmoid(logits_sum / relaxation_heat[0])
    vectors_full = (
        small_full[:, 0, 2 * mask_rows : 2 * mask_rows + 8, :shard_rows]
        .transpose(1, 0, 2)
        .reshape(8, D)
        .astype(f32)
    )
    gains_full = vectors_full[:2]
    shifts_full = vectors_full[2:]
    bias_up = small_full[0, :, 2 * mask_rows + 8 :].reshape(1, -1).astype(f32)

    flat_in = layer_activations.reshape(row_count, D)
    qkv_bias = jnp.concatenate([shifts_full[0], jnp.zeros((D,), f32), shifts_full[1]])
    proj_low = (dot(flat_in, full_qkv) + qkv_bias).astype(bf16)
    head_shape = (seq_count, SEQ_LEN, HEADS, HEAD_DIM)
    queries = proj_low[:, :D].reshape(head_shape)
    keys_low = proj_low[:, D : 2 * D].reshape(head_shape)
    values_low = proj_low[:, 2 * D :].reshape(head_shape)
    live = lax.broadcasted_iota(jnp.int32, (seq_count, SEQ_LEN), 1) < token_counts_each[:, None]
    attended = [
        attend(queries[s], keys_low[s], values_low[s], natural_log_gate, live[s])
        for s in range(seq_count)
    ]
    context_low = jnp.concatenate(
        [item[0].reshape(SEQ_LEN, D).astype(bf16) for item in attended], axis=0
    )
    first_sum = flat_in.astype(f32) + dot(context_low, full_out) + shifts_full[2]
    hidden, normed_one, inv_one = layer_norm(first_sum, gains_full[0], shifts_full[4])
    hidden_low = hidden.astype(bf16)
    pre_act = dot(hidden_low, full_up) + bias_up
    act_low = jax.nn.gelu(pre_act, approximate=False).astype(bf16)
    second_sum = hidden + dot_last(act_low, full_down_t) + shifts_full[3]
    result, normed_two, inv_two = layer_norm(second_sum, gains_full[1], shifts_full[5])
    cot_flat = loss_grad_result.reshape(row_count, D).astype(f32)
    grad_second, grad_gain_two, grad_shift_two = norm_back(
        cot_flat, normed_two, inv_two, gains_full[1]
    )
    grad_second_low = grad_second.astype(bf16)
    grad_w_down_t = dot_first(grad_second_low, act_low)
    grad_act = dot(grad_second_low, full_down_t)
    grad_pre = (grad_act * gelu_slope(pre_act)).astype(bf16)
    grad_bias_up = jnp.sum(grad_pre, axis=0, dtype=f32)
    grad_w_up = dot_first(hidden_low, grad_pre)
    grad_hidden = grad_second + dot_last(grad_pre, full_up)
    grad_first, grad_gain_one, grad_shift_one = norm_back(
        grad_hidden, normed_one, inv_one, gains_full[0]
    )
    grad_first_low = grad_first.astype(bf16)
    grad_w_out = dot_first(context_low, grad_first_low)
    grad_context = dot_last(grad_first_low, full_out).astype(bf16).reshape(head_shape)
    back = [
        attend_back(
            queries[s],
            keys_low[s],
            values_low[s],
            natural_log_gate,
            live[s],
            attended[s][1],
            grad_context[s],
        )
        for s in range(seq_count)
    ]
    grad_mask = sum(item[3] for item in back)
    grad_projected = jnp.concatenate(
        [
            jnp.concatenate(
                [item[part].reshape(SEQ_LEN, D).astype(bf16) for item in back], axis=0
            )
            for part in range(3)
        ],
        axis=1,
    )
    grad_w_qkv = dot_first(flat_in, grad_projected)
    grad_inputs = grad_first + dot_last(grad_projected, full_qkv)
    grad_vectors = jnp.stack(
        [
            grad_gain_one,
            grad_gain_two,
            jnp.sum(grad_projected[:, :D], axis=0, dtype=f32),
            jnp.sum(grad_projected[:, 2 * D :], axis=0, dtype=f32),
            jnp.sum(grad_first, axis=0),
            jnp.sum(grad_second, axis=0),
            grad_shift_one,
            grad_shift_two,
        ]
    )
    big = jnp.concatenate(
        [
            blocks_of(item, rows_dp, cols_ffn)
            for item in (grad_w_qkv, grad_w_out, grad_w_up, grad_w_down_t)
        ],
        axis=-1,
    ).reshape(rows_dp * cols_ffn, shard_rows, -1)
    vector_blocks = jnp.broadcast_to(
        grad_vectors.reshape(8, rows_dp, 1, shard_rows).transpose(1, 2, 0, 3),
        (rows_dp, cols_ffn, 8, shard_rows),
    )
    bias_blocks = jnp.broadcast_to(
        grad_bias_up.reshape(1, cols_ffn, -1, mask_cols),
        (rows_dp, cols_ffn, ff_cols // mask_cols, mask_cols),
    )
    little = jnp.concatenate(
        [
            blocks_of(grad_mask, rows_dp, cols_ffn),
            jnp.pad(vector_blocks, ((0, 0), (0, 0), (0, 0), (0, mask_cols - shard_rows))),
            bias_blocks,
        ],
        axis=2,
    ).reshape(rows_dp * cols_ffn, -1, mask_cols)
    big = lax.psum_scatter(big, AXES, scatter_dimension=0, tiled=True)[0]
    little = lax.psum_scatter(little, AXES, scatter_dimension=0, tiled=True)[0]

    own_mixed = (
        learned_gate_scores.astype(f32) + fixed_jitter_matrix.astype(f32)
    ) / relaxation_heat[0]
    grad_logits = little[:mask_rows] * (jax.nn.sigmoid(-own_mixed) / relaxation_heat[0])
    return (
        result.astype(bf16).reshape(layer_activations.shape),
        grad_inputs.reshape(layer_activations.shape),
        big[:, :qkv_cols],
        big[:, qkv_cols : qkv_cols + out_cols],
        big[:, qkv_cols + out_cols : qkv_cols + out_cols + ff_cols],
        little[mask_rows + 8 :].reshape(-1),
        big[:, qkv_cols + out_cols + ff_cols :].T,
        little[mask_rows : mask_rows + 2, :shard_rows],
        little[mask_rows + 2 : mask_rows + 8, :shard_rows],
        grad_logits,
    )


def partners():
    i = lax.axis_index("dp")
    f = lax.axis_index("ffn")
    core = i + 1 - 2 * (i % 2)
    ix = i + 2 - 4 * ((i // 2) % 2)
    iy = (i + 4) % 8
    idg = (ix + 4) % 8
    return i, f, core, ix, iy, idg


def enter_barrier(me):
    i, f, core, ix, iy, idg = me
    sem = pltpu.get_barrier_semaphore()
    mates = [(i, (f + k) % 4) for k in (1, 2, 3)] + [(core, f), (ix, f), (iy, f)]
    for to in mates:
        pl.semaphore_signal(sem, inc=1, device_id=to, device_id_type=MESH)
    pl.semaphore_wait(sem, len(mates))


class Exchange:
    def __init__(self, me, ssem, rsem):
        self.me, self.ssem, self.rsem = me, ssem, rsem
        self.sent = []

    def copy(self, src, dst, n, to):
        return pltpu.make_async_remote_copy(
            src_ref=src,
            dst_ref=dst,
            send_sem=self.ssem.at[n],
            recv_sem=self.rsem.at[n],
            device_id=to,
            device_id_type=MESH,
        )

    def send(self, src, dst, n, to):
        self.copy(src, dst, n, to).start()
        self.sent.append((n, len(src.shape) == 3))

    def recv(self, ref, n):
        self.copy(ref, ref, n, (self.me[0], self.me[1])).wait_recv()

    def finish(self):
        for n, is_block in self.sent:
            ref = self.block(0) if is_block else self.piece(0, 0)
            self.copy(ref, ref, n, (self.me[0], self.me[1])).wait_send()


class Gather(Exchange):
    def __init__(self, me, src, dst, ssem, rsem, lsem):
        super().__init__(me, ssem, rsem)
        self.src, self.dst, self.lsem = src, dst, lsem
        self.rows = src.shape[0]

    def piece(self, i, p):
        return self.dst.at[p, pl.ds(i * self.rows, self.rows)]

    def block(self, i):
        return self.dst.at[:, pl.ds(i * self.rows, self.rows)]

    def local(self):
        i, f = self.me[:2]
        return pltpu.make_async_copy(self.src, self.piece(i, f), self.lsem)

    def s0(self):
        i, f, core, ix, iy, idg = self.me
        own = self.piece(i, f)
        self.local().start()
        for k in (1, 2, 3):
            self.send(self.src, own, 3 - k, (i, (f + k) % 4))
        self.send(self.src, own, 3, (ix, f))
        self.send(self.src, own, 7, (iy, f))

    def s1(self):
        i, f, core, ix, iy, idg = self.me
        for k in (1, 2, 3):
            ref = self.piece(i, (f + k) % 4)
            self.recv(ref, k - 1)
            self.send(ref, ref, 3 + k, (ix, f))
            self.send(ref, ref, 7 + k, (iy, f))
        self.local().wait()
        self.send(self.block(i), self.block(i), 15, (core, f))

    def s2(self):
        i, f, core, ix, iy, idg = self.me
        for k in range(4):
            p = (f + k) % 4
            rx, ry = self.piece(ix, p), self.piece(iy, p)
            self.recv(rx, 3 + k)
            if k % 2:
                self.send(rx, rx, 11 + k, (iy, f))
            self.recv(ry, 7 + k)
            if k % 2 == 0:
                self.send(ry, ry, 11 + k, (ix, f))
        self.send(self.block(ix), self.block(ix), 16, (core, f))
        self.send(self.block(iy), self.block(iy), 17, (core, f))

    def s3(self):
        i, f, core, ix, iy, idg = self.me
        for k in range(4):
            self.recv(self.piece(idg, (f + k) % 4), 11 + k)
        self.send(self.block(idg), self.block(idg), 18, (core, f))

    def s4(self):
        i, f, core, ix, iy, idg = self.me
        for n, b in ((15, i), (16, ix), (17, iy), (18, idg)):
            self.recv(self.block(b + core - i), n)


class Scatter(Exchange):
    def __init__(self, me, part, got, out, ssem, rsem):
        super().__init__(me, ssem, rsem)
        self.part, self.out = part, out
        self.rc, self.rq, self.rx, self.ry, self.rz = got
        self.rows = part.shape[1] // 8

    def piece(self, i, p):
        return self.part.at[p, pl.ds(pl.multiple_of(i * self.rows, self.rows), self.rows)]

    def block(self, i):
        return self.part.at[:, pl.ds(pl.multiple_of(i * self.rows, self.rows), self.rows)]

    def add(self, ref, *refs):
        total = ref[...].astype(f32)
        for other in refs:
            total = total + other[...].astype(f32)
        ref[...] = total.astype(ref.dtype)

    def r0(self):
        i, f, core, ix, iy, idg = self.me
        for n, b in ((3, idg), (1, ix), (2, iy), (0, i)):
            self.send(self.block(b + core - i), self.rc.at[n], n, (core, f))

    def r1(self):
        i, f, core, ix, iy, idg = self.me
        self.recv(self.rc.at[3], 3)
        for k in range(4):
            p = (f + k) % 4
            self.add(self.piece(idg, p), self.rc.at[3, p])
            self.send(self.piece(idg, p), self.rq.at[k], 4 + k, (iy if k % 2 else ix, f))
        self.recv(self.rc.at[1], 1)
        for k in (0, 2, 1, 3):
            p = (f + k) % 4
            self.add(self.piece(ix, p), self.rc.at[1, p])
            if k % 2 == 0:
                self.send(self.piece(ix, p), self.rx.at[k], 8 + k, (ix, f))
        self.recv(self.rc.at[2], 2)
        for k in (1, 3, 0, 2):
            p = (f + k) % 4
            self.add(self.piece(iy, p), self.rc.at[2, p])
            if k % 2:
                self.send(self.piece(iy, p), self.ry.at[k], 12 + k, (iy, f))
        self.recv(self.rc.at[0], 0)
        for k in range(4):
            p = (f + k) % 4
            self.add(self.piece(i, p), self.rc.at[0, p])

    def r2(self):
        i, f, core, ix, iy, idg = self.me
        for k in range(4):
            self.recv(self.rq.at[k], 4 + k)
            ref = self.piece(ix if k % 2 else iy, (f + k) % 4)
            self.add(ref, self.rq.at[k])
            if k % 2:
                self.send(ref, self.rx.at[k], 8 + k, (ix, f))
            else:
                self.send(ref, self.ry.at[k], 12 + k, (iy, f))

    def r3(self):
        i, f, core, ix, iy, idg = self.me
        for k in (1, 2, 3, 0):
            self.recv(self.rx.at[k], 8 + k)
            self.recv(self.ry.at[k], 12 + k)
            ref = self.piece(i, (f + k) % 4)
            if k:
                self.add(ref, self.rx.at[k], self.ry.at[k])
                self.send(ref, self.rz.at[3 - k], 19 - k, (i, (f + k) % 4))
            else:
                self.out[...] = (
                    ref[...].astype(f32) + self.rx[k].astype(f32) + self.ry[k].astype(f32)
                )

    def r4(self):
        total = self.out[...]
        for k in range(3):
            self.recv(self.rz.at[k], 16 + k)
            total = total + self.rz[k].astype(f32)
        self.out[...] = total


def scatter_buffers(lead, rows, cols, kind):
    return [
        pltpu.VMEM(lead + shape, kind)
        for shape in ((4, 4, rows, cols),) + ((4, rows, cols),) * 3 + ((3, rows, cols),)
    ]


HD=64
def dg(a,b,ca,cb): return lax.dot_general(a,b,(((ca,),(cb,)),((),())),preferred_element_type=f32)

def log_sigmoid(z):
    return jnp.minimum(z, 0.0) - jnp.log1p(jnp.exp(-jnp.abs(z)))

def prepare_mask(s_v, lens, heat, msk, mrows, srows):
    inv = 1.0 / heat[0]
    n = srows
    rows = []
    for i in range(8):
        row = []
        for f in range(4):
            a = s_v[f, pl.ds(i * n, mrows), :].astype(f32) + s_v[f, pl.ds(i * n + mrows, mrows), :].astype(f32)
            row.append(log_sigmoid(a * inv))
        rows.append(jnp.concatenate(row, axis=1))
    lmt = jnp.concatenate(rows, axis=0).T
    key = lax.broadcasted_iota(jnp.int32, lmt.shape, 0)
    for s in range(msk.shape[0]):
        msk[s] = jnp.where(key < lens[s], lmt, -1e30)

def prepare_columns(s_v, col, mrows, srows, cols):
    for i in range(8):
        v = s_v[0, pl.ds(i * srows + 2 * mrows, 16), :].astype(f32)
        col[pl.ds(i * cols, cols), :] = v.T[:cols, :]

def project(f, a_v, x, col, qkv):
    w = a_v[f, :, :576]
    for s in range(2):
        acc = dg(w, x[s * 512:(s + 1) * 512, :], 0, 1)
        base = 576 * f
        lo = 0
        while lo < 576:
            g = base + lo
            kind = g // 768
            hi = min(576, (kind + 1) * 768 - base)
            part = acc[lo:hi]
            b = g - kind * 768
            if kind == 0:
                part = (part + col[b:b + hi - lo, 2:3]) * 0.125
            elif kind == 2:
                part = part + col[b:b + hi - lo, 3:4]
            qkv[s, g:g + hi - lo, :] = part.astype(bf16)
            lo = hi

def attend_head(qkv, msk, ctx, ptbuf, slot, s, h):
    q = qkv[s, pl.ds(h * HD, HD), :]
    k = qkv[s, pl.ds(768 + h * HD, HD), :]
    v = qkv[s, pl.ds(1536 + h * HD, HD), :]
    st = dg(k, q, 0, 0) + msk[s]
    e = jnp.exp(st - jnp.max(st, axis=0, keepdims=True))
    p = (e * (1.0 / jnp.sum(e, axis=0, keepdims=True))).astype(bf16)
    ptbuf[slot] = p
    ctx[s, pl.ds(h * HD, HD), :] = dg(v, p, 1, 0).astype(bf16)

def attend_all(qkv, msk, ctx, pt, ptbuf, psem, per=2, hook=None):
    steps = 24 // per
    def body(t, carry):
        slot = t % 2
        @pl.when(t >= 2)
        def _():
            pltpu.make_async_copy(ptbuf.at[slot], pt.at[t - 2], psem.at[slot]).wait()
        s = t // (12 // per)
        for u in range(per):
            h = (t % (12 // per)) * per + u
            attend_head(qkv, msk, ctx, ptbuf.at[slot], u, s, h)
        pltpu.make_async_copy(ptbuf.at[slot], pt.at[t], psem.at[slot]).start()
        if hook is not None:
            hook(t)
        return carry
    lax.fori_loop(0, steps, body, 0)
    for t in (steps - 2, steps - 1):
        pltpu.make_async_copy(ptbuf.at[t % 2], pt.at[t], psem.at[t % 2]).wait()

PER = 2


def forward_kernel(pack, small, x, lens, heat, wfull, sfull, qkv, ctx, pt, a_v, s_v, col, msk, ptbuf, ssem, rsem, lsem, psem):
    me = partners()
    enter_barrier(me)
    little, attn, up, down = [
        Gather(me, src, dst, ssem.at[g], rsem.at[g], lsem.at[g])
        for g, (src, dst) in enumerate([(small, sfull)] + [(pack.at[g], wfull.at[g]) for g in range(3)])
    ]
    little.s0(); attn.s0()
    little.s1(); attn.s1(); up.s0()
    little.s2(); attn.s2(); up.s1()
    little.s3(); down.s0(); little.s4()
    c0 = pltpu.make_async_copy(sfull, s_v, lsem.at[4])
    c0.start()
    c0.wait()
    prepare_columns(s_v, col, 64, 144, 96)
    attn.s3(); up.s2()
    prepare_mask(s_v, lens, heat, msk, 64, 144)
    down.s1(); attn.s4()
    c1 = pltpu.make_async_copy(wfull.at[0], a_v, lsem.at[5])
    c1.start()
    c1.wait()
    for f in range(4):
        project(f, a_v, x, col, qkv)
    def hook(t):
        for at, step in ((0, up.s3), (3, down.s2), (4, up.s4), (8, down.s3)):
            pl.when(t == at)(step)
    attend_all(qkv, msk, ctx, pt, ptbuf, psem, PER, hook)
    down.s4()
    for g in (little, attn, up, down):
        g.finish()


def forward_call(pack, small, x, lens, heat):
    any_ = pl.BlockSpec(memory_space=pl.ANY)
    vm = pl.BlockSpec(memory_space=pltpu.VMEM)
    sm = pl.BlockSpec(memory_space=pltpu.SMEM)
    sd = jax.ShapeDtypeStruct
    dma = pltpu.SemaphoreType.DMA
    return pl.pallas_call(
        forward_kernel,
        out_shape=(
            sd((3, 4, 768, 768), bf16),
            sd((4, 1152, 128), bf16),
            sd((2, 2304, 512), bf16),
            sd((2, 768, 512), bf16),
            sd((24 // PER, PER, 512, 512), bf16),
        ),
        in_specs=[any_, any_, vm, sm, sm],
        out_specs=(any_, any_, vm, vm, any_),
        scratch_shapes=[
            pltpu.VMEM((4, 768, 768), bf16),
            pltpu.VMEM((4, 1152, 128), bf16),
            pltpu.VMEM((768, 16), f32),
            pltpu.VMEM((2, 512, 512), f32),
            pltpu.VMEM((2, PER, 512, 512), bf16),
            dma((4, 19)),
            dma((4, 19)),
            dma((6,)),
            dma((2,)),
        ],
        compiler_params=pltpu.CompilerParams(collective_id=0, has_side_effects=True, vmem_limit_bytes=60 << 20),
        name="gather_and_attend",
    )(pack, small, x, lens, heat)


def norm_rows(v):
    mean = jnp.mean(v, axis=-1, keepdims=True)
    c = v - mean
    inv = lax.rsqrt(jnp.mean(c * c, axis=-1, keepdims=True) + 1e-6)
    return c * inv, inv

def norm_rows_back(g, normed, inv, gain):
    e = g * gain
    return inv * (e - jnp.mean(e, axis=-1, keepdims=True) - normed * jnp.mean(e * normed, axis=-1, keepdims=True))

def mid_kernel(wfull, ctx, x, cot, vec, bup, out, act, gp, hlow, gslow, gf, gfl, gctx, sums, gbup, a_v, u_v, d_v, wout, slope, wsem):
    s = pl.program_id(0)
    cps = [pltpu.make_async_copy(wfull.at[g], v, wsem.at[g]) for g, v in enumerate((a_v, u_v, d_v))]
    @pl.when(s == 0)
    def _():
        for c in cps: c.start()
        cps[0].wait()
        for f in range(4):
            wout[:, 192 * f:192 * f + 192] = a_v[f, :, 576:]
        cps[1].wait()
        cps[2].wait()
    first = x[...].astype(f32) + dg(ctx[0], wout[...], 0, 0) + vec[4:5]
    n1, inv1 = norm_rows(first)
    hidden = n1 * vec[0:1] + vec[6:7]
    hl = hidden.astype(bf16)
    hlow[...] = hl
    acc = hidden + vec[5:6]
    for f in range(4):
        pre = dg(hl, u_v[f], 1, 0) + bup[:, 768 * f:768 * f + 768]
        phi = 0.5 * (1.0 + lax.erf(pre * 0.7071067811865476))
        slope[f] = phi + pre * (jnp.exp(-0.5 * pre * pre) * 0.3989422804014327)
        a = (pre * phi).astype(bf16)
        act[:, 768 * f:768 * f + 768] = a
        acc = acc + dg(a, d_v[f], 1, 1)
    n2, inv2 = norm_rows(acc)
    out[...] = (n2 * vec[1:2] + vec[7:8]).astype(bf16)
    g = cot[...].astype(f32)
    gs = norm_rows_back(g, n2, inv2, vec[1:2])
    gsl = gs.astype(bf16)
    gslow[...] = gsl
    gh = gs
    for f in range(4):
        ga = dg(gsl, d_v[f], 1, 0)
        p = (ga * slope[f]).astype(bf16)
        gp[:, 768 * f:768 * f + 768] = p
        b = jnp.sum(p.astype(f32), axis=0, keepdims=True)
        old = jnp.where(s == 0, 0.0, gbup[:, 768 * f:768 * f + 768])
        gbup[:, 768 * f:768 * f + 768] = old + b
        gh = gh + dg(p, u_v[f], 1, 1)
    gfirst = norm_rows_back(gh, n1, inv1, vec[0:1])
    gf[...] = gfirst
    gfl[...] = gfirst.astype(bf16)
    gctx[0] = dg(wout[...], gfirst.astype(bf16), 1, 1).astype(bf16)
    rs = lambda v: jnp.sum(v, axis=0, keepdims=True)
    rows = jnp.concatenate([rs(gh * n1), rs(g * n2), jnp.zeros((2, 768), f32), rs(gfirst), rs(gs), rs(gh), rs(g)], axis=0)
    sums[...] = jnp.where(s == 0, 0.0, sums[...]) + rows

def mid_call(wfull, ctx, x, cot, vec, bup):
    T = 512
    any_ = pl.BlockSpec(memory_space=pl.ANY)
    tok = lambda n: pl.BlockSpec((T, n), lambda s: (s, 0))
    tr = pl.BlockSpec((1, 768, T), lambda s: (s, 0, 0))
    const = lambda sh: pl.BlockSpec(sh, lambda s: (0,) * len(sh))
    sd = jax.ShapeDtypeStruct
    return pl.pallas_call(mid_kernel, grid=(2,),
        out_shape=(sd((1024, 768), bf16), sd((1024, 3072), bf16), sd((1024, 3072), bf16), sd((1024, 768), bf16), sd((1024, 768), bf16), sd((1024, 768), f32), sd((1024, 768), bf16), sd((2, 768, 512), bf16), sd((8, 768), f32), sd((1, 3072), f32)),
        in_specs=[any_, tr, tok(768), tok(768), const((8, 768)), const((1, 3072))],
        out_specs=(tok(768), tok(3072), tok(3072), tok(768), tok(768), tok(768), tok(768), tr, const((8, 768)), const((1, 3072))),
        scratch_shapes=[pltpu.VMEM((4, 768, 768), bf16)] * 3 + [pltpu.VMEM((768, 768), bf16), pltpu.VMEM((4, T, 768), f32), pltpu.SemaphoreType.DMA((3,))],
        compiler_params=pltpu.CompilerParams(vmem_limit_bytes=62 << 20), name="feed_forward")(wfull, ctx, x, cot, vec, bup)

def attend_head_back(qkv, gctx, p_ref, dproj, gm, s, h):
    q = qkv[s, pl.ds(h * HD, HD), :]
    k = qkv[s, pl.ds(768 + h * HD, HD), :]
    v = qkv[s, pl.ds(1536 + h * HD, HD), :]
    go = gctx[s, pl.ds(h * HD, HD), :]
    p = p_ref[...]
    dp = dg(v, go, 0, 0)
    pf = p.astype(f32)
    drow = jnp.sum(pf * dp, axis=0, keepdims=True)
    ds = pf * (dp - drow)
    dsl = ds.astype(bf16)
    dproj[s, pl.ds(1536 + h * HD, HD), :] = dg(go, p, 1, 1).astype(bf16)
    dproj[s, pl.ds(768 + h * HD, HD), :] = dg(q, dsl, 1, 1).astype(bf16)
    dproj[s, pl.ds(h * HD, HD), :] = (dg(k, dsl, 1, 0) * 0.125).astype(bf16)
    return ds

def attend_all_back(qkv, gctx, pt, ptbuf, psem, dproj, gm, per, hook=None):
    steps = 24 // per
    gm[...] = jnp.zeros(gm.shape, f32)
    def body(t, carry):
        slot = t % 2
        pltpu.make_async_copy(pt.at[t], ptbuf.at[slot], psem.at[slot]).wait()
        s = t // (12 // per)
        tot = None
        for u in range(per):
            h = (t % (12 // per)) * per + u
            ds = attend_head_back(qkv, gctx, ptbuf.at[slot, u], dproj, gm, s, h)
            tot = ds if tot is None else tot + ds
        gm[...] += tot
        @pl.when(t + 2 < steps)
        def _():
            pltpu.make_async_copy(pt.at[t + 2], ptbuf.at[slot], psem.at[slot]).start()
        if hook is not None:
            hook(t)
        return carry
    lax.fori_loop(0, steps, body, 0)

def little_part(lpart, gm, sums, gbup):
    lpart[...] = jnp.zeros(lpart.shape, f32)
    table = gm[...].T
    for f in range(4):
        for i in range(8):
            lpart[f, 80 * i:80 * i + 64, :] = table[64 * i:64 * i + 64, 128 * f:128 * f + 128]
            lpart[f, 80 * i + 64:80 * i + 72, :96] = sums[:, 96 * i:96 * i + 96]
            for r in range(6):
                lpart[f, 80 * i + 72 + r:80 * i + 73 + r, :] = gbup[:, 768 * f + 128 * r:768 * f + 128 * r + 128]


def backward_kernel(wfull, qkv_h, pt, gctx_h, ctx_h, act, gp, hlow, gslow, x, gfl_h, gf, sums_in, gbup, gin, obig, olit,
                    part, lpart, rc, rq, rx, ry, rz, lrc, lrq, lrx, lry, lrz, gm, sums,
                    lhs, chunk, qkv, gctx, ctx, gfl, dproj, ptbuf, gbuf, ssem, rsem, lsem, csem, isem, psem, gsem):
    me = partners()
    col = lambda src, f: src.at[:, pl.ds(768 * f, 768)]
    cp = pltpu.make_async_copy
    chunks = [cp(col(act, f), chunk.at[f % 2], csem.at[f % 2]) for f in range(4)] + [cp(col(gp, f), chunk.at[f % 2], csem.at[f % 2]) for f in range(4)]
    l0 = cp(gslow, lhs.at[0], lsem.at[0]); l1 = cp(hlow, lhs.at[1], lsem.at[1]); l2 = cp(x, lhs.at[0], lsem.at[0])
    l0.start(); chunks[0].start(); chunks[1].start(); l1.start()
    ins = [cp(a, b, isem.at[n]) for n, (a, b) in enumerate(((ctx_h, ctx), (gfl_h, gfl), (qkv_h, qkv), (gctx_h, gctx)))]
    for c in ins: c.start()
    for t in range(2): cp(pt.at[t], ptbuf.at[t], psem.at[t]).start()
    enter_barrier(me)
    attn, up, down = [
        Scatter(me, part.at[g], [b.at[g] for b in (rc, rq, rx, ry, rz)], obig.at[g], ssem.at[g], rsem.at[g]) for g in range(3)
    ]
    little = Scatter(me, lpart, (lrc, lrq, lrx, lry, lrz), olit, ssem.at[3], rsem.at[3])
    l0.wait()
    for n in range(8):
        g, f = (2, 1)[n // 4], n % 4
        if n == 4:
            down.r0()
            l2.start()
            l1.wait()
        chunks[n].wait()
        part[g, f] = dg(lhs[n // 4], chunk[n % 2], 0, 0).astype(bf16)
        if n < 6: chunks[n + 2].start()
    up.r0()
    for c in ins: c.wait()
    dwo = dg(ctx[0], gfl[0:512], 1, 0) + dg(ctx[1], gfl[512:1024], 1, 0)
    for f in range(4):
        part[0, f, :, 576:] = dwo[:, 192 * f:192 * f + 192].astype(bf16)
    def hook(t):
        for at, step in ((0, down.r1), (1, up.r1), (3, down.r2), (5, down.r3), (6, up.r2), (9, up.r3), (10, down.r4)):
            pl.when(t == at)(step)
    attend_all_back(qkv, gctx, pt, ptbuf, psem, dproj, gm, PER, hook)
    ones = jnp.ones((8, 512), bf16)
    sums[...] = sums_in[...]
    sums[2:3] = (dg(ones, dproj[0, 0:768], 1, 1) + dg(ones, dproj[1, 0:768], 1, 1))[0:1]
    sums[3:4] = (dg(ones, dproj[0, 1536:2304], 1, 1) + dg(ones, dproj[1, 1536:2304], 1, 1))[0:1]
    little_part(lpart, gm, sums, gbup)
    little.r0()
    aw = [cp(wfull.at[0, f], chunk.at[f % 2, pl.ds(0, 768)], csem.at[f % 2]) for f in range(4)]
    aw[0].start(); aw[1].start()
    gi = [cp(gf.at[pl.ds(512 * s, 512)], gbuf.at[s], gsem.at[s]) for s in range(2)]
    for c in gi: c.start()
    l2.wait()
    for f in range(4):
        r = slice(576 * f, 576 * f + 576)
        part[0, f, :, :576] = (dg(lhs[0, 0:512], dproj[0, r], 0, 1) + dg(lhs[0, 512:1024], dproj[1, r], 0, 1)).astype(bf16)
    attn.r0()
    little.r1()
    for f in range(4):
        aw[f].wait()
        if f == 0:
            for c in gi: c.wait()
        for s in range(2):
            gbuf[s] = gbuf[s] + dg(dproj[s, 576 * f:576 * f + 576], chunk[f % 2, 0:768, :576], 0, 1)
        if f < 2: aw[f + 2].start()
        if f == 1:
            attn.r1()
            little.r2()
        if f == 2:
            little.r3()
    go = [cp(gbuf.at[s], gin.at[pl.ds(512 * s, 512)], gsem.at[s]) for s in range(2)]
    for c in go: c.start()
    up.r4()
    attn.r2()
    little.r4()
    attn.r3()
    attn.r4()
    for c in go: c.wait()
    for g in (attn, up, down, little):
        g.finish()


def backward_call(*ops):
    any_ = pl.BlockSpec(memory_space=pl.ANY); vm = pl.BlockSpec(memory_space=pltpu.VMEM)
    sd = jax.ShapeDtypeStruct
    dma = pltpu.SemaphoreType.DMA
    V = pltpu.VMEM
    return pl.pallas_call(backward_kernel,
        out_shape=(sd((1024, 768), f32), sd((3, 96, 768), f32), sd((80, 128), f32)),
        in_specs=[any_] * 12 + [vm] * 2, out_specs=(any_, vm, vm),
        scratch_shapes=[V((3, 4, 768, 768), bf16), V((4, 640, 128), f32)] + scatter_buffers((3,), 96, 768, bf16) + scatter_buffers((), 80, 128, f32)
            + [V((512, 512), f32), V((8, 768), f32)]
            + [V((2, 1024, 768), bf16), V((2, 1024, 768), bf16), V((2, 2304, 512), bf16), V((2, 768, 512), bf16), V((2, 768, 512), bf16), V((1024, 768), bf16),
            V((2, 2304, 512), bf16), V((2, PER, 512, 512), bf16), V((2, 512, 768), f32), dma((4, 19)), dma((4, 19)), dma((2,)), dma((2,)), dma((4,)), dma((2,)), dma((2,))],
        compiler_params=pltpu.CompilerParams(collective_id=1, has_side_effects=True, vmem_limit_bytes=63 << 20), name="attend_back_and_reduce")(*ops)


def own_device(
    layer_activations,
    token_counts_each,
    attention_triple_matrix,
    attention_final_matrix,
    feedfwd_expand_matrix,
    feedfwd_expand_offset,
    feedfwd_contract_matrix,
    layernorm_scales,
    offset_vectors,
    learned_gate_scores,
    fixed_jitter_matrix,
    relaxation_heat,
    loss_grad_result,
):
    pack = jnp.stack(
        [
            jnp.concatenate([attention_triple_matrix, attention_final_matrix], axis=1),
            feedfwd_expand_matrix,
            feedfwd_contract_matrix.T,
        ]
    )
    vectors = jnp.concatenate([layernorm_scales, offset_vectors], axis=0)
    small = jnp.concatenate(
        [
            learned_gate_scores,
            fixed_jitter_matrix,
            jnp.pad(vectors, ((0, 0), (0, 32))),
            jnp.pad(feedfwd_expand_offset.reshape(6, 128), ((0, 2), (0, 0))),
        ],
        axis=0,
    )
    x = layer_activations.reshape(1024, D)
    cot = loss_grad_result.reshape(1024, D)
    weights, small_full, qkv, ctx, probs = forward_call(pack, small, x, token_counts_each, relaxation_heat)
    small_full = small_full.reshape(4, 8, 144, 128)
    vectors_full = small_full[0, :, 128:136, :96].transpose(1, 0, 2).reshape(8, D).astype(f32)
    bias_up = small_full[:, 0, 136:142].reshape(1, 3072).astype(f32)
    result, act, grad_pre, hidden_low, grad_second_low, grad_first, grad_first_low, grad_ctx, sums, grad_bias = mid_call(
        weights, ctx, x, cot, vectors_full, bias_up
    )
    grad_inputs, big, little = backward_call(
        weights, qkv, probs, grad_ctx, ctx, act, grad_pre, hidden_low, grad_second_low, x, grad_first_low, grad_first,
        sums, grad_bias,
    )
    own_mixed = (
        learned_gate_scores.astype(f32) + fixed_jitter_matrix.astype(f32)
    ) / relaxation_heat[0]
    grad_logits = little[:64] * (jax.nn.sigmoid(-own_mixed) / relaxation_heat[0])
    return (
        result.reshape(layer_activations.shape),
        grad_inputs.reshape(layer_activations.shape),
        big[0, :, :576],
        big[0, :, 576:],
        big[1],
        little[72:78].reshape(-1),
        big[2].T,
        little[64:66, :96],
        little[66:72, :96],
        grad_logits,
    )


def solution(mesh):
    in_specs = (
        P(AXES, None, None),
        P(AXES),
        P("dp", "ffn"),
        P("dp", "ffn"),
        P("dp", "ffn"),
        P("ffn"),
        P("ffn", "dp"),
        P(None, "dp"),
        P(None, "dp"),
        P("dp", "ffn"),
        P("dp", "ffn"),
        P(),
        P(AXES, None, None),
    )
    out_specs = (
        P(AXES, None, None),
        P(AXES, None, None),
        P("dp", "ffn"),
        P("dp", "ffn"),
        P("dp", "ffn"),
        P("ffn"),
        P("ffn", "dp"),
        P(None, "dp"),
        P(None, "dp"),
        P("dp", "ffn"),
    )
    own = (mesh.shape["dp"], mesh.shape["ffn"]) == (8, 4)
    return jax.shard_map(
        own_device if own else general_device, mesh=mesh, in_specs=in_specs, out_specs=out_specs, check_vma=False
    )
```

```python
import functools

import jax
import jax.numpy as jnp
from jax import lax
from jax.experimental import pallas as pl
from jax.experimental.pallas import tpu as pltpu
from jax.sharding import PartitionSpec as P

D = 768
HEADS = 12
HEAD_DIM = 64
SEQ_LEN = 512
AXES = ("dp", "ffn")
norm_eps = 1e-06
f32 = jnp.float32
bf16 = jnp.bfloat16
MESH = pl.DeviceIdType.MESH


def dot_first(left, right):
    return lax.dot_general(left, right, (((0,), (0,)), ((), ())), preferred_element_type=f32)


def dot_last(left, right):
    return lax.dot_general(left, right, (((1,), (1,)), ((), ())), preferred_element_type=f32)


def dot(left, right):
    return jnp.dot(left, right, preferred_element_type=f32)


def layer_norm(values, gain, shift):
    mean_row = jnp.mean(values, axis=-1, keepdims=True)
    centered = values - mean_row
    inv_std = lax.rsqrt(jnp.mean(centered * centered, axis=-1, keepdims=True) + norm_eps)
    normed = centered * inv_std
    return (normed * gain + shift, normed, inv_std)


def norm_back(grad_out, normed, inv_std, gain):
    grad_normed = grad_out * gain
    grad_in = inv_std * (
        grad_normed
        - jnp.mean(grad_normed, axis=-1, keepdims=True)
        - normed * jnp.mean(grad_normed * normed, axis=-1, keepdims=True)
    )
    return (grad_in, jnp.sum(grad_out * normed, axis=0), jnp.sum(grad_out, axis=0))


def gelu_slope(values):
    return (
        0.5 * (1.0 + lax.erf(values * 0.7071067811865476))
        + values * jnp.exp(-0.5 * values * values) * 0.3989422804014327
    )


def score_block(queries, keys_low, natural_log_gate, live):
    scores = (
        jnp.einsum("qhd,khd->hqk", queries, keys_low, preferred_element_type=f32)
        * HEAD_DIM ** (-0.5)
        + natural_log_gate
    )
    return jnp.where(live[None, None, :], scores, -1e30)


def attend(queries, keys_low, values_low, natural_log_gate, live):
    scores = score_block(queries, keys_low, natural_log_gate, live)
    peak = jnp.max(scores, axis=-1, keepdims=True)
    shifted_exp = jnp.exp(scores - peak)
    total_exp = jnp.sum(shifted_exp, axis=-1, keepdims=True)
    probs_low = (shifted_exp / total_exp).astype(bf16)
    context = jnp.einsum("hqk,khd->qhd", probs_low, values_low, preferred_element_type=f32)
    return (context, peak + jnp.log(total_exp))


def attend_back(queries, keys_low, values_low, natural_log_gate, live, log_total, grad_context):
    scores = score_block(queries, keys_low, natural_log_gate, live)
    probs = jnp.exp(scores - log_total)
    grad_probs = jnp.einsum("qhd,khd->hqk", grad_context, values_low, preferred_element_type=f32)
    grad_values = jnp.einsum(
        "hqk,qhd->khd", probs.astype(bf16), grad_context, preferred_element_type=f32
    )
    grad_scores = probs * (grad_probs - jnp.sum(probs * grad_probs, axis=-1, keepdims=True))
    grad_mask = jnp.sum(grad_scores, axis=0)
    grad_scores_low = grad_scores.astype(bf16)
    grad_queries = jnp.einsum(
        "hqk,khd->qhd", grad_scores_low, keys_low, preferred_element_type=f32
    ) * HEAD_DIM ** (-0.5)
    grad_keys = jnp.einsum(
        "hqk,qhd->khd", grad_scores_low, queries, preferred_element_type=f32
    ) * HEAD_DIM ** (-0.5)
    return (grad_queries, grad_keys, grad_values, grad_mask)


def gather_weights(pack, small):
    rows_dp = lax.axis_size("dp")
    cols_ffn = lax.axis_size("ffn")
    full = lax.all_gather(pack[None], AXES, axis=0, tiled=True)
    full = full.reshape(rows_dp, cols_ffn, *pack.shape)
    small_full = lax.all_gather(small[None], AXES, axis=0, tiled=True)
    return full, small_full.reshape(rows_dp, cols_ffn, *small.shape)


def columns(blocks):
    rows_dp, cols_ffn, rows, cols = blocks.shape
    return blocks.transpose(0, 2, 1, 3).reshape(rows_dp * rows, cols_ffn * cols)


def blocks_of(full, rows_dp, cols_ffn):
    rows, cols = full.shape
    return full.reshape(rows_dp, rows // rows_dp, cols_ffn, cols // cols_ffn).transpose(0, 2, 1, 3)


def general_device(
    layer_activations,
    token_counts_each,
    attention_triple_matrix,
    attention_final_matrix,
    feedfwd_expand_matrix,
    feedfwd_expand_offset,
    feedfwd_contract_matrix,
    layernorm_scales,
    offset_vectors,
    learned_gate_scores,
    fixed_jitter_matrix,
    relaxation_heat,
    loss_grad_result,
):
    rows_dp = lax.axis_size("dp")
    cols_ffn = lax.axis_size("ffn")
    seq_count = layer_activations.shape[0]
    row_count = seq_count * SEQ_LEN
    shard_rows = attention_triple_matrix.shape[0]
    qkv_cols = attention_triple_matrix.shape[1]
    out_cols = attention_final_matrix.shape[1]
    ff_cols = feedfwd_expand_matrix.shape[1]

    pack = jnp.concatenate(
        [
            attention_triple_matrix,
            attention_final_matrix,
            feedfwd_expand_matrix,
            feedfwd_contract_matrix.T,
        ],
        axis=1,
    )
    mask_cols = learned_gate_scores.shape[1]
    vectors = jnp.concatenate([layernorm_scales, offset_vectors], axis=0)
    small = jnp.concatenate(
        [
            learned_gate_scores,
            fixed_jitter_matrix,
            jnp.pad(vectors, ((0, 0), (0, mask_cols - vectors.shape[1]))),
            feedfwd_expand_offset.reshape(-1, mask_cols),
        ],
        axis=0,
    )
    full, small_full = gather_weights(pack, small)
    full_qkv = columns(full[..., :qkv_cols])
    full_out = columns(full[..., qkv_cols : qkv_cols + out_cols])
    full_up = columns(full[..., qkv_cols + out_cols : qkv_cols + out_cols + ff_cols])
    full_down_t = columns(full[..., qkv_cols + out_cols + ff_cols :])
    mask_rows = learned_gate_scores.shape[0]
    logits_sum = columns(small_full[:, :, :mask_rows]).astype(f32) + columns(
        small_full[:, :, mask_rows : 2 * mask_rows]
    ).astype(f32)
    natural_log_gate = jax.nn.log_sigmoid(logits_sum / relaxation_heat[0])
    vectors_full = (
        small_full[:, 0, 2 * mask_rows : 2 * mask_rows + 8, :shard_rows]
        .transpose(1, 0, 2)
        .reshape(8, D)
        .astype(f32)
    )
    gains_full = vectors_full[:2]
    shifts_full = vectors_full[2:]
    bias_up = small_full[0, :, 2 * mask_rows + 8 :].reshape(1, -1).astype(f32)

    flat_in = layer_activations.reshape(row_count, D)
    qkv_bias = jnp.concatenate([shifts_full[0], jnp.zeros((D,), f32), shifts_full[1]])
    proj_low = (dot(flat_in, full_qkv) + qkv_bias).astype(bf16)
    head_shape = (seq_count, SEQ_LEN, HEADS, HEAD_DIM)
    queries = proj_low[:, :D].reshape(head_shape)
    keys_low = proj_low[:, D : 2 * D].reshape(head_shape)
    values_low = proj_low[:, 2 * D :].reshape(head_shape)
    live = lax.broadcasted_iota(jnp.int32, (seq_count, SEQ_LEN), 1) < token_counts_each[:, None]
    attended = [
        attend(queries[s], keys_low[s], values_low[s], natural_log_gate, live[s])
        for s in range(seq_count)
    ]
    context_low = jnp.concatenate(
        [item[0].reshape(SEQ_LEN, D).astype(bf16) for item in attended], axis=0
    )
    first_sum = flat_in.astype(f32) + dot(context_low, full_out) + shifts_full[2]
    hidden, normed_one, inv_one = layer_norm(first_sum, gains_full[0], shifts_full[4])
    hidden_low = hidden.astype(bf16)
    pre_act = dot(hidden_low, full_up) + bias_up
    act_low = jax.nn.gelu(pre_act, approximate=False).astype(bf16)
    second_sum = hidden + dot_last(act_low, full_down_t) + shifts_full[3]
    result, normed_two, inv_two = layer_norm(second_sum, gains_full[1], shifts_full[5])
    cot_flat = loss_grad_result.reshape(row_count, D).astype(f32)
    grad_second, grad_gain_two, grad_shift_two = norm_back(
        cot_flat, normed_two, inv_two, gains_full[1]
    )
    grad_second_low = grad_second.astype(bf16)
    grad_w_down_t = dot_first(grad_second_low, act_low)
    grad_act = dot(grad_second_low, full_down_t)
    grad_pre = (grad_act * gelu_slope(pre_act)).astype(bf16)
    grad_bias_up = jnp.sum(grad_pre, axis=0, dtype=f32)
    grad_w_up = dot_first(hidden_low, grad_pre)
    grad_hidden = grad_second + dot_last(grad_pre, full_up)
    grad_first, grad_gain_one, grad_shift_one = norm_back(
        grad_hidden, normed_one, inv_one, gains_full[0]
    )
    grad_first_low = grad_first.astype(bf16)
    grad_w_out = dot_first(context_low, grad_first_low)
    grad_context = dot_last(grad_first_low, full_out).astype(bf16).reshape(head_shape)
    back = [
        attend_back(
            queries[s],
            keys_low[s],
            values_low[s],
            natural_log_gate,
            live[s],
            attended[s][1],
            grad_context[s],
        )
        for s in range(seq_count)
    ]
    grad_mask = sum(item[3] for item in back)
    grad_projected = jnp.concatenate(
        [
            jnp.concatenate(
                [item[part].reshape(SEQ_LEN, D).astype(bf16) for item in back], axis=0
            )
            for part in range(3)
        ],
        axis=1,
    )
    grad_w_qkv = dot_first(flat_in, grad_projected)
    grad_inputs = grad_first + dot_last(grad_projected, full_qkv)
    grad_vectors = jnp.stack(
        [
            grad_gain_one,
            grad_gain_two,
            jnp.sum(grad_projected[:, :D], axis=0, dtype=f32),
            jnp.sum(grad_projected[:, 2 * D :], axis=0, dtype=f32),
            jnp.sum(grad_first, axis=0),
            jnp.sum(grad_second, axis=0),
            grad_shift_one,
            grad_shift_two,
        ]
    )
    big = jnp.concatenate(
        [
            blocks_of(item, rows_dp, cols_ffn)
            for item in (grad_w_qkv, grad_w_out, grad_w_up, grad_w_down_t)
        ],
        axis=-1,
    ).reshape(rows_dp * cols_ffn, shard_rows, -1)
    vector_blocks = jnp.broadcast_to(
        grad_vectors.reshape(8, rows_dp, 1, shard_rows).transpose(1, 2, 0, 3),
        (rows_dp, cols_ffn, 8, shard_rows),
    )
    bias_blocks = jnp.broadcast_to(
        grad_bias_up.reshape(1, cols_ffn, -1, mask_cols),
        (rows_dp, cols_ffn, ff_cols // mask_cols, mask_cols),
    )
    little = jnp.concatenate(
        [
            blocks_of(grad_mask, rows_dp, cols_ffn),
            jnp.pad(vector_blocks, ((0, 0), (0, 0), (0, 0), (0, mask_cols - shard_rows))),
            bias_blocks,
        ],
        axis=2,
    ).reshape(rows_dp * cols_ffn, -1, mask_cols)
    big = lax.psum_scatter(big, AXES, scatter_dimension=0, tiled=True)[0]
    little = lax.psum_scatter(little, AXES, scatter_dimension=0, tiled=True)[0]

    own_mixed = (
        learned_gate_scores.astype(f32) + fixed_jitter_matrix.astype(f32)
    ) / relaxation_heat[0]
    grad_logits = little[:mask_rows] * (jax.nn.sigmoid(-own_mixed) / relaxation_heat[0])
    return (
        result.astype(bf16).reshape(layer_activations.shape),
        grad_inputs.reshape(layer_activations.shape),
        big[:, :qkv_cols],
        big[:, qkv_cols : qkv_cols + out_cols],
        big[:, qkv_cols + out_cols : qkv_cols + out_cols + ff_cols],
        little[mask_rows + 8 :].reshape(-1),
        big[:, qkv_cols + out_cols + ff_cols :].T,
        little[mask_rows : mask_rows + 2, :shard_rows],
        little[mask_rows + 2 : mask_rows + 8, :shard_rows],
        grad_logits,
    )


def partners():
    i = lax.axis_index("dp")
    f = lax.axis_index("ffn")
    core = i + 1 - 2 * (i % 2)
    ix = i + 2 - 4 * ((i // 2) % 2)
    iy = (i + 4) % 8
    idg = (ix + 4) % 8
    return i, f, core, ix, iy, idg


def enter_barrier(me):
    i, f, core, ix, iy, idg = me
    sem = pltpu.get_barrier_semaphore()
    mates = [(i, (f + k) % 4) for k in (1, 2, 3)] + [(core, f), (ix, f), (iy, f)]
    for to in mates:
        pl.semaphore_signal(sem, inc=1, device_id=to, device_id_type=MESH)
    pl.semaphore_wait(sem, len(mates))


class Exchange:
    def __init__(self, me, ssem, rsem):
        self.me, self.ssem, self.rsem = me, ssem, rsem
        self.sent = []

    def copy(self, src, dst, n, to):
        return pltpu.make_async_remote_copy(
            src_ref=src,
            dst_ref=dst,
            send_sem=self.ssem.at[n],
            recv_sem=self.rsem.at[n],
            device_id=to,
            device_id_type=MESH,
        )

    def send(self, src, dst, n, to):
        self.copy(src, dst, n, to).start()
        self.sent.append((n, len(src.shape) == 3))

    def recv(self, ref, n):
        self.copy(ref, ref, n, (self.me[0], self.me[1])).wait_recv()

    def finish(self):
        for n, is_block in self.sent:
            ref = self.block(0) if is_block else self.piece(0, 0)
            self.copy(ref, ref, n, (self.me[0], self.me[1])).wait_send()


class Gather(Exchange):
    def __init__(self, me, src, dst, ssem, rsem, lsem):
        super().__init__(me, ssem, rsem)
        self.src, self.dst, self.lsem = src, dst, lsem
        self.rows = src.shape[0]

    def piece(self, i, p):
        return self.dst.at[p, pl.ds(i * self.rows, self.rows)]

    def block(self, i):
        return self.dst.at[:, pl.ds(i * self.rows, self.rows)]

    def local(self):
        i, f = self.me[:2]
        return pltpu.make_async_copy(self.src, self.piece(i, f), self.lsem)

    def s0(self):
        i, f, core, ix, iy, idg = self.me
        own = self.piece(i, f)
        self.local().start()
        for k in (1, 2, 3):
            self.send(self.src, own, 3 - k, (i, (f + k) % 4))
        self.send(self.src, own, 3, (ix, f))
        self.send(self.src, own, 7, (iy, f))

    def s1(self):
        i, f, core, ix, iy, idg = self.me
        for k in (1, 2, 3):
            ref = self.piece(i, (f + k) % 4)
            self.recv(ref, k - 1)
            self.send(ref, ref, 3 + k, (ix, f))
            self.send(ref, ref, 7 + k, (iy, f))
        self.local().wait()
        self.send(self.block(i), self.block(i), 15, (core, f))

    def s2(self):
        i, f, core, ix, iy, idg = self.me
        for k in range(4):
            p = (f + k) % 4
            rx, ry = self.piece(ix, p), self.piece(iy, p)
            self.recv(rx, 3 + k)
            if k % 2:
                self.send(rx, rx, 11 + k, (iy, f))
            self.recv(ry, 7 + k)
            if k % 2 == 0:
                self.send(ry, ry, 11 + k, (ix, f))
        self.send(self.block(ix), self.block(ix), 16, (core, f))
        self.send(self.block(iy), self.block(iy), 17, (core, f))

    def s3(self):
        i, f, core, ix, iy, idg = self.me
        for k in range(4):
            self.recv(self.piece(idg, (f + k) % 4), 11 + k)
        self.send(self.block(idg), self.block(idg), 18, (core, f))

    def s4(self):
        i, f, core, ix, iy, idg = self.me
        for n, b in ((15, i), (16, ix), (17, iy), (18, idg)):
            self.recv(self.block(b + core - i), n)


class Scatter(Exchange):
    def __init__(self, me, part, got, out, ssem, rsem):
        super().__init__(me, ssem, rsem)
        self.part, self.out = part, out
        self.rc, self.rq, self.rx, self.ry, self.rz = got
        i = me[0]
        self.c = i % 2
        self.xy = i // 2
        self.xyx = self.xy + 1 - 2 * (self.xy % 2)
        self.xyy = (self.xy + 2) % 4
        self.xyd = (self.xyx + 2) % 4

    def at(self, k):
        return (self.me[1] + k) % 4

    def piece(self, k, xy):
        return self.part.at[self.at(k), xy, self.c]

    def finish(self):
        for n, is_block in self.sent:
            ref = self.rc.at[0] if is_block else self.rx.at[0]
            self.copy(ref, ref, n, (self.me[0], self.me[1])).wait_send()

    def add(self, ref, *refs):
        if len(refs) == 1:
            ref[...] = ref[...] + refs[0][...]
            return
        total = ref[...].astype(f32)
        for other in refs:
            total = total + other[...].astype(f32)
        ref[...] = total.astype(ref.dtype)

    def c_(self, k):
        self.send(self.part.at[self.at(k), :, 1 - self.c], self.rc.at[k], k, (self.me[2], self.me[1]))

    def q(self, k):
        i, f, core, ix, iy, idg = self.me
        self.recv(self.rc.at[k], k)
        ref = self.piece(k, self.xyd)
        self.add(ref, self.rc.at[k, self.xyd])
        self.send(ref, self.rq.at[k], 4 + k, (iy if k % 2 else ix, f))
        refx, refy = self.piece(k, self.xyx), self.piece(k, self.xyy)
        if k % 2:
            self.add(refy, self.rc.at[k, self.xyy])
            self.send(refy, self.ry.at[k], 12 + k, (iy, f))
            self.add(refx, self.rc.at[k, self.xyx])
        else:
            self.add(refx, self.rc.at[k, self.xyx])
            self.send(refx, self.rx.at[k], 8 + k, (ix, f))
            self.add(refy, self.rc.at[k, self.xyy])
        self.add(self.piece(k, self.xy), self.rc.at[k, self.xy])

    def t(self, k):
        i, f, core, ix, iy, idg = self.me
        self.recv(self.rq.at[k], 4 + k)
        ref = self.piece(k, self.xyx if k % 2 else self.xyy)
        self.add(ref, self.rq.at[k])
        if k % 2:
            self.send(ref, self.rx.at[k], 8 + k, (ix, f))
        else:
            self.send(ref, self.ry.at[k], 12 + k, (iy, f))

    def w(self, k):
        i, f, core, ix, iy, idg = self.me
        self.recv(self.rx.at[k], 8 + k)
        self.recv(self.ry.at[k], 12 + k)
        ref = self.piece(k, self.xy)
        if k:
            self.add(ref, self.rx.at[k], self.ry.at[k])
            self.send(ref, self.rz.at[3 - k], 19 - k, (i, (f + k) % 4))
        else:
            self.out[...] = ref[...].astype(f32) + self.rx[k].astype(f32) + self.ry[k].astype(f32)

    def e(self):
        total = self.out[...]
        for k in range(3):
            self.recv(self.rz.at[k], 16 + k)
            total = total + self.rz[k].astype(f32)
        self.out[...] = total


def scatter_buffers(lead, rows, cols, kind):
    return [
        pltpu.VMEM(lead + shape, kind)
        for shape in ((4, 4, rows, cols),) + ((4, rows, cols),) * 3 + ((3, rows, cols),)
    ]


HD=64
def dg(a,b,ca,cb): return lax.dot_general(a,b,(((ca,),(cb,)),((),())),preferred_element_type=f32)

def log_sigmoid(z):
    return jnp.minimum(z, 0.0) - jnp.log1p(jnp.exp(-jnp.abs(z)))

def prepare_mask(s_v, lens, heat, msk, mrows, srows):
    inv = 1.0 / heat[0]
    n = srows
    rows = []
    for i in range(8):
        row = []
        for f in range(4):
            a = s_v[f, pl.ds(i * n, mrows), :].astype(f32) + s_v[f, pl.ds(i * n + mrows, mrows), :].astype(f32)
            row.append(log_sigmoid(a * inv))
        rows.append(jnp.concatenate(row, axis=1))
    lmt = jnp.concatenate(rows, axis=0).T
    key = lax.broadcasted_iota(jnp.int32, lmt.shape, 0)
    for s in range(msk.shape[0]):
        msk[s] = jnp.where(key < lens[s], lmt, -1e30)

def prepare_columns(s_v, col, mrows, srows, cols):
    for i in range(8):
        v = s_v[0, pl.ds(i * srows + 2 * mrows, 16), :].astype(f32)
        col[pl.ds(i * cols, cols), :] = v.T[:cols, :]

def project(f, a_v, x, col, qkv):
    w = a_v[f, :, :576]
    for s in range(2):
        acc = dg(w, x[s * 512:(s + 1) * 512, :], 0, 1)
        base = 576 * f
        lo = 0
        while lo < 576:
            g = base + lo
            kind = g // 768
            hi = min(576, (kind + 1) * 768 - base)
            part = acc[lo:hi]
            b = g - kind * 768
            if kind == 0:
                part = (part + col[b:b + hi - lo, 2:3]) * 0.125
            elif kind == 2:
                part = part + col[b:b + hi - lo, 3:4]
            qkv[s, g:g + hi - lo, :] = part.astype(bf16)
            lo = hi

def attend_head(qkv, msk, ctx, ptbuf, slot, s, h):
    q = qkv[s, pl.ds(h * HD, HD), :]
    k = qkv[s, pl.ds(768 + h * HD, HD), :]
    v = qkv[s, pl.ds(1536 + h * HD, HD), :]
    st = dg(k, q, 0, 0) + msk[s]
    e = jnp.exp(st - jnp.max(st, axis=0, keepdims=True))
    p = (e * (1.0 / jnp.sum(e, axis=0, keepdims=True))).astype(bf16)
    ptbuf[slot] = p
    ctx[s, pl.ds(h * HD, HD), :] = dg(v, p, 1, 0).astype(bf16)

def attend_all(qkv, msk, ctx, pt, ptbuf, psem, per=2, hook=None):
    steps = 24 // per
    def body(t, carry):
        slot = t % 2
        @pl.when(t >= 2)
        def _():
            pltpu.make_async_copy(ptbuf.at[slot], pt.at[t - 2], psem.at[slot]).wait()
        s = t // (12 // per)
        for u in range(per):
            h = (t % (12 // per)) * per + u
            attend_head(qkv, msk, ctx, ptbuf.at[slot], u, s, h)
        pltpu.make_async_copy(ptbuf.at[slot], pt.at[t], psem.at[slot]).start()
        if hook is not None:
            hook(t)
        return carry
    lax.fori_loop(0, steps, body, 0)
    for t in (steps - 2, steps - 1):
        pltpu.make_async_copy(ptbuf.at[t % 2], pt.at[t], psem.at[t % 2]).wait()

PER = 2


def forward_kernel(pack, small, x, lens, heat, wfull, sfull, qkv, ctx, pt, a_v, s_v, col, msk, ptbuf, ssem, rsem, lsem, psem):
    me = partners()
    enter_barrier(me)
    little, attn, up, down = [
        Gather(me, src, dst, ssem.at[g], rsem.at[g], lsem.at[g])
        for g, (src, dst) in enumerate([(small, sfull)] + [(pack.at[g], wfull.at[g]) for g in range(3)])
    ]
    little.s0(); attn.s0()
    little.s1(); attn.s1(); up.s0()
    little.s2(); attn.s2(); up.s1()
    little.s3(); down.s0(); little.s4()
    c0 = pltpu.make_async_copy(sfull, s_v, lsem.at[4])
    c0.start()
    c0.wait()
    prepare_columns(s_v, col, 64, 144, 96)
    attn.s3(); up.s2()
    prepare_mask(s_v, lens, heat, msk, 64, 144)
    down.s1(); attn.s4()
    c1 = pltpu.make_async_copy(wfull.at[0], a_v, lsem.at[5])
    c1.start()
    c1.wait()
    for f in range(4):
        project(f, a_v, x, col, qkv)
    def hook(t):
        for at, step in ((0, up.s3), (3, down.s2), (4, up.s4), (8, down.s3)):
            pl.when(t == at)(step)
    attend_all(qkv, msk, ctx, pt, ptbuf, psem, PER, hook)
    down.s4()
    for g in (little, attn, up, down):
        g.finish()


def forward_call(pack, small, x, lens, heat):
    any_ = pl.BlockSpec(memory_space=pl.ANY)
    vm = pl.BlockSpec(memory_space=pltpu.VMEM)
    sm = pl.BlockSpec(memory_space=pltpu.SMEM)
    sd = jax.ShapeDtypeStruct
    dma = pltpu.SemaphoreType.DMA
    return pl.pallas_call(
        forward_kernel,
        out_shape=(
            sd((3, 4, 768, 768), bf16),
            sd((4, 1152, 128), bf16),
            sd((2, 2304, 512), bf16),
            sd((2, 768, 512), bf16),
            sd((24 // PER, PER, 512, 512), bf16),
        ),
        in_specs=[any_, any_, vm, sm, sm],
        out_specs=(any_, any_, vm, vm, any_),
        scratch_shapes=[
            pltpu.VMEM((4, 768, 768), bf16),
            pltpu.VMEM((4, 1152, 128), bf16),
            pltpu.VMEM((768, 16), f32),
            pltpu.VMEM((2, 512, 512), f32),
            pltpu.VMEM((2, PER, 512, 512), bf16),
            dma((4, 19)),
            dma((4, 19)),
            dma((6,)),
            dma((2,)),
        ],
        compiler_params=pltpu.CompilerParams(collective_id=0, has_side_effects=True, vmem_limit_bytes=60 << 20),
        name="gather_and_attend",
    )(pack, small, x, lens, heat)


def norm_rows(v):
    mean = jnp.mean(v, axis=-1, keepdims=True)
    c = v - mean
    inv = lax.rsqrt(jnp.mean(c * c, axis=-1, keepdims=True) + 1e-6)
    return c * inv, inv

def norm_rows_back(g, normed, inv, gain):
    e = g * gain
    return inv * (e - jnp.mean(e, axis=-1, keepdims=True) - normed * jnp.mean(e * normed, axis=-1, keepdims=True))

def mid_kernel(wfull, ctx, x, cot, vec, bup, out, act, gp, hlow, gslow, gf, gfl, gctx, sums, gbup, a_v, u_v, d_v, wout, slope, wsem):
    s = pl.program_id(0)
    cps = [pltpu.make_async_copy(wfull.at[g], v, wsem.at[g]) for g, v in enumerate((a_v, u_v, d_v))]
    @pl.when(s == 0)
    def _():
        for c in cps: c.start()
        cps[0].wait()
        for f in range(4):
            wout[:, 192 * f:192 * f + 192] = a_v[f, :, 576:]
        cps[1].wait()
        cps[2].wait()
    first = x[...].astype(f32) + dg(ctx[0], wout[...], 0, 0) + vec[4:5]
    n1, inv1 = norm_rows(first)
    hidden = n1 * vec[0:1] + vec[6:7]
    hl = hidden.astype(bf16)
    hlow[...] = hl
    acc = hidden + vec[5:6]
    for f in range(4):
        pre = dg(hl, u_v[f], 1, 0) + bup[:, 768 * f:768 * f + 768]
        phi = 0.5 * (1.0 + lax.erf(pre * 0.7071067811865476))
        slope[f] = phi + pre * (jnp.exp(-0.5 * pre * pre) * 0.3989422804014327)
        a = (pre * phi).astype(bf16)
        act[:, 768 * f:768 * f + 768] = a
        acc = acc + dg(a, d_v[f], 1, 1)
    n2, inv2 = norm_rows(acc)
    out[...] = (n2 * vec[1:2] + vec[7:8]).astype(bf16)
    g = cot[...].astype(f32)
    gs = norm_rows_back(g, n2, inv2, vec[1:2])
    gsl = gs.astype(bf16)
    gslow[...] = gsl
    gh = gs
    for f in range(4):
        ga = dg(gsl, d_v[f], 1, 0)
        p = (ga * slope[f]).astype(bf16)
        gp[:, 768 * f:768 * f + 768] = p
        b = jnp.sum(p.astype(f32), axis=0, keepdims=True)
        old = jnp.where(s == 0, 0.0, gbup[:, 768 * f:768 * f + 768])
        gbup[:, 768 * f:768 * f + 768] = old + b
        gh = gh + dg(p, u_v[f], 1, 1)
    gfirst = norm_rows_back(gh, n1, inv1, vec[0:1])
    gf[...] = gfirst
    gfl[...] = gfirst.astype(bf16)
    gctx[0] = dg(wout[...], gfirst.astype(bf16), 1, 1).astype(bf16)
    rs = lambda v: jnp.sum(v, axis=0, keepdims=True)
    rows = jnp.concatenate([rs(gh * n1), rs(g * n2), jnp.zeros((2, 768), f32), rs(gfirst), rs(gs), rs(gh), rs(g)], axis=0)
    sums[...] = jnp.where(s == 0, 0.0, sums[...]) + rows

def mid_call(wfull, ctx, x, cot, vec, bup):
    T = 512
    any_ = pl.BlockSpec(memory_space=pl.ANY)
    tok = lambda n: pl.BlockSpec((T, n), lambda s: (s, 0))
    tr = pl.BlockSpec((1, 768, T), lambda s: (s, 0, 0))
    const = lambda sh: pl.BlockSpec(sh, lambda s: (0,) * len(sh))
    sd = jax.ShapeDtypeStruct
    return pl.pallas_call(mid_kernel, grid=(2,),
        out_shape=(sd((1024, 768), bf16), sd((1024, 3072), bf16), sd((1024, 3072), bf16), sd((1024, 768), bf16), sd((1024, 768), bf16), sd((1024, 768), f32), sd((1024, 768), bf16), sd((2, 768, 512), bf16), sd((8, 768), f32), sd((1, 3072), f32)),
        in_specs=[any_, tr, tok(768), tok(768), const((8, 768)), const((1, 3072))],
        out_specs=(tok(768), tok(3072), tok(3072), tok(768), tok(768), tok(768), tok(768), tr, const((8, 768)), const((1, 3072))),
        scratch_shapes=[pltpu.VMEM((4, 768, 768), bf16)] * 3 + [pltpu.VMEM((768, 768), bf16), pltpu.VMEM((4, T, 768), f32), pltpu.SemaphoreType.DMA((3,))],
        compiler_params=pltpu.CompilerParams(vmem_limit_bytes=62 << 20), name="feed_forward")(wfull, ctx, x, cot, vec, bup)

def attend_head_back(qkv, gctx, p_ref, dproj, gm, s, h):
    q = qkv[s, pl.ds(h * HD, HD), :]
    k = qkv[s, pl.ds(768 + h * HD, HD), :]
    v = qkv[s, pl.ds(1536 + h * HD, HD), :]
    go = gctx[s, pl.ds(h * HD, HD), :]
    p = p_ref[...]
    dp = dg(v, go, 0, 0)
    pf = p.astype(f32)
    drow = jnp.sum(pf * dp, axis=0, keepdims=True)
    ds = pf * (dp - drow)
    dsl = ds.astype(bf16)
    dproj[s, pl.ds(1536 + h * HD, HD), :] = dg(go, p, 1, 1).astype(bf16)
    dproj[s, pl.ds(768 + h * HD, HD), :] = dg(q, dsl, 1, 1).astype(bf16)
    dproj[s, pl.ds(h * HD, HD), :] = (dg(k, dsl, 1, 0) * 0.125).astype(bf16)
    return ds

def attend_all_back(qkv, gctx, pt, ptbuf, psem, dproj, gm, per, hook=None):
    steps = 24 // per
    gm[...] = jnp.zeros(gm.shape, f32)
    def body(t, carry):
        slot = t % 2
        pltpu.make_async_copy(pt.at[t], ptbuf.at[slot], psem.at[slot]).wait()
        s = t // (12 // per)
        tot = None
        for u in range(per):
            h = (t % (12 // per)) * per + u
            ds = attend_head_back(qkv, gctx, ptbuf.at[slot, u], dproj, gm, s, h)
            tot = ds if tot is None else tot + ds
        gm[...] += tot
        @pl.when(t + 2 < steps)
        def _():
            pltpu.make_async_copy(pt.at[t + 2], ptbuf.at[slot], psem.at[slot]).start()
        if hook is not None:
            hook(t)
        return carry
    lax.fori_loop(0, steps, body, 0)

ORDER = (1, 2, 3, 0)


def small_rows(part, gm, sums, gbup):
    table = gm[...].T
    zero = jnp.zeros((8, 32), f32)
    for f in range(4):
        bias = jnp.concatenate(
            [gbup[:, 768 * f + 128 * r : 768 * f + 128 * r + 128] for r in range(6)] + [jnp.zeros((2, 128), f32)], axis=0
        )
        for i in range(8):
            ref = part.at[f, i // 2, i % 2]
            for j in range(4):
                at = 64 * i + 16 * j
                ref[96:112, 128 * j : 128 * j + 128] = table[at : at + 16, 128 * f : 128 * f + 128].astype(bf16)
            rows = jnp.concatenate([sums[:, 96 * i : 96 * i + 96], zero], axis=1)
            ref[96:112, 512:640] = jnp.concatenate([rows, bias], axis=0).astype(bf16)
            ref[96:112, 640:768] = jnp.zeros((16, 128), bf16)


def backward_kernel(wfull, qkv_h, pt, gctx_h, ctx_h, act, gp, hlow, gslow, x, gfl_h, gf, sums_in, gbup, gin, obig, oattn,
                    part, apart, rc, rq, rx, ry, rz, arc, arq, arx, ary, arz, gm, sums,
                    lhs, chunk, qkv, gctx, ctx, gfl, dproj, ptbuf, gbuf, ssem, rsem, lsem, csem, isem, psem, gsem):
    me = partners()
    cp = pltpu.make_async_copy
    at = [(me[1] + k) % 4 for k in range(4)]
    def chunk_copy(n):
        src = (act, gp)[n // 4].at[:, pl.ds(pl.multiple_of(768 * at[ORDER[n % 4]], 768), 768)]
        return cp(src, chunk.at[n % 2], csem.at[n % 2])
    l0 = cp(gslow, lhs.at[0], lsem.at[0]); l1 = cp(hlow, lhs.at[1], lsem.at[1]); l2 = cp(x, lhs.at[0], lsem.at[0])
    l0.start(); chunk_copy(0).start(); chunk_copy(1).start(); l1.start()
    ins = [cp(a, b, isem.at[n]) for n, (a, b) in enumerate(((ctx_h, ctx), (gfl_h, gfl), (qkv_h, qkv), (gctx_h, gctx)))]
    for c in ins: c.start()
    for t in range(2): cp(pt.at[t], ptbuf.at[t], psem.at[t]).start()
    up, down = [
        Scatter(me, part.at[g], [b.at[g] for b in (rc, rq, rx, ry, rz)], obig.at[g], ssem.at[g], rsem.at[g]) for g in range(2)
    ]
    attn = Scatter(me, apart, (arc, arq, arx, ary, arz), oattn, ssem.at[2], rsem.at[2])
    before, loop, dots = steps_between(attn, up, down)
    l0.wait()
    for n in range(8):
        g, k = (down, up)[n // 4], ORDER[n % 4]
        if n == 4:
            l2.start()
            l1.wait()
        chunk_copy(n).wait()
        g.part[at[k]] = dg(lhs[n // 4], chunk[n % 2], 0, 0).astype(bf16).reshape(4, 2, 96, 768)
        if n < 6: chunk_copy(n + 2).start()
        if n == 0:
            enter_barrier(me)
        g.c_(k)
        run_steps(before.get(n, ()))
    for c in ins: c.wait()
    dwo = dg(ctx[0], gfl[0:512], 1, 0) + dg(ctx[1], gfl[512:1024], 1, 0)
    for f in range(4):
        attn.part[f, :, :, 0:96, 576:] = dwo[:, 192 * f:192 * f + 192].astype(bf16).reshape(4, 2, 96, 192)
    run_steps(before[8])
    def hook(t):
        for at_t in sorted(loop):
            pl.when(t == at_t)(functools.partial(run_steps, loop[at_t]))
    attend_all_back(qkv, gctx, pt, ptbuf, psem, dproj, gm, PER, hook)
    ones = jnp.ones((8, 512), bf16)
    sums[...] = sums_in[...]
    sums[2:3] = (dg(ones, dproj[0, 0:768], 1, 1) + dg(ones, dproj[1, 0:768], 1, 1))[0:1]
    sums[3:4] = (dg(ones, dproj[0, 1536:2304], 1, 1) + dg(ones, dproj[1, 1536:2304], 1, 1))[0:1]
    small_rows(attn.part, gm, sums, gbup)
    l2.wait()
    for n, k in enumerate(ORDER):
        r = pl.ds(pl.multiple_of(576 * at[k], 576), 576)
        dw = dg(lhs[0, 0:512], dproj[0, r, :], 0, 1) + dg(lhs[0, 512:1024], dproj[1, r, :], 0, 1)
        attn.part[at[k], :, :, 0:96, :576] = dw.astype(bf16).reshape(4, 2, 96, 576)
        attn.c_(k)
        run_steps(dots.get(n, ()))
    aw = [cp(wfull.at[0, f], chunk.at[f % 2, pl.ds(0, 768)], csem.at[f % 2]) for f in range(4)]
    aw[0].start(); aw[1].start()
    gi = [cp(gf.at[pl.ds(512 * s, 512)], gbuf.at[s], gsem.at[s]) for s in range(2)]
    for c in gi: c.start()
    for f in range(4):
        aw[f].wait()
        if f == 0:
            for c in gi: c.wait()
        for s in range(2):
            gbuf[s] = gbuf[s] + dg(dproj[s, 576 * f:576 * f + 576], chunk[f % 2, 0:768, :576], 0, 1)
            run_steps(dots.get(4 + 2 * f + s, ()))
        if f < 2: aw[f + 2].start()
    go = [cp(gbuf.at[s], gin.at[pl.ds(512 * s, 512)], gsem.at[s]) for s in range(2)]
    for c in go: c.start()
    run_steps(dots.get(12, ()))
    for c in go: c.wait()
    for g in (attn, up, down):
        g.finish()


def steps_between(attn, up, down):
    before = {
        2: [(down.q, 1)],
        3: [(down.q, 2)],
        4: [(down.q, 3)],
        5: [(down.q, 0), (down.t, 1)],
        6: [(down.t, 2), (up.q, 1)],
        7: [(up.q, 2)],
        8: [(down.t, 3), (up.q, 3)],
    }
    loop = {
        0: [(down.t, 0), (up.q, 0)],
        2: [(down.w, 2)],
        3: [(down.w, 1), (up.t, 1)],
        4: [(up.t, 2)],
        7: [(up.t, 3)],
        8: [(down.w, 3)],
        9: [(up.t, 0)],
        10: [(down.w, 0)],
        11: [(down.e,), (up.w, 2)],
    }
    dots = {
        0: [(up.w, 1), (up.w, 0)],
        1: [(up.w, 3)],
        2: [(attn.q, 1)],
        3: [(attn.q, 2)],
        5: [(attn.q, 3)],
        8: [(attn.t, 1)],
        12: [(attn.t, 2), (up.e,), (attn.t, 3), (attn.q, 0), (attn.w, 1), (attn.w, 3), (attn.w, 2), (attn.t, 0), (attn.w, 0), (attn.e,)],
    }
    return before, loop, dots


def run_steps(todo):
    for step, *arg in todo:
        step(*arg)


def backward_call(*ops):
    any_ = pl.BlockSpec(memory_space=pl.ANY); vm = pl.BlockSpec(memory_space=pltpu.VMEM)
    sd = jax.ShapeDtypeStruct
    dma = pltpu.SemaphoreType.DMA
    V = pltpu.VMEM
    return pl.pallas_call(backward_kernel,
        out_shape=(sd((1024, 768), f32), sd((2, 96, 768), f32), sd((112, 768), f32)),
        in_specs=[any_] * 12 + [vm] * 2, out_specs=(any_, vm, vm),
        scratch_shapes=[V((2, 4, 4, 2, 96, 768), bf16), V((4, 4, 2, 112, 768), bf16)] + scatter_buffers((2,), 96, 768, bf16) + scatter_buffers((), 112, 768, bf16)
            + [V((512, 512), f32), V((8, 768), f32)]
            + [V((2, 1024, 768), bf16), V((2, 1024, 768), bf16), V((2, 2304, 512), bf16), V((2, 768, 512), bf16), V((2, 768, 512), bf16), V((1024, 768), bf16),
            V((2, 2304, 512), bf16), V((2, PER, 512, 512), bf16), V((2, 512, 768), f32), dma((3, 19)), dma((3, 19)), dma((2,)), dma((2,)), dma((4,)), dma((2,)), dma((2,))],
        compiler_params=pltpu.CompilerParams(collective_id=1, has_side_effects=True, vmem_limit_bytes=63 << 20), name="attend_back_and_reduce")(*ops)


def hand_out_kernel(gin, big, attn, gate, jitter, heat, gin_o, qkv, out, up, down, bias, gains, shifts, logits, sem):
    n = 8
    rows = gin.shape[0] // n
    cps = [pltpu.make_async_copy(gin.at[pl.ds(r * rows, rows)], gin_o.at[pl.ds(r * rows, rows)], sem.at[r]) for r in range(n)]
    for c in cps: c.start()
    qkv[...] = attn[:96, :576]
    out[...] = attn[:96, 576:]
    up[...] = big[0]
    down[...] = big[1].T
    inv = 1.0 / heat[0]
    table = jnp.concatenate([attn[96:112, 128 * j:128 * j + 128] for j in range(4)], axis=0)
    mixed = (gate[...].astype(f32) + jitter[...].astype(f32)) * inv
    logits[...] = table * (inv / (1.0 + jnp.exp(mixed)))
    gains[...] = attn[96:98, 512:608]
    shifts[...] = attn[98:104, 512:608]
    bias[...] = attn[104:110, 512:640]
    for c in cps: c.wait()


def hand_out_call(gin, big, attn, gate, jitter, heat):
    any_ = pl.BlockSpec(memory_space=pl.ANY); vm = pl.BlockSpec(memory_space=pltpu.VMEM); sm = pl.BlockSpec(memory_space=pltpu.SMEM)
    sd = lambda *s: jax.ShapeDtypeStruct(s, f32)
    return pl.pallas_call(hand_out_kernel,
        out_shape=(sd(1024, 768), sd(96, 576), sd(96, 192), sd(96, 768), sd(768, 96), sd(6, 128), sd(2, 96), sd(6, 96), sd(64, 128)),
        in_specs=[any_, vm, vm, vm, vm, sm], out_specs=(any_,) + (vm,) * 8,
        scratch_shapes=[pltpu.SemaphoreType.DMA((8,))],
        compiler_params=pltpu.CompilerParams(vmem_limit_bytes=32 << 20), name="hand_out")(gin, big, attn, gate, jitter, heat)


def own_device(
    layer_activations,
    token_counts_each,
    attention_triple_matrix,
    attention_final_matrix,
    feedfwd_expand_matrix,
    feedfwd_expand_offset,
    feedfwd_contract_matrix,
    layernorm_scales,
    offset_vectors,
    learned_gate_scores,
    fixed_jitter_matrix,
    relaxation_heat,
    loss_grad_result,
):
    pack = jnp.stack(
        [
            jnp.concatenate([attention_triple_matrix, attention_final_matrix], axis=1),
            feedfwd_expand_matrix,
            feedfwd_contract_matrix.T,
        ]
    )
    vectors = jnp.concatenate([layernorm_scales, offset_vectors], axis=0)
    small = jnp.concatenate(
        [
            learned_gate_scores,
            fixed_jitter_matrix,
            jnp.pad(vectors, ((0, 0), (0, 32))),
            jnp.pad(feedfwd_expand_offset.reshape(6, 128), ((0, 2), (0, 0))),
        ],
        axis=0,
    )
    x = layer_activations.reshape(1024, D)
    cot = loss_grad_result.reshape(1024, D)
    weights, small_full, qkv, ctx, probs = forward_call(pack, small, x, token_counts_each, relaxation_heat)
    small_full = small_full.reshape(4, 8, 144, 128)
    vectors_full = small_full[0, :, 128:136, :96].transpose(1, 0, 2).reshape(8, D).astype(f32)
    bias_up = small_full[:, 0, 136:142].reshape(1, 3072).astype(f32)
    result, act, grad_pre, hidden_low, grad_second_low, grad_first, grad_first_low, grad_ctx, sums, grad_bias = mid_call(
        weights, ctx, x, cot, vectors_full, bias_up
    )
    grad_inputs, big, attn = backward_call(
        weights, qkv, probs, grad_ctx, ctx, act, grad_pre, hidden_low, grad_second_low, x, grad_first_low, grad_first,
        sums, grad_bias,
    )
    grad_inputs, g_qkv, g_out, g_up, g_down, g_bias, g_gains, g_shifts, g_logits = hand_out_call(
        grad_inputs, big, attn, learned_gate_scores, fixed_jitter_matrix, relaxation_heat
    )
    return (
        result.reshape(layer_activations.shape),
        grad_inputs.reshape(layer_activations.shape),
        g_qkv,
        g_out,
        g_up,
        g_bias.reshape(-1),
        g_down,
        g_gains,
        g_shifts,
        g_logits,
    )


def solution(mesh):
    in_specs = (
        P(AXES, None, None),
        P(AXES),
        P("dp", "ffn"),
        P("dp", "ffn"),
        P("dp", "ffn"),
        P("ffn"),
        P("ffn", "dp"),
        P(None, "dp"),
        P(None, "dp"),
        P("dp", "ffn"),
        P("dp", "ffn"),
        P(),
        P(AXES, None, None),
    )
    out_specs = (
        P(AXES, None, None),
        P(AXES, None, None),
        P("dp", "ffn"),
        P("dp", "ffn"),
        P("dp", "ffn"),
        P("ffn"),
        P("ffn", "dp"),
        P(None, "dp"),
        P(None, "dp"),
        P("dp", "ffn"),
    )
    own = (mesh.shape["dp"], mesh.shape["ffn"]) == (8, 4)
    return jax.shard_map(
        own_device if own else general_device, mesh=mesh, in_specs=in_specs, out_specs=out_specs, check_vma=False
    )
```

```python
import functools

import jax
import jax.numpy as jnp
from jax import lax
from jax.experimental import pallas as pl
from jax.experimental.pallas import tpu as pltpu
from jax.sharding import PartitionSpec as P

D = 768
HEADS = 12
HEAD_DIM = 64
SEQ_LEN = 512
AXES = ("dp", "ffn")
norm_eps = 1e-06
f32 = jnp.float32
bf16 = jnp.bfloat16
MESH = pl.DeviceIdType.MESH


def dot_first(left, right):
    return lax.dot_general(left, right, (((0,), (0,)), ((), ())), preferred_element_type=f32)


def dot_last(left, right):
    return lax.dot_general(left, right, (((1,), (1,)), ((), ())), preferred_element_type=f32)


def dot(left, right):
    return jnp.dot(left, right, preferred_element_type=f32)


def layer_norm(values, gain, shift):
    mean_row = jnp.mean(values, axis=-1, keepdims=True)
    centered = values - mean_row
    inv_std = lax.rsqrt(jnp.mean(centered * centered, axis=-1, keepdims=True) + norm_eps)
    normed = centered * inv_std
    return (normed * gain + shift, normed, inv_std)


def norm_back(grad_out, normed, inv_std, gain):
    grad_normed = grad_out * gain
    grad_in = inv_std * (
        grad_normed
        - jnp.mean(grad_normed, axis=-1, keepdims=True)
        - normed * jnp.mean(grad_normed * normed, axis=-1, keepdims=True)
    )
    return (grad_in, jnp.sum(grad_out * normed, axis=0), jnp.sum(grad_out, axis=0))


def gelu_slope(values):
    return (
        0.5 * (1.0 + lax.erf(values * 0.7071067811865476))
        + values * jnp.exp(-0.5 * values * values) * 0.3989422804014327
    )


def score_block(queries, keys_low, natural_log_gate, live):
    scores = (
        jnp.einsum("qhd,khd->hqk", queries, keys_low, preferred_element_type=f32)
        * HEAD_DIM ** (-0.5)
        + natural_log_gate
    )
    return jnp.where(live[None, None, :], scores, -1e30)


def attend(queries, keys_low, values_low, natural_log_gate, live):
    scores = score_block(queries, keys_low, natural_log_gate, live)
    peak = jnp.max(scores, axis=-1, keepdims=True)
    shifted_exp = jnp.exp(scores - peak)
    total_exp = jnp.sum(shifted_exp, axis=-1, keepdims=True)
    probs_low = (shifted_exp / total_exp).astype(bf16)
    context = jnp.einsum("hqk,khd->qhd", probs_low, values_low, preferred_element_type=f32)
    return (context, peak + jnp.log(total_exp))


def attend_back(queries, keys_low, values_low, natural_log_gate, live, log_total, grad_context):
    scores = score_block(queries, keys_low, natural_log_gate, live)
    probs = jnp.exp(scores - log_total)
    grad_probs = jnp.einsum("qhd,khd->hqk", grad_context, values_low, preferred_element_type=f32)
    grad_values = jnp.einsum(
        "hqk,qhd->khd", probs.astype(bf16), grad_context, preferred_element_type=f32
    )
    grad_scores = probs * (grad_probs - jnp.sum(probs * grad_probs, axis=-1, keepdims=True))
    grad_mask = jnp.sum(grad_scores, axis=0)
    grad_scores_low = grad_scores.astype(bf16)
    grad_queries = jnp.einsum(
        "hqk,khd->qhd", grad_scores_low, keys_low, preferred_element_type=f32
    ) * HEAD_DIM ** (-0.5)
    grad_keys = jnp.einsum(
        "hqk,qhd->khd", grad_scores_low, queries, preferred_element_type=f32
    ) * HEAD_DIM ** (-0.5)
    return (grad_queries, grad_keys, grad_values, grad_mask)


def gather_weights(pack, small):
    rows_dp = lax.axis_size("dp")
    cols_ffn = lax.axis_size("ffn")
    full = lax.all_gather(pack[None], AXES, axis=0, tiled=True)
    full = full.reshape(rows_dp, cols_ffn, *pack.shape)
    small_full = lax.all_gather(small[None], AXES, axis=0, tiled=True)
    return full, small_full.reshape(rows_dp, cols_ffn, *small.shape)


def columns(blocks):
    rows_dp, cols_ffn, rows, cols = blocks.shape
    return blocks.transpose(0, 2, 1, 3).reshape(rows_dp * rows, cols_ffn * cols)


def blocks_of(full, rows_dp, cols_ffn):
    rows, cols = full.shape
    return full.reshape(rows_dp, rows // rows_dp, cols_ffn, cols // cols_ffn).transpose(0, 2, 1, 3)


def general_device(
    layer_activations,
    token_counts_each,
    attention_triple_matrix,
    attention_final_matrix,
    feedfwd_expand_matrix,
    feedfwd_expand_offset,
    feedfwd_contract_matrix,
    layernorm_scales,
    offset_vectors,
    learned_gate_scores,
    fixed_jitter_matrix,
    relaxation_heat,
    loss_grad_result,
):
    rows_dp = lax.axis_size("dp")
    cols_ffn = lax.axis_size("ffn")
    seq_count = layer_activations.shape[0]
    row_count = seq_count * SEQ_LEN
    shard_rows = attention_triple_matrix.shape[0]
    qkv_cols = attention_triple_matrix.shape[1]
    out_cols = attention_final_matrix.shape[1]
    ff_cols = feedfwd_expand_matrix.shape[1]

    pack = jnp.concatenate(
        [
            attention_triple_matrix,
            attention_final_matrix,
            feedfwd_expand_matrix,
            feedfwd_contract_matrix.T,
        ],
        axis=1,
    )
    mask_cols = learned_gate_scores.shape[1]
    vectors = jnp.concatenate([layernorm_scales, offset_vectors], axis=0)
    small = jnp.concatenate(
        [
            learned_gate_scores,
            fixed_jitter_matrix,
            jnp.pad(vectors, ((0, 0), (0, mask_cols - vectors.shape[1]))),
            feedfwd_expand_offset.reshape(-1, mask_cols),
        ],
        axis=0,
    )
    full, small_full = gather_weights(pack, small)
    full_qkv = columns(full[..., :qkv_cols])
    full_out = columns(full[..., qkv_cols : qkv_cols + out_cols])
    full_up = columns(full[..., qkv_cols + out_cols : qkv_cols + out_cols + ff_cols])
    full_down_t = columns(full[..., qkv_cols + out_cols + ff_cols :])
    mask_rows = learned_gate_scores.shape[0]
    logits_sum = columns(small_full[:, :, :mask_rows]).astype(f32) + columns(
        small_full[:, :, mask_rows : 2 * mask_rows]
    ).astype(f32)
    natural_log_gate = jax.nn.log_sigmoid(logits_sum / relaxation_heat[0])
    vectors_full = (
        small_full[:, 0, 2 * mask_rows : 2 * mask_rows + 8, :shard_rows]
        .transpose(1, 0, 2)
        .reshape(8, D)
        .astype(f32)
    )
    gains_full = vectors_full[:2]
    shifts_full = vectors_full[2:]
    bias_up = small_full[0, :, 2 * mask_rows + 8 :].reshape(1, -1).astype(f32)

    flat_in = layer_activations.reshape(row_count, D)
    qkv_bias = jnp.concatenate([shifts_full[0], jnp.zeros((D,), f32), shifts_full[1]])
    proj_low = (dot(flat_in, full_qkv) + qkv_bias).astype(bf16)
    head_shape = (seq_count, SEQ_LEN, HEADS, HEAD_DIM)
    queries = proj_low[:, :D].reshape(head_shape)
    keys_low = proj_low[:, D : 2 * D].reshape(head_shape)
    values_low = proj_low[:, 2 * D :].reshape(head_shape)
    live = lax.broadcasted_iota(jnp.int32, (seq_count, SEQ_LEN), 1) < token_counts_each[:, None]
    attended = [
        attend(queries[s], keys_low[s], values_low[s], natural_log_gate, live[s])
        for s in range(seq_count)
    ]
    context_low = jnp.concatenate(
        [item[0].reshape(SEQ_LEN, D).astype(bf16) for item in attended], axis=0
    )
    first_sum = flat_in.astype(f32) + dot(context_low, full_out) + shifts_full[2]
    hidden, normed_one, inv_one = layer_norm(first_sum, gains_full[0], shifts_full[4])
    hidden_low = hidden.astype(bf16)
    pre_act = dot(hidden_low, full_up) + bias_up
    act_low = jax.nn.gelu(pre_act, approximate=False).astype(bf16)
    second_sum = hidden + dot_last(act_low, full_down_t) + shifts_full[3]
    result, normed_two, inv_two = layer_norm(second_sum, gains_full[1], shifts_full[5])
    cot_flat = loss_grad_result.reshape(row_count, D).astype(f32)
    grad_second, grad_gain_two, grad_shift_two = norm_back(
        cot_flat, normed_two, inv_two, gains_full[1]
    )
    grad_second_low = grad_second.astype(bf16)
    grad_w_down_t = dot_first(grad_second_low, act_low)
    grad_act = dot(grad_second_low, full_down_t)
    grad_pre = (grad_act * gelu_slope(pre_act)).astype(bf16)
    grad_bias_up = jnp.sum(grad_pre, axis=0, dtype=f32)
    grad_w_up = dot_first(hidden_low, grad_pre)
    grad_hidden = grad_second + dot_last(grad_pre, full_up)
    grad_first, grad_gain_one, grad_shift_one = norm_back(
        grad_hidden, normed_one, inv_one, gains_full[0]
    )
    grad_first_low = grad_first.astype(bf16)
    grad_w_out = dot_first(context_low, grad_first_low)
    grad_context = dot_last(grad_first_low, full_out).astype(bf16).reshape(head_shape)
    back = [
        attend_back(
            queries[s],
            keys_low[s],
            values_low[s],
            natural_log_gate,
            live[s],
            attended[s][1],
            grad_context[s],
        )
        for s in range(seq_count)
    ]
    grad_mask = sum(item[3] for item in back)
    grad_projected = jnp.concatenate(
        [
            jnp.concatenate(
                [item[part].reshape(SEQ_LEN, D).astype(bf16) for item in back], axis=0
            )
            for part in range(3)
        ],
        axis=1,
    )
    grad_w_qkv = dot_first(flat_in, grad_projected)
    grad_inputs = grad_first + dot_last(grad_projected, full_qkv)
    grad_vectors = jnp.stack(
        [
            grad_gain_one,
            grad_gain_two,
            jnp.sum(grad_projected[:, :D], axis=0, dtype=f32),
            jnp.sum(grad_projected[:, 2 * D :], axis=0, dtype=f32),
            jnp.sum(grad_first, axis=0),
            jnp.sum(grad_second, axis=0),
            grad_shift_one,
            grad_shift_two,
        ]
    )
    big = jnp.concatenate(
        [
            blocks_of(item, rows_dp, cols_ffn)
            for item in (grad_w_qkv, grad_w_out, grad_w_up, grad_w_down_t)
        ],
        axis=-1,
    ).reshape(rows_dp * cols_ffn, shard_rows, -1)
    vector_blocks = jnp.broadcast_to(
        grad_vectors.reshape(8, rows_dp, 1, shard_rows).transpose(1, 2, 0, 3),
        (rows_dp, cols_ffn, 8, shard_rows),
    )
    bias_blocks = jnp.broadcast_to(
        grad_bias_up.reshape(1, cols_ffn, -1, mask_cols),
        (rows_dp, cols_ffn, ff_cols // mask_cols, mask_cols),
    )
    little = jnp.concatenate(
        [
            blocks_of(grad_mask, rows_dp, cols_ffn),
            jnp.pad(vector_blocks, ((0, 0), (0, 0), (0, 0), (0, mask_cols - shard_rows))),
            bias_blocks,
        ],
        axis=2,
    ).reshape(rows_dp * cols_ffn, -1, mask_cols)
    big = lax.psum_scatter(big, AXES, scatter_dimension=0, tiled=True)[0]
    little = lax.psum_scatter(little, AXES, scatter_dimension=0, tiled=True)[0]

    own_mixed = (
        learned_gate_scores.astype(f32) + fixed_jitter_matrix.astype(f32)
    ) / relaxation_heat[0]
    grad_logits = little[:mask_rows] * (jax.nn.sigmoid(-own_mixed) / relaxation_heat[0])
    return (
        result.astype(bf16).reshape(layer_activations.shape),
        grad_inputs.reshape(layer_activations.shape),
        big[:, :qkv_cols],
        big[:, qkv_cols : qkv_cols + out_cols],
        big[:, qkv_cols + out_cols : qkv_cols + out_cols + ff_cols],
        little[mask_rows + 8 :].reshape(-1),
        big[:, qkv_cols + out_cols + ff_cols :].T,
        little[mask_rows : mask_rows + 2, :shard_rows],
        little[mask_rows + 2 : mask_rows + 8, :shard_rows],
        grad_logits,
    )


def partners():
    i = lax.axis_index("dp")
    f = lax.axis_index("ffn")
    core = i + 1 - 2 * (i % 2)
    ix = i + 2 - 4 * ((i // 2) % 2)
    iy = (i + 4) % 8
    idg = (ix + 4) % 8
    return i, f, core, ix, iy, idg


def enter_barrier(me):
    i, f, core, ix, iy, idg = me
    sem = pltpu.get_barrier_semaphore()
    mates = [(i, (f + k) % 4) for k in (1, 2, 3)] + [(core, f), (ix, f), (iy, f)]
    for to in mates:
        pl.semaphore_signal(sem, inc=1, device_id=to, device_id_type=MESH)
    pl.semaphore_wait(sem, len(mates))


class Exchange:
    def __init__(self, me, ssem, rsem):
        self.me, self.ssem, self.rsem = me, ssem, rsem
        self.sent = []

    def copy(self, src, dst, n, to):
        return pltpu.make_async_remote_copy(
            src_ref=src,
            dst_ref=dst,
            send_sem=self.ssem.at[n],
            recv_sem=self.rsem.at[n],
            device_id=to,
            device_id_type=MESH,
        )

    def send(self, src, dst, n, to):
        self.copy(src, dst, n, to).start()
        self.sent.append((n, len(src.shape) == 3))

    def recv(self, ref, n):
        self.copy(ref, ref, n, (self.me[0], self.me[1])).wait_recv()

    def finish(self):
        for n, is_block in self.sent:
            ref = self.block(0) if is_block else self.piece(0, 0)
            self.copy(ref, ref, n, (self.me[0], self.me[1])).wait_send()


class Gather(Exchange):
    def __init__(self, me, dst, ssem, rsem, rows, stride, offset=0, src=None, lsem=None):
        super().__init__(me, ssem, rsem)
        self.dst, self.rows, self.stride, self.offset, self.lsem = dst, rows, stride, offset, lsem
        self.src = src

    def span(self, i):
        return pl.ds(pl.multiple_of(i * self.stride + self.offset, 16), self.rows)

    def piece(self, i, p):
        return self.dst.at[p, self.span(i)]

    def block(self, i):
        return self.dst.at[:, self.span(i)]

    def own(self):
        return self.piece(self.me[0], self.me[1]) if self.src is None else self.src

    def local(self):
        i, f = self.me[:2]
        return pltpu.make_async_copy(self.src, self.piece(i, f), self.lsem)

    def sz(self, _):
        i, f, core, ix, iy, idg = self.me
        if self.src is not None:
            self.local().start()
        for k in (1, 2, 3):
            self.send(self.own(), self.piece(i, f), 3 - k, (i, (f + k) % 4))

    def sp(self, _):
        i, f, core, ix, iy, idg = self.me
        self.send(self.own(), self.piece(i, f), 3, (ix, f))
        self.send(self.own(), self.piece(i, f), 7, (iy, f))

    def z(self, k):
        i, f, core, ix, iy, idg = self.me
        ref = self.piece(i, (f + k) % 4)
        self.recv(ref, k - 1)
        self.send(ref, ref, 3 + k, (ix, f))
        self.send(ref, ref, 7 + k, (iy, f))

    def o(self, _):
        i, f, core, ix, iy, idg = self.me
        if self.src is not None:
            self.local().wait()
        self.send(self.block(i), self.block(i), 15, (core, f))

    def d(self, k):
        i, f, core, ix, iy, idg = self.me
        p = (f + k) % 4
        rx, ry = self.piece(ix, p), self.piece(iy, p)
        self.recv(rx, 3 + k)
        self.recv(ry, 7 + k)
        if k % 2:
            self.send(rx, rx, 11 + k, (iy, f))
        else:
            self.send(ry, ry, 11 + k, (ix, f))

    def b(self, _):
        i, f, core, ix, iy, idg = self.me
        self.send(self.block(ix), self.block(ix), 16, (core, f))
        self.send(self.block(iy), self.block(iy), 17, (core, f))

    def h(self, _):
        i, f, core, ix, iy, idg = self.me
        for k in range(4):
            self.recv(self.piece(idg, (f + k) % 4), 11 + k)
        self.send(self.block(idg), self.block(idg), 18, (core, f))

    def r(self, _):
        i, f, core, ix, iy, idg = self.me
        for n, other in ((15, i), (16, ix), (17, iy), (18, idg)):
            self.recv(self.block(other + core - i), n)


class Scatter(Exchange):
    def __init__(self, me, part, got, out, ssem, rsem):
        super().__init__(me, ssem, rsem)
        self.part, self.out = part, out
        self.rc, self.rq, self.rx, self.ry, self.rz = got
        i = me[0]
        self.c = i % 2
        self.xy = i // 2
        self.xyx = self.xy + 1 - 2 * (self.xy % 2)
        self.xyy = (self.xy + 2) % 4
        self.xyd = (self.xyx + 2) % 4

    def at(self, k):
        return (self.me[1] + k) % 4

    def piece(self, k, xy):
        return self.part.at[self.at(k), xy, self.c]

    def finish(self):
        for n, is_block in self.sent:
            ref = self.rc.at[0] if is_block else self.rx.at[0]
            self.copy(ref, ref, n, (self.me[0], self.me[1])).wait_send()

    def add(self, ref, *refs):
        if len(refs) == 1:
            ref[...] = ref[...] + refs[0][...]
            return
        total = ref[...].astype(f32)
        for other in refs:
            total = total + other[...].astype(f32)
        ref[...] = total.astype(ref.dtype)

    def c_(self, k):
        self.send(self.part.at[self.at(k), :, 1 - self.c], self.rc.at[k], k, (self.me[2], self.me[1]))

    def q(self, k):
        i, f, core, ix, iy, idg = self.me
        self.recv(self.rc.at[k], k)
        ref = self.piece(k, self.xyd)
        self.add(ref, self.rc.at[k, self.xyd])
        self.send(ref, self.rq.at[k], 4 + k, (iy if k % 2 else ix, f))
        refx, refy = self.piece(k, self.xyx), self.piece(k, self.xyy)
        if k % 2:
            self.add(refy, self.rc.at[k, self.xyy])
            self.send(refy, self.ry.at[k], 12 + k, (iy, f))
            self.add(refx, self.rc.at[k, self.xyx])
        else:
            self.add(refx, self.rc.at[k, self.xyx])
            self.send(refx, self.rx.at[k], 8 + k, (ix, f))
            self.add(refy, self.rc.at[k, self.xyy])
        self.add(self.piece(k, self.xy), self.rc.at[k, self.xy])

    def t(self, k):
        i, f, core, ix, iy, idg = self.me
        self.recv(self.rq.at[k], 4 + k)
        ref = self.piece(k, self.xyx if k % 2 else self.xyy)
        self.add(ref, self.rq.at[k])
        if k % 2:
            self.send(ref, self.rx.at[k], 8 + k, (ix, f))
        else:
            self.send(ref, self.ry.at[k], 12 + k, (iy, f))

    def w(self, k):
        i, f, core, ix, iy, idg = self.me
        self.recv(self.rx.at[k], 8 + k)
        self.recv(self.ry.at[k], 12 + k)
        ref = self.piece(k, self.xy)
        if k:
            self.add(ref, self.rx.at[k], self.ry.at[k])
            self.send(ref, self.rz.at[3 - k], 19 - k, (i, (f + k) % 4))
        else:
            self.out[...] = ref[...].astype(f32) + self.rx[k].astype(f32) + self.ry[k].astype(f32)

    def e(self):
        total = self.out[...]
        for k in range(3):
            self.recv(self.rz.at[k], 16 + k)
            total = total + self.rz[k].astype(f32)
        self.out[...] = total


def scatter_buffers(lead, rows, cols, kind):
    return [
        pltpu.VMEM(lead + shape, kind)
        for shape in ((4, 4, rows, cols),) + ((4, rows, cols),) * 3 + ((3, rows, cols),)
    ]


HD=64
def dg(a,b,ca,cb): return lax.dot_general(a,b,(((ca,),(cb,)),((),())),preferred_element_type=f32)

def log_sigmoid(z):
    return jnp.minimum(z, 0.0) - jnp.log1p(jnp.exp(-jnp.abs(z)))

def prepare_mask(s_v, lens, heat, msk, mrows, srows):
    inv = 1.0 / heat[0]
    n = srows
    rows = []
    for i in range(8):
        row = []
        for f in range(4):
            a = s_v[f, pl.ds(i * n, mrows), :].astype(f32) + s_v[f, pl.ds(i * n + mrows, mrows), :].astype(f32)
            row.append(log_sigmoid(a * inv))
        rows.append(jnp.concatenate(row, axis=1))
    lmt = jnp.concatenate(rows, axis=0).T
    key = lax.broadcasted_iota(jnp.int32, lmt.shape, 0)
    for s in range(msk.shape[0]):
        msk[s] = jnp.where(key < lens[s], lmt, -1e30)

def prepare_columns(v_v, col, cols):
    for i in range(8):
        v = v_v[0, pl.ds(i * 16, 16), :].astype(f32)
        col[pl.ds(i * cols, cols), :] = v.T[:cols, :]

def project(f, s, a_v, x, col, qkv):
    acc = dg(a_v[f, :, :576], x[s * 512:(s + 1) * 512, :], 0, 1)
    lo = 0
    while lo < 576:
        g = 576 * f + lo
        kind = g // 768
        hi = min(576, (kind + 1) * 768 - 576 * f)
        part = acc[lo:hi]
        b = g - kind * 768
        if kind == 0:
            part = (part + col[b:b + hi - lo, 2:3]) * 0.125
        elif kind == 2:
            part = part + col[b:b + hi - lo, 3:4]
        qkv[s, g:g + hi - lo, :] = part.astype(bf16)
        lo = hi


def attend_head(qkv, msk, ctx, ptbuf, slot, s, h):
    q = qkv[s, pl.ds(h * HD, HD), :]
    k = qkv[s, pl.ds(768 + h * HD, HD), :]
    v = qkv[s, pl.ds(1536 + h * HD, HD), :]
    st = dg(k, q, 0, 0) + msk[s]
    e = jnp.exp(st - jnp.max(st, axis=0, keepdims=True))
    p = (e * (1.0 / jnp.sum(e, axis=0, keepdims=True))).astype(bf16)
    ptbuf[slot] = p
    ctx[s, pl.ds(h * HD, HD), :] = dg(v, p, 1, 0).astype(bf16)

def attend_all(qkv, msk, ctx, pt, ptbuf, psem, per=2, hook=None):
    steps = 24 // per
    def body(t, carry):
        slot = t % 2
        @pl.when(t >= 2)
        def _():
            pltpu.make_async_copy(ptbuf.at[slot], pt.at[t - 2], psem.at[slot]).wait()
        s = t // (12 // per)
        for u in range(per):
            h = (t % (12 // per)) * per + u
            attend_head(qkv, msk, ctx, ptbuf.at[slot], u, s, h)
        pltpu.make_async_copy(ptbuf.at[slot], pt.at[t], psem.at[slot]).start()
        if hook is not None:
            hook(t)
        return carry
    lax.fori_loop(0, steps, body, 0)
    for t in (steps - 2, steps - 1):
        pltpu.make_async_copy(ptbuf.at[t % 2], pt.at[t], psem.at[t % 2]).wait()

PER = 2


def norm_rows(v):
    mean = jnp.mean(v, axis=-1, keepdims=True)
    c = v - mean
    inv = lax.rsqrt(jnp.mean(c * c, axis=-1, keepdims=True) + 1e-6)
    return c * inv, inv

def norm_rows_back(g, normed, inv, gain):
    e = g * gain
    return inv * (e - jnp.mean(e, axis=-1, keepdims=True) - normed * jnp.mean(e * normed, axis=-1, keepdims=True))

def gather_steps(vec, a0, a1, small, up, down):
    return {
        'first': [(vec.sz, 0), (a0.sz, 0), (a1.sz, 0), (small.sz, 0), (vec.sp, 0), (a0.sp, 0), (a1.sp, 0), (small.sp, 0), (vec.z, 1), (vec.z, 2), (vec.z, 3), (vec.o, 0), (vec.d, 0), (a0.d, 0), (a0.z, 1), (a1.d, 0), (small.d, 0), (vec.d, 1), (vec.d, 2), (a0.z, 2), (vec.d, 3), (vec.b, 0), (a0.z, 3), (a0.o, 0), (a0.d, 1), (a1.z, 1), (vec.h, 0), (a1.z, 2), (up.sz, 0), (vec.r, 0), (a0.d, 2), (a1.z, 3), (a1.o, 0), (a0.d, 3), (a0.b, 0), (small.z, 1), (small.z, 2), (a1.d, 1), (small.z, 3), (small.o, 0), (a1.d, 2), (down.sz, 0), (up.sp, 0), (a0.h, 0), (a1.d, 3), (a1.b, 0), (up.z, 1), (small.d, 1), (a0.r, 0), (small.d, 2), (small.d, 3), (small.b, 0), (up.z, 2), (a1.h, 0), (up.d, 0), (a1.r, 0)],
        'P0': [(up.z, 3)],
        'P2': [(up.d, 1)],
        'P3': [(small.h, 0)],
        'P6': [(down.z, 1)],
        'W': [(small.r, 0)],
        0: [(up.d, 2), (down.z, 2)],
        1: [(down.sp, 0)],
        2: [(up.d, 3)],
        3: [(down.z, 3)],
        4: [(down.d, 1)],
        9: [(down.d, 2)],
        11: [(up.h, 0), (down.d, 0)],
        'UP': [(up.o, 0), (up.b, 0), (down.o, 0), (down.d, 3), (down.b, 0), (up.r, 0)],
        'F00': [(down.h, 0)],
        'LAST': [(down.r, 0)],
    }


def front_kernel(triple, final, expand, bup_in, contract, scales, offsets, gate, jitter, heat, lens, x, cot,
                 wud, wa, qkv_o, ctx_o, pt, out, act, gp, hlow, gslow, gflow, gf, gctx, sums, gbup,
                 a_v, u_v, s_v, v_v, wout, col, msk, ptbuf, qkv, ctx, x_s, cot_s, slope, act_s, n1_s, inv_s, vec, bup,
                 gsl_s, gf_s, gfl_s, ssem, rsem, lsem, psem, isem, osem):
    me = partners()
    i, f = me[0], me[1]
    cp = pltpu.make_async_copy
    xc = cp(x, x_s, isem.at[0]); xc.start()
    cc = cp(cot, cot_s, isem.at[1]); cc.start()
    rows = pl.ds(pl.multiple_of(96 * i, 96), 96)
    a_v[f, rows, :576] = triple[...]
    a_v[f, rows, 576:] = final[...]
    at = lambda o, n: pl.ds(pl.multiple_of(o, 16), n)
    s_v[f, at(128 * i, 64), :] = gate[...]
    s_v[f, at(128 * i + 64, 64), :] = jitter[...]
    vectors = jnp.concatenate([scales[...].astype(f32), offsets[...].astype(f32)], axis=0)
    bias = bup_in[...].astype(f32)
    v_v[f, at(16 * i, 16), :] = jnp.concatenate(
        [jnp.concatenate([vectors, jnp.zeros((8, 32), f32)], axis=1)]
        + [bias, jnp.zeros((2, 128), f32)], axis=0
    ).astype(bf16)
    enter_barrier(me)
    a0, a1 = [Gather(me, a_v, ssem.at[n], rsem.at[n], 48, 96, 48 * n) for n in range(2)]
    small = Gather(me, s_v, ssem.at[2], rsem.at[2], 128, 128)
    vectors = Gather(me, v_v, ssem.at[5], rsem.at[5], 16, 16)
    up = Gather(me, wud.at[0], ssem.at[3], rsem.at[3], 96, 96, 0, expand, lsem.at[0])
    down = Gather(me, wud.at[1], ssem.at[4], rsem.at[4], 96, 96, 0, contract, lsem.at[1])
    steps = gather_steps(vectors, a0, a1, small, up, down)
    after = lambda name: run_steps(steps.get(name, ()))
    after("first")
    wac = cp(a_v, wa, osem.at[0]); wac.start()
    prepare_columns(v_v, col, 96)
    xc.wait()
    for ff in range(4):
        for s in range(2):
            project(ff, s, a_v, x_s, col, qkv)
            after("P%d" % (2 * ff + s))
    after("W")
    prepare_mask(s_v, lens, heat, msk, 64, 128)
    for n in range(8):
        vec[:, 96 * n : 96 * n + 96] = v_v[0, 16 * n : 16 * n + 16, :].astype(f32)[0:8, :96]
    for ff in range(4):
        tail = v_v[ff, 0:16, :].astype(f32)
        for r in range(6):
            bup[:, 768 * ff + 128 * r : 768 * ff + 128 * r + 128] = tail[8 + r : 9 + r]
    for ff in range(4):
        wout[:, 192 * ff:192 * ff + 192] = a_v[ff, :, 576:]
    def hook(t):
        for n in range(12):
            if steps.get(n):
                pl.when(t == n)(functools.partial(run_steps, steps[n]))
    qc = [cp(qkv.at[s], qkv_o.at[s], osem.at[1 + s]) for s in range(2)]
    for c in qc: c.start()
    attend_all(qkv, msk, ctx, pt, ptbuf, psem, PER, hook)
    oc = cp(ctx, ctx_o, osem.at[3]); oc.start()
    uc = cp(wud.at[0], u_v, isem.at[2])
    dc = cp(wud.at[1], a_v, isem.at[3])
    ac = [cp(act_s.at[s], act.at[pl.ds(512 * s, 512)], osem.at[4 + s]) for s in range(2)]
    hc = [cp(x_s.at[pl.ds(512 * s, 512)], hlow.at[pl.ds(512 * s, 512)], osem.at[6 + s]) for s in range(2)]
    for s in range(2):
        sl = pl.ds(512 * s, 512)
        first = x_s[sl].astype(f32) + dg(ctx[s], wout[...], 0, 0) + vec[4:5]
        n1, inv1 = norm_rows(first)
        n1_s[s] = n1
        inv_s[s] = inv1
        hl = (n1 * vec[0:1] + vec[6:7]).astype(bf16)
        x_s[sl] = hl
        hc[s].start()
        after("O%d" % s)
        if s == 0:
            after("UP")
            uc.start()
            uc.wait()
        for ff in range(4):
            pre = dg(x_s[sl], u_v[ff], 1, 0) + bup[:, 768 * ff:768 * ff + 768]
            phi = 0.5 * (1.0 + lax.erf(pre * 0.7071067811865476))
            slope[s, ff] = phi + pre * (jnp.exp(-0.5 * pre * pre) * 0.3989422804014327)
            act_s[s, :, 768 * ff:768 * ff + 768] = (pre * phi).astype(bf16)
            after("F%d%d" % (s, ff))
        ac[s].start()
    after("LAST")
    wac.wait()
    a0.finish()
    a1.finish()
    dc.start()
    dc.wait()
    for c in qc: c.wait()
    outs = lambda s, only=range(6): [[
        lambda: cp(cot_s.at[pl.ds(512 * s, 512)], out.at[pl.ds(512 * s, 512)], osem.at[8]),
        lambda: cp(act_s.at[s], gp.at[pl.ds(512 * s, 512)], osem.at[9]),
        lambda: cp(gsl_s, gslow.at[pl.ds(512 * s, 512)], osem.at[10]),
        lambda: cp(gfl_s, gflow.at[pl.ds(512 * s, 512)], osem.at[11]),
        lambda: cp(gf_s, gf.at[pl.ds(512 * s, 512)], osem.at[12]),
        lambda: cp(qkv.at[s, pl.ds(0, 768)], gctx.at[s], osem.at[13]),
    ][n]() for n in only]
    cc.wait()
    total = None
    for s in range(2):
        sl = pl.ds(512 * s, 512)
        n1, inv1 = n1_s[s], inv_s[s]
        acc = n1 * vec[0:1] + vec[6:7] + vec[5:6]
        for ff in range(4):
            acc = acc + dg(act_s[s, :, 768 * ff:768 * ff + 768], a_v[ff], 1, 1)
        n2, inv2 = norm_rows(acc)
        g = cot_s[sl].astype(f32)
        gs = norm_rows_back(g, n2, inv2, vec[1:2])
        rs = lambda v: jnp.sum(v, axis=0, keepdims=True)
        s_gain2, s_cot, s_gs = rs(g * n2), rs(g), rs(gs)
        cot_s[sl] = (n2 * vec[1:2] + vec[7:8]).astype(bf16)
        if s:
            for c in outs(s - 1, (2, 3, 4)): c.wait()
        gsl = gs.astype(bf16)
        gsl_s[...] = gsl
        ac[s].wait()
        gh = gs
        for ff in range(4):
            p = (dg(gsl, a_v[ff], 1, 0) * slope[s, ff]).astype(bf16)
            act_s[s, :, 768 * ff:768 * ff + 768] = p
            b = rs(p.astype(f32))
            cols = slice(768 * ff, 768 * ff + 768)
            gbup[:, cols] = gbup[:, cols] + b if s else b
            gh = gh + dg(p, u_v[ff], 1, 1)
        gfirst = norm_rows_back(gh, n1, inv1, vec[0:1])
        gf_s[...] = gfirst
        gfl = gfirst.astype(bf16)
        gfl_s[...] = gfl
        if s == 0:
            oc.wait()
        qkv[s, 0:768, :] = dg(wout[...], gfl, 1, 1).astype(bf16)
        part = jnp.concatenate([rs(gh * n1), s_gain2, jnp.zeros((2, 768), f32), rs(gfirst), s_gs, rs(gh), s_cot], axis=0)
        total = part if total is None else total + part
        if s:
            for c in outs(0, (0, 1, 5)): c.wait()
        for c in outs(s): c.start()
    sums[...] = total
    for c in outs(1): c.wait()
    for c in hc: c.wait()
    for g in (small, up, down, vectors):
        g.finish()


def front_call(*ops):
    any_ = pl.BlockSpec(memory_space=pl.ANY)
    vm = pl.BlockSpec(memory_space=pltpu.VMEM)
    sm = pl.BlockSpec(memory_space=pltpu.SMEM)
    sd = jax.ShapeDtypeStruct
    dma = pltpu.SemaphoreType.DMA
    V = pltpu.VMEM
    tok = sd((1024, 768), bf16)
    wide = sd((1024, 3072), bf16)
    return pl.pallas_call(
        front_kernel,
        out_shape=(
            sd((2, 4, 768, 768), bf16), sd((4, 768, 768), bf16), sd((2, 2304, 512), bf16), sd((2, 768, 512), bf16),
            sd((24 // PER, PER, 512, 512), bf16), tok, wide, wide, tok, tok, tok, sd((1024, 768), f32), sd((2, 768, 512), bf16),
            sd((8, 768), f32), sd((1, 3072), f32),
        ),
        in_specs=[vm, vm, any_, vm, any_, vm, vm, vm, vm, sm, sm, any_, any_],
        out_specs=(any_,) * 13 + (vm, vm),
        scratch_shapes=[
            V((4, 768, 768), bf16), V((4, 768, 768), bf16), V((4, 1024, 128), bf16), V((4, 128, 128), bf16), V((768, 768), bf16),
            V((768, 16), f32), V((2, 512, 512), f32), V((2, PER, 512, 512), bf16), V((2, 2304, 512), bf16), V((2, 768, 512), bf16),
            V((1024, 768), bf16), V((1024, 768), bf16), V((2, 4, 512, 768), SLOPE), V((2, 512, 3072), bf16), V((2, 512, 768), f32),
            V((2, 512, 1), f32), V((8, 768), f32), V((1, 3072), f32), V((512, 768), bf16), V((512, 768), f32), V((512, 768), bf16),
            dma((6, 19)), dma((6, 19)), dma((2,)), dma((2,)), dma((4,)), dma((14,)),
        ],
        compiler_params=pltpu.CompilerParams(collective_id=0, has_side_effects=True, vmem_limit_bytes=63 << 20),
        name="gather_attend_feed_forward",
    )(*ops)


SLOPE = f32


def attend_head_back(qkv, gctx, p_ref, dproj, gm, s, h):
    q = qkv[s, pl.ds(h * HD, HD), :]
    k = qkv[s, pl.ds(768 + h * HD, HD), :]
    v = qkv[s, pl.ds(1536 + h * HD, HD), :]
    go = gctx[s, pl.ds(h * HD, HD), :]
    p = p_ref[...]
    dp = dg(v, go, 0, 0)
    pf = p.astype(f32)
    drow = jnp.sum(pf * dp, axis=0, keepdims=True)
    ds = pf * (dp - drow)
    dsl = ds.astype(bf16)
    dproj[s, pl.ds(1536 + h * HD, HD), :] = dg(go, p, 1, 1).astype(bf16)
    dproj[s, pl.ds(768 + h * HD, HD), :] = dg(q, dsl, 1, 1).astype(bf16)
    dproj[s, pl.ds(h * HD, HD), :] = (dg(k, dsl, 1, 0) * 0.125).astype(bf16)
    return ds

def attend_all_back(qkv, gctx, pt, ptbuf, psem, dproj, gm, per, hook=None):
    steps = 24 // per
    gm[...] = jnp.zeros(gm.shape, f32)
    def body(t, carry):
        slot = t % 2
        pltpu.make_async_copy(pt.at[t], ptbuf.at[slot], psem.at[slot]).wait()
        s = t // (12 // per)
        tot = None
        for u in range(per):
            h = (t % (12 // per)) * per + u
            ds = attend_head_back(qkv, gctx, ptbuf.at[slot, u], dproj, gm, s, h)
            tot = ds if tot is None else tot + ds
        gm[...] += tot
        @pl.when(t + 2 < steps)
        def _():
            pltpu.make_async_copy(pt.at[t + 2], ptbuf.at[slot], psem.at[slot]).start()
        if hook is not None:
            hook(t)
        return carry
    lax.fori_loop(0, steps, body, 0)

ORDER = (1, 2, 3, 0)


def small_rows(part, gm, sums, gbup):
    table = gm[...].T
    zero = jnp.zeros((8, 32), f32)
    for f in range(4):
        bias = jnp.concatenate(
            [gbup[:, 768 * f + 128 * r : 768 * f + 128 * r + 128] for r in range(6)] + [jnp.zeros((2, 128), f32)], axis=0
        )
        for i in range(8):
            ref = part.at[f, i // 2, i % 2]
            for j in range(4):
                at = 64 * i + 16 * j
                ref[96:112, 128 * j : 128 * j + 128] = table[at : at + 16, 128 * f : 128 * f + 128].astype(bf16)
            rows = jnp.concatenate([sums[:, 96 * i : 96 * i + 96], zero], axis=1)
            ref[96:112, 512:640] = jnp.concatenate([rows, bias], axis=0).astype(bf16)
            ref[96:112, 640:768] = jnp.zeros((16, 128), bf16)


def backward_kernel(wfull, qkv_h, pt, gctx_h, ctx_h, act, gp, hlow, gslow, x, gfl_h, gf, sums_in, gbup, gin, obig, oattn,
                    part, apart, rc, rq, rx, ry, rz, arc, arq, arx, ary, arz, gm, sums,
                    lhs, chunk, qkv, gctx, ctx, gfl, dproj, ptbuf, gbuf, ssem, rsem, lsem, csem, isem, psem, gsem):
    me = partners()
    cp = pltpu.make_async_copy
    at = [(me[1] + k) % 4 for k in range(4)]
    def chunk_copy(n):
        src = (act, gp)[n // 4].at[:, pl.ds(pl.multiple_of(768 * at[ORDER[n % 4]], 768), 768)]
        return cp(src, chunk.at[n % 2], csem.at[n % 2])
    l0 = cp(gslow, lhs.at[0], lsem.at[0]); l1 = cp(hlow, lhs.at[1], lsem.at[1]); l2 = cp(x, lhs.at[0], lsem.at[0])
    l0.start(); chunk_copy(0).start(); chunk_copy(1).start(); l1.start()
    ins = [cp(a, b, isem.at[n]) for n, (a, b) in enumerate(((ctx_h, ctx), (gfl_h, gfl), (qkv_h, qkv), (gctx_h, gctx)))]
    for c in ins: c.start()
    for t in range(2): cp(pt.at[t], ptbuf.at[t], psem.at[t]).start()
    up, down = [
        Scatter(me, part.at[g], [b.at[g] for b in (rc, rq, rx, ry, rz)], obig.at[g], ssem.at[g], rsem.at[g]) for g in range(2)
    ]
    attn = Scatter(me, apart, (arc, arq, arx, ary, arz), oattn, ssem.at[2], rsem.at[2])
    before, loop, dots = steps_between(attn, up, down)
    l0.wait()
    for n in range(8):
        g, k = (down, up)[n // 4], ORDER[n % 4]
        if n == 4:
            l2.start()
            l1.wait()
        chunk_copy(n).wait()
        g.part[at[k]] = dg(lhs[n // 4], chunk[n % 2], 0, 0).astype(bf16).reshape(4, 2, 96, 768)
        if n < 6: chunk_copy(n + 2).start()
        if n == 0:
            enter_barrier(me)
        g.c_(k)
        run_steps(before.get(n, ()))
    for c in ins: c.wait()
    dwo = dg(ctx[0], gfl[0:512], 1, 0) + dg(ctx[1], gfl[512:1024], 1, 0)
    for f in range(4):
        attn.part[f, :, :, 0:96, 576:] = dwo[:, 192 * f:192 * f + 192].astype(bf16).reshape(4, 2, 96, 192)
    run_steps(before[8])
    def hook(t):
        for at_t in sorted(loop):
            pl.when(t == at_t)(functools.partial(run_steps, loop[at_t]))
    attend_all_back(qkv, gctx, pt, ptbuf, psem, dproj, gm, PER, hook)
    ones = jnp.ones((8, 512), bf16)
    sums[...] = sums_in[...]
    sums[2:3] = (dg(ones, dproj[0, 0:768], 1, 1) + dg(ones, dproj[1, 0:768], 1, 1))[0:1]
    sums[3:4] = (dg(ones, dproj[0, 1536:2304], 1, 1) + dg(ones, dproj[1, 1536:2304], 1, 1))[0:1]
    small_rows(attn.part, gm, sums, gbup)
    l2.wait()
    for n, k in enumerate(ORDER):
        r = pl.ds(pl.multiple_of(576 * at[k], 576), 576)
        dw = dg(lhs[0, 0:512], dproj[0, r, :], 0, 1) + dg(lhs[0, 512:1024], dproj[1, r, :], 0, 1)
        attn.part[at[k], :, :, 0:96, :576] = dw.astype(bf16).reshape(4, 2, 96, 576)
        attn.c_(k)
        run_steps(dots.get(n, ()))
    aw = [cp(wfull.at[f], chunk.at[f % 2, pl.ds(0, 768)], csem.at[f % 2]) for f in range(4)]
    aw[0].start(); aw[1].start()
    gi = [cp(gf.at[pl.ds(512 * s, 512)], gbuf.at[s], gsem.at[s]) for s in range(2)]
    for c in gi: c.start()
    for f in range(4):
        aw[f].wait()
        if f == 0:
            for c in gi: c.wait()
        for s in range(2):
            gbuf[s] = gbuf[s] + dg(dproj[s, 576 * f:576 * f + 576], chunk[f % 2, 0:768, :576], 0, 1)
            run_steps(dots.get(4 + 2 * f + s, ()))
        if f < 2: aw[f + 2].start()
    go = [cp(gbuf.at[s], gin.at[pl.ds(512 * s, 512)], gsem.at[s]) for s in range(2)]
    for c in go: c.start()
    run_steps(dots.get(12, ()))
    for c in go: c.wait()
    for g in (attn, up, down):
        g.finish()


def steps_between(attn, up, down):
    before = {
        2: [(down.q, 1)],
        3: [(down.q, 2)],
        4: [(down.q, 3)],
        5: [(down.q, 0), (down.t, 1)],
        6: [(down.t, 2), (up.q, 1)],
        7: [(up.q, 2)],
        8: [(down.t, 3), (up.q, 3)],
    }
    loop = {
        0: [(down.t, 0), (up.q, 0)],
        2: [(down.w, 2)],
        3: [(down.w, 1), (up.t, 1)],
        4: [(up.t, 2)],
        7: [(up.t, 3)],
        8: [(down.w, 3)],
        9: [(up.t, 0)],
        10: [(down.w, 0)],
        11: [(down.e,), (up.w, 2)],
    }
    dots = {
        0: [(up.w, 1), (up.w, 0)],
        1: [(up.w, 3)],
        2: [(attn.q, 1)],
        3: [(attn.q, 2)],
        5: [(attn.q, 3)],
        8: [(attn.t, 1)],
        12: [(attn.t, 2), (up.e,), (attn.t, 3), (attn.q, 0), (attn.w, 1), (attn.w, 3), (attn.w, 2), (attn.t, 0), (attn.w, 0), (attn.e,)],
    }
    return before, loop, dots


def run_steps(todo):
    for step, *arg in todo:
        step(*arg)


def backward_call(*ops):
    any_ = pl.BlockSpec(memory_space=pl.ANY); vm = pl.BlockSpec(memory_space=pltpu.VMEM)
    sd = jax.ShapeDtypeStruct
    dma = pltpu.SemaphoreType.DMA
    V = pltpu.VMEM
    return pl.pallas_call(backward_kernel,
        out_shape=(sd((1024, 768), f32), sd((2, 96, 768), f32), sd((112, 768), f32)),
        in_specs=[any_] * 12 + [vm] * 2, out_specs=(any_, vm, vm),
        scratch_shapes=[V((2, 4, 4, 2, 96, 768), bf16), V((4, 4, 2, 112, 768), bf16)] + scatter_buffers((2,), 96, 768, bf16) + scatter_buffers((), 112, 768, bf16)
            + [V((512, 512), f32), V((8, 768), f32)]
            + [V((2, 1024, 768), bf16), V((2, 1024, 768), bf16), V((2, 2304, 512), bf16), V((2, 768, 512), bf16), V((2, 768, 512), bf16), V((1024, 768), bf16),
            V((2, 2304, 512), bf16), V((2, PER, 512, 512), bf16), V((2, 512, 768), f32), dma((3, 19)), dma((3, 19)), dma((2,)), dma((2,)), dma((4,)), dma((2,)), dma((2,))],
        compiler_params=pltpu.CompilerParams(collective_id=1, has_side_effects=True, vmem_limit_bytes=63 << 20), name="attend_back_and_reduce")(*ops)


def hand_out_kernel(gin, res, big, attn_h, gate_h, jitter_h, heat, gin_o, res_o, qkv, out, up, down, bias, gains, shifts, logits,
                    gbuf, rbuf, bbuf, attn, gate, jitter, sem):
    cp = pltpu.make_async_copy
    n = 4
    rows = gin.shape[0] // n
    moves = [(a.at[pl.ds(r * rows, rows)], b.at[pl.ds(r * rows, rows)], c.at[pl.ds(r * rows, rows)])
             for r in range(n) for a, b, c in ((gin, gbuf, gin_o), (res, rbuf, res_o))]
    moves += [(big.at[0], bbuf.at[0], up), (big.at[1], bbuf.at[1], down)]
    small = [cp(a, b, sem.at[m]) for m, (a, b) in enumerate(((attn_h, attn), (gate_h, gate), (jitter_h, jitter)))]
    ins = [cp(a, b, sem.at[3 + m]) for m, (a, b, c) in enumerate(moves)]
    outs = [cp(b, c, sem.at[13 + m]) for m, (a, b, c) in enumerate(moves)]
    for c in small + ins: c.start()
    for c in small: c.wait()
    qkv[...] = attn[:96, :576]
    out[...] = attn[:96, 576:]
    inv = 1.0 / heat[0]
    table = jnp.concatenate([attn[96:112, 128 * j:128 * j + 128] for j in range(4)], axis=0)
    mixed = (gate[...].astype(f32) + jitter[...].astype(f32)) * inv
    logits[...] = table * (inv / (1.0 + jnp.exp(mixed)))
    gains[...] = attn[96:98, 512:608]
    shifts[...] = attn[98:104, 512:608]
    bias[...] = attn[104:110, 512:640]
    for a, b in zip(ins, outs):
        a.wait()
        b.start()
    for c in outs: c.wait()


def hand_out_call(gin, res, big, attn, gate, jitter, heat):
    any_ = pl.BlockSpec(memory_space=pl.ANY); vm = pl.BlockSpec(memory_space=pltpu.VMEM); sm = pl.BlockSpec(memory_space=pltpu.SMEM)
    sd = lambda *s: jax.ShapeDtypeStruct(s, f32)
    V = pltpu.VMEM
    return pl.pallas_call(hand_out_kernel,
        out_shape=(sd(1024, 768), jax.ShapeDtypeStruct((1024, 768), bf16), sd(96, 576), sd(96, 192), sd(96, 768), sd(96, 768), sd(6, 128), sd(2, 96), sd(6, 96), sd(64, 128)),
        in_specs=[any_] * 6 + [sm], out_specs=(any_, any_, vm, vm, any_, any_) + (vm,) * 4,
        scratch_shapes=[V((1024, 768), f32), V((1024, 768), bf16), V((2, 96, 768), f32), V((112, 768), f32), V((64, 128), bf16), V((64, 128), bf16), pltpu.SemaphoreType.DMA((23,))],
        compiler_params=pltpu.CompilerParams(vmem_limit_bytes=63 << 20), name="hand_out")(gin, res, big, attn, gate, jitter, heat)


def own_device(
    layer_activations,
    token_counts_each,
    attention_triple_matrix,
    attention_final_matrix,
    feedfwd_expand_matrix,
    feedfwd_expand_offset,
    feedfwd_contract_matrix,
    layernorm_scales,
    offset_vectors,
    learned_gate_scores,
    fixed_jitter_matrix,
    relaxation_heat,
    loss_grad_result,
):
    x = layer_activations.reshape(1024, D)
    cot = loss_grad_result.reshape(1024, D)
    (
        _, attn_full, qkv, ctx, probs, result, act, grad_pre, hidden_low, grad_second_low, grad_first_low, grad_first, grad_ctx,
        sums, grad_bias,
    ) = front_call(
        attention_triple_matrix, attention_final_matrix, feedfwd_expand_matrix, feedfwd_expand_offset.reshape(6, 128),
        feedfwd_contract_matrix.T, layernorm_scales, offset_vectors, learned_gate_scores, fixed_jitter_matrix, relaxation_heat,
        token_counts_each, x, cot,
    )
    grad_inputs, big, attn = backward_call(
        attn_full, qkv, probs, grad_ctx, ctx, act, grad_pre, hidden_low, grad_second_low, x, grad_first_low, grad_first,
        sums, grad_bias,
    )
    grad_inputs, result, g_qkv, g_out, g_up, g_down, g_bias, g_gains, g_shifts, g_logits = hand_out_call(
        grad_inputs, result, big, attn, learned_gate_scores, fixed_jitter_matrix, relaxation_heat
    )
    return (
        result.reshape(layer_activations.shape),
        grad_inputs.reshape(layer_activations.shape),
        g_qkv,
        g_out,
        g_up,
        g_bias.reshape(-1),
        g_down.T,
        g_gains,
        g_shifts,
        g_logits,
    )


def solution(mesh):
    in_specs = (
        P(AXES, None, None),
        P(AXES),
        P("dp", "ffn"),
        P("dp", "ffn"),
        P("dp", "ffn"),
        P("ffn"),
        P("ffn", "dp"),
        P(None, "dp"),
        P(None, "dp"),
        P("dp", "ffn"),
        P("dp", "ffn"),
        P(),
        P(AXES, None, None),
    )
    out_specs = (
        P(AXES, None, None),
        P(AXES, None, None),
        P("dp", "ffn"),
        P("dp", "ffn"),
        P("dp", "ffn"),
        P("ffn"),
        P("ffn", "dp"),
        P(None, "dp"),
        P(None, "dp"),
        P("dp", "ffn"),
    )
    own = (mesh.shape["dp"], mesh.shape["ffn"]) == (8, 4)
    return jax.shard_map(
        own_device if own else general_device, mesh=mesh, in_specs=in_specs, out_specs=out_specs, check_vma=False
    )
```

```python
import functools

import jax
import jax.numpy as jnp
from jax import lax
from jax.experimental import pallas as pl
from jax.experimental.pallas import tpu as pltpu
from jax.sharding import PartitionSpec as P

D = 768
HEADS = 12
HEAD_DIM = 64
SEQ_LEN = 512
AXES = ("dp", "ffn")
norm_eps = 1e-06
f32 = jnp.float32
bf16 = jnp.bfloat16
MESH = pl.DeviceIdType.MESH


def dot_first(left, right):
    return lax.dot_general(left, right, (((0,), (0,)), ((), ())), preferred_element_type=f32)


def dot_last(left, right):
    return lax.dot_general(left, right, (((1,), (1,)), ((), ())), preferred_element_type=f32)


def dot(left, right):
    return jnp.dot(left, right, preferred_element_type=f32)


def layer_norm(values, gain, shift):
    mean_row = jnp.mean(values, axis=-1, keepdims=True)
    centered = values - mean_row
    inv_std = lax.rsqrt(jnp.mean(centered * centered, axis=-1, keepdims=True) + norm_eps)
    normed = centered * inv_std
    return (normed * gain + shift, normed, inv_std)


def norm_back(grad_out, normed, inv_std, gain):
    grad_normed = grad_out * gain
    grad_in = inv_std * (
        grad_normed
        - jnp.mean(grad_normed, axis=-1, keepdims=True)
        - normed * jnp.mean(grad_normed * normed, axis=-1, keepdims=True)
    )
    return (grad_in, jnp.sum(grad_out * normed, axis=0), jnp.sum(grad_out, axis=0))


def gelu_slope(values):
    return (
        0.5 * (1.0 + lax.erf(values * 0.7071067811865476))
        + values * jnp.exp(-0.5 * values * values) * 0.3989422804014327
    )


def score_block(queries, keys_low, natural_log_gate, live):
    scores = (
        jnp.einsum("qhd,khd->hqk", queries, keys_low, preferred_element_type=f32)
        * HEAD_DIM ** (-0.5)
        + natural_log_gate
    )
    return jnp.where(live[None, None, :], scores, -1e30)


def attend(queries, keys_low, values_low, natural_log_gate, live):
    scores = score_block(queries, keys_low, natural_log_gate, live)
    peak = jnp.max(scores, axis=-1, keepdims=True)
    shifted_exp = jnp.exp(scores - peak)
    total_exp = jnp.sum(shifted_exp, axis=-1, keepdims=True)
    probs_low = (shifted_exp / total_exp).astype(bf16)
    context = jnp.einsum("hqk,khd->qhd", probs_low, values_low, preferred_element_type=f32)
    return (context, peak + jnp.log(total_exp))


def attend_back(queries, keys_low, values_low, natural_log_gate, live, log_total, grad_context):
    scores = score_block(queries, keys_low, natural_log_gate, live)
    probs = jnp.exp(scores - log_total)
    grad_probs = jnp.einsum("qhd,khd->hqk", grad_context, values_low, preferred_element_type=f32)
    grad_values = jnp.einsum(
        "hqk,qhd->khd", probs.astype(bf16), grad_context, preferred_element_type=f32
    )
    grad_scores = probs * (grad_probs - jnp.sum(probs * grad_probs, axis=-1, keepdims=True))
    grad_mask = jnp.sum(grad_scores, axis=0)
    grad_scores_low = grad_scores.astype(bf16)
    grad_queries = jnp.einsum(
        "hqk,khd->qhd", grad_scores_low, keys_low, preferred_element_type=f32
    ) * HEAD_DIM ** (-0.5)
    grad_keys = jnp.einsum(
        "hqk,qhd->khd", grad_scores_low, queries, preferred_element_type=f32
    ) * HEAD_DIM ** (-0.5)
    return (grad_queries, grad_keys, grad_values, grad_mask)


def gather_weights(pack, small):
    rows_dp = lax.axis_size("dp")
    cols_ffn = lax.axis_size("ffn")
    full = lax.all_gather(pack[None], AXES, axis=0, tiled=True)
    full = full.reshape(rows_dp, cols_ffn, *pack.shape)
    small_full = lax.all_gather(small[None], AXES, axis=0, tiled=True)
    return full, small_full.reshape(rows_dp, cols_ffn, *small.shape)


def columns(blocks):
    rows_dp, cols_ffn, rows, cols = blocks.shape
    return blocks.transpose(0, 2, 1, 3).reshape(rows_dp * rows, cols_ffn * cols)


def blocks_of(full, rows_dp, cols_ffn):
    rows, cols = full.shape
    return full.reshape(rows_dp, rows // rows_dp, cols_ffn, cols // cols_ffn).transpose(0, 2, 1, 3)


def general_device(
    layer_activations,
    token_counts_each,
    attention_triple_matrix,
    attention_final_matrix,
    feedfwd_expand_matrix,
    feedfwd_expand_offset,
    feedfwd_contract_matrix,
    layernorm_scales,
    offset_vectors,
    learned_gate_scores,
    fixed_jitter_matrix,
    relaxation_heat,
    loss_grad_result,
):
    rows_dp = lax.axis_size("dp")
    cols_ffn = lax.axis_size("ffn")
    seq_count = layer_activations.shape[0]
    row_count = seq_count * SEQ_LEN
    shard_rows = attention_triple_matrix.shape[0]
    qkv_cols = attention_triple_matrix.shape[1]
    out_cols = attention_final_matrix.shape[1]
    ff_cols = feedfwd_expand_matrix.shape[1]

    pack = jnp.concatenate(
        [
            attention_triple_matrix,
            attention_final_matrix,
            feedfwd_expand_matrix,
            feedfwd_contract_matrix.T,
        ],
        axis=1,
    )
    mask_cols = learned_gate_scores.shape[1]
    vectors = jnp.concatenate([layernorm_scales, offset_vectors], axis=0)
    small = jnp.concatenate(
        [
            learned_gate_scores,
            fixed_jitter_matrix,
            jnp.pad(vectors, ((0, 0), (0, mask_cols - vectors.shape[1]))),
            feedfwd_expand_offset.reshape(-1, mask_cols),
        ],
        axis=0,
    )
    full, small_full = gather_weights(pack, small)
    full_qkv = columns(full[..., :qkv_cols])
    full_out = columns(full[..., qkv_cols : qkv_cols + out_cols])
    full_up = columns(full[..., qkv_cols + out_cols : qkv_cols + out_cols + ff_cols])
    full_down_t = columns(full[..., qkv_cols + out_cols + ff_cols :])
    mask_rows = learned_gate_scores.shape[0]
    logits_sum = columns(small_full[:, :, :mask_rows]).astype(f32) + columns(
        small_full[:, :, mask_rows : 2 * mask_rows]
    ).astype(f32)
    natural_log_gate = jax.nn.log_sigmoid(logits_sum / relaxation_heat[0])
    vectors_full = (
        small_full[:, 0, 2 * mask_rows : 2 * mask_rows + 8, :shard_rows]
        .transpose(1, 0, 2)
        .reshape(8, D)
        .astype(f32)
    )
    gains_full = vectors_full[:2]
    shifts_full = vectors_full[2:]
    bias_up = small_full[0, :, 2 * mask_rows + 8 :].reshape(1, -1).astype(f32)

    flat_in = layer_activations.reshape(row_count, D)
    qkv_bias = jnp.concatenate([shifts_full[0], jnp.zeros((D,), f32), shifts_full[1]])
    proj_low = (dot(flat_in, full_qkv) + qkv_bias).astype(bf16)
    head_shape = (seq_count, SEQ_LEN, HEADS, HEAD_DIM)
    queries = proj_low[:, :D].reshape(head_shape)
    keys_low = proj_low[:, D : 2 * D].reshape(head_shape)
    values_low = proj_low[:, 2 * D :].reshape(head_shape)
    live = lax.broadcasted_iota(jnp.int32, (seq_count, SEQ_LEN), 1) < token_counts_each[:, None]
    attended = [
        attend(queries[s], keys_low[s], values_low[s], natural_log_gate, live[s])
        for s in range(seq_count)
    ]
    context_low = jnp.concatenate(
        [item[0].reshape(SEQ_LEN, D).astype(bf16) for item in attended], axis=0
    )
    first_sum = flat_in.astype(f32) + dot(context_low, full_out) + shifts_full[2]
    hidden, normed_one, inv_one = layer_norm(first_sum, gains_full[0], shifts_full[4])
    hidden_low = hidden.astype(bf16)
    pre_act = dot(hidden_low, full_up) + bias_up
    act_low = jax.nn.gelu(pre_act, approximate=False).astype(bf16)
    second_sum = hidden + dot_last(act_low, full_down_t) + shifts_full[3]
    result, normed_two, inv_two = layer_norm(second_sum, gains_full[1], shifts_full[5])
    cot_flat = loss_grad_result.reshape(row_count, D).astype(f32)
    grad_second, grad_gain_two, grad_shift_two = norm_back(
        cot_flat, normed_two, inv_two, gains_full[1]
    )
    grad_second_low = grad_second.astype(bf16)
    grad_w_down_t = dot_first(grad_second_low, act_low)
    grad_act = dot(grad_second_low, full_down_t)
    grad_pre = (grad_act * gelu_slope(pre_act)).astype(bf16)
    grad_bias_up = jnp.sum(grad_pre, axis=0, dtype=f32)
    grad_w_up = dot_first(hidden_low, grad_pre)
    grad_hidden = grad_second + dot_last(grad_pre, full_up)
    grad_first, grad_gain_one, grad_shift_one = norm_back(
        grad_hidden, normed_one, inv_one, gains_full[0]
    )
    grad_first_low = grad_first.astype(bf16)
    grad_w_out = dot_first(context_low, grad_first_low)
    grad_context = dot_last(grad_first_low, full_out).astype(bf16).reshape(head_shape)
    back = [
        attend_back(
            queries[s],
            keys_low[s],
            values_low[s],
            natural_log_gate,
            live[s],
            attended[s][1],
            grad_context[s],
        )
        for s in range(seq_count)
    ]
    grad_mask = sum(item[3] for item in back)
    grad_projected = jnp.concatenate(
        [
            jnp.concatenate(
                [item[part].reshape(SEQ_LEN, D).astype(bf16) for item in back], axis=0
            )
            for part in range(3)
        ],
        axis=1,
    )
    grad_w_qkv = dot_first(flat_in, grad_projected)
    grad_inputs = grad_first + dot_last(grad_projected, full_qkv)
    grad_vectors = jnp.stack(
        [
            grad_gain_one,
            grad_gain_two,
            jnp.sum(grad_projected[:, :D], axis=0, dtype=f32),
            jnp.sum(grad_projected[:, 2 * D :], axis=0, dtype=f32),
            jnp.sum(grad_first, axis=0),
            jnp.sum(grad_second, axis=0),
            grad_shift_one,
            grad_shift_two,
        ]
    )
    big = jnp.concatenate(
        [
            blocks_of(item, rows_dp, cols_ffn)
            for item in (grad_w_qkv, grad_w_out, grad_w_up, grad_w_down_t)
        ],
        axis=-1,
    ).reshape(rows_dp * cols_ffn, shard_rows, -1)
    vector_blocks = jnp.broadcast_to(
        grad_vectors.reshape(8, rows_dp, 1, shard_rows).transpose(1, 2, 0, 3),
        (rows_dp, cols_ffn, 8, shard_rows),
    )
    bias_blocks = jnp.broadcast_to(
        grad_bias_up.reshape(1, cols_ffn, -1, mask_cols),
        (rows_dp, cols_ffn, ff_cols // mask_cols, mask_cols),
    )
    little = jnp.concatenate(
        [
            blocks_of(grad_mask, rows_dp, cols_ffn),
            jnp.pad(vector_blocks, ((0, 0), (0, 0), (0, 0), (0, mask_cols - shard_rows))),
            bias_blocks,
        ],
        axis=2,
    ).reshape(rows_dp * cols_ffn, -1, mask_cols)
    big = lax.psum_scatter(big, AXES, scatter_dimension=0, tiled=True)[0]
    little = lax.psum_scatter(little, AXES, scatter_dimension=0, tiled=True)[0]

    own_mixed = (
        learned_gate_scores.astype(f32) + fixed_jitter_matrix.astype(f32)
    ) / relaxation_heat[0]
    grad_logits = little[:mask_rows] * (jax.nn.sigmoid(-own_mixed) / relaxation_heat[0])
    return (
        result.astype(bf16).reshape(layer_activations.shape),
        grad_inputs.reshape(layer_activations.shape),
        big[:, :qkv_cols],
        big[:, qkv_cols : qkv_cols + out_cols],
        big[:, qkv_cols + out_cols : qkv_cols + out_cols + ff_cols],
        little[mask_rows + 8 :].reshape(-1),
        big[:, qkv_cols + out_cols + ff_cols :].T,
        little[mask_rows : mask_rows + 2, :shard_rows],
        little[mask_rows + 2 : mask_rows + 8, :shard_rows],
        grad_logits,
    )


def partners():
    i = lax.axis_index("dp")
    f = lax.axis_index("ffn")
    core = i + 1 - 2 * (i % 2)
    ix = i + 2 - 4 * ((i // 2) % 2)
    iy = (i + 4) % 8
    idg = (ix + 4) % 8
    return i, f, core, ix, iy, idg


def enter_barrier(me):
    i, f, core, ix, iy, idg = me
    sem = pltpu.get_barrier_semaphore()
    mates = [(i, (f + k) % 4) for k in (1, 2, 3)] + [(core, f), (ix, f), (iy, f)]
    for to in mates:
        pl.semaphore_signal(sem, inc=1, device_id=to, device_id_type=MESH)
    pl.semaphore_wait(sem, len(mates))


class Exchange:
    def __init__(self, me, ssem, rsem):
        self.me, self.ssem, self.rsem = me, ssem, rsem
        self.sent = []

    def copy(self, src, dst, n, to):
        return pltpu.make_async_remote_copy(
            src_ref=src,
            dst_ref=dst,
            send_sem=self.ssem.at[n],
            recv_sem=self.rsem.at[n],
            device_id=to,
            device_id_type=MESH,
        )

    def send(self, src, dst, n, to):
        self.copy(src, dst, n, to).start()
        self.sent.append((n, len(src.shape) == 3))

    def recv(self, ref, n):
        self.copy(ref, ref, n, (self.me[0], self.me[1])).wait_recv()

    def finish(self):
        for n, is_block in self.sent:
            ref = self.block(0) if is_block else self.piece(0, 0)
            self.copy(ref, ref, n, (self.me[0], self.me[1])).wait_send()


class Gather(Exchange):
    def __init__(self, me, dst, ssem, rsem, rows, stride, offset=0, src=None, lsem=None):
        super().__init__(me, ssem, rsem)
        self.dst, self.rows, self.stride, self.offset, self.lsem = dst, rows, stride, offset, lsem
        self.src = src

    def span(self, i):
        return pl.ds(pl.multiple_of(i * self.stride + self.offset, 16), self.rows)

    def piece(self, i, p):
        return self.dst.at[p, self.span(i)]

    def block(self, i):
        return self.dst.at[:, self.span(i)]

    def own(self):
        return self.piece(self.me[0], self.me[1]) if self.src is None else self.src

    def local(self):
        i, f = self.me[:2]
        return pltpu.make_async_copy(self.src, self.piece(i, f), self.lsem)

    def sz(self, _):
        i, f, core, ix, iy, idg = self.me
        if self.src is not None:
            self.local().start()
        for k in (1, 2, 3):
            self.send(self.own(), self.piece(i, f), 3 - k, (i, (f + k) % 4))

    def sp(self, _):
        i, f, core, ix, iy, idg = self.me
        self.send(self.own(), self.piece(i, f), 3, (ix, f))
        self.send(self.own(), self.piece(i, f), 7, (iy, f))

    def z(self, k):
        i, f, core, ix, iy, idg = self.me
        ref = self.piece(i, (f + k) % 4)
        self.recv(ref, k - 1)
        self.send(ref, ref, 3 + k, (ix, f))
        self.send(ref, ref, 7 + k, (iy, f))

    def o(self, _):
        i, f, core, ix, iy, idg = self.me
        if self.src is not None:
            self.local().wait()
        self.send(self.block(i), self.block(i), 15, (core, f))

    def d(self, k):
        i, f, core, ix, iy, idg = self.me
        p = (f + k) % 4
        rx, ry = self.piece(ix, p), self.piece(iy, p)
        self.recv(rx, 3 + k)
        self.recv(ry, 7 + k)
        if k % 2:
            self.send(rx, rx, 11 + k, (iy, f))
        else:
            self.send(ry, ry, 11 + k, (ix, f))

    def b(self, _):
        i, f, core, ix, iy, idg = self.me
        self.send(self.block(ix), self.block(ix), 16, (core, f))
        self.send(self.block(iy), self.block(iy), 17, (core, f))

    def h(self, _):
        i, f, core, ix, iy, idg = self.me
        for k in range(4):
            self.recv(self.piece(idg, (f + k) % 4), 11 + k)
        self.send(self.block(idg), self.block(idg), 18, (core, f))

    def r(self, _):
        i, f, core, ix, iy, idg = self.me
        for n, other in ((15, i), (16, ix), (17, iy), (18, idg)):
            self.recv(self.block(other + core - i), n)


class Scatter(Exchange):
    def __init__(self, me, part, got, out, ssem, rsem):
        super().__init__(me, ssem, rsem)
        self.part, self.out = part, out
        self.rc, self.rq, self.rx, self.ry, self.rz = got
        i = me[0]
        self.c = i % 2
        self.xy = i // 2
        self.xyx = self.xy + 1 - 2 * (self.xy % 2)
        self.xyy = (self.xy + 2) % 4
        self.xyd = (self.xyx + 2) % 4

    def at(self, k):
        return (self.me[1] + k) % 4

    def piece(self, k, xy):
        return self.part.at[self.at(k), xy, self.c]

    def finish(self):
        for n, is_block in self.sent:
            ref = self.rc.at[0] if is_block else self.rx.at[0]
            self.copy(ref, ref, n, (self.me[0], self.me[1])).wait_send()

    def add(self, ref, *refs):
        if len(refs) == 1:
            ref[...] = ref[...] + refs[0][...]
            return
        total = ref[...].astype(f32)
        for other in refs:
            total = total + other[...].astype(f32)
        ref[...] = total.astype(ref.dtype)

    def c_(self, k):
        self.send(self.part.at[self.at(k), :, 1 - self.c], self.rc.at[k], k, (self.me[2], self.me[1]))

    def q(self, k):
        i, f, core, ix, iy, idg = self.me
        self.recv(self.rc.at[k], k)
        ref = self.piece(k, self.xyd)
        self.add(ref, self.rc.at[k, self.xyd])
        self.send(ref, self.rq.at[k], 4 + k, (iy if k % 2 else ix, f))
        refx, refy = self.piece(k, self.xyx), self.piece(k, self.xyy)
        if k % 2:
            self.add(refy, self.rc.at[k, self.xyy])
            self.send(refy, self.ry.at[k], 12 + k, (iy, f))
            self.add(refx, self.rc.at[k, self.xyx])
        else:
            self.add(refx, self.rc.at[k, self.xyx])
            self.send(refx, self.rx.at[k], 8 + k, (ix, f))
            self.add(refy, self.rc.at[k, self.xyy])
        self.add(self.piece(k, self.xy), self.rc.at[k, self.xy])

    def t(self, k):
        i, f, core, ix, iy, idg = self.me
        self.recv(self.rq.at[k], 4 + k)
        ref = self.piece(k, self.xyx if k % 2 else self.xyy)
        self.add(ref, self.rq.at[k])
        if k % 2:
            self.send(ref, self.rx.at[k], 8 + k, (ix, f))
        else:
            self.send(ref, self.ry.at[k], 12 + k, (iy, f))

    def w(self, k):
        i, f, core, ix, iy, idg = self.me
        self.recv(self.rx.at[k], 8 + k)
        self.recv(self.ry.at[k], 12 + k)
        ref = self.piece(k, self.xy)
        if k:
            self.add(ref, self.rx.at[k], self.ry.at[k])
            self.send(ref, self.rz.at[3 - k], 19 - k, (i, (f + k) % 4))
        else:
            self.out[...] = ref[...].astype(f32) + self.rx[k].astype(f32) + self.ry[k].astype(f32)

    def e(self):
        total = self.out[...]
        for k in range(3):
            self.recv(self.rz.at[k], 16 + k)
            total = total + self.rz[k].astype(f32)
        self.out[...] = total


def scatter_buffers(rows, cols):
    return [
        pltpu.VMEM(shape, bf16)
        for shape in ((4, 4, 2, rows, cols), (4, 4, rows, cols)) + ((4, rows, cols),) * 3 + ((3, rows, cols),)
    ]


HD=64
def dg(a,b,ca,cb): return lax.dot_general(a,b,(((ca,),(cb,)),((),())),preferred_element_type=f32)

def log_sigmoid(z):
    return jnp.minimum(z, 0.0) - jnp.log1p(jnp.exp(-jnp.abs(z)))

def prepare_mask(s_v, lens, heat, msk, mrows, srows):
    inv = 1.0 / heat[0]
    n = srows
    rows = []
    for i in range(8):
        row = []
        for f in range(4):
            a = s_v[f, pl.ds(i * n, mrows), :].astype(f32) + s_v[f, pl.ds(i * n + mrows, mrows), :].astype(f32)
            row.append(log_sigmoid(a * inv))
        rows.append(jnp.concatenate(row, axis=1))
    lmt = jnp.concatenate(rows, axis=0).T
    key = lax.broadcasted_iota(jnp.int32, lmt.shape, 0)
    for s in range(msk.shape[0]):
        msk[s] = jnp.where(key < lens[s], lmt, -1e30)

def prepare_columns(v_v, col, cols):
    for i in range(8):
        v = v_v[0, pl.ds(i * 16, 16), :].astype(f32)
        col[pl.ds(i * cols, cols), :] = v.T[:cols, :]

def project(f, s, a_v, x, col, qkv):
    acc = dg(a_v[f, :, :576], x[s * 512:(s + 1) * 512, :], 0, 1)
    lo = 0
    while lo < 576:
        g = 576 * f + lo
        kind = g // 768
        hi = min(576, (kind + 1) * 768 - 576 * f)
        part = acc[lo:hi]
        b = g - kind * 768
        if kind == 0:
            part = (part + col[b:b + hi - lo, 2:3]) * 0.125
        elif kind == 2:
            part = part + col[b:b + hi - lo, 3:4]
        qkv[s, g:g + hi - lo, :] = part.astype(bf16)
        lo = hi


def attend_head(qkv, msk, ctx, ptbuf, slot, s, h):
    q = qkv[s, pl.ds(h * HD, HD), :]
    k = qkv[s, pl.ds(768 + h * HD, HD), :]
    v = qkv[s, pl.ds(1536 + h * HD, HD), :]
    st = dg(k, q, 0, 0) + msk[s]
    e = jnp.exp(st - jnp.max(st, axis=0, keepdims=True))
    p = (e * (1.0 / jnp.sum(e, axis=0, keepdims=True))).astype(bf16)
    ptbuf[slot] = p
    ctx[s, pl.ds(h * HD, HD), :] = dg(v, p, 1, 0).astype(bf16)

def attend_all(qkv, msk, ctx, pt, ptbuf, psem, per, hook):
    steps = 24 // per
    out = lambda t: pltpu.make_async_copy(
        ptbuf.at[t % 2], pt.at[pl.ds(t * per, per)], psem.at[t % 2]
    )
    def body(t, carry):
        @pl.when(t >= 2)
        def _():
            out(t - 2).wait()
        s = t // (12 // per)
        for u in range(per):
            h = (t % (12 // per)) * per + u
            attend_head(qkv, msk, ctx, ptbuf.at[t % 2], u, s, h)
        out(t).start()
        hook(t)
        return carry
    lax.fori_loop(0, steps, body, 0)
    for t in (steps - 2, steps - 1):
        out(t).wait()


FORWARD_HEADS = 2
BACKWARD_HEADS = 2


def norm_rows(v):
    mean = jnp.mean(v, axis=-1, keepdims=True)
    c = v - mean
    inv = lax.rsqrt(jnp.mean(c * c, axis=-1, keepdims=True) + 1e-6)
    return c * inv, inv

def norm_rows_back(g, normed, inv, gain):
    e = g * gain
    return inv * (e - jnp.mean(e, axis=-1, keepdims=True) - normed * jnp.mean(e * normed, axis=-1, keepdims=True))

def gather_steps(vec, a0, a1, a2, small, up, down):
    return {
        'first': [(vec.sz, 0), (a0.sz, 0), (small.sz, 0), (a1.sz, 0), (a2.sz, 0), (vec.sp, 0), (a0.sp, 0), (small.sp, 0), (a1.sp, 0), (a2.sp, 0), (vec.z, 1), (vec.z, 2), (vec.z, 3), (vec.o, 0), (vec.d, 0), (a0.d, 0), (a0.z, 1), (small.d, 0), (a0.z, 2), (a1.d, 0), (a0.z, 3), (a0.o, 0), (a2.d, 0), (vec.d, 1), (vec.d, 2), (vec.d, 3), (vec.b, 0), (small.z, 1), (small.z, 2), (a0.d, 1), (small.z, 3), (small.o, 0), (a0.d, 2), (a1.z, 1), (a1.z, 2), (a0.d, 3), (a0.b, 0), (a1.z, 3), (a1.o, 0), (vec.h, 0), (small.d, 1), (a2.z, 1), (small.d, 2), (vec.r, 0), (small.d, 3), (small.b, 0), (a2.z, 2), (a0.h, 0), (a2.z, 3), (up.sz, 0), (up.sp, 0), (a2.o, 0), (a1.d, 1), (a1.d, 2), (a0.r, 0), (a1.d, 3), (a1.b, 0), (a2.d, 1), (small.h, 0), (a2.d, 2), (a2.d, 3), (a2.b, 0), (small.r, 0), (up.z, 1), (up.d, 0), (a1.h, 0), (a2.h, 0), (up.z, 2), (a1.r, 0), (a2.r, 0)],
        'P3': [(up.d, 1)],
        'P5': [(up.z, 3), (up.o, 0)],
        'P6': [(down.sz, 0)],
        0: [(up.d, 2)],
        1: [(down.z, 1)],
        3: [(up.d, 3), (up.b, 0)],
        4: [(down.sp, 0), (down.z, 2)],
        7: [(down.z, 3), (down.o, 0)],
        8: [(up.h, 0), (down.d, 1)],
        10: [(down.d, 0)],
        'UP': [(up.r, 0)],
        'O0': [(down.d, 2)],
        'F02': [(down.d, 3), (down.b, 0)],
        'F11': [(down.h, 0)],
        'LAST': [(down.r, 0)],
    }


def front_kernel(triple, final, expand, bup_in, contract, scales, offsets, gate, jitter, heat, lens, x, cot,
                 wu, wd, wa, qkv_o, ctx_o, pt, out, act, gp, hlow, gslow, gflow, gf, gctx, sums, gbup,
                 a_v, u_v, s_v, v_v, usrc, wout, col, msk, ptbuf, qkv, ctx, x_s, cot_s, slope, act_s, n1_s, inv_s, vec, bup,
                 gsl_s, gf_s, gfl_s, ssem, rsem, lsem, psem, isem, osem):
    me = partners()
    i, f = me[0], me[1]
    cp = pltpu.make_async_copy
    xc = cp(x, x_s, isem.at[0]); xc.start()
    cc = cp(cot, cot_s, isem.at[1]); cc.start()
    rows = pl.ds(pl.multiple_of(96 * i, 96), 96)
    a_v[f, rows, :576] = triple[...]
    a_v[f, rows, 576:640] = final[:, :64]
    usrc[:, :768] = expand[...]
    usrc[:, 768:] = final[:, 64:]
    at = lambda o, n: pl.ds(pl.multiple_of(o, 16), n)
    s_v[f, at(128 * i, 64), :] = gate[...]
    s_v[f, at(128 * i + 64, 64), :] = jitter[...]
    vectors = jnp.concatenate([scales[...].astype(f32), offsets[...].astype(f32)], axis=0)
    bias = bup_in[...].astype(f32)
    v_v[f, at(16 * i, 16), :] = jnp.concatenate(
        [jnp.concatenate([vectors, jnp.zeros((8, 32), f32)], axis=1)]
        + [bias, jnp.zeros((2, 128), f32)], axis=0
    ).astype(bf16)
    enter_barrier(me)
    attn_v = a_v.at[:, :, pl.ds(0, 640)]
    a0, a1, a2 = [Gather(me, attn_v, ssem.at[n], rsem.at[n], 32, 96, 32 * n) for n in range(3)]
    small = Gather(me, s_v, ssem.at[6], rsem.at[6], 128, 128)
    vectors = Gather(me, v_v, ssem.at[5], rsem.at[5], 16, 16)
    up = Gather(me, wu, ssem.at[3], rsem.at[3], 96, 96, 0, usrc, lsem.at[0])
    down = Gather(me, wd, ssem.at[4], rsem.at[4], 96, 96, 0, contract, lsem.at[1])
    steps = gather_steps(vectors, a0, a1, a2, small, up, down)
    after = lambda name: run_steps(steps.get(name, ()))
    after("first")
    wac = cp(attn_v, wa, osem.at[0]); wac.start()
    prepare_columns(v_v, col, 96)
    xc.wait()
    for ff in range(4):
        for s in range(2):
            project(ff, s, a_v, x_s, col, qkv)
            after("P%d" % (2 * ff + s))
    after("W")
    prepare_mask(s_v, lens, heat, msk, 64, 128)
    for n in range(8):
        vec[:, 96 * n : 96 * n + 96] = v_v[0, 16 * n : 16 * n + 16, :].astype(f32)[0:8, :96]
    for ff in range(4):
        tail = v_v[ff, 0:16, :].astype(f32)
        for r in range(6):
            bup[:, 768 * ff + 128 * r : 768 * ff + 128 * r + 128] = tail[8 + r : 9 + r]
    def hook(t):
        for n in range(24 // FORWARD_HEADS):
            if steps.get(n):
                pl.when(t == n)(functools.partial(run_steps, steps[n]))
    qc = [cp(qkv.at[s], qkv_o.at[s], osem.at[1 + s]) for s in range(2)]
    for c in qc: c.start()
    attend_all(qkv, msk, ctx, pt, ptbuf, psem, FORWARD_HEADS, hook)
    oc = cp(ctx, ctx_o, osem.at[3]); oc.start()
    uc = cp(wu, u_v, isem.at[2])
    dc = cp(wd, a_v, isem.at[3])
    after("UP")
    uc.start()
    uc.wait()
    for ff in range(4):
        wout[:, 192 * ff:192 * ff + 64] = a_v[ff, :, 576:640]
        wout[:, 192 * ff + 64:192 * ff + 192] = u_v[ff, :, 768:896]
    ac = [cp(act_s.at[s], act.at[pl.ds(512 * s, 512)], osem.at[4 + s]) for s in range(2)]
    hc = [cp(x_s.at[pl.ds(512 * s, 512)], hlow.at[pl.ds(512 * s, 512)], osem.at[6 + s]) for s in range(2)]
    for s in range(2):
        sl = pl.ds(512 * s, 512)
        first = x_s[sl].astype(f32) + dg(ctx[s], wout[...], 0, 0) + vec[4:5]
        n1, inv1 = norm_rows(first)
        n1_s[s] = n1
        inv_s[s] = inv1
        hl = (n1 * vec[0:1] + vec[6:7]).astype(bf16)
        x_s[sl] = hl
        hc[s].start()
        after("O%d" % s)
        for ff in range(4):
            pre = dg(x_s[sl], u_v[ff, :, :768], 1, 0) + bup[:, 768 * ff:768 * ff + 768]
            phi = 0.5 * (1.0 + lax.erf(pre * 0.7071067811865476))
            slope[s, ff] = phi + pre * (jnp.exp(-0.5 * pre * pre) * 0.3989422804014327)
            act_s[s, :, 768 * ff:768 * ff + 768] = (pre * phi).astype(bf16)
            after("F%d%d" % (s, ff))
        ac[s].start()
    after("LAST")
    wac.wait()
    for g in (a0, a1, a2):
        g.finish()
    dc.start()
    dc.wait()
    for c in qc: c.wait()
    outs = lambda s, only=range(6): [[
        lambda: cp(cot_s.at[pl.ds(512 * s, 512)], out.at[pl.ds(512 * s, 512)], osem.at[8]),
        lambda: cp(act_s.at[s], gp.at[pl.ds(512 * s, 512)], osem.at[9]),
        lambda: cp(gsl_s, gslow.at[pl.ds(512 * s, 512)], osem.at[10]),
        lambda: cp(gfl_s, gflow.at[pl.ds(512 * s, 512)], osem.at[11]),
        lambda: cp(gf_s, gf.at[pl.ds(512 * s, 512)], osem.at[12]),
        lambda: cp(qkv.at[s, pl.ds(0, 768)], gctx.at[s], osem.at[13]),
    ][n]() for n in only]
    cc.wait()
    total = None
    for s in range(2):
        sl = pl.ds(512 * s, 512)
        n1, inv1 = n1_s[s], inv_s[s]
        acc = n1 * vec[0:1] + vec[6:7] + vec[5:6]
        for ff in range(4):
            acc = acc + dg(act_s[s, :, 768 * ff:768 * ff + 768], a_v[ff], 1, 1)
        n2, inv2 = norm_rows(acc)
        g = cot_s[sl].astype(f32)
        gs = norm_rows_back(g, n2, inv2, vec[1:2])
        rs = lambda v: jnp.sum(v, axis=0, keepdims=True)
        s_gain2, s_cot, s_gs = rs(g * n2), rs(g), rs(gs)
        cot_s[sl] = (n2 * vec[1:2] + vec[7:8]).astype(bf16)
        if s:
            for c in outs(s - 1, (2, 3, 4)): c.wait()
        gsl = gs.astype(bf16)
        gsl_s[...] = gsl
        ac[s].wait()
        gh = gs
        for ff in range(4):
            p = (dg(gsl, a_v[ff], 1, 0) * slope[s, ff]).astype(bf16)
            act_s[s, :, 768 * ff:768 * ff + 768] = p
            b = rs(p.astype(f32))
            cols = slice(768 * ff, 768 * ff + 768)
            gbup[:, cols] = gbup[:, cols] + b if s else b
            gh = gh + dg(p, u_v[ff, :, :768], 1, 1)
        gfirst = norm_rows_back(gh, n1, inv1, vec[0:1])
        gf_s[...] = gfirst
        gfl = gfirst.astype(bf16)
        gfl_s[...] = gfl
        if s == 0:
            oc.wait()
        qkv[s, 0:768, :] = dg(wout[...], gfl, 1, 1).astype(bf16)
        part = jnp.concatenate([rs(gh * n1), s_gain2, jnp.zeros((2, 768), f32), rs(gfirst), s_gs, rs(gh), s_cot], axis=0)
        total = part if total is None else total + part
        if s:
            for c in outs(0, (0, 1, 5)): c.wait()
        for c in outs(s): c.start()
    sums[...] = total
    for c in outs(1): c.wait()
    for c in hc: c.wait()
    for g in (small, up, down, vectors):
        g.finish()


def front_call(*ops):
    any_ = pl.BlockSpec(memory_space=pl.ANY)
    vm = pl.BlockSpec(memory_space=pltpu.VMEM)
    sm = pl.BlockSpec(memory_space=pltpu.SMEM)
    sd = jax.ShapeDtypeStruct
    dma = pltpu.SemaphoreType.DMA
    V = pltpu.VMEM
    tok = sd((1024, 768), bf16)
    wide = sd((1024, 3072), bf16)
    return pl.pallas_call(
        front_kernel,
        out_shape=(
            sd((4, 768, 896), bf16), sd((4, 768, 768), bf16), sd((4, 768, 640), bf16), sd((2, 2304, 512), bf16), sd((2, 768, 512), bf16),
            sd((24, 512, 512), bf16), tok, wide, wide, tok, tok, tok, sd((1024, 768), f32), sd((2, 768, 512), bf16),
            sd((8, 768), f32), sd((1, 3072), f32),
        ),
        in_specs=[vm, vm, vm, vm, any_, vm, vm, vm, vm, sm, sm, any_, any_],
        out_specs=(any_,) * 14 + (vm, vm),
        scratch_shapes=[
            V((4, 768, 768), bf16), V((4, 768, 896), bf16), V((4, 1024, 128), bf16), V((4, 128, 128), bf16), V((96, 896), bf16), V((768, 768), bf16),
            V((768, 16), f32), V((2, 512, 512), f32), V((2, FORWARD_HEADS, 512, 512), bf16), V((2, 2304, 512), bf16), V((2, 768, 512), bf16),
            V((1024, 768), bf16), V((1024, 768), bf16), V((2, 4, 512, 768), SLOPE), V((2, 512, 3072), bf16), V((2, 512, 768), f32),
            V((2, 512, 1), f32), V((8, 768), f32), V((1, 3072), f32), V((512, 768), bf16), V((512, 768), f32), V((512, 768), bf16),
            dma((7, 19)), dma((7, 19)), dma((2,)), dma((2,)), dma((4,)), dma((14,)),
        ],
        compiler_params=pltpu.CompilerParams(collective_id=0, has_side_effects=True, vmem_limit_bytes=63 << 20),
        name="gather_attend_feed_forward",
    )(*ops)


SLOPE = f32


def attend_head_back(qkv, gctx, p_ref, dproj, gm, s, h):
    q = qkv[s, pl.ds(h * HD, HD), :]
    k = qkv[s, pl.ds(768 + h * HD, HD), :]
    v = qkv[s, pl.ds(1536 + h * HD, HD), :]
    go = gctx[s, pl.ds(h * HD, HD), :]
    p = p_ref[...]
    dp = dg(v, go, 0, 0)
    pf = p.astype(f32)
    drow = jnp.sum(pf * dp, axis=0, keepdims=True)
    ds = pf * (dp - drow)
    dsl = ds.astype(bf16)
    dproj[s, pl.ds(1536 + h * HD, HD), :] = dg(go, p, 1, 1).astype(bf16)
    dproj[s, pl.ds(768 + h * HD, HD), :] = dg(q, dsl, 1, 1).astype(bf16)
    dproj[s, pl.ds(h * HD, HD), :] = (dg(k, dsl, 1, 0) * 0.125).astype(bf16)
    return ds

def attend_all_back(qkv, gctx, pt, ptbuf, psem, dproj, gm, per, hook):
    steps = 24 // per
    gm[...] = jnp.zeros(gm.shape, f32)
    load = lambda t: pltpu.make_async_copy(
        pt.at[pl.ds(t * per, per)], ptbuf.at[t % 2], psem.at[t % 2]
    )
    def body(t, carry):
        load(t).wait()
        s = t // (12 // per)
        tot = None
        for u in range(per):
            h = (t % (12 // per)) * per + u
            ds = attend_head_back(qkv, gctx, ptbuf.at[t % 2, u], dproj, gm, s, h)
            tot = ds if tot is None else tot + ds
        gm[...] += tot
        @pl.when(t + 2 < steps)
        def _():
            load(t + 2).start()
        hook(t)
        return carry
    lax.fori_loop(0, steps, body, 0)


ORDER = (1, 2, 3, 0)


def small_rows(part, gm, sums, gbup):
    table = gm[...].T
    zero = jnp.zeros((8, 32), f32)
    for f in range(4):
        bias = jnp.concatenate(
            [gbup[:, 768 * f + 128 * r : 768 * f + 128 * r + 128] for r in range(6)] + [jnp.zeros((2, 128), f32)], axis=0
        )
        for i in range(8):
            ref = part.at[f, i // 2, i % 2]
            for j in range(4):
                at = 64 * i + 16 * j
                ref[96:112, 128 * j : 128 * j + 128] = table[at : at + 16, 128 * f : 128 * f + 128].astype(bf16)
            rows = jnp.concatenate([sums[:, 96 * i : 96 * i + 96], zero], axis=1)
            ref[96:112, 512:640] = jnp.concatenate([rows, bias], axis=0).astype(bf16)


def backward_kernel(wfull, qkv_h, pt, gctx_h, ctx_h, act, gp, hlow, gslow, x, gfl_h, gf, sums_in, gbup, gin, oup, odown, oattn,
                    upart, urc, urq, urx, ury, urz, dpart, drc, drq, drx, dry, drz, apart, arc, arq, arx, ary, arz, gm, sums,
                    lhs, chunk, qkv, gctx, ctx, gfl, dproj, ptbuf, gbuf, ssem, rsem, lsem, csem, isem, psem, gsem):
    me = partners()
    cp = pltpu.make_async_copy
    at = [(me[1] + k) % 4 for k in range(4)]
    def chunk_copy(n):
        src = (act, gp)[n // 4].at[:, pl.ds(pl.multiple_of(768 * at[ORDER[n % 4]], 768), 768)]
        return cp(src, chunk.at[n % 2], csem.at[n % 2])
    l0 = cp(gslow, lhs.at[0], lsem.at[0]); l1 = cp(hlow, lhs.at[1], lsem.at[1]); l2 = cp(x, lhs.at[0], lsem.at[0])
    l0.start(); chunk_copy(0).start(); chunk_copy(1).start(); l1.start()
    ins = [cp(a, b, isem.at[n]) for n, (a, b) in enumerate(((ctx_h, ctx), (gfl_h, gfl), (qkv_h, qkv), (gctx_h, gctx)))]
    for c in ins: c.start()
    for t in range(2): cp(pt.at[pl.ds(t * BACKWARD_HEADS, BACKWARD_HEADS)], ptbuf.at[t], psem.at[t]).start()
    up = Scatter(me, upart, (urc, urq, urx, ury, urz), oup, ssem.at[0], rsem.at[0])
    down = Scatter(me, dpart, (drc, drq, drx, dry, drz), odown, ssem.at[1], rsem.at[1])
    attn = Scatter(me, apart, (arc, arq, arx, ary, arz), oattn, ssem.at[2], rsem.at[2])
    before, loop, dots = steps_between(attn, up, down)
    l0.wait()
    for n in range(8):
        g, k = (down, up)[n // 4], ORDER[n % 4]
        if n == 4:
            l2.start()
            for c in ins: c.wait()
            dwo = (dg(ctx[0], gfl[0:512], 1, 0) + dg(ctx[1], gfl[512:1024], 1, 0)).astype(bf16)
            for f in range(4):
                attn.part[f, :, :, 0:96, 576:] = dwo[:, 192 * f:192 * f + 64].reshape(4, 2, 96, 64)
                up.part[f, :, :, :, 768:] = dwo[:, 192 * f + 64:192 * f + 192].reshape(4, 2, 96, 128)
            l1.wait()
        chunk_copy(n).wait()
        g.part[at[k], :, :, :, 0:768] = dg(lhs[n // 4], chunk[n % 2], 0, 0).astype(bf16).reshape(4, 2, 96, 768)
        if n < 6: chunk_copy(n + 2).start()
        if n == 0:
            enter_barrier(me)
        g.c_(k)
        run_steps(before.get(n, ()))
    def hook(t):
        for at_t in sorted(loop):
            pl.when(t == at_t)(functools.partial(run_steps, loop[at_t]))
    attend_all_back(qkv, gctx, pt, ptbuf, psem, dproj, gm, BACKWARD_HEADS, hook)
    ones = jnp.ones((8, 512), bf16)
    sums[...] = sums_in[...]
    sums[2:3] = (dg(ones, dproj[0, 0:768], 1, 1) + dg(ones, dproj[1, 0:768], 1, 1))[0:1]
    sums[3:4] = (dg(ones, dproj[0, 1536:2304], 1, 1) + dg(ones, dproj[1, 1536:2304], 1, 1))[0:1]
    small_rows(attn.part, gm, sums, gbup)
    l2.wait()
    for n, k in enumerate(ORDER):
        r = pl.ds(pl.multiple_of(576 * at[k], 576), 576)
        dw = dg(lhs[0, 0:512], dproj[0, r, :], 0, 1) + dg(lhs[0, 512:1024], dproj[1, r, :], 0, 1)
        attn.part[at[k], :, :, 0:96, :576] = dw.astype(bf16).reshape(4, 2, 96, 576)
        attn.c_(k)
        run_steps(dots.get(n, ()))
    aw = [cp(wfull.at[f], chunk.at[f % 2, pl.ds(0, 768), pl.ds(0, 640)], csem.at[f % 2]) for f in range(4)]
    aw[0].start(); aw[1].start()
    gi = [cp(gf.at[pl.ds(512 * s, 512)], gbuf.at[s], gsem.at[s]) for s in range(2)]
    for c in gi: c.start()
    for f in range(4):
        aw[f].wait()
        if f == 0:
            for c in gi: c.wait()
        for s in range(2):
            gbuf[s] = gbuf[s] + dg(dproj[s, 576 * f:576 * f + 576], chunk[f % 2, 0:768, :576], 0, 1)
            run_steps(dots.get(4 + 2 * f + s, ()))
        if f < 2: aw[f + 2].start()
    go = [cp(gbuf.at[s], gin.at[pl.ds(512 * s, 512)], gsem.at[s]) for s in range(2)]
    for c in go: c.start()
    run_steps(dots.get(12, ()))
    for c in go: c.wait()
    for g in (attn, up, down):
        g.finish()


def steps_between(attn, up, down):
    before = {
        2: [(down.q, 1)],
        3: [(down.q, 2)],
        4: [(down.q, 3), (down.q, 0), (down.t, 1)],
        5: [(down.t, 2)],
        6: [(up.q, 1)],
        7: [(up.q, 2), (down.t, 3)],
    }
    loop = {
        0: [(down.t, 0), (up.q, 3)],
        1: [(up.q, 0)],
        2: [(down.w, 2)],
        3: [(down.w, 1)],
        4: [(up.t, 1)],
        5: [(up.t, 2)],
        7: [(down.w, 0)],
        8: [(down.w, 3)],
        9: [(up.t, 3)],
        10: [(up.t, 0)],
    }
    dots = {
        0: [(down.e,), (up.w, 2)],
        1: [(up.w, 1)],
        2: [(attn.q, 1), (up.w, 0)],
        3: [(attn.q, 2), (up.w, 3)],
        5: [(attn.q, 3)],
        7: [(attn.t, 1)],
        10: [(attn.t, 2)],
        12: [(attn.t, 3), (attn.q, 0), (attn.w, 1), (up.e,), (attn.w, 3), (attn.w, 2), (attn.t, 0), (attn.w, 0), (attn.e,)],
    }
    return before, loop, dots


def run_steps(todo):
    for step, *arg in todo:
        step(*arg)


def backward_call(*ops):
    any_ = pl.BlockSpec(memory_space=pl.ANY); vm = pl.BlockSpec(memory_space=pltpu.VMEM)
    sd = jax.ShapeDtypeStruct
    dma = pltpu.SemaphoreType.DMA
    V = pltpu.VMEM
    return pl.pallas_call(backward_kernel,
        out_shape=(sd((1024, 768), f32), sd((96, 896), f32), sd((96, 768), f32), sd((112, 640), f32)),
        in_specs=[any_] * 12 + [vm] * 2, out_specs=(any_, vm, vm, vm),
        scratch_shapes=scatter_buffers(96, 896) + scatter_buffers(96, 768) + scatter_buffers(112, 640)
            + [V((512, 512), f32), V((8, 768), f32)]
            + [V((2, 1024, 768), bf16), V((2, 1024, 768), bf16), V((2, 2304, 512), bf16), V((2, 768, 512), bf16), V((2, 768, 512), bf16), V((1024, 768), bf16),
            V((2, 2304, 512), bf16), V((2, BACKWARD_HEADS, 512, 512), bf16), V((2, 512, 768), f32), dma((3, 19)), dma((3, 19)), dma((2,)), dma((2,)), dma((4,)), dma((2,)), dma((2,))],
        compiler_params=pltpu.CompilerParams(collective_id=1, has_side_effects=True, vmem_limit_bytes=63 << 20), name="attend_back_and_reduce")(*ops)


def hand_out_kernel(gin, res, gup, gdown, attn_h, gate_h, jitter_h, heat, gin_o, res_o, qkv, out, up, down, bias, gains, shifts, logits,
                    gbuf, rbuf, ubuf, dbuf, attn, gate, jitter, sem):
    cp = pltpu.make_async_copy
    n = 4
    rows = gin.shape[0] // n
    moves = [(a.at[pl.ds(r * rows, rows)], b.at[pl.ds(r * rows, rows)], c.at[pl.ds(r * rows, rows)])
             for r in range(n) for a, b, c in ((gin, gbuf, gin_o), (res, rbuf, res_o))]
    moves += [(gdown, dbuf, down), (gup, ubuf, None)]
    small = [cp(a, b, sem.at[m]) for m, (a, b) in enumerate(((attn_h, attn), (gate_h, gate), (jitter_h, jitter)))]
    ins = [cp(a, b, sem.at[3 + m]) for m, (a, b, c) in enumerate(moves)]
    outs = [cp(b, c, sem.at[13 + m]) for m, (a, b, c) in enumerate(moves[:-1])]
    for c in small + ins: c.start()
    for c in small: c.wait()
    qkv[...] = attn[:96, :576]
    inv = 1.0 / heat[0]
    table = jnp.concatenate([attn[96:112, 128 * j:128 * j + 128] for j in range(4)], axis=0)
    mixed = (gate[...].astype(f32) + jitter[...].astype(f32)) * inv
    logits[...] = table * (inv / (1.0 + jnp.exp(mixed)))
    gains[...] = attn[96:98, 512:608]
    shifts[...] = attn[98:104, 512:608]
    bias[...] = attn[104:110, 512:640]
    for a, b in zip(ins, outs):
        a.wait()
        b.start()
    ins[-1].wait()
    up[...] = ubuf[:, :768]
    out[:, :64] = attn[:96, 576:]
    out[:, 64:] = ubuf[:, 768:]
    for c in outs: c.wait()


def hand_out_call(gin, res, gup, gdown, attn, gate, jitter, heat):
    any_ = pl.BlockSpec(memory_space=pl.ANY); vm = pl.BlockSpec(memory_space=pltpu.VMEM); sm = pl.BlockSpec(memory_space=pltpu.SMEM)
    sd = lambda *s: jax.ShapeDtypeStruct(s, f32)
    V = pltpu.VMEM
    return pl.pallas_call(hand_out_kernel,
        out_shape=(sd(1024, 768), jax.ShapeDtypeStruct((1024, 768), bf16), sd(96, 576), sd(96, 192), sd(96, 768), sd(96, 768), sd(6, 128), sd(2, 96), sd(6, 96), sd(64, 128)),
        in_specs=[any_] * 7 + [sm], out_specs=(any_, any_, vm, vm, vm, any_) + (vm,) * 4,
        scratch_shapes=[V((1024, 768), f32), V((1024, 768), bf16), V((96, 896), f32), V((96, 768), f32), V((112, 640), f32), V((64, 128), bf16), V((64, 128), bf16), pltpu.SemaphoreType.DMA((23,))],
        compiler_params=pltpu.CompilerParams(vmem_limit_bytes=63 << 20), name="hand_out")(gin, res, gup, gdown, attn, gate, jitter, heat)


def own_device(
    layer_activations,
    token_counts_each,
    attention_triple_matrix,
    attention_final_matrix,
    feedfwd_expand_matrix,
    feedfwd_expand_offset,
    feedfwd_contract_matrix,
    layernorm_scales,
    offset_vectors,
    learned_gate_scores,
    fixed_jitter_matrix,
    relaxation_heat,
    loss_grad_result,
):
    x = layer_activations.reshape(1024, D)
    cot = loss_grad_result.reshape(1024, D)
    (
        _, _, attn_full, qkv, ctx, probs, result, act, grad_pre, hidden_low, grad_second_low, grad_first_low, grad_first, grad_ctx,
        sums, grad_bias,
    ) = front_call(
        attention_triple_matrix, attention_final_matrix, feedfwd_expand_matrix, feedfwd_expand_offset.reshape(6, 128),
        feedfwd_contract_matrix.T, layernorm_scales, offset_vectors, learned_gate_scores, fixed_jitter_matrix, relaxation_heat,
        token_counts_each, x, cot,
    )
    grad_inputs, up, down, attn = backward_call(
        attn_full, qkv, probs, grad_ctx, ctx, act, grad_pre, hidden_low, grad_second_low, x, grad_first_low, grad_first,
        sums, grad_bias,
    )
    grad_inputs, result, g_qkv, g_out, g_up, g_down, g_bias, g_gains, g_shifts, g_logits = hand_out_call(
        grad_inputs, result, up, down, attn, learned_gate_scores, fixed_jitter_matrix, relaxation_heat
    )
    return (
        result.reshape(layer_activations.shape),
        grad_inputs.reshape(layer_activations.shape),
        g_qkv,
        g_out,
        g_up,
        g_bias.reshape(-1),
        g_down.T,
        g_gains,
        g_shifts,
        g_logits,
    )


def solution(mesh):
    in_specs = (
        P(AXES, None, None),
        P(AXES),
        P("dp", "ffn"),
        P("dp", "ffn"),
        P("dp", "ffn"),
        P("ffn"),
        P("ffn", "dp"),
        P(None, "dp"),
        P(None, "dp"),
        P("dp", "ffn"),
        P("dp", "ffn"),
        P(),
        P(AXES, None, None),
    )
    out_specs = (
        P(AXES, None, None),
        P(AXES, None, None),
        P("dp", "ffn"),
        P("dp", "ffn"),
        P("dp", "ffn"),
        P("ffn"),
        P("ffn", "dp"),
        P(None, "dp"),
        P(None, "dp"),
        P("dp", "ffn"),
    )
    own = (mesh.shape["dp"], mesh.shape["ffn"]) == (8, 4)
    return jax.shard_map(
        own_device if own else general_device, mesh=mesh, in_specs=in_specs, out_specs=out_specs, check_vma=False
    )
```

```python
import functools

import jax
import jax.numpy as jnp
from jax import lax
from jax.experimental import pallas as pl
from jax.experimental.pallas import tpu as pltpu
from jax.sharding import PartitionSpec as P

D = 768
HEADS = 12
HEAD_DIM = 64
SEQ_LEN = 512
AXES = ("dp", "ffn")
norm_eps = 1e-06
f32 = jnp.float32
bf16 = jnp.bfloat16
MESH = pl.DeviceIdType.MESH


def dot_first(left, right):
    return lax.dot_general(left, right, (((0,), (0,)), ((), ())), preferred_element_type=f32)


def dot_last(left, right):
    return lax.dot_general(left, right, (((1,), (1,)), ((), ())), preferred_element_type=f32)


def dot(left, right):
    return jnp.dot(left, right, preferred_element_type=f32)


def layer_norm(values, gain, shift):
    mean_row = jnp.mean(values, axis=-1, keepdims=True)
    centered = values - mean_row
    inv_std = lax.rsqrt(jnp.mean(centered * centered, axis=-1, keepdims=True) + norm_eps)
    normed = centered * inv_std
    return (normed * gain + shift, normed, inv_std)


def norm_back(grad_out, normed, inv_std, gain):
    grad_normed = grad_out * gain
    grad_in = inv_std * (
        grad_normed
        - jnp.mean(grad_normed, axis=-1, keepdims=True)
        - normed * jnp.mean(grad_normed * normed, axis=-1, keepdims=True)
    )
    return (grad_in, jnp.sum(grad_out * normed, axis=0), jnp.sum(grad_out, axis=0))


def gelu_slope(values):
    return (
        0.5 * (1.0 + lax.erf(values * 0.7071067811865476))
        + values * jnp.exp(-0.5 * values * values) * 0.3989422804014327
    )


def score_block(queries, keys_low, natural_log_gate, live):
    scores = (
        jnp.einsum("qhd,khd->hqk", queries, keys_low, preferred_element_type=f32)
        * HEAD_DIM ** (-0.5)
        + natural_log_gate
    )
    return jnp.where(live[None, None, :], scores, -1e30)


def attend(queries, keys_low, values_low, natural_log_gate, live):
    scores = score_block(queries, keys_low, natural_log_gate, live)
    peak = jnp.max(scores, axis=-1, keepdims=True)
    shifted_exp = jnp.exp(scores - peak)
    total_exp = jnp.sum(shifted_exp, axis=-1, keepdims=True)
    probs_low = (shifted_exp / total_exp).astype(bf16)
    context = jnp.einsum("hqk,khd->qhd", probs_low, values_low, preferred_element_type=f32)
    return (context, peak + jnp.log(total_exp))


def attend_back(queries, keys_low, values_low, natural_log_gate, live, log_total, grad_context):
    scores = score_block(queries, keys_low, natural_log_gate, live)
    probs = jnp.exp(scores - log_total)
    grad_probs = jnp.einsum("qhd,khd->hqk", grad_context, values_low, preferred_element_type=f32)
    grad_values = jnp.einsum(
        "hqk,qhd->khd", probs.astype(bf16), grad_context, preferred_element_type=f32
    )
    grad_scores = probs * (grad_probs - jnp.sum(probs * grad_probs, axis=-1, keepdims=True))
    grad_mask = jnp.sum(grad_scores, axis=0)
    grad_scores_low = grad_scores.astype(bf16)
    grad_queries = jnp.einsum(
        "hqk,khd->qhd", grad_scores_low, keys_low, preferred_element_type=f32
    ) * HEAD_DIM ** (-0.5)
    grad_keys = jnp.einsum(
        "hqk,qhd->khd", grad_scores_low, queries, preferred_element_type=f32
    ) * HEAD_DIM ** (-0.5)
    return (grad_queries, grad_keys, grad_values, grad_mask)


def gather_weights(pack, small):
    rows_dp = lax.axis_size("dp")
    cols_ffn = lax.axis_size("ffn")
    full = lax.all_gather(pack[None], AXES, axis=0, tiled=True)
    full = full.reshape(rows_dp, cols_ffn, *pack.shape)
    small_full = lax.all_gather(small[None], AXES, axis=0, tiled=True)
    return full, small_full.reshape(rows_dp, cols_ffn, *small.shape)


def columns(blocks):
    rows_dp, cols_ffn, rows, cols = blocks.shape
    return blocks.transpose(0, 2, 1, 3).reshape(rows_dp * rows, cols_ffn * cols)


def blocks_of(full, rows_dp, cols_ffn):
    rows, cols = full.shape
    return full.reshape(rows_dp, rows // rows_dp, cols_ffn, cols // cols_ffn).transpose(0, 2, 1, 3)


def general_device(
    layer_activations,
    token_counts_each,
    attention_triple_matrix,
    attention_final_matrix,
    feedfwd_expand_matrix,
    feedfwd_expand_offset,
    feedfwd_contract_matrix,
    layernorm_scales,
    offset_vectors,
    learned_gate_scores,
    fixed_jitter_matrix,
    relaxation_heat,
    loss_grad_result,
):
    rows_dp = lax.axis_size("dp")
    cols_ffn = lax.axis_size("ffn")
    seq_count = layer_activations.shape[0]
    row_count = seq_count * SEQ_LEN
    shard_rows = attention_triple_matrix.shape[0]
    qkv_cols = attention_triple_matrix.shape[1]
    out_cols = attention_final_matrix.shape[1]
    ff_cols = feedfwd_expand_matrix.shape[1]

    pack = jnp.concatenate(
        [
            attention_triple_matrix,
            attention_final_matrix,
            feedfwd_expand_matrix,
            feedfwd_contract_matrix.T,
        ],
        axis=1,
    )
    mask_cols = learned_gate_scores.shape[1]
    vectors = jnp.concatenate([layernorm_scales, offset_vectors], axis=0)
    small = jnp.concatenate(
        [
            learned_gate_scores,
            fixed_jitter_matrix,
            jnp.pad(vectors, ((0, 0), (0, mask_cols - vectors.shape[1]))),
            feedfwd_expand_offset.reshape(-1, mask_cols),
        ],
        axis=0,
    )
    full, small_full = gather_weights(pack, small)
    full_qkv = columns(full[..., :qkv_cols])
    full_out = columns(full[..., qkv_cols : qkv_cols + out_cols])
    full_up = columns(full[..., qkv_cols + out_cols : qkv_cols + out_cols + ff_cols])
    full_down_t = columns(full[..., qkv_cols + out_cols + ff_cols :])
    mask_rows = learned_gate_scores.shape[0]
    logits_sum = columns(small_full[:, :, :mask_rows]).astype(f32) + columns(
        small_full[:, :, mask_rows : 2 * mask_rows]
    ).astype(f32)
    natural_log_gate = jax.nn.log_sigmoid(logits_sum / relaxation_heat[0])
    vectors_full = (
        small_full[:, 0, 2 * mask_rows : 2 * mask_rows + 8, :shard_rows]
        .transpose(1, 0, 2)
        .reshape(8, D)
        .astype(f32)
    )
    gains_full = vectors_full[:2]
    shifts_full = vectors_full[2:]
    bias_up = small_full[0, :, 2 * mask_rows + 8 :].reshape(1, -1).astype(f32)

    flat_in = layer_activations.reshape(row_count, D)
    qkv_bias = jnp.concatenate([shifts_full[0], jnp.zeros((D,), f32), shifts_full[1]])
    proj_low = (dot(flat_in, full_qkv) + qkv_bias).astype(bf16)
    head_shape = (seq_count, SEQ_LEN, HEADS, HEAD_DIM)
    queries = proj_low[:, :D].reshape(head_shape)
    keys_low = proj_low[:, D : 2 * D].reshape(head_shape)
    values_low = proj_low[:, 2 * D :].reshape(head_shape)
    live = lax.broadcasted_iota(jnp.int32, (seq_count, SEQ_LEN), 1) < token_counts_each[:, None]
    attended = [
        attend(queries[s], keys_low[s], values_low[s], natural_log_gate, live[s])
        for s in range(seq_count)
    ]
    context_low = jnp.concatenate(
        [item[0].reshape(SEQ_LEN, D).astype(bf16) for item in attended], axis=0
    )
    first_sum = flat_in.astype(f32) + dot(context_low, full_out) + shifts_full[2]
    hidden, normed_one, inv_one = layer_norm(first_sum, gains_full[0], shifts_full[4])
    hidden_low = hidden.astype(bf16)
    pre_act = dot(hidden_low, full_up) + bias_up
    act_low = jax.nn.gelu(pre_act, approximate=False).astype(bf16)
    second_sum = hidden + dot_last(act_low, full_down_t) + shifts_full[3]
    result, normed_two, inv_two = layer_norm(second_sum, gains_full[1], shifts_full[5])
    cot_flat = loss_grad_result.reshape(row_count, D).astype(f32)
    grad_second, grad_gain_two, grad_shift_two = norm_back(
        cot_flat, normed_two, inv_two, gains_full[1]
    )
    grad_second_low = grad_second.astype(bf16)
    grad_w_down_t = dot_first(grad_second_low, act_low)
    grad_act = dot(grad_second_low, full_down_t)
    grad_pre = (grad_act * gelu_slope(pre_act)).astype(bf16)
    grad_bias_up = jnp.sum(grad_pre, axis=0, dtype=f32)
    grad_w_up = dot_first(hidden_low, grad_pre)
    grad_hidden = grad_second + dot_last(grad_pre, full_up)
    grad_first, grad_gain_one, grad_shift_one = norm_back(
        grad_hidden, normed_one, inv_one, gains_full[0]
    )
    grad_first_low = grad_first.astype(bf16)
    grad_w_out = dot_first(context_low, grad_first_low)
    grad_context = dot_last(grad_first_low, full_out).astype(bf16).reshape(head_shape)
    back = [
        attend_back(
            queries[s],
            keys_low[s],
            values_low[s],
            natural_log_gate,
            live[s],
            attended[s][1],
            grad_context[s],
        )
        for s in range(seq_count)
    ]
    grad_mask = sum(item[3] for item in back)
    grad_projected = jnp.concatenate(
        [
            jnp.concatenate(
                [item[part].reshape(SEQ_LEN, D).astype(bf16) for item in back], axis=0
            )
            for part in range(3)
        ],
        axis=1,
    )
    grad_w_qkv = dot_first(flat_in, grad_projected)
    grad_inputs = grad_first + dot_last(grad_projected, full_qkv)
    grad_vectors = jnp.stack(
        [
            grad_gain_one,
            grad_gain_two,
            jnp.sum(grad_projected[:, :D], axis=0, dtype=f32),
            jnp.sum(grad_projected[:, 2 * D :], axis=0, dtype=f32),
            jnp.sum(grad_first, axis=0),
            jnp.sum(grad_second, axis=0),
            grad_shift_one,
            grad_shift_two,
        ]
    )
    big = jnp.concatenate(
        [
            blocks_of(item, rows_dp, cols_ffn)
            for item in (grad_w_qkv, grad_w_out, grad_w_up, grad_w_down_t)
        ],
        axis=-1,
    ).reshape(rows_dp * cols_ffn, shard_rows, -1)
    vector_blocks = jnp.broadcast_to(
        grad_vectors.reshape(8, rows_dp, 1, shard_rows).transpose(1, 2, 0, 3),
        (rows_dp, cols_ffn, 8, shard_rows),
    )
    bias_blocks = jnp.broadcast_to(
        grad_bias_up.reshape(1, cols_ffn, -1, mask_cols),
        (rows_dp, cols_ffn, ff_cols // mask_cols, mask_cols),
    )
    little = jnp.concatenate(
        [
            blocks_of(grad_mask, rows_dp, cols_ffn),
            jnp.pad(vector_blocks, ((0, 0), (0, 0), (0, 0), (0, mask_cols - shard_rows))),
            bias_blocks,
        ],
        axis=2,
    ).reshape(rows_dp * cols_ffn, -1, mask_cols)
    big = lax.psum_scatter(big, AXES, scatter_dimension=0, tiled=True)[0]
    little = lax.psum_scatter(little, AXES, scatter_dimension=0, tiled=True)[0]

    own_mixed = (
        learned_gate_scores.astype(f32) + fixed_jitter_matrix.astype(f32)
    ) / relaxation_heat[0]
    grad_logits = little[:mask_rows] * (jax.nn.sigmoid(-own_mixed) / relaxation_heat[0])
    return (
        result.astype(bf16).reshape(layer_activations.shape),
        grad_inputs.reshape(layer_activations.shape),
        big[:, :qkv_cols],
        big[:, qkv_cols : qkv_cols + out_cols],
        big[:, qkv_cols + out_cols : qkv_cols + out_cols + ff_cols],
        little[mask_rows + 8 :].reshape(-1),
        big[:, qkv_cols + out_cols + ff_cols :].T,
        little[mask_rows : mask_rows + 2, :shard_rows],
        little[mask_rows + 2 : mask_rows + 8, :shard_rows],
        grad_logits,
    )


def partners():
    i = lax.axis_index("dp")
    f = lax.axis_index("ffn")
    core = i + 1 - 2 * (i % 2)
    ix = i + 2 - 4 * ((i // 2) % 2)
    iy = (i + 4) % 8
    idg = (ix + 4) % 8
    return i, f, core, ix, iy, idg


def enter_barrier(me):
    i, f, core, ix, iy, idg = me
    sem = pltpu.get_barrier_semaphore()
    mates = [(i, (f + k) % 4) for k in (1, 2, 3)] + [(core, f), (ix, f), (iy, f)]
    for to in mates:
        pl.semaphore_signal(sem, inc=1, device_id=to, device_id_type=MESH)
    pl.semaphore_wait(sem, len(mates))


class Exchange:
    def __init__(self, me, ssem, rsem):
        self.me, self.ssem, self.rsem = me, ssem, rsem

    def copy(self, src, dst, send, recv, to):
        return pltpu.make_async_remote_copy(
            src_ref=src,
            dst_ref=dst,
            send_sem=self.ssem.at[send],
            recv_sem=self.rsem.at[recv],
            device_id=to,
            device_id_type=MESH,
        )

    def send(self, src, dst, send, recv, to):
        self.copy(src, dst, send, recv, to).start()

    def recv(self, ref, n):
        self.copy(ref, ref, 0, n, (self.me[0], self.me[1])).wait_recv()

    def sent(self, ref, n):
        self.copy(ref, ref, n, 0, (self.me[0], self.me[1])).wait_send()


class Gather(Exchange):
    def __init__(self, me, dst, ssem, rsem, rows, stride, offset=0, src=None, lsem=None):
        super().__init__(me, ssem, rsem)
        self.dst, self.rows, self.stride, self.offset, self.lsem = dst, rows, stride, offset, lsem
        self.src = src

    def span(self, i):
        return pl.ds(pl.multiple_of(i * self.stride + self.offset, 16), self.rows)

    def piece(self, i, p):
        return self.dst.at[p, self.span(i)]

    def block(self, i):
        return self.dst.at[:, self.span(i)]

    def own(self):
        return self.piece(self.me[0], self.me[1]) if self.src is None else self.src

    def local(self):
        i, f = self.me[:2]
        return pltpu.make_async_copy(self.src, self.piece(i, f), self.lsem)

    def sz(self, _):
        i, f, core, ix, iy, idg = self.me
        if self.src is not None:
            self.local().start()
        for k in (1, 2, 3):
            self.send(self.own(), self.piece(i, f), 0, 3 - k, (i, (f + k) % 4))

    def sp(self, _):
        i, f, core, ix, iy, idg = self.me
        self.send(self.own(), self.piece(i, f), 1, 3, (ix, f))
        self.send(self.own(), self.piece(i, f), 1, 3, (iy, f))

    def z(self, k):
        i, f, core, ix, iy, idg = self.me
        ref = self.piece(i, (f + k) % 4)
        self.recv(ref, k - 1)
        self.send(ref, ref, 1, 3 + k, (ix, f))
        self.send(ref, ref, 1, 3 + k, (iy, f))

    def o(self, _):
        i, f, core, ix, iy, idg = self.me
        if self.src is not None:
            self.local().wait()
        self.send(self.block(i), self.block(i), 1, 8, (core, f))

    def d(self, k):
        i, f, core, ix, iy, idg = self.me
        p = (f + k) % 4
        rx, ry = self.piece(ix, p), self.piece(iy, p)
        self.recv(self.bytes_of(2, 1), 3 + k)
        if k % 2:
            self.send(rx, rx, 1, 7, (iy, f))
        else:
            self.send(ry, ry, 1, 7, (ix, f))

    def b(self, _):
        i, f, core, ix, iy, idg = self.me
        self.send(self.block(ix), self.block(ix), 1, 8, (core, f))
        self.send(self.block(iy), self.block(iy), 1, 8, (core, f))

    def h(self, _):
        i, f, core, ix, iy, idg = self.me
        self.recv(self.bytes_of(4, 1), 7)
        self.send(self.block(idg), self.block(idg), 1, 8, (core, f))

    def r(self, _):
        self.recv(self.bytes_of(4, 4), 8)

    def bytes_of(self, n, m):
        return self.dst.at[pl.ds(0, n), pl.ds(0, m * self.rows)]

    def finish(self):
        self.sent(self.bytes_of(3, 1), 0)
        self.sent(self.bytes_of(4, 7), 1)


class Scatter(Exchange):
    def __init__(self, me, part, got, out, ssem, rsem):
        super().__init__(me, ssem, rsem)
        self.part, self.out = part, out
        self.rc, self.rq, self.rx, self.ry, self.rz = got
        i = me[0]
        self.c = i % 2
        self.xy = i // 2
        self.xyx = self.xy + 1 - 2 * (self.xy % 2)
        self.xyy = (self.xy + 2) % 4
        self.xyd = (self.xyx + 2) % 4

    def at(self, k):
        return (self.me[1] + k) % 4

    def piece(self, k, xy):
        return self.part.at[self.at(k), xy, self.c]

    def finish(self):
        self.sent(self.rc, 0)
        self.sent(self.rc.at[pl.ds(0, 3)], 1)
        self.sent(self.rz, 2)

    def add(self, ref, *refs):
        if len(refs) == 1:
            ref[...] = ref[...] + refs[0][...]
            return
        total = ref[...].astype(f32)
        for other in refs:
            total = total + other[...].astype(f32)
        ref[...] = total.astype(ref.dtype)

    def c_(self, k):
        self.send(self.part.at[self.at(k), :, 1 - self.c], self.rc.at[k], 0, k, (self.me[2], self.me[1]))

    def q(self, k):
        i, f, core, ix, iy, idg = self.me
        self.recv(self.rc.at[k], k)
        ref = self.piece(k, self.xyd)
        self.add(ref, self.rc.at[k, self.xyd])
        self.send(ref, self.rq.at[k], 1, 4 + k, (iy if k % 2 else ix, f))
        refx, refy = self.piece(k, self.xyx), self.piece(k, self.xyy)
        if k % 2:
            self.add(refy, self.rc.at[k, self.xyy])
            self.send(refy, self.ry.at[k], 1, 8 + k, (iy, f))
            self.add(refx, self.rc.at[k, self.xyx])
        else:
            self.add(refx, self.rc.at[k, self.xyx])
            self.send(refx, self.rx.at[k], 1, 8 + k, (ix, f))
            self.add(refy, self.rc.at[k, self.xyy])
        self.add(self.piece(k, self.xy), self.rc.at[k, self.xy])

    def t(self, k):
        i, f, core, ix, iy, idg = self.me
        self.recv(self.rq.at[k], 4 + k)
        ref = self.piece(k, self.xyx if k % 2 else self.xyy)
        self.add(ref, self.rq.at[k])
        if k % 2:
            self.send(ref, self.rx.at[k], 1, 8 + k, (ix, f))
        else:
            self.send(ref, self.ry.at[k], 1, 8 + k, (iy, f))

    def w(self, k):
        i, f, core, ix, iy, idg = self.me
        self.recv(self.rx.at[pl.ds(0, 2)], 8 + k)
        ref = self.piece(k, self.xy)
        if k:
            self.add(ref, self.rx.at[k], self.ry.at[k])
            self.send(ref, self.rz.at[3 - k], 2, 12, (i, (f + k) % 4))
        else:
            self.out[...] = ref[...].astype(f32) + self.rx[k].astype(f32) + self.ry[k].astype(f32)

    def e(self):
        total = self.out[...]
        self.recv(self.rz, 12)
        for k in range(3):
            total = total + self.rz[k].astype(f32)
        self.out[...] = total


def scatter_buffers(rows, cols):
    return [
        pltpu.VMEM(shape, bf16)
        for shape in ((4, 4, 2, rows, cols), (4, 4, rows, cols)) + ((4, rows, cols),) * 3 + ((3, rows, cols),)
    ]


HD=64
def dg(a,b,ca,cb): return lax.dot_general(a,b,(((ca,),(cb,)),((),())),preferred_element_type=f32)

def log_sigmoid(z):
    return jnp.minimum(z, 0.0) - jnp.log1p(jnp.exp(-jnp.abs(z)))

def prepare_mask(s_v, lens, heat, msk, mrows, srows):
    inv = 1.0 / heat[0]
    n = srows
    rows = []
    for i in range(8):
        row = []
        for f in range(4):
            a = s_v[f, pl.ds(i * n, mrows), :].astype(f32) + s_v[f, pl.ds(i * n + mrows, mrows), :].astype(f32)
            row.append(log_sigmoid(a * inv))
        rows.append(jnp.concatenate(row, axis=1))
    lmt = jnp.concatenate(rows, axis=0).T
    key = lax.broadcasted_iota(jnp.int32, lmt.shape, 0)
    for s in range(msk.shape[0]):
        msk[s] = jnp.where(key < lens[s], lmt, -1e30)

def prepare_columns(v_v, col, cols):
    for i in range(8):
        v = v_v[0, pl.ds(i * 16, 16), :].astype(f32)
        col[pl.ds(i * cols, cols), :] = v.T[:cols, :]

def project(f, s, a_v, x, col, qkv):
    acc = dg(a_v[f, :, :576], x[s * 512:(s + 1) * 512, :], 0, 1)
    lo = 0
    while lo < 576:
        g = 576 * f + lo
        kind = g // 768
        hi = min(576, (kind + 1) * 768 - 576 * f)
        part = acc[lo:hi]
        b = g - kind * 768
        if kind == 0:
            part = (part + col[b:b + hi - lo, 2:3]) * 0.125
        elif kind == 2:
            part = part + col[b:b + hi - lo, 3:4]
        qkv[s, g:g + hi - lo, :] = part.astype(bf16)
        lo = hi


def attend_head(qkv, msk, ctx, ptbuf, slot, s, h):
    q = qkv[s, pl.ds(h * HD, HD), :]
    k = qkv[s, pl.ds(768 + h * HD, HD), :]
    v = qkv[s, pl.ds(1536 + h * HD, HD), :]
    st = dg(k, q, 0, 0) + msk[s]
    e = jnp.exp(st - jnp.max(st, axis=0, keepdims=True))
    p = (e * (1.0 / jnp.sum(e, axis=0, keepdims=True))).astype(bf16)
    ptbuf[slot] = p
    ctx[s, pl.ds(h * HD, HD), :] = dg(v, p, 1, 0).astype(bf16)

def attend_all(qkv, msk, ctx, pt, ptbuf, psem, per, hook):
    steps = 24 // per
    out = lambda t: pltpu.make_async_copy(
        ptbuf.at[t % 2], pt.at[pl.ds(t * per, per)], psem.at[t % 2]
    )
    def body(t, carry):
        @pl.when(t >= 2)
        def _():
            out(t - 2).wait()
        s = t // (12 // per)
        for u in range(per):
            h = (t % (12 // per)) * per + u
            attend_head(qkv, msk, ctx, ptbuf.at[t % 2], u, s, h)
        out(t).start()
        hook(t)
        return carry
    lax.fori_loop(0, steps, body, 0)
    for t in (steps - 2, steps - 1):
        out(t).wait()


FORWARD_HEADS = 4
BACKWARD_HEADS = 3


def norm_rows(v):
    mean = jnp.mean(v, axis=-1, keepdims=True)
    c = v - mean
    inv = lax.rsqrt(jnp.mean(c * c, axis=-1, keepdims=True) + 1e-6)
    return c * inv, inv

def norm_rows_back(g, normed, inv, gain):
    e = g * gain
    return inv * (e - jnp.mean(e, axis=-1, keepdims=True) - normed * jnp.mean(e * normed, axis=-1, keepdims=True))

def gather_steps(vec, a0, a1, a2, small, up, down):
    return {
        'first': [(vec.sz, 0), (a0.sz, 0), (small.sz, 0), (a1.sz, 0), (a2.sz, 0), (vec.sp, 0), (a0.sp, 0), (small.sp, 0), (a1.sp, 0), (a2.sp, 0), (vec.z, 1), (vec.z, 2), (vec.z, 3), (vec.o, 0), (vec.d, 0), (a0.d, 0), (a0.z, 1), (small.d, 0), (a0.z, 2), (a1.d, 0), (a0.z, 3), (a0.o, 0), (a2.d, 0), (vec.d, 1), (vec.d, 2), (vec.d, 3), (vec.b, 0), (small.z, 1), (small.z, 2), (a0.d, 1), (small.z, 3), (small.o, 0), (a0.d, 2), (a1.z, 1), (a1.z, 2), (a0.d, 3), (a0.b, 0), (a1.z, 3), (a1.o, 0), (vec.h, 0), (small.d, 1), (a2.z, 1), (small.d, 2), (vec.r, 0), (small.d, 3), (small.b, 0), (a2.z, 2), (a0.h, 0), (a2.z, 3), (up.sz, 0), (up.sp, 0), (a2.o, 0), (a1.d, 1), (a1.d, 2), (a0.r, 0), (a1.d, 3), (a1.b, 0), (a2.d, 1), (small.h, 0), (a2.d, 2), (a2.d, 3), (a2.b, 0), (small.r, 0), (up.z, 1), (up.d, 0), (a1.h, 0), (a2.h, 0), (up.z, 2), (a1.r, 0), (a2.r, 0)],
        'P3': [(up.d, 1)],
        'P5': [(up.z, 3), (up.o, 0)],
        'P6': [(down.sz, 0)],
        0: [(up.d, 2), (down.z, 1)],
        1: [(up.d, 3), (up.b, 0)],
        2: [(down.sp, 0), (down.z, 2)],
        3: [(down.z, 3), (down.o, 0)],
        4: [(up.h, 0), (down.d, 1)],
        5: [(down.d, 0)],
        'UP': [(up.r, 0)],
        'O0': [(down.d, 2)],
        'F01': [(down.d, 3), (down.b, 0)],
        'F11': [(down.h, 0)],
        'LAST': [(down.r, 0)],
    }


def front_kernel(triple, final, expand, bup_in, contract, scales, offsets, gate, jitter, heat, lens, x, cot,
                 wa, qkv_o, ctx_o, pt, out, act, gp, hlow, gslow, gflow, gf, gctx, sums, gbup,
                 a_v, u_v, d_v, s_v, v_v, usrc, wout, col, msk, ptbuf, qkv, ctx, x_s, cot_s, slope, act_s, n1_s, inv_s, vec, bup,
                 gsl_s, gf_s, gfl_s, ssem, rsem, lsem, psem, isem, osem):
    me = partners()
    i, f = me[0], me[1]
    cp = pltpu.make_async_copy
    xc = cp(x, x_s, isem.at[0]); xc.start()
    cc = cp(cot, cot_s, isem.at[1]); cc.start()
    rows = pl.ds(pl.multiple_of(96 * i, 96), 96)
    a_v[f, rows, :576] = triple[...]
    a_v[f, rows, 576:640] = final[:, :64]
    usrc[:, :768] = expand[...]
    usrc[:, 768:] = final[:, 64:]
    at = lambda o, n: pl.ds(pl.multiple_of(o, 16), n)
    s_v[f, at(128 * i, 64), :] = gate[...]
    s_v[f, at(128 * i + 64, 64), :] = jitter[...]
    vectors = jnp.concatenate([scales[...].astype(f32), offsets[...].astype(f32)], axis=0)
    bias = bup_in[...].astype(f32)
    v_v[f, at(16 * i, 16), :] = jnp.concatenate(
        [jnp.concatenate([vectors, jnp.zeros((8, 32), f32)], axis=1)]
        + [bias, jnp.zeros((2, 128), f32)], axis=0
    ).astype(bf16)
    enter_barrier(me)
    attn_v = a_v
    a0, a1, a2 = [Gather(me, attn_v, ssem.at[n], rsem.at[n], 32, 96, 32 * n) for n in range(3)]
    small = Gather(me, s_v, ssem.at[6], rsem.at[6], 128, 128)
    vectors = Gather(me, v_v, ssem.at[5], rsem.at[5], 16, 16)
    up = Gather(me, u_v, ssem.at[3], rsem.at[3], 96, 96, 0, usrc, lsem.at[0])
    down = Gather(me, d_v, ssem.at[4], rsem.at[4], 96, 96, 0, contract, lsem.at[1])
    steps = gather_steps(vectors, a0, a1, a2, small, up, down)
    after = lambda name: run_steps(steps.get(name, ()))
    after("first")
    wac = cp(attn_v, wa, osem.at[0]); wac.start()
    prepare_columns(v_v, col, 96)
    xc.wait()
    for ff in range(4):
        for s in range(2):
            project(ff, s, a_v, x_s, col, qkv)
            after("P%d" % (2 * ff + s))
    after("W")
    prepare_mask(s_v, lens, heat, msk, 64, 128)
    for n in range(8):
        vec[:, 96 * n : 96 * n + 96] = v_v[0, 16 * n : 16 * n + 16, :].astype(f32)[0:8, :96]
    for ff in range(4):
        tail = v_v[ff, 0:16, :].astype(f32)
        for r in range(6):
            bup[:, 768 * ff + 128 * r : 768 * ff + 128 * r + 128] = tail[8 + r : 9 + r]
    def hook(t):
        for n in range(24 // FORWARD_HEADS):
            if steps.get(n):
                pl.when(t == n)(functools.partial(run_steps, steps[n]))
    qc = [cp(qkv.at[s], qkv_o.at[s], osem.at[1 + s]) for s in range(2)]
    for c in qc: c.start()
    attend_all(qkv, msk, ctx, pt, ptbuf, psem, FORWARD_HEADS, hook)
    oc = cp(ctx, ctx_o, osem.at[3]); oc.start()
    after("UP")
    for ff in range(4):
        wout[:, 192 * ff:192 * ff + 64] = a_v[ff, :, 576:640]
        wout[:, 192 * ff + 64:192 * ff + 192] = u_v[ff, :, 768:896]
    ac = [cp(act_s.at[s], act.at[pl.ds(512 * s, 512)], osem.at[4 + s]) for s in range(2)]
    hc = [cp(x_s.at[pl.ds(512 * s, 512)], hlow.at[pl.ds(512 * s, 512)], osem.at[6 + s]) for s in range(2)]
    for s in range(2):
        sl = pl.ds(512 * s, 512)
        first = x_s[sl].astype(f32) + dg(ctx[s], wout[...], 0, 0) + vec[4:5]
        n1, inv1 = norm_rows(first)
        n1_s[s] = n1
        inv_s[s] = inv1
        hl = (n1 * vec[0:1] + vec[6:7]).astype(bf16)
        x_s[sl] = hl
        hc[s].start()
        after("O%d" % s)
        for ff in range(4):
            pre = dg(x_s[sl], u_v[ff, :, :768], 1, 0) + bup[:, 768 * ff:768 * ff + 768]
            phi = 0.5 * (1.0 + lax.erf(pre * 0.7071067811865476))
            slope[s, ff] = (phi + pre * (jnp.exp(-0.5 * pre * pre) * 0.3989422804014327)).astype(SLOPE)
            act_s[s, :, 768 * ff:768 * ff + 768] = (pre * phi).astype(bf16)
            after("F%d%d" % (s, ff))
        ac[s].start()
    after("LAST")
    wac.wait()
    for c in qc: c.wait()
    outs = lambda s, only=range(6): [[
        lambda: cp(cot_s.at[pl.ds(512 * s, 512)], out.at[pl.ds(512 * s, 512)], osem.at[8]),
        lambda: cp(act_s.at[s], gp.at[pl.ds(512 * s, 512)], osem.at[9]),
        lambda: cp(gsl_s, gslow.at[pl.ds(512 * s, 512)], osem.at[10]),
        lambda: cp(gfl_s, gflow.at[pl.ds(512 * s, 512)], osem.at[11]),
        lambda: cp(gf_s, gf.at[pl.ds(512 * s, 512)], osem.at[12]),
        lambda: cp(qkv.at[s, pl.ds(0, 768)], gctx.at[s], osem.at[13]),
    ][n]() for n in only]
    cc.wait()
    total = None
    for s in range(2):
        sl = pl.ds(512 * s, 512)
        n1, inv1 = n1_s[s], inv_s[s]
        acc = n1 * vec[0:1] + vec[6:7] + vec[5:6]
        for ff in range(4):
            acc = acc + dg(act_s[s, :, 768 * ff:768 * ff + 768], d_v[ff], 1, 1)
        n2, inv2 = norm_rows(acc)
        g = cot_s[sl].astype(f32)
        gs = norm_rows_back(g, n2, inv2, vec[1:2])
        rs = lambda v: jnp.sum(v, axis=0, keepdims=True)
        s_gain2, s_cot, s_gs = rs(g * n2), rs(g), rs(gs)
        cot_s[sl] = (n2 * vec[1:2] + vec[7:8]).astype(bf16)
        if s:
            for c in outs(s - 1, (2, 3, 4)): c.wait()
        gsl = gs.astype(bf16)
        gsl_s[...] = gsl
        ac[s].wait()
        gh = gs
        for ff in range(4):
            p = (dg(gsl, d_v[ff], 1, 0) * slope[s, ff].astype(f32)).astype(bf16)
            act_s[s, :, 768 * ff:768 * ff + 768] = p
            b = rs(p.astype(f32))
            cols = slice(768 * ff, 768 * ff + 768)
            gbup[:, cols] = gbup[:, cols] + b if s else b
            gh = gh + dg(p, u_v[ff, :, :768], 1, 1)
        gfirst = norm_rows_back(gh, n1, inv1, vec[0:1])
        gf_s[...] = gfirst
        gfl = gfirst.astype(bf16)
        gfl_s[...] = gfl
        if s == 0:
            oc.wait()
        qkv[s, 0:768, :] = dg(wout[...], gfl, 1, 1).astype(bf16)
        part = jnp.concatenate([rs(gh * n1), s_gain2, jnp.zeros((2, 768), f32), rs(gfirst), s_gs, rs(gh), s_cot], axis=0)
        total = part if total is None else total + part
        if s:
            for c in outs(0, (0, 1, 5)): c.wait()
        for c in outs(s): c.start()
    sums[...] = total
    for c in outs(1): c.wait()
    for c in hc: c.wait()
    for g in (a0, a1, a2, small, up, down, vectors):
        g.finish()


def front_call(*ops):
    any_ = pl.BlockSpec(memory_space=pl.ANY)
    vm = pl.BlockSpec(memory_space=pltpu.VMEM)
    sm = pl.BlockSpec(memory_space=pltpu.SMEM)
    sd = jax.ShapeDtypeStruct
    dma = pltpu.SemaphoreType.DMA
    V = pltpu.VMEM
    tok = sd((1024, 768), bf16)
    wide = sd((1024, 3072), bf16)
    return pl.pallas_call(
        front_kernel,
        out_shape=(
            sd((4, 768, 640), bf16), sd((2, 2304, 512), bf16), sd((2, 768, 512), bf16),
            sd((24, 512, 512), bf16), tok, wide, wide, tok, tok, tok, sd((1024, 768), f32), sd((2, 768, 512), bf16),
            sd((8, 768), f32), sd((1, 3072), f32),
        ),
        in_specs=[vm, vm, vm, vm, any_, vm, vm, vm, vm, sm, sm, any_, any_],
        out_specs=(any_,) * 12 + (vm, vm),
        scratch_shapes=[
            V((4, 768, 640), bf16), V((4, 768, 896), bf16), V((4, 768, 768), bf16), V((4, 1024, 128), bf16), V((4, 128, 128), bf16), V((96, 896), bf16), V((768, 768), bf16),
            V((768, 16), f32), V((2, 512, 512), f32), V((2, FORWARD_HEADS, 512, 512), bf16), V((2, 2304, 512), bf16), V((2, 768, 512), bf16),
            V((1024, 768), bf16), V((1024, 768), bf16), V((2, 4, 512, 768), SLOPE), V((2, 512, 3072), bf16), V((2, 512, 768), f32),
            V((2, 512, 1), f32), V((8, 768), f32), V((1, 3072), f32), V((512, 768), bf16), V((512, 768), f32), V((512, 768), bf16),
            dma((7, 2)), dma((7, 9)), dma((2,)), dma((2,)), dma((4,)), dma((14,)),
        ],
        compiler_params=pltpu.CompilerParams(collective_id=0, has_side_effects=True, vmem_limit_bytes=63 << 20),
        name="gather_attend_feed_forward",
    )(*ops)


SLOPE = f32


def attend_head_back(qkv, gctx, p_ref, dproj, gm, s, h):
    q = qkv[s, pl.ds(h * HD, HD), :]
    k = qkv[s, pl.ds(768 + h * HD, HD), :]
    v = qkv[s, pl.ds(1536 + h * HD, HD), :]
    go = gctx[s, pl.ds(h * HD, HD), :]
    p = p_ref[...]
    dp = dg(v, go, 0, 0)
    pf = p.astype(f32)
    drow = jnp.sum(pf * dp, axis=0, keepdims=True)
    ds = pf * (dp - drow)
    dsl = ds.astype(bf16)
    dproj[s, pl.ds(1536 + h * HD, HD), :] = dg(go, p, 1, 1).astype(bf16)
    dproj[s, pl.ds(768 + h * HD, HD), :] = dg(q, dsl, 1, 1).astype(bf16)
    dproj[s, pl.ds(h * HD, HD), :] = (dg(k, dsl, 1, 0) * 0.125).astype(bf16)
    return ds

def attend_all_back(qkv, gctx, pt, ptbuf, psem, dproj, gm, per, hook):
    steps = 24 // per
    gm[...] = jnp.zeros(gm.shape, f32)
    load = lambda t: pltpu.make_async_copy(
        pt.at[pl.ds(t * per, per)], ptbuf.at[t % 2], psem.at[t % 2]
    )
    def body(t, carry):
        load(t).wait()
        s = t // (12 // per)
        tot = None
        for u in range(per):
            h = (t % (12 // per)) * per + u
            ds = attend_head_back(qkv, gctx, ptbuf.at[t % 2, u], dproj, gm, s, h)
            tot = ds if tot is None else tot + ds
        gm[...] += tot
        @pl.when(t + 2 < steps)
        def _():
            load(t + 2).start()
        hook(t)
        return carry
    lax.fori_loop(0, steps, body, 0)


ORDER = (1, 2, 3, 0)


def small_rows(part, gm, sums, gbup):
    table = gm[...].T
    zero = jnp.zeros((8, 32), f32)
    for f in range(4):
        bias = jnp.concatenate(
            [gbup[:, 768 * f + 128 * r : 768 * f + 128 * r + 128] for r in range(6)] + [jnp.zeros((2, 128), f32)], axis=0
        )
        for i in range(8):
            ref = part.at[f, i // 2, i % 2]
            for j in range(4):
                at = 64 * i + 16 * j
                ref[96:112, 128 * j : 128 * j + 128] = table[at : at + 16, 128 * f : 128 * f + 128].astype(bf16)
            rows = jnp.concatenate([sums[:, 96 * i : 96 * i + 96], zero], axis=1)
            ref[96:112, 512:640] = jnp.concatenate([rows, bias], axis=0).astype(bf16)


def backward_kernel(wfull, qkv_h, pt, gctx_h, ctx_h, act, gp, hlow, gslow, x, gfl_h, gf, sums_in, gbup, gin, oup, odown, oattn,
                    upart, urc, urq, urx, ury, urz, dpart, drc, drq, drx, dry, drz, apart, arc, arq, arx, ary, arz, gm, sums,
                    lhs, chunk, qkv, gctx, ctx, gfl, dproj, ptbuf, gbuf, ssem, rsem, lsem, csem, isem, psem, gsem):
    me = partners()
    cp = pltpu.make_async_copy
    at = [(me[1] + k) % 4 for k in range(4)]
    def chunk_copy(n):
        src = (act, gp)[n // 4].at[:, pl.ds(pl.multiple_of(768 * at[ORDER[n % 4]], 768), 768)]
        return cp(src, chunk.at[n % 2], csem.at[n % 2])
    l0 = cp(gslow, lhs.at[0], lsem.at[0]); l1 = cp(hlow, lhs.at[1], lsem.at[1]); l2 = cp(x, lhs.at[0], lsem.at[0])
    l0.start(); chunk_copy(0).start(); chunk_copy(1).start(); l1.start()
    ins = [cp(a, b, isem.at[n]) for n, (a, b) in enumerate(((ctx_h, ctx), (gfl_h, gfl), (qkv_h, qkv), (gctx_h, gctx)))]
    for c in ins: c.start()
    for t in range(2): cp(pt.at[pl.ds(t * BACKWARD_HEADS, BACKWARD_HEADS)], ptbuf.at[t], psem.at[t]).start()
    up = Scatter(me, upart, (urc, urq, urx, ury, urz), oup, ssem.at[0], rsem.at[0])
    down = Scatter(me, dpart, (drc, drq, drx, dry, drz), odown, ssem.at[1], rsem.at[1])
    attn = Scatter(me, apart, (arc, arq, arx, ary, arz), oattn, ssem.at[2], rsem.at[2])
    before, loop, dots = steps_between(attn, up, down)
    l0.wait()
    for n in range(8):
        g, k = (down, up)[n // 4], ORDER[n % 4]
        if n == 4:
            l2.start()
            for c in ins: c.wait()
            dwo = (dg(ctx[0], gfl[0:512], 1, 0) + dg(ctx[1], gfl[512:1024], 1, 0)).astype(bf16)
            for f in range(4):
                attn.part[f, :, :, 0:96, 576:] = dwo[:, 192 * f:192 * f + 64].reshape(4, 2, 96, 64)
                up.part[f, :, :, :, 768:] = dwo[:, 192 * f + 64:192 * f + 192].reshape(4, 2, 96, 128)
            l1.wait()
        chunk_copy(n).wait()
        g.part[at[k], :, :, :, 0:768] = dg(lhs[n // 4], chunk[n % 2], 0, 0).astype(bf16).reshape(4, 2, 96, 768)
        if n < 6: chunk_copy(n + 2).start()
        if n == 0:
            enter_barrier(me)
        g.c_(k)
        run_steps(before.get(n, ()))
    def hook(t):
        for at_t in sorted(loop):
            pl.when(t == at_t)(functools.partial(run_steps, loop[at_t]))
    attend_all_back(qkv, gctx, pt, ptbuf, psem, dproj, gm, BACKWARD_HEADS, hook)
    ones = jnp.ones((8, 512), bf16)
    sums[...] = sums_in[...]
    sums[2:3] = (dg(ones, dproj[0, 0:768], 1, 1) + dg(ones, dproj[1, 0:768], 1, 1))[0:1]
    sums[3:4] = (dg(ones, dproj[0, 1536:2304], 1, 1) + dg(ones, dproj[1, 1536:2304], 1, 1))[0:1]
    small_rows(attn.part, gm, sums, gbup)
    l2.wait()
    for n, k in enumerate(ORDER):
        r = pl.ds(pl.multiple_of(576 * at[k], 576), 576)
        dw = dg(lhs[0, 0:512], dproj[0, r, :], 0, 1) + dg(lhs[0, 512:1024], dproj[1, r, :], 0, 1)
        attn.part[at[k], :, :, 0:96, :576] = dw.astype(bf16).reshape(4, 2, 96, 576)
        attn.c_(k)
        run_steps(dots.get(n, ()))
    aw = [cp(wfull.at[f], chunk.at[f % 2, pl.ds(0, 768), pl.ds(0, 640)], csem.at[f % 2]) for f in range(4)]
    aw[0].start(); aw[1].start()
    gi = [cp(gf.at[pl.ds(512 * s, 512)], gbuf.at[s], gsem.at[s]) for s in range(2)]
    for c in gi: c.start()
    for f in range(4):
        aw[f].wait()
        if f == 0:
            for c in gi: c.wait()
        for s in range(2):
            gbuf[s] = gbuf[s] + dg(dproj[s, 576 * f:576 * f + 576], chunk[f % 2, 0:768, :576], 0, 1)
            run_steps(dots.get(4 + 2 * f + s, ()))
        if f < 2: aw[f + 2].start()
    go = [cp(gbuf.at[s], gin.at[pl.ds(512 * s, 512)], gsem.at[s]) for s in range(2)]
    for c in go: c.start()
    run_steps(dots.get(12, ()))
    for c in go: c.wait()
    for g in (attn, up, down):
        g.finish()


def steps_between(attn, up, down):
    before = {
        2: [(down.q, 1)],
        3: [(down.q, 2)],
        4: [(down.q, 3), (down.q, 0), (down.t, 1)],
        5: [(down.t, 2)],
        6: [(up.q, 1)],
        7: [(up.q, 2), (down.t, 3)],
    }
    loop = {
        0: [(down.t, 0), (up.q, 3), (up.q, 0)],
        1: [(down.w, 2)],
        2: [(down.w, 1)],
        3: [(up.t, 1), (up.t, 2)],
        5: [(down.w, 0)],
        6: [(up.t, 3), (down.w, 3)],
        7: [(up.t, 0)],
    }
    dots = {
        0: [(down.e,)],
        1: [(up.w, 2)],
        2: [(attn.q, 1), (up.w, 1)],
        3: [(attn.q, 2), (up.w, 0)],
        5: [(attn.q, 3), (up.w, 3)],
        7: [(attn.t, 1)],
        10: [(attn.t, 2)],
        12: [(attn.t, 3), (attn.q, 0), (attn.w, 1), (up.e,), (attn.w, 3), (attn.w, 2), (attn.t, 0), (attn.w, 0), (attn.e,)],
    }
    return before, loop, dots


def run_steps(todo):
    for step, *arg in todo:
        step(*arg)


def backward_call(*ops):
    any_ = pl.BlockSpec(memory_space=pl.ANY); vm = pl.BlockSpec(memory_space=pltpu.VMEM)
    sd = jax.ShapeDtypeStruct
    dma = pltpu.SemaphoreType.DMA
    V = pltpu.VMEM
    return pl.pallas_call(backward_kernel,
        out_shape=(sd((1024, 768), f32), sd((96, 896), f32), sd((96, 768), f32), sd((112, 640), f32)),
        in_specs=[any_] * 12 + [vm] * 2, out_specs=(any_, vm, vm, vm),
        scratch_shapes=scatter_buffers(96, 896) + scatter_buffers(96, 768) + scatter_buffers(112, 640)
            + [V((512, 512), f32), V((8, 768), f32)]
            + [V((2, 1024, 768), bf16), V((2, 1024, 768), bf16), V((2, 2304, 512), bf16), V((2, 768, 512), bf16), V((2, 768, 512), bf16), V((1024, 768), bf16),
            V((2, 2304, 512), bf16), V((2, BACKWARD_HEADS, 512, 512), bf16), V((2, 512, 768), f32), dma((3, 3)), dma((3, 13)), dma((2,)), dma((2,)), dma((4,)), dma((2,)), dma((2,))],
        compiler_params=pltpu.CompilerParams(collective_id=1, has_side_effects=True, vmem_limit_bytes=63 << 20), name="attend_back_and_reduce")(*ops)


def hand_out_kernel(gin, res, gup, gdown, attn_h, gate_h, jitter_h, heat, gin_o, res_o, qkv, out, up, down, bias, gains, shifts, logits,
                    gbuf, rbuf, ubuf, dbuf, attn, gate, jitter, sem):
    cp = pltpu.make_async_copy
    n = 4
    rows = gin.shape[0] // n
    moves = [(a.at[pl.ds(r * rows, rows)], b.at[pl.ds(r * rows, rows)], c.at[pl.ds(r * rows, rows)])
             for r in range(n) for a, b, c in ((gin, gbuf, gin_o), (res, rbuf, res_o))]
    moves += [(gdown, dbuf, down), (gup, ubuf, None)]
    small = [cp(a, b, sem.at[m]) for m, (a, b) in enumerate(((attn_h, attn), (gate_h, gate), (jitter_h, jitter)))]
    ins = [cp(a, b, sem.at[3 + m]) for m, (a, b, c) in enumerate(moves)]
    outs = [cp(b, c, sem.at[13 + m]) for m, (a, b, c) in enumerate(moves[:-1])]
    for c in small + ins: c.start()
    for c in small: c.wait()
    qkv[...] = attn[:96, :576]
    inv = 1.0 / heat[0]
    table = jnp.concatenate([attn[96:112, 128 * j:128 * j + 128] for j in range(4)], axis=0)
    mixed = (gate[...].astype(f32) + jitter[...].astype(f32)) * inv
    logits[...] = table * (inv / (1.0 + jnp.exp(mixed)))
    gains[...] = attn[96:98, 512:608]
    shifts[...] = attn[98:104, 512:608]
    bias[...] = attn[104:110, 512:640]
    for a, b in zip(ins, outs):
        a.wait()
        b.start()
    ins[-1].wait()
    up[...] = ubuf[:, :768]
    out[:, :64] = attn[:96, 576:]
    out[:, 64:] = ubuf[:, 768:]
    for c in outs: c.wait()


def hand_out_call(gin, res, gup, gdown, attn, gate, jitter, heat):
    any_ = pl.BlockSpec(memory_space=pl.ANY); vm = pl.BlockSpec(memory_space=pltpu.VMEM); sm = pl.BlockSpec(memory_space=pltpu.SMEM)
    sd = lambda *s: jax.ShapeDtypeStruct(s, f32)
    V = pltpu.VMEM
    return pl.pallas_call(hand_out_kernel,
        out_shape=(sd(1024, 768), jax.ShapeDtypeStruct((1024, 768), bf16), sd(96, 576), sd(96, 192), sd(96, 768), sd(96, 768), sd(6, 128), sd(2, 96), sd(6, 96), sd(64, 128)),
        in_specs=[any_] * 7 + [sm], out_specs=(any_, any_, vm, vm, vm, any_) + (vm,) * 4,
        scratch_shapes=[V((1024, 768), f32), V((1024, 768), bf16), V((96, 896), f32), V((96, 768), f32), V((112, 640), f32), V((64, 128), bf16), V((64, 128), bf16), pltpu.SemaphoreType.DMA((23,))],
        compiler_params=pltpu.CompilerParams(vmem_limit_bytes=63 << 20), name="hand_out")(gin, res, gup, gdown, attn, gate, jitter, heat)


def own_device(
    layer_activations,
    token_counts_each,
    attention_triple_matrix,
    attention_final_matrix,
    feedfwd_expand_matrix,
    feedfwd_expand_offset,
    feedfwd_contract_matrix,
    layernorm_scales,
    offset_vectors,
    learned_gate_scores,
    fixed_jitter_matrix,
    relaxation_heat,
    loss_grad_result,
):
    x = layer_activations.reshape(1024, D)
    cot = loss_grad_result.reshape(1024, D)
    (
        attn_full, qkv, ctx, probs, result, act, grad_pre, hidden_low, grad_second_low, grad_first_low, grad_first, grad_ctx,
        sums, grad_bias,
    ) = front_call(
        attention_triple_matrix, attention_final_matrix, feedfwd_expand_matrix, feedfwd_expand_offset.reshape(6, 128),
        feedfwd_contract_matrix.T, layernorm_scales, offset_vectors, learned_gate_scores, fixed_jitter_matrix, relaxation_heat,
        token_counts_each, x, cot,
    )
    grad_inputs, up, down, attn = backward_call(
        attn_full, qkv, probs, grad_ctx, ctx, act, grad_pre, hidden_low, grad_second_low, x, grad_first_low, grad_first,
        sums, grad_bias,
    )
    grad_inputs, result, g_qkv, g_out, g_up, g_down, g_bias, g_gains, g_shifts, g_logits = hand_out_call(
        grad_inputs, result, up, down, attn, learned_gate_scores, fixed_jitter_matrix, relaxation_heat
    )
    return (
        result.reshape(layer_activations.shape),
        grad_inputs.reshape(layer_activations.shape),
        g_qkv,
        g_out,
        g_up,
        g_bias.reshape(-1),
        g_down.T,
        g_gains,
        g_shifts,
        g_logits,
    )


def solution(mesh):
    in_specs = (
        P(AXES, None, None),
        P(AXES),
        P("dp", "ffn"),
        P("dp", "ffn"),
        P("dp", "ffn"),
        P("ffn"),
        P("ffn", "dp"),
        P(None, "dp"),
        P(None, "dp"),
        P("dp", "ffn"),
        P("dp", "ffn"),
        P(),
        P(AXES, None, None),
    )
    out_specs = (
        P(AXES, None, None),
        P(AXES, None, None),
        P("dp", "ffn"),
        P("dp", "ffn"),
        P("dp", "ffn"),
        P("ffn"),
        P("ffn", "dp"),
        P(None, "dp"),
        P(None, "dp"),
        P("dp", "ffn"),
    )
    own = (mesh.shape["dp"], mesh.shape["ffn"]) == (8, 4)
    return jax.shard_map(
        own_device if own else general_device, mesh=mesh, in_specs=in_specs, out_specs=out_specs, check_vma=False
    )
```

```python
import functools

import jax
import jax.numpy as jnp
from jax import lax
from jax.experimental import pallas as pl
from jax.experimental.pallas import tpu as pltpu
from jax.sharding import PartitionSpec as P

D = 768
HEADS = 12
HEAD_DIM = 64
SEQ_LEN = 512
AXES = ("dp", "ffn")
norm_eps = 1e-06
f32 = jnp.float32
bf16 = jnp.bfloat16
MESH = pl.DeviceIdType.MESH


def dot_first(left, right):
    return lax.dot_general(left, right, (((0,), (0,)), ((), ())), preferred_element_type=f32)


def dot_last(left, right):
    return lax.dot_general(left, right, (((1,), (1,)), ((), ())), preferred_element_type=f32)


def dot(left, right):
    return jnp.dot(left, right, preferred_element_type=f32)


def layer_norm(values, gain, shift):
    mean_row = jnp.mean(values, axis=-1, keepdims=True)
    centered = values - mean_row
    inv_std = lax.rsqrt(jnp.mean(centered * centered, axis=-1, keepdims=True) + norm_eps)
    normed = centered * inv_std
    return (normed * gain + shift, normed, inv_std)


def norm_back(grad_out, normed, inv_std, gain):
    grad_normed = grad_out * gain
    grad_in = inv_std * (
        grad_normed
        - jnp.mean(grad_normed, axis=-1, keepdims=True)
        - normed * jnp.mean(grad_normed * normed, axis=-1, keepdims=True)
    )
    return (grad_in, jnp.sum(grad_out * normed, axis=0), jnp.sum(grad_out, axis=0))


def gelu_slope(values):
    return (
        0.5 * (1.0 + lax.erf(values * 0.7071067811865476))
        + values * jnp.exp(-0.5 * values * values) * 0.3989422804014327
    )


def score_block(queries, keys_low, natural_log_gate, live):
    scores = (
        jnp.einsum("qhd,khd->hqk", queries, keys_low, preferred_element_type=f32)
        * HEAD_DIM ** (-0.5)
        + natural_log_gate
    )
    return jnp.where(live[None, None, :], scores, -1e30)


def attend(queries, keys_low, values_low, natural_log_gate, live):
    scores = score_block(queries, keys_low, natural_log_gate, live)
    peak = jnp.max(scores, axis=-1, keepdims=True)
    shifted_exp = jnp.exp(scores - peak)
    total_exp = jnp.sum(shifted_exp, axis=-1, keepdims=True)
    probs_low = (shifted_exp / total_exp).astype(bf16)
    context = jnp.einsum("hqk,khd->qhd", probs_low, values_low, preferred_element_type=f32)
    return (context, peak + jnp.log(total_exp))


def attend_back(queries, keys_low, values_low, natural_log_gate, live, log_total, grad_context):
    scores = score_block(queries, keys_low, natural_log_gate, live)
    probs = jnp.exp(scores - log_total)
    grad_probs = jnp.einsum("qhd,khd->hqk", grad_context, values_low, preferred_element_type=f32)
    grad_values = jnp.einsum(
        "hqk,qhd->khd", probs.astype(bf16), grad_context, preferred_element_type=f32
    )
    grad_scores = probs * (grad_probs - jnp.sum(probs * grad_probs, axis=-1, keepdims=True))
    grad_mask = jnp.sum(grad_scores, axis=0)
    grad_scores_low = grad_scores.astype(bf16)
    grad_queries = jnp.einsum(
        "hqk,khd->qhd", grad_scores_low, keys_low, preferred_element_type=f32
    ) * HEAD_DIM ** (-0.5)
    grad_keys = jnp.einsum(
        "hqk,qhd->khd", grad_scores_low, queries, preferred_element_type=f32
    ) * HEAD_DIM ** (-0.5)
    return (grad_queries, grad_keys, grad_values, grad_mask)


def gather_weights(pack, small):
    rows_dp = lax.axis_size("dp")
    cols_ffn = lax.axis_size("ffn")
    full = lax.all_gather(pack[None], AXES, axis=0, tiled=True)
    full = full.reshape(rows_dp, cols_ffn, *pack.shape)
    small_full = lax.all_gather(small[None], AXES, axis=0, tiled=True)
    return full, small_full.reshape(rows_dp, cols_ffn, *small.shape)


def columns(blocks):
    rows_dp, cols_ffn, rows, cols = blocks.shape
    return blocks.transpose(0, 2, 1, 3).reshape(rows_dp * rows, cols_ffn * cols)


def blocks_of(full, rows_dp, cols_ffn):
    rows, cols = full.shape
    return full.reshape(rows_dp, rows // rows_dp, cols_ffn, cols // cols_ffn).transpose(0, 2, 1, 3)


def general_device(
    layer_activations,
    token_counts_each,
    attention_triple_matrix,
    attention_final_matrix,
    feedfwd_expand_matrix,
    feedfwd_expand_offset,
    feedfwd_contract_matrix,
    layernorm_scales,
    offset_vectors,
    learned_gate_scores,
    fixed_jitter_matrix,
    relaxation_heat,
    loss_grad_result,
):
    rows_dp = lax.axis_size("dp")
    cols_ffn = lax.axis_size("ffn")
    seq_count = layer_activations.shape[0]
    row_count = seq_count * SEQ_LEN
    shard_rows = attention_triple_matrix.shape[0]
    qkv_cols = attention_triple_matrix.shape[1]
    out_cols = attention_final_matrix.shape[1]
    ff_cols = feedfwd_expand_matrix.shape[1]

    pack = jnp.concatenate(
        [
            attention_triple_matrix,
            attention_final_matrix,
            feedfwd_expand_matrix,
            feedfwd_contract_matrix.T,
        ],
        axis=1,
    )
    mask_cols = learned_gate_scores.shape[1]
    vectors = jnp.concatenate([layernorm_scales, offset_vectors], axis=0)
    small = jnp.concatenate(
        [
            learned_gate_scores,
            fixed_jitter_matrix,
            jnp.pad(vectors, ((0, 0), (0, mask_cols - vectors.shape[1]))),
            feedfwd_expand_offset.reshape(-1, mask_cols),
        ],
        axis=0,
    )
    full, small_full = gather_weights(pack, small)
    full_qkv = columns(full[..., :qkv_cols])
    full_out = columns(full[..., qkv_cols : qkv_cols + out_cols])
    full_up = columns(full[..., qkv_cols + out_cols : qkv_cols + out_cols + ff_cols])
    full_down_t = columns(full[..., qkv_cols + out_cols + ff_cols :])
    mask_rows = learned_gate_scores.shape[0]
    logits_sum = columns(small_full[:, :, :mask_rows]).astype(f32) + columns(
        small_full[:, :, mask_rows : 2 * mask_rows]
    ).astype(f32)
    natural_log_gate = jax.nn.log_sigmoid(logits_sum / relaxation_heat[0])
    vectors_full = (
        small_full[:, 0, 2 * mask_rows : 2 * mask_rows + 8, :shard_rows]
        .transpose(1, 0, 2)
        .reshape(8, D)
        .astype(f32)
    )
    gains_full = vectors_full[:2]
    shifts_full = vectors_full[2:]
    bias_up = small_full[0, :, 2 * mask_rows + 8 :].reshape(1, -1).astype(f32)

    flat_in = layer_activations.reshape(row_count, D)
    qkv_bias = jnp.concatenate([shifts_full[0], jnp.zeros((D,), f32), shifts_full[1]])
    proj_low = (dot(flat_in, full_qkv) + qkv_bias).astype(bf16)
    head_shape = (seq_count, SEQ_LEN, HEADS, HEAD_DIM)
    queries = proj_low[:, :D].reshape(head_shape)
    keys_low = proj_low[:, D : 2 * D].reshape(head_shape)
    values_low = proj_low[:, 2 * D :].reshape(head_shape)
    live = lax.broadcasted_iota(jnp.int32, (seq_count, SEQ_LEN), 1) < token_counts_each[:, None]
    attended = [
        attend(queries[s], keys_low[s], values_low[s], natural_log_gate, live[s])
        for s in range(seq_count)
    ]
    context_low = jnp.concatenate(
        [item[0].reshape(SEQ_LEN, D).astype(bf16) for item in attended], axis=0
    )
    first_sum = flat_in.astype(f32) + dot(context_low, full_out) + shifts_full[2]
    hidden, normed_one, inv_one = layer_norm(first_sum, gains_full[0], shifts_full[4])
    hidden_low = hidden.astype(bf16)
    pre_act = dot(hidden_low, full_up) + bias_up
    act_low = jax.nn.gelu(pre_act, approximate=False).astype(bf16)
    second_sum = hidden + dot_last(act_low, full_down_t) + shifts_full[3]
    result, normed_two, inv_two = layer_norm(second_sum, gains_full[1], shifts_full[5])
    cot_flat = loss_grad_result.reshape(row_count, D).astype(f32)
    grad_second, grad_gain_two, grad_shift_two = norm_back(
        cot_flat, normed_two, inv_two, gains_full[1]
    )
    grad_second_low = grad_second.astype(bf16)
    grad_w_down_t = dot_first(grad_second_low, act_low)
    grad_act = dot(grad_second_low, full_down_t)
    grad_pre = (grad_act * gelu_slope(pre_act)).astype(bf16)
    grad_bias_up = jnp.sum(grad_pre, axis=0, dtype=f32)
    grad_w_up = dot_first(hidden_low, grad_pre)
    grad_hidden = grad_second + dot_last(grad_pre, full_up)
    grad_first, grad_gain_one, grad_shift_one = norm_back(
        grad_hidden, normed_one, inv_one, gains_full[0]
    )
    grad_first_low = grad_first.astype(bf16)
    grad_w_out = dot_first(context_low, grad_first_low)
    grad_context = dot_last(grad_first_low, full_out).astype(bf16).reshape(head_shape)
    back = [
        attend_back(
            queries[s],
            keys_low[s],
            values_low[s],
            natural_log_gate,
            live[s],
            attended[s][1],
            grad_context[s],
        )
        for s in range(seq_count)
    ]
    grad_mask = sum(item[3] for item in back)
    grad_projected = jnp.concatenate(
        [
            jnp.concatenate(
                [item[part].reshape(SEQ_LEN, D).astype(bf16) for item in back], axis=0
            )
            for part in range(3)
        ],
        axis=1,
    )
    grad_w_qkv = dot_first(flat_in, grad_projected)
    grad_inputs = grad_first + dot_last(grad_projected, full_qkv)
    grad_vectors = jnp.stack(
        [
            grad_gain_one,
            grad_gain_two,
            jnp.sum(grad_projected[:, :D], axis=0, dtype=f32),
            jnp.sum(grad_projected[:, 2 * D :], axis=0, dtype=f32),
            jnp.sum(grad_first, axis=0),
            jnp.sum(grad_second, axis=0),
            grad_shift_one,
            grad_shift_two,
        ]
    )
    big = jnp.concatenate(
        [
            blocks_of(item, rows_dp, cols_ffn)
            for item in (grad_w_qkv, grad_w_out, grad_w_up, grad_w_down_t)
        ],
        axis=-1,
    ).reshape(rows_dp * cols_ffn, shard_rows, -1)
    vector_blocks = jnp.broadcast_to(
        grad_vectors.reshape(8, rows_dp, 1, shard_rows).transpose(1, 2, 0, 3),
        (rows_dp, cols_ffn, 8, shard_rows),
    )
    bias_blocks = jnp.broadcast_to(
        grad_bias_up.reshape(1, cols_ffn, -1, mask_cols),
        (rows_dp, cols_ffn, ff_cols // mask_cols, mask_cols),
    )
    little = jnp.concatenate(
        [
            blocks_of(grad_mask, rows_dp, cols_ffn),
            jnp.pad(vector_blocks, ((0, 0), (0, 0), (0, 0), (0, mask_cols - shard_rows))),
            bias_blocks,
        ],
        axis=2,
    ).reshape(rows_dp * cols_ffn, -1, mask_cols)
    big = lax.psum_scatter(big, AXES, scatter_dimension=0, tiled=True)[0]
    little = lax.psum_scatter(little, AXES, scatter_dimension=0, tiled=True)[0]

    own_mixed = (
        learned_gate_scores.astype(f32) + fixed_jitter_matrix.astype(f32)
    ) / relaxation_heat[0]
    grad_logits = little[:mask_rows] * (jax.nn.sigmoid(-own_mixed) / relaxation_heat[0])
    return (
        result.astype(bf16).reshape(layer_activations.shape),
        grad_inputs.reshape(layer_activations.shape),
        big[:, :qkv_cols],
        big[:, qkv_cols : qkv_cols + out_cols],
        big[:, qkv_cols + out_cols : qkv_cols + out_cols + ff_cols],
        little[mask_rows + 8 :].reshape(-1),
        big[:, qkv_cols + out_cols + ff_cols :].T,
        little[mask_rows : mask_rows + 2, :shard_rows],
        little[mask_rows + 2 : mask_rows + 8, :shard_rows],
        grad_logits,
    )


def partners():
    i = lax.axis_index("dp")
    f = lax.axis_index("ffn")
    core = i + 1 - 2 * (i % 2)
    ix = i + 2 - 4 * ((i // 2) % 2)
    iy = (i + 4) % 8
    idg = (ix + 4) % 8
    return i, f, core, ix, iy, idg


def enter_barrier(me):
    i, f, core, ix, iy, idg = me
    sem = pltpu.get_barrier_semaphore()
    mates = [(i, (f + k) % 4) for k in (1, 2, 3)] + [(core, f), (ix, f), (iy, f)]
    for to in mates:
        pl.semaphore_signal(sem, inc=1, device_id=to, device_id_type=MESH)
    pl.semaphore_wait(sem, len(mates))


class Exchange:
    def __init__(self, me, ssem, rsem):
        self.me, self.ssem, self.rsem = me, ssem, rsem

    def copy(self, src, dst, send, recv, to):
        return pltpu.make_async_remote_copy(
            src_ref=src,
            dst_ref=dst,
            send_sem=self.ssem.at[send],
            recv_sem=self.rsem.at[recv],
            device_id=to,
            device_id_type=MESH,
        )

    def send(self, src, dst, send, recv, to):
        self.copy(src, dst, send, recv, to).start()

    def recv(self, ref, n):
        self.copy(ref, ref, 0, n, (self.me[0], self.me[1])).wait_recv()

    def sent(self, ref, n):
        self.copy(ref, ref, n, 0, (self.me[0], self.me[1])).wait_send()


class Gather(Exchange):
    def __init__(self, me, dst, ssem, rsem, rows, stride, offset=0, src=None, lsem=None):
        super().__init__(me, ssem, rsem)
        self.dst, self.rows, self.stride, self.offset, self.lsem = dst, rows, stride, offset, lsem
        self.src = src

    def span(self, i):
        return pl.ds(pl.multiple_of(i * self.stride + self.offset, 16), self.rows)

    def piece(self, i, p):
        return self.dst.at[p, self.span(i)]

    def block(self, i):
        return self.dst.at[:, self.span(i)]

    def own(self):
        return self.piece(self.me[0], self.me[1]) if self.src is None else self.src

    def local(self):
        i, f = self.me[:2]
        return pltpu.make_async_copy(self.src, self.piece(i, f), self.lsem)

    def sz(self, _):
        i, f, core, ix, iy, idg = self.me
        if self.src is not None:
            self.local().start()
        for k in (1, 2, 3):
            self.send(self.own(), self.piece(i, f), 0, 3 - k, (i, (f + k) % 4))

    def sp(self, _):
        i, f, core, ix, iy, idg = self.me
        self.send(self.own(), self.piece(i, f), 1, 3, (ix, f))
        self.send(self.own(), self.piece(i, f), 1, 3, (iy, f))

    def z(self, k):
        i, f, core, ix, iy, idg = self.me
        ref = self.piece(i, (f + k) % 4)
        self.recv(ref, k - 1)
        self.send(ref, ref, 1, 3 + k, (ix, f))
        self.send(ref, ref, 1, 3 + k, (iy, f))

    def o(self, _):
        i, f, core, ix, iy, idg = self.me
        if self.src is not None:
            self.local().wait()
        self.send(self.block(i), self.block(i), 1, 8, (core, f))

    def d(self, k):
        i, f, core, ix, iy, idg = self.me
        p = (f + k) % 4
        rx, ry = self.piece(ix, p), self.piece(iy, p)
        self.recv(self.bytes_of(2, 1), 3 + k)
        if k % 2:
            self.send(rx, rx, 1, 7, (iy, f))
        else:
            self.send(ry, ry, 1, 7, (ix, f))

    def b(self, _):
        i, f, core, ix, iy, idg = self.me
        self.send(self.block(ix), self.block(ix), 1, 8, (core, f))
        self.send(self.block(iy), self.block(iy), 1, 8, (core, f))

    def h(self, _):
        i, f, core, ix, iy, idg = self.me
        self.recv(self.bytes_of(4, 1), 7)
        self.send(self.block(idg), self.block(idg), 1, 8, (core, f))

    def r(self, _):
        self.recv(self.bytes_of(4, 4), 8)

    def bytes_of(self, n, m):
        return self.dst.at[pl.ds(0, n), pl.ds(0, m * self.rows)]

    def finish(self):
        self.sent(self.bytes_of(3, 1), 0)
        self.sent(self.bytes_of(4, 7), 1)


class Scatter(Exchange):
    def __init__(self, me, part, got, out, ssem, rsem):
        super().__init__(me, ssem, rsem)
        self.part, self.out = part, out
        self.rc, self.rq, self.rx, self.ry, self.rz = got
        i = me[0]
        self.c = i % 2
        self.xy = i // 2
        self.xyx = self.xy + 1 - 2 * (self.xy % 2)
        self.xyy = (self.xy + 2) % 4
        self.xyd = (self.xyx + 2) % 4

    def at(self, k):
        return (self.me[1] + k) % 4

    def piece(self, k, xy):
        return self.part.at[self.at(k), xy, self.c]

    def finish(self):
        self.sent(self.rc, 0)
        self.sent(self.rc.at[pl.ds(0, 3)], 1)
        self.sent(self.rz, 2)

    def add(self, ref, *refs):
        if len(refs) == 1:
            ref[...] = ref[...] + refs[0][...]
            return
        total = ref[...].astype(f32)
        for other in refs:
            total = total + other[...].astype(f32)
        ref[...] = total.astype(ref.dtype)

    def c_(self, k):
        self.send(self.part.at[self.at(k), :, 1 - self.c], self.rc.at[k], 0, k, (self.me[2], self.me[1]))

    def q(self, k):
        i, f, core, ix, iy, idg = self.me
        self.recv(self.rc.at[k], k)
        ref = self.piece(k, self.xyd)
        self.add(ref, self.rc.at[k, self.xyd])
        self.send(ref, self.rq.at[k], 1, 4 + k, (iy if k % 2 else ix, f))
        refx, refy = self.piece(k, self.xyx), self.piece(k, self.xyy)
        if k % 2:
            self.add(refy, self.rc.at[k, self.xyy])
            self.send(refy, self.ry.at[k], 1, 8 + k, (iy, f))
            self.add(refx, self.rc.at[k, self.xyx])
        else:
            self.add(refx, self.rc.at[k, self.xyx])
            self.send(refx, self.rx.at[k], 1, 8 + k, (ix, f))
            self.add(refy, self.rc.at[k, self.xyy])
        self.add(self.piece(k, self.xy), self.rc.at[k, self.xy])

    def t(self, k):
        i, f, core, ix, iy, idg = self.me
        self.recv(self.rq.at[k], 4 + k)
        ref = self.piece(k, self.xyx if k % 2 else self.xyy)
        self.add(ref, self.rq.at[k])
        if k % 2:
            self.send(ref, self.rx.at[k], 1, 8 + k, (ix, f))
        else:
            self.send(ref, self.ry.at[k], 1, 8 + k, (iy, f))

    def w(self, k):
        i, f, core, ix, iy, idg = self.me
        self.recv(self.rx.at[pl.ds(0, 2)], 8 + k)
        ref = self.piece(k, self.xy)
        if k:
            self.add(ref, self.rx.at[k], self.ry.at[k])
            self.send(ref, self.rz.at[3 - k], 2, 12, (i, (f + k) % 4))
        else:
            self.out[...] = ref[...].astype(f32) + self.rx[k].astype(f32) + self.ry[k].astype(f32)

    def e(self):
        total = self.out[...]
        self.recv(self.rz, 12)
        for k in range(3):
            total = total + self.rz[k].astype(f32)
        self.out[...] = total


def scatter_buffers(rows, cols):
    return [
        pltpu.VMEM(shape, bf16)
        for shape in ((4, 4, 2, rows, cols), (4, 4, rows, cols)) + ((4, rows, cols),) * 3 + ((3, rows, cols),)
    ]


HD=64
def dg(a,b,ca,cb): return lax.dot_general(a,b,(((ca,),(cb,)),((),())),preferred_element_type=f32)

def log_sigmoid(z):
    return jnp.minimum(z, 0.0) - jnp.log1p(jnp.exp(-jnp.abs(z)))

def prepare_mask(s_v, lens, heat, msk, mrows, srows):
    inv = 1.0 / heat[0]
    n = srows
    rows = []
    for i in range(8):
        row = []
        for f in range(4):
            a = s_v[f, pl.ds(i * n, mrows), :].astype(f32) + s_v[f, pl.ds(i * n + mrows, mrows), :].astype(f32)
            row.append(log_sigmoid(a * inv))
        rows.append(jnp.concatenate(row, axis=1))
    lmt = jnp.concatenate(rows, axis=0).T
    key = lax.broadcasted_iota(jnp.int32, lmt.shape, 0)
    for s in range(msk.shape[0]):
        msk[s] = jnp.where(key < lens[s], lmt, -1e30)

def prepare_columns(v_v, col, cols):
    for i in range(8):
        v = v_v[0, pl.ds(i * 16, 16), :].astype(f32)
        col[pl.ds(i * cols, cols), :] = v.T[:cols, :]

def project(f, s, a_v, x, col, qkv):
    acc = dg(a_v[f, :, :576], x[s * 512:(s + 1) * 512, :], 0, 1)
    lo = 0
    while lo < 576:
        g = 576 * f + lo
        kind = g // 768
        hi = min(576, (kind + 1) * 768 - 576 * f)
        part = acc[lo:hi]
        b = g - kind * 768
        if kind == 0:
            part = (part + col[b:b + hi - lo, 2:3]) * 0.125
        elif kind == 2:
            part = part + col[b:b + hi - lo, 3:4]
        qkv[s, g:g + hi - lo, :] = part.astype(bf16)
        lo = hi


def attend_head(qkv, msk, ctx, ptbuf, slot, s, h):
    q = qkv[s, pl.ds(h * HD, HD), :]
    k = qkv[s, pl.ds(768 + h * HD, HD), :]
    v = qkv[s, pl.ds(1536 + h * HD, HD), :]
    st = dg(k, q, 0, 0) + msk[s]
    e = jnp.exp(st - jnp.max(st, axis=0, keepdims=True))
    p = (e * (1.0 / jnp.sum(e, axis=0, keepdims=True))).astype(bf16)
    ptbuf[slot] = p
    ctx[s, pl.ds(h * HD, HD), :] = dg(v, p, 1, 0).astype(bf16)

def attend_all(qkv, msk, ctx, pt, ptbuf, psem, per, hook):
    steps = 24 // per
    out = lambda t: pltpu.make_async_copy(
        ptbuf.at[t % 2], pt.at[pl.ds(t * per, per)], psem.at[t % 2]
    )
    def body(t, carry):
        @pl.when(t >= 2)
        def _():
            out(t - 2).wait()
        s = t // (12 // per)
        for u in range(per):
            h = (t % (12 // per)) * per + u
            attend_head(qkv, msk, ctx, ptbuf.at[t % 2], u, s, h)
        out(t).start()
        hook(t)
        return carry
    lax.fori_loop(0, steps, body, 0)
    for t in (steps - 2, steps - 1):
        out(t).wait()


FORWARD_HEADS = 4
BACKWARD_HEADS = 3


def norm_rows(v):
    mean = jnp.mean(v, axis=-1, keepdims=True)
    c = v - mean
    inv = lax.rsqrt(jnp.mean(c * c, axis=-1, keepdims=True) + 1e-6)
    return c * inv, inv

def norm_rows_back(g, normed, inv, gain):
    e = g * gain
    return inv * (e - jnp.mean(e, axis=-1, keepdims=True) - normed * jnp.mean(e * normed, axis=-1, keepdims=True))

def gather_steps(vec, a0, a1, a2, small, up, down):
    return {
        'first': [(vec.sz, 0), (a0.sz, 0), (small.sz, 0), (a1.sz, 0), (a2.sz, 0), (vec.sp, 0), (a0.sp, 0), (small.sp, 0), (a1.sp, 0), (a2.sp, 0), (vec.z, 1), (vec.z, 2), (vec.z, 3), (vec.o, 0), (vec.d, 0), (a0.d, 0), (a0.z, 1), (small.d, 0), (a0.z, 2), (a1.d, 0), (a0.z, 3), (a0.o, 0), (a2.d, 0), (vec.d, 1), (vec.d, 2), (vec.d, 3), (vec.b, 0), (small.z, 1), (small.z, 2), (a0.d, 1), (small.z, 3), (small.o, 0), (a0.d, 2), (a1.z, 1), (a1.z, 2), (a0.d, 3), (a0.b, 0), (a1.z, 3), (a1.o, 0), (vec.h, 0), (small.d, 1), (a2.z, 1), (small.d, 2), (vec.r, 0), (small.d, 3), (small.b, 0), (a2.z, 2), (a0.h, 0), (a2.z, 3), (up.sz, 0), (up.sp, 0), (a2.o, 0), (a1.d, 1), (a1.d, 2), (a0.r, 0), (a1.d, 3), (a1.b, 0), (a2.d, 1), (small.h, 0), (a2.d, 2), (a2.d, 3), (a2.b, 0), (small.r, 0), (up.z, 1), (up.d, 0), (a1.h, 0), (a2.h, 0), (up.z, 2), (a1.r, 0), (a2.r, 0)],
        'P3': [(up.d, 1)],
        'P5': [(up.z, 3), (up.o, 0)],
        'P6': [(down.sz, 0)],
        0: [(up.d, 2), (down.z, 1)],
        1: [(up.d, 3), (up.b, 0)],
        2: [(down.sp, 0), (down.z, 2)],
        3: [(down.z, 3), (down.o, 0)],
        4: [(up.h, 0), (down.d, 1)],
        5: [(down.d, 0)],
        'UP': [(up.r, 0)],
        'O0': [(down.d, 2)],
        'F01': [(down.d, 3), (down.b, 0)],
        'F11': [(down.h, 0)],
        'LAST': [(down.r, 0)],
    }


def front_kernel(triple, final, expand, bup_in, contract, scales, offsets, gate, jitter, heat, lens, x, cot,
                 wa, qkv_o, ctx_o, pt, out, act, gp, hlow, gslow, gflow, gf, gctx, sums, gbup,
                 a_v, u_v, d_v, s_v, v_v, usrc, wout, col, msk, ptbuf, qkv, ctx, x_s, cot_s, slope, act_s, n1_s, inv_s, vec, bup,
                 gsl_s, gf_s, gfl_s, ssem, rsem, lsem, psem, isem, osem):
    me = partners()
    i, f = me[0], me[1]
    cp = pltpu.make_async_copy
    xc = cp(x, x_s, isem.at[0]); xc.start()
    cc = cp(cot, cot_s, isem.at[1]); cc.start()
    rows = pl.ds(pl.multiple_of(96 * i, 96), 96)
    a_v[f, rows, :576] = triple[...]
    a_v[f, rows, 576:640] = final[:, :64]
    usrc[:, :768] = expand[...]
    usrc[:, 768:] = final[:, 64:]
    at = lambda o, n: pl.ds(pl.multiple_of(o, 16), n)
    s_v[f, at(128 * i, 64), :] = gate[...]
    s_v[f, at(128 * i + 64, 64), :] = jitter[...]
    vectors = jnp.concatenate([scales[...].astype(f32), offsets[...].astype(f32)], axis=0)
    bias = bup_in[...].astype(f32)
    v_v[f, at(16 * i, 16), :] = jnp.concatenate(
        [jnp.concatenate([vectors, jnp.zeros((8, 32), f32)], axis=1)]
        + [bias, jnp.zeros((2, 128), f32)], axis=0
    ).astype(bf16)
    enter_barrier(me)
    attn_v = a_v
    a0, a1, a2 = [Gather(me, attn_v, ssem.at[n], rsem.at[n], 32, 96, 32 * n) for n in range(3)]
    small = Gather(me, s_v, ssem.at[6], rsem.at[6], 128, 128)
    vectors = Gather(me, v_v, ssem.at[5], rsem.at[5], 16, 16)
    up = Gather(me, u_v, ssem.at[3], rsem.at[3], 96, 96, 0, usrc, lsem.at[0])
    down = Gather(me, d_v, ssem.at[4], rsem.at[4], 96, 96, 0, contract, lsem.at[1])
    steps = gather_steps(vectors, a0, a1, a2, small, up, down)
    after = lambda name: run_steps(steps.get(name, ()))
    after("first")
    wac = cp(attn_v, wa, osem.at[0]); wac.start()
    prepare_columns(v_v, col, 96)
    xc.wait()
    for ff in range(4):
        for s in range(2):
            project(ff, s, a_v, x_s, col, qkv)
            after("P%d" % (2 * ff + s))
    after("W")
    prepare_mask(s_v, lens, heat, msk, 64, 128)
    for n in range(8):
        vec[:, 96 * n : 96 * n + 96] = v_v[0, 16 * n : 16 * n + 16, :].astype(f32)[0:8, :96]
    for ff in range(4):
        tail = v_v[ff, 0:16, :].astype(f32)
        for r in range(6):
            bup[:, 768 * ff + 128 * r : 768 * ff + 128 * r + 128] = tail[8 + r : 9 + r]
    def hook(t):
        for n in range(24 // FORWARD_HEADS):
            if steps.get(n):
                pl.when(t == n)(functools.partial(run_steps, steps[n]))
    qc = [cp(qkv.at[s], qkv_o.at[s], osem.at[1 + s]) for s in range(2)]
    for c in qc: c.start()
    attend_all(qkv, msk, ctx, pt, ptbuf, psem, FORWARD_HEADS, hook)
    oc = cp(ctx, ctx_o, osem.at[3]); oc.start()
    after("UP")
    for ff in range(4):
        wout[:, 192 * ff:192 * ff + 64] = a_v[ff, :, 576:640]
        wout[:, 192 * ff + 64:192 * ff + 192] = u_v[ff, :, 768:896]
    ac = [cp(act_s.at[s], act.at[pl.ds(512 * s, 512)], osem.at[4 + s]) for s in range(2)]
    hc = [cp(x_s.at[pl.ds(512 * s, 512)], hlow.at[pl.ds(512 * s, 512)], osem.at[6 + s]) for s in range(2)]
    for s in range(2):
        sl = pl.ds(512 * s, 512)
        first = x_s[sl].astype(f32) + dg(ctx[s], wout[...], 0, 0) + vec[4:5]
        n1, inv1 = norm_rows(first)
        n1_s[s] = n1
        inv_s[s] = inv1
        hl = (n1 * vec[0:1] + vec[6:7]).astype(bf16)
        x_s[sl] = hl
        hc[s].start()
        after("O%d" % s)
        for ff in range(4):
            pre = dg(x_s[sl], u_v[ff, :, :768], 1, 0) + bup[:, 768 * ff:768 * ff + 768]
            phi = 0.5 * (1.0 + lax.erf(pre * 0.7071067811865476))
            slope[s, ff] = (phi + pre * (jnp.exp(-0.5 * pre * pre) * 0.3989422804014327)).astype(SLOPE)
            act_s[s, :, 768 * ff:768 * ff + 768] = (pre * phi).astype(bf16)
            after("F%d%d" % (s, ff))
        ac[s].start()
    after("LAST")
    wac.wait()
    for c in qc: c.wait()
    outs = lambda s, only=range(6): [[
        lambda: cp(cot_s.at[pl.ds(512 * s, 512)], out.at[pl.ds(512 * s, 512)], osem.at[8]),
        lambda: cp(act_s.at[s], gp.at[pl.ds(512 * s, 512)], osem.at[9]),
        lambda: cp(gsl_s, gslow.at[pl.ds(512 * s, 512)], osem.at[10]),
        lambda: cp(gfl_s, gflow.at[pl.ds(512 * s, 512)], osem.at[11]),
        lambda: cp(gf_s, gf.at[pl.ds(512 * s, 512)], osem.at[12]),
        lambda: cp(qkv.at[s, pl.ds(0, 768)], gctx.at[s], osem.at[13]),
    ][n]() for n in only]
    cc.wait()
    total = None
    for s in range(2):
        sl = pl.ds(512 * s, 512)
        n1, inv1 = n1_s[s], inv_s[s]
        acc = n1 * vec[0:1] + vec[6:7] + vec[5:6]
        for ff in range(4):
            acc = acc + dg(act_s[s, :, 768 * ff:768 * ff + 768], d_v[ff], 1, 1)
        n2, inv2 = norm_rows(acc)
        g = cot_s[sl].astype(f32)
        gs = norm_rows_back(g, n2, inv2, vec[1:2])
        rs = lambda v: jnp.sum(v, axis=0, keepdims=True)
        s_gain2, s_cot, s_gs = rs(g * n2), rs(g), rs(gs)
        cot_s[sl] = (n2 * vec[1:2] + vec[7:8]).astype(bf16)
        if s:
            for c in outs(0, (0, 1, 5)): c.wait()
        for c in outs(s, (0,)): c.start()
        if s:
            for c in outs(s - 1, (2, 3, 4)): c.wait()
        gsl = gs.astype(bf16)
        gsl_s[...] = gsl
        for c in outs(s, (2,)): c.start()
        ac[s].wait()
        gh = gs
        for ff in range(4):
            p = (dg(gsl, d_v[ff], 1, 0) * slope[s, ff].astype(f32)).astype(bf16)
            act_s[s, :, 768 * ff:768 * ff + 768] = p
            cols = pl.ds(768 * ff, 768)
            cp(act_s.at[s, :, cols], gp.at[pl.ds(512 * s, 512), cols], osem.at[9]).start()
            b = rs(p.astype(f32))
            cols = slice(768 * ff, 768 * ff + 768)
            gbup[:, cols] = gbup[:, cols] + b if s else b
            gh = gh + dg(p, u_v[ff, :, :768], 1, 1)
        gfirst = norm_rows_back(gh, n1, inv1, vec[0:1])
        gf_s[...] = gfirst
        gfl = gfirst.astype(bf16)
        gfl_s[...] = gfl
        if s == 0:
            oc.wait()
        qkv[s, 0:768, :] = dg(wout[...], gfl, 1, 1).astype(bf16)
        part = jnp.concatenate([rs(gh * n1), s_gain2, jnp.zeros((2, 768), f32), rs(gfirst), s_gs, rs(gh), s_cot], axis=0)
        total = part if total is None else total + part
        for c in outs(s, (3, 4, 5)): c.start()
    sums[...] = total
    for c in outs(1): c.wait()
    for c in hc: c.wait()
    for g in (a0, a1, a2, small, up, down, vectors):
        g.finish()


def front_call(*ops):
    any_ = pl.BlockSpec(memory_space=pl.ANY)
    vm = pl.BlockSpec(memory_space=pltpu.VMEM)
    sm = pl.BlockSpec(memory_space=pltpu.SMEM)
    sd = jax.ShapeDtypeStruct
    dma = pltpu.SemaphoreType.DMA
    V = pltpu.VMEM
    tok = sd((1024, 768), bf16)
    wide = sd((1024, 3072), bf16)
    return pl.pallas_call(
        front_kernel,
        out_shape=(
            sd((4, 768, 640), bf16), sd((2, 2304, 512), bf16), sd((2, 768, 512), bf16),
            sd((24, 512, 512), bf16), tok, wide, wide, tok, tok, tok, sd((1024, 768), f32), sd((2, 768, 512), bf16),
            sd((8, 768), f32), sd((1, 3072), f32),
        ),
        in_specs=[vm, vm, vm, vm, any_, vm, vm, vm, vm, sm, sm, any_, any_],
        out_specs=(any_,) * 12 + (vm, vm),
        scratch_shapes=[
            V((4, 768, 640), bf16), V((4, 768, 896), bf16), V((4, 768, 768), bf16), V((4, 1024, 128), bf16), V((4, 128, 128), bf16), V((96, 896), bf16), V((768, 768), bf16),
            V((768, 16), f32), V((2, 512, 512), f32), V((2, FORWARD_HEADS, 512, 512), bf16), V((2, 2304, 512), bf16), V((2, 768, 512), bf16),
            V((1024, 768), bf16), V((1024, 768), bf16), V((2, 4, 512, 768), SLOPE), V((2, 512, 3072), bf16), V((2, 512, 768), f32),
            V((2, 512, 1), f32), V((8, 768), f32), V((1, 3072), f32), V((512, 768), bf16), V((512, 768), f32), V((512, 768), bf16),
            dma((7, 2)), dma((7, 9)), dma((2,)), dma((2,)), dma((4,)), dma((14,)),
        ],
        compiler_params=pltpu.CompilerParams(collective_id=0, has_side_effects=True, vmem_limit_bytes=63 << 20),
        name="gather_attend_feed_forward",
    )(*ops)


SLOPE = f32


def attend_head_back(qkv, gctx, p_ref, dproj, gm, s, h):
    q = qkv[s, pl.ds(h * HD, HD), :]
    k = qkv[s, pl.ds(768 + h * HD, HD), :]
    v = qkv[s, pl.ds(1536 + h * HD, HD), :]
    go = gctx[s, pl.ds(h * HD, HD), :]
    p = p_ref[...]
    dp = dg(v, go, 0, 0)
    pf = p.astype(f32)
    drow = jnp.sum(pf * dp, axis=0, keepdims=True)
    ds = pf * (dp - drow)
    dsl = ds.astype(bf16)
    dproj[s, pl.ds(1536 + h * HD, HD), :] = dg(go, p, 1, 1).astype(bf16)
    dproj[s, pl.ds(768 + h * HD, HD), :] = dg(q, dsl, 1, 1).astype(bf16)
    dproj[s, pl.ds(h * HD, HD), :] = (dg(k, dsl, 1, 0) * 0.125).astype(bf16)
    return ds

def attend_all_back(qkv, gctx, pt, ptbuf, psem, dproj, gm, per, hook):
    steps = 24 // per
    gm[...] = jnp.zeros(gm.shape, f32)
    load = lambda t: pltpu.make_async_copy(
        pt.at[pl.ds(t * per, per)], ptbuf.at[t % 2], psem.at[t % 2]
    )
    def body(t, carry):
        load(t).wait()
        s = t // (12 // per)
        tot = None
        for u in range(per):
            h = (t % (12 // per)) * per + u
            ds = attend_head_back(qkv, gctx, ptbuf.at[t % 2, u], dproj, gm, s, h)
            tot = ds if tot is None else tot + ds
        gm[...] += tot
        @pl.when(t + 2 < steps)
        def _():
            load(t + 2).start()
        hook(t)
        return carry
    lax.fori_loop(0, steps, body, 0)


ORDER = (1, 2, 3, 0)


def small_rows(part, gm, sums, gbup):
    table = gm[...].T
    zero = jnp.zeros((8, 32), f32)
    for f in range(4):
        bias = jnp.concatenate(
            [gbup[:, 768 * f + 128 * r : 768 * f + 128 * r + 128] for r in range(6)] + [jnp.zeros((2, 128), f32)], axis=0
        )
        for i in range(8):
            ref = part.at[f, i // 2, i % 2]
            for j in range(4):
                at = 64 * i + 16 * j
                ref[96:112, 128 * j : 128 * j + 128] = table[at : at + 16, 128 * f : 128 * f + 128].astype(bf16)
            rows = jnp.concatenate([sums[:, 96 * i : 96 * i + 96], zero], axis=1)
            ref[96:112, 512:640] = jnp.concatenate([rows, bias], axis=0).astype(bf16)


def backward_kernel(wfull, qkv_h, pt, gctx_h, ctx_h, act, gp, hlow, gslow, x, gfl_h, gf, sums_in, gbup, gin, oup, odown, oattn,
                    upart, urc, urq, urx, ury, urz, dpart, drc, drq, drx, dry, drz, apart, arc, arq, arx, ary, arz, gm, sums,
                    lhs, chunk, qkv, gctx, ctx, gfl, dproj, ptbuf, gbuf, ssem, rsem, lsem, csem, isem, psem, gsem):
    me = partners()
    cp = pltpu.make_async_copy
    at = [(me[1] + k) % 4 for k in range(4)]
    def chunk_copy(n):
        src = (act, gp)[n // 4].at[:, pl.ds(pl.multiple_of(768 * at[ORDER[n % 4]], 768), 768)]
        return cp(src, chunk.at[n % 2], csem.at[n % 2])
    l0 = cp(gslow, lhs.at[0], lsem.at[0]); l1 = cp(hlow, lhs.at[1], lsem.at[1]); l2 = cp(x, lhs.at[0], lsem.at[0])
    l0.start(); chunk_copy(0).start(); chunk_copy(1).start(); l1.start()
    ins = [cp(a, b, isem.at[n]) for n, (a, b) in enumerate(((ctx_h, ctx), (gfl_h, gfl), (qkv_h, qkv), (gctx_h, gctx)))]
    for c in ins: c.start()
    for t in range(2): cp(pt.at[pl.ds(t * BACKWARD_HEADS, BACKWARD_HEADS)], ptbuf.at[t], psem.at[t]).start()
    up = Scatter(me, upart, (urc, urq, urx, ury, urz), oup, ssem.at[0], rsem.at[0])
    down = Scatter(me, dpart, (drc, drq, drx, dry, drz), odown, ssem.at[1], rsem.at[1])
    attn = Scatter(me, apart, (arc, arq, arx, ary, arz), oattn, ssem.at[2], rsem.at[2])
    before, loop, dots = steps_between(attn, up, down)
    l0.wait()
    for n in range(8):
        g, k = (down, up)[n // 4], ORDER[n % 4]
        if n == 4:
            l2.start()
            for c in ins: c.wait()
            dwo = (dg(ctx[0], gfl[0:512], 1, 0) + dg(ctx[1], gfl[512:1024], 1, 0)).astype(bf16)
            for f in range(4):
                attn.part[f, :, :, 0:96, 576:] = dwo[:, 192 * f:192 * f + 64].reshape(4, 2, 96, 64)
                up.part[f, :, :, :, 768:] = dwo[:, 192 * f + 64:192 * f + 192].reshape(4, 2, 96, 128)
            l1.wait()
        chunk_copy(n).wait()
        g.part[at[k], :, :, :, 0:768] = dg(lhs[n // 4], chunk[n % 2], 0, 0).astype(bf16).reshape(4, 2, 96, 768)
        if n < 6: chunk_copy(n + 2).start()
        if n == 0:
            enter_barrier(me)
        g.c_(k)
        run_steps(before.get(n, ()))
    def hook(t):
        for at_t in sorted(loop):
            pl.when(t == at_t)(functools.partial(run_steps, loop[at_t]))
    attend_all_back(qkv, gctx, pt, ptbuf, psem, dproj, gm, BACKWARD_HEADS, hook)
    ones = jnp.ones((8, 512), bf16)
    sums[...] = sums_in[...]
    sums[2:3] = (dg(ones, dproj[0, 0:768], 1, 1) + dg(ones, dproj[1, 0:768], 1, 1))[0:1]
    sums[3:4] = (dg(ones, dproj[0, 1536:2304], 1, 1) + dg(ones, dproj[1, 1536:2304], 1, 1))[0:1]
    small_rows(attn.part, gm, sums, gbup)
    l2.wait()
    for n, k in enumerate(ORDER):
        r = pl.ds(pl.multiple_of(576 * at[k], 576), 576)
        dw = dg(lhs[0, 0:512], dproj[0, r, :], 0, 1) + dg(lhs[0, 512:1024], dproj[1, r, :], 0, 1)
        attn.part[at[k], :, :, 0:96, :576] = dw.astype(bf16).reshape(4, 2, 96, 576)
        attn.c_(k)
        run_steps(dots.get(n, ()))
    aw = [cp(wfull.at[f], chunk.at[f % 2, pl.ds(0, 768), pl.ds(0, 640)], csem.at[f % 2]) for f in range(4)]
    aw[0].start(); aw[1].start()
    gi = [cp(gf.at[pl.ds(512 * s, 512)], gbuf.at[s], gsem.at[s]) for s in range(2)]
    for c in gi: c.start()
    for f in range(4):
        aw[f].wait()
        if f == 0:
            for c in gi: c.wait()
        for s in range(2):
            gbuf[s] = gbuf[s] + dg(dproj[s, 576 * f:576 * f + 576], chunk[f % 2, 0:768, :576], 0, 1)
            run_steps(dots.get(4 + 2 * f + s, ()))
        if f < 2: aw[f + 2].start()
    go = [cp(gbuf.at[s], gin.at[pl.ds(512 * s, 512)], gsem.at[s]) for s in range(2)]
    for c in go: c.start()
    run_steps(dots.get(12, ()))
    for c in go: c.wait()
    for g in (attn, up, down):
        g.finish()


def steps_between(attn, up, down):
    before = {
        2: [(down.q, 1)],
        3: [(down.q, 2)],
        4: [(down.q, 3), (down.q, 0), (down.t, 1)],
        5: [(down.t, 2)],
        6: [(up.q, 1)],
        7: [(up.q, 2), (down.t, 3)],
    }
    loop = {
        0: [(down.t, 0), (up.q, 3), (up.q, 0)],
        1: [(down.w, 2)],
        2: [(down.w, 1)],
        3: [(up.t, 1), (up.t, 2)],
        5: [(down.w, 0)],
        6: [(up.t, 3), (down.w, 3)],
        7: [(up.t, 0)],
    }
    dots = {
        0: [(down.e,)],
        1: [(up.w, 2)],
        2: [(attn.q, 1), (up.w, 1)],
        3: [(attn.q, 2), (up.w, 0)],
        5: [(attn.q, 3), (up.w, 3)],
        7: [(attn.t, 1)],
        10: [(attn.t, 2)],
        12: [(attn.t, 3), (attn.q, 0), (attn.w, 1), (up.e,), (attn.w, 3), (attn.w, 2), (attn.t, 0), (attn.w, 0), (attn.e,)],
    }
    return before, loop, dots


def run_steps(todo):
    for step, *arg in todo:
        step(*arg)


def backward_call(*ops):
    any_ = pl.BlockSpec(memory_space=pl.ANY); vm = pl.BlockSpec(memory_space=pltpu.VMEM)
    sd = jax.ShapeDtypeStruct
    dma = pltpu.SemaphoreType.DMA
    V = pltpu.VMEM
    return pl.pallas_call(backward_kernel,
        out_shape=(sd((1024, 768), f32), sd((96, 896), f32), sd((96, 768), f32), sd((112, 640), f32)),
        in_specs=[any_] * 12 + [vm] * 2, out_specs=(any_, vm, vm, vm),
        scratch_shapes=scatter_buffers(96, 896) + scatter_buffers(96, 768) + scatter_buffers(112, 640)
            + [V((512, 512), f32), V((8, 768), f32)]
            + [V((2, 1024, 768), bf16), V((2, 1024, 768), bf16), V((2, 2304, 512), bf16), V((2, 768, 512), bf16), V((2, 768, 512), bf16), V((1024, 768), bf16),
            V((2, 2304, 512), bf16), V((2, BACKWARD_HEADS, 512, 512), bf16), V((2, 512, 768), f32), dma((3, 3)), dma((3, 13)), dma((2,)), dma((2,)), dma((4,)), dma((2,)), dma((2,))],
        compiler_params=pltpu.CompilerParams(collective_id=1, has_side_effects=True, vmem_limit_bytes=63 << 20), name="attend_back_and_reduce")(*ops)


def hand_out_kernel(gin, res, gup, gdown, attn_h, gate_h, jitter_h, heat, gin_o, res_o, qkv, out, up, down, bias, gains, shifts, logits,
                    gbuf, rbuf, ubuf, dbuf, attn, gate, jitter, sem):
    cp = pltpu.make_async_copy
    n = 4
    rows = gin.shape[0] // n
    moves = [(a.at[pl.ds(r * rows, rows)], b.at[pl.ds(r * rows, rows)], c.at[pl.ds(r * rows, rows)])
             for r in range(n) for a, b, c in ((gin, gbuf, gin_o), (res, rbuf, res_o))]
    moves += [(gdown, dbuf, down), (gup, ubuf, None)]
    small = [cp(a, b, sem.at[m]) for m, (a, b) in enumerate(((attn_h, attn), (gate_h, gate), (jitter_h, jitter)))]
    ins = [cp(a, b, sem.at[3 + m]) for m, (a, b, c) in enumerate(moves)]
    outs = [cp(b, c, sem.at[13 + m]) for m, (a, b, c) in enumerate(moves[:-1])]
    for c in small + ins: c.start()
    for c in small: c.wait()
    qkv[...] = attn[:96, :576]
    inv = 1.0 / heat[0]
    table = jnp.concatenate([attn[96:112, 128 * j:128 * j + 128] for j in range(4)], axis=0)
    mixed = (gate[...].astype(f32) + jitter[...].astype(f32)) * inv
    logits[...] = table * (inv / (1.0 + jnp.exp(mixed)))
    gains[...] = attn[96:98, 512:608]
    shifts[...] = attn[98:104, 512:608]
    bias[...] = attn[104:110, 512:640]
    for a, b in zip(ins, outs):
        a.wait()
        b.start()
    ins[-1].wait()
    up[...] = ubuf[:, :768]
    out[:, :64] = attn[:96, 576:]
    out[:, 64:] = ubuf[:, 768:]
    for c in outs: c.wait()


def hand_out_call(gin, res, gup, gdown, attn, gate, jitter, heat):
    any_ = pl.BlockSpec(memory_space=pl.ANY); vm = pl.BlockSpec(memory_space=pltpu.VMEM); sm = pl.BlockSpec(memory_space=pltpu.SMEM)
    sd = lambda *s: jax.ShapeDtypeStruct(s, f32)
    V = pltpu.VMEM
    return pl.pallas_call(hand_out_kernel,
        out_shape=(sd(1024, 768), jax.ShapeDtypeStruct((1024, 768), bf16), sd(96, 576), sd(96, 192), sd(96, 768), sd(96, 768), sd(6, 128), sd(2, 96), sd(6, 96), sd(64, 128)),
        in_specs=[any_] * 7 + [sm], out_specs=(any_, any_, vm, vm, vm, any_) + (vm,) * 4,
        scratch_shapes=[V((1024, 768), f32), V((1024, 768), bf16), V((96, 896), f32), V((96, 768), f32), V((112, 640), f32), V((64, 128), bf16), V((64, 128), bf16), pltpu.SemaphoreType.DMA((23,))],
        compiler_params=pltpu.CompilerParams(vmem_limit_bytes=63 << 20), name="hand_out")(gin, res, gup, gdown, attn, gate, jitter, heat)


def own_device(
    layer_activations,
    token_counts_each,
    attention_triple_matrix,
    attention_final_matrix,
    feedfwd_expand_matrix,
    feedfwd_expand_offset,
    feedfwd_contract_matrix,
    layernorm_scales,
    offset_vectors,
    learned_gate_scores,
    fixed_jitter_matrix,
    relaxation_heat,
    loss_grad_result,
):
    x = layer_activations.reshape(1024, D)
    cot = loss_grad_result.reshape(1024, D)
    (
        attn_full, qkv, ctx, probs, result, act, grad_pre, hidden_low, grad_second_low, grad_first_low, grad_first, grad_ctx,
        sums, grad_bias,
    ) = front_call(
        attention_triple_matrix, attention_final_matrix, feedfwd_expand_matrix, feedfwd_expand_offset.reshape(6, 128),
        feedfwd_contract_matrix.T, layernorm_scales, offset_vectors, learned_gate_scores, fixed_jitter_matrix, relaxation_heat,
        token_counts_each, x, cot,
    )
    grad_inputs, up, down, attn = backward_call(
        attn_full, qkv, probs, grad_ctx, ctx, act, grad_pre, hidden_low, grad_second_low, x, grad_first_low, grad_first,
        sums, grad_bias,
    )
    grad_inputs, result, g_qkv, g_out, g_up, g_down, g_bias, g_gains, g_shifts, g_logits = hand_out_call(
        grad_inputs, result, up, down, attn, learned_gate_scores, fixed_jitter_matrix, relaxation_heat
    )
    return (
        result.reshape(layer_activations.shape),
        grad_inputs.reshape(layer_activations.shape),
        g_qkv,
        g_out,
        g_up,
        g_bias.reshape(-1),
        g_down.T,
        g_gains,
        g_shifts,
        g_logits,
    )


def solution(mesh):
    in_specs = (
        P(AXES, None, None),
        P(AXES),
        P("dp", "ffn"),
        P("dp", "ffn"),
        P("dp", "ffn"),
        P("ffn"),
        P("ffn", "dp"),
        P(None, "dp"),
        P(None, "dp"),
        P("dp", "ffn"),
        P("dp", "ffn"),
        P(),
        P(AXES, None, None),
    )
    out_specs = (
        P(AXES, None, None),
        P(AXES, None, None),
        P("dp", "ffn"),
        P("dp", "ffn"),
        P("dp", "ffn"),
        P("ffn"),
        P("ffn", "dp"),
        P(None, "dp"),
        P(None, "dp"),
        P("dp", "ffn"),
    )
    own = (mesh.shape["dp"], mesh.shape["ffn"]) == (8, 4)
    return jax.shard_map(
        own_device if own else general_device, mesh=mesh, in_specs=in_specs, out_specs=out_specs, check_vma=False
    )
```

```python
import functools

import jax
import jax.numpy as jnp
from jax import lax
from jax.experimental import pallas as pl
from jax.experimental.pallas import tpu as pltpu
from jax.sharding import PartitionSpec as P

D = 768
HEADS = 12
HEAD_DIM = 64
SEQ_LEN = 512
AXES = ("dp", "ffn")
norm_eps = 1e-06
f32 = jnp.float32
bf16 = jnp.bfloat16
MESH = pl.DeviceIdType.MESH


def dot_first(left, right):
    return lax.dot_general(left, right, (((0,), (0,)), ((), ())), preferred_element_type=f32)


def dot_last(left, right):
    return lax.dot_general(left, right, (((1,), (1,)), ((), ())), preferred_element_type=f32)


def dot(left, right):
    return jnp.dot(left, right, preferred_element_type=f32)


def layer_norm(values, gain, shift):
    mean_row = jnp.mean(values, axis=-1, keepdims=True)
    centered = values - mean_row
    inv_std = lax.rsqrt(jnp.mean(centered * centered, axis=-1, keepdims=True) + norm_eps)
    normed = centered * inv_std
    return (normed * gain + shift, normed, inv_std)


def norm_back(grad_out, normed, inv_std, gain):
    grad_normed = grad_out * gain
    grad_in = inv_std * (
        grad_normed
        - jnp.mean(grad_normed, axis=-1, keepdims=True)
        - normed * jnp.mean(grad_normed * normed, axis=-1, keepdims=True)
    )
    return (grad_in, jnp.sum(grad_out * normed, axis=0), jnp.sum(grad_out, axis=0))


def gelu_slope(values):
    return (
        0.5 * (1.0 + lax.erf(values * 0.7071067811865476))
        + values * jnp.exp(-0.5 * values * values) * 0.3989422804014327
    )


def score_block(queries, keys_low, natural_log_gate, live):
    scores = (
        jnp.einsum("qhd,khd->hqk", queries, keys_low, preferred_element_type=f32)
        * HEAD_DIM ** (-0.5)
        + natural_log_gate
    )
    return jnp.where(live[None, None, :], scores, -1e30)


def attend(queries, keys_low, values_low, natural_log_gate, live):
    scores = score_block(queries, keys_low, natural_log_gate, live)
    peak = jnp.max(scores, axis=-1, keepdims=True)
    shifted_exp = jnp.exp(scores - peak)
    total_exp = jnp.sum(shifted_exp, axis=-1, keepdims=True)
    probs_low = (shifted_exp / total_exp).astype(bf16)
    context = jnp.einsum("hqk,khd->qhd", probs_low, values_low, preferred_element_type=f32)
    return (context, peak + jnp.log(total_exp))


def attend_back(queries, keys_low, values_low, natural_log_gate, live, log_total, grad_context):
    scores = score_block(queries, keys_low, natural_log_gate, live)
    probs = jnp.exp(scores - log_total)
    grad_probs = jnp.einsum("qhd,khd->hqk", grad_context, values_low, preferred_element_type=f32)
    grad_values = jnp.einsum(
        "hqk,qhd->khd", probs.astype(bf16), grad_context, preferred_element_type=f32
    )
    grad_scores = probs * (grad_probs - jnp.sum(probs * grad_probs, axis=-1, keepdims=True))
    grad_mask = jnp.sum(grad_scores, axis=0)
    grad_scores_low = grad_scores.astype(bf16)
    grad_queries = jnp.einsum(
        "hqk,khd->qhd", grad_scores_low, keys_low, preferred_element_type=f32
    ) * HEAD_DIM ** (-0.5)
    grad_keys = jnp.einsum(
        "hqk,qhd->khd", grad_scores_low, queries, preferred_element_type=f32
    ) * HEAD_DIM ** (-0.5)
    return (grad_queries, grad_keys, grad_values, grad_mask)


def gather_weights(pack, small):
    rows_dp = lax.axis_size("dp")
    cols_ffn = lax.axis_size("ffn")
    full = lax.all_gather(pack[None], AXES, axis=0, tiled=True)
    full = full.reshape(rows_dp, cols_ffn, *pack.shape)
    small_full = lax.all_gather(small[None], AXES, axis=0, tiled=True)
    return full, small_full.reshape(rows_dp, cols_ffn, *small.shape)


def columns(blocks):
    rows_dp, cols_ffn, rows, cols = blocks.shape
    return blocks.transpose(0, 2, 1, 3).reshape(rows_dp * rows, cols_ffn * cols)


def blocks_of(full, rows_dp, cols_ffn):
    rows, cols = full.shape
    return full.reshape(rows_dp, rows // rows_dp, cols_ffn, cols // cols_ffn).transpose(0, 2, 1, 3)


def general_device(
    layer_activations,
    token_counts_each,
    attention_triple_matrix,
    attention_final_matrix,
    feedfwd_expand_matrix,
    feedfwd_expand_offset,
    feedfwd_contract_matrix,
    layernorm_scales,
    offset_vectors,
    learned_gate_scores,
    fixed_jitter_matrix,
    relaxation_heat,
    loss_grad_result,
):
    rows_dp = lax.axis_size("dp")
    cols_ffn = lax.axis_size("ffn")
    seq_count = layer_activations.shape[0]
    row_count = seq_count * SEQ_LEN
    shard_rows = attention_triple_matrix.shape[0]
    qkv_cols = attention_triple_matrix.shape[1]
    out_cols = attention_final_matrix.shape[1]
    ff_cols = feedfwd_expand_matrix.shape[1]

    pack = jnp.concatenate(
        [
            attention_triple_matrix,
            attention_final_matrix,
            feedfwd_expand_matrix,
            feedfwd_contract_matrix.T,
        ],
        axis=1,
    )
    mask_cols = learned_gate_scores.shape[1]
    vectors = jnp.concatenate([layernorm_scales, offset_vectors], axis=0)
    small = jnp.concatenate(
        [
            learned_gate_scores,
            fixed_jitter_matrix,
            jnp.pad(vectors, ((0, 0), (0, mask_cols - vectors.shape[1]))),
            feedfwd_expand_offset.reshape(-1, mask_cols),
        ],
        axis=0,
    )
    full, small_full = gather_weights(pack, small)
    full_qkv = columns(full[..., :qkv_cols])
    full_out = columns(full[..., qkv_cols : qkv_cols + out_cols])
    full_up = columns(full[..., qkv_cols + out_cols : qkv_cols + out_cols + ff_cols])
    full_down_t = columns(full[..., qkv_cols + out_cols + ff_cols :])
    mask_rows = learned_gate_scores.shape[0]
    logits_sum = columns(small_full[:, :, :mask_rows]).astype(f32) + columns(
        small_full[:, :, mask_rows : 2 * mask_rows]
    ).astype(f32)
    natural_log_gate = jax.nn.log_sigmoid(logits_sum / relaxation_heat[0])
    vectors_full = (
        small_full[:, 0, 2 * mask_rows : 2 * mask_rows + 8, :shard_rows]
        .transpose(1, 0, 2)
        .reshape(8, D)
        .astype(f32)
    )
    gains_full = vectors_full[:2]
    shifts_full = vectors_full[2:]
    bias_up = small_full[0, :, 2 * mask_rows + 8 :].reshape(1, -1).astype(f32)

    flat_in = layer_activations.reshape(row_count, D)
    qkv_bias = jnp.concatenate([shifts_full[0], jnp.zeros((D,), f32), shifts_full[1]])
    proj_low = (dot(flat_in, full_qkv) + qkv_bias).astype(bf16)
    head_shape = (seq_count, SEQ_LEN, HEADS, HEAD_DIM)
    queries = proj_low[:, :D].reshape(head_shape)
    keys_low = proj_low[:, D : 2 * D].reshape(head_shape)
    values_low = proj_low[:, 2 * D :].reshape(head_shape)
    live = lax.broadcasted_iota(jnp.int32, (seq_count, SEQ_LEN), 1) < token_counts_each[:, None]
    attended = [
        attend(queries[s], keys_low[s], values_low[s], natural_log_gate, live[s])
        for s in range(seq_count)
    ]
    context_low = jnp.concatenate(
        [item[0].reshape(SEQ_LEN, D).astype(bf16) for item in attended], axis=0
    )
    first_sum = flat_in.astype(f32) + dot(context_low, full_out) + shifts_full[2]
    hidden, normed_one, inv_one = layer_norm(first_sum, gains_full[0], shifts_full[4])
    hidden_low = hidden.astype(bf16)
    pre_act = dot(hidden_low, full_up) + bias_up
    act_low = jax.nn.gelu(pre_act, approximate=False).astype(bf16)
    second_sum = hidden + dot_last(act_low, full_down_t) + shifts_full[3]
    result, normed_two, inv_two = layer_norm(second_sum, gains_full[1], shifts_full[5])
    cot_flat = loss_grad_result.reshape(row_count, D).astype(f32)
    grad_second, grad_gain_two, grad_shift_two = norm_back(
        cot_flat, normed_two, inv_two, gains_full[1]
    )
    grad_second_low = grad_second.astype(bf16)
    grad_w_down_t = dot_first(grad_second_low, act_low)
    grad_act = dot(grad_second_low, full_down_t)
    grad_pre = (grad_act * gelu_slope(pre_act)).astype(bf16)
    grad_bias_up = jnp.sum(grad_pre, axis=0, dtype=f32)
    grad_w_up = dot_first(hidden_low, grad_pre)
    grad_hidden = grad_second + dot_last(grad_pre, full_up)
    grad_first, grad_gain_one, grad_shift_one = norm_back(
        grad_hidden, normed_one, inv_one, gains_full[0]
    )
    grad_first_low = grad_first.astype(bf16)
    grad_w_out = dot_first(context_low, grad_first_low)
    grad_context = dot_last(grad_first_low, full_out).astype(bf16).reshape(head_shape)
    back = [
        attend_back(
            queries[s],
            keys_low[s],
            values_low[s],
            natural_log_gate,
            live[s],
            attended[s][1],
            grad_context[s],
        )
        for s in range(seq_count)
    ]
    grad_mask = sum(item[3] for item in back)
    grad_projected = jnp.concatenate(
        [
            jnp.concatenate(
                [item[part].reshape(SEQ_LEN, D).astype(bf16) for item in back], axis=0
            )
            for part in range(3)
        ],
        axis=1,
    )
    grad_w_qkv = dot_first(flat_in, grad_projected)
    grad_inputs = grad_first + dot_last(grad_projected, full_qkv)
    grad_vectors = jnp.stack(
        [
            grad_gain_one,
            grad_gain_two,
            jnp.sum(grad_projected[:, :D], axis=0, dtype=f32),
            jnp.sum(grad_projected[:, 2 * D :], axis=0, dtype=f32),
            jnp.sum(grad_first, axis=0),
            jnp.sum(grad_second, axis=0),
            grad_shift_one,
            grad_shift_two,
        ]
    )
    big = jnp.concatenate(
        [
            blocks_of(item, rows_dp, cols_ffn)
            for item in (grad_w_qkv, grad_w_out, grad_w_up, grad_w_down_t)
        ],
        axis=-1,
    ).reshape(rows_dp * cols_ffn, shard_rows, -1)
    vector_blocks = jnp.broadcast_to(
        grad_vectors.reshape(8, rows_dp, 1, shard_rows).transpose(1, 2, 0, 3),
        (rows_dp, cols_ffn, 8, shard_rows),
    )
    bias_blocks = jnp.broadcast_to(
        grad_bias_up.reshape(1, cols_ffn, -1, mask_cols),
        (rows_dp, cols_ffn, ff_cols // mask_cols, mask_cols),
    )
    little = jnp.concatenate(
        [
            blocks_of(grad_mask, rows_dp, cols_ffn),
            jnp.pad(vector_blocks, ((0, 0), (0, 0), (0, 0), (0, mask_cols - shard_rows))),
            bias_blocks,
        ],
        axis=2,
    ).reshape(rows_dp * cols_ffn, -1, mask_cols)
    big = lax.psum_scatter(big, AXES, scatter_dimension=0, tiled=True)[0]
    little = lax.psum_scatter(little, AXES, scatter_dimension=0, tiled=True)[0]

    own_mixed = (
        learned_gate_scores.astype(f32) + fixed_jitter_matrix.astype(f32)
    ) / relaxation_heat[0]
    grad_logits = little[:mask_rows] * (jax.nn.sigmoid(-own_mixed) / relaxation_heat[0])
    return (
        result.astype(bf16).reshape(layer_activations.shape),
        grad_inputs.reshape(layer_activations.shape),
        big[:, :qkv_cols],
        big[:, qkv_cols : qkv_cols + out_cols],
        big[:, qkv_cols + out_cols : qkv_cols + out_cols + ff_cols],
        little[mask_rows + 8 :].reshape(-1),
        big[:, qkv_cols + out_cols + ff_cols :].T,
        little[mask_rows : mask_rows + 2, :shard_rows],
        little[mask_rows + 2 : mask_rows + 8, :shard_rows],
        grad_logits,
    )


def partners():
    i = lax.axis_index("dp")
    f = lax.axis_index("ffn")
    core = i + 1 - 2 * (i % 2)
    ix = i + 2 - 4 * ((i // 2) % 2)
    iy = (i + 4) % 8
    idg = (ix + 4) % 8
    return i, f, core, ix, iy, idg


def enter_barrier(me):
    i, f, core, ix, iy, idg = me
    sem = pltpu.get_barrier_semaphore()
    mates = [(i, (f + k) % 4) for k in (1, 2, 3)] + [(core, f), (ix, f), (iy, f)]
    for to in mates:
        pl.semaphore_signal(sem, inc=1, device_id=to, device_id_type=MESH)
    pl.semaphore_wait(sem, len(mates))


class Exchange:
    def __init__(self, me, ssem, rsem):
        self.me, self.ssem, self.rsem = me, ssem, rsem

    def copy(self, src, dst, send, recv, to):
        return pltpu.make_async_remote_copy(
            src_ref=src,
            dst_ref=dst,
            send_sem=self.ssem.at[send],
            recv_sem=self.rsem.at[recv],
            device_id=to,
            device_id_type=MESH,
        )

    def send(self, src, dst, send, recv, to):
        self.copy(src, dst, send, recv, to).start()

    def recv(self, ref, n):
        self.copy(ref, ref, 0, n, (self.me[0], self.me[1])).wait_recv()

    def sent(self, ref, n):
        self.copy(ref, ref, n, 0, (self.me[0], self.me[1])).wait_send()


class Gather(Exchange):
    def __init__(self, me, dst, ssem, rsem, rows, stride, offset=0, src=None, lsem=None):
        super().__init__(me, ssem, rsem)
        self.dst, self.rows, self.stride, self.offset, self.lsem = dst, rows, stride, offset, lsem
        self.src = src

    def span(self, i):
        return pl.ds(pl.multiple_of(i * self.stride + self.offset, 16), self.rows)

    def piece(self, i, p):
        return self.dst.at[p, self.span(i)]

    def block(self, i):
        return self.dst.at[:, self.span(i)]

    def own(self):
        return self.piece(self.me[0], self.me[1]) if self.src is None else self.src

    def local(self):
        i, f = self.me[:2]
        return pltpu.make_async_copy(self.src, self.piece(i, f), self.lsem)

    def sz(self, _):
        i, f, core, ix, iy, idg = self.me
        if self.src is not None:
            self.local().start()
        for k in (1, 2, 3):
            self.send(self.own(), self.piece(i, f), 0, 3 - k, (i, (f + k) % 4))

    def sp(self, _):
        i, f, core, ix, iy, idg = self.me
        self.send(self.own(), self.piece(i, f), 1, 3, (ix, f))
        self.send(self.own(), self.piece(i, f), 1, 3, (iy, f))

    def z(self, k):
        i, f, core, ix, iy, idg = self.me
        ref = self.piece(i, (f + k) % 4)
        self.recv(ref, k - 1)
        self.send(ref, ref, 1, 3 + k, (ix, f))
        self.send(ref, ref, 1, 3 + k, (iy, f))

    def o(self, _):
        i, f, core, ix, iy, idg = self.me
        if self.src is not None:
            self.local().wait()
        self.send(self.block(i), self.block(i), 1, 8, (core, f))

    def d(self, k):
        i, f, core, ix, iy, idg = self.me
        p = (f + k) % 4
        rx, ry = self.piece(ix, p), self.piece(iy, p)
        self.recv(self.bytes_of(2, 1), 3 + k)
        if k % 2:
            self.send(rx, rx, 1, 7, (iy, f))
        else:
            self.send(ry, ry, 1, 7, (ix, f))

    def b(self, _):
        i, f, core, ix, iy, idg = self.me
        self.send(self.block(ix), self.block(ix), 1, 8, (core, f))
        self.send(self.block(iy), self.block(iy), 1, 8, (core, f))

    def h(self, _):
        i, f, core, ix, iy, idg = self.me
        self.recv(self.bytes_of(4, 1), 7)
        self.send(self.block(idg), self.block(idg), 1, 8, (core, f))

    def r(self, _):
        self.recv(self.bytes_of(4, 4), 8)

    def bytes_of(self, n, m):
        return self.dst.at[pl.ds(0, n), pl.ds(0, m * self.rows)]

    def finish(self):
        self.sent(self.bytes_of(3, 1), 0)
        self.sent(self.bytes_of(4, 7), 1)


class Scatter(Exchange):
    def __init__(self, me, part, got, out, ssem, rsem):
        super().__init__(me, ssem, rsem)
        self.part, self.out = part, out
        self.rc, self.rq, self.rx, self.ry, self.rz = got
        i = me[0]
        self.c = i % 2
        self.xy = i // 2
        self.xyx = self.xy + 1 - 2 * (self.xy % 2)
        self.xyy = (self.xy + 2) % 4
        self.xyd = (self.xyx + 2) % 4

    def at(self, k):
        return (self.me[1] + k) % 4

    def piece(self, k, xy):
        return self.part.at[self.at(k), xy, self.c]

    def finish(self):
        self.sent(self.rc, 0)
        self.sent(self.rc.at[pl.ds(0, 3)], 1)
        self.sent(self.rz, 2)

    def add(self, ref, *refs):
        if len(refs) == 1:
            ref[...] = ref[...] + refs[0][...]
            return
        total = ref[...].astype(f32)
        for other in refs:
            total = total + other[...].astype(f32)
        ref[...] = total.astype(ref.dtype)

    def c_(self, k):
        self.send(self.part.at[self.at(k), :, 1 - self.c], self.rc.at[k], 0, k, (self.me[2], self.me[1]))

    def q(self, k):
        i, f, core, ix, iy, idg = self.me
        self.recv(self.rc.at[k], k)
        ref = self.piece(k, self.xyd)
        self.add(ref, self.rc.at[k, self.xyd])
        self.send(ref, self.rq.at[k], 1, 4 + k, (iy if k % 2 else ix, f))
        refx, refy = self.piece(k, self.xyx), self.piece(k, self.xyy)
        if k % 2:
            self.add(refy, self.rc.at[k, self.xyy])
            self.send(refy, self.ry.at[k], 1, 8 + k, (iy, f))
            self.add(refx, self.rc.at[k, self.xyx])
        else:
            self.add(refx, self.rc.at[k, self.xyx])
            self.send(refx, self.rx.at[k], 1, 8 + k, (ix, f))
            self.add(refy, self.rc.at[k, self.xyy])
        self.add(self.piece(k, self.xy), self.rc.at[k, self.xy])

    def t(self, k):
        i, f, core, ix, iy, idg = self.me
        self.recv(self.rq.at[k], 4 + k)
        ref = self.piece(k, self.xyx if k % 2 else self.xyy)
        self.add(ref, self.rq.at[k])
        if k % 2:
            self.send(ref, self.rx.at[k], 1, 8 + k, (ix, f))
        else:
            self.send(ref, self.ry.at[k], 1, 8 + k, (iy, f))

    def w(self, k):
        i, f, core, ix, iy, idg = self.me
        self.recv(self.rx.at[pl.ds(0, 2)], 8 + k)
        ref = self.piece(k, self.xy)
        if k:
            self.add(ref, self.rx.at[k], self.ry.at[k])
            self.send(ref, self.rz.at[3 - k], 2, 12, (i, (f + k) % 4))
        else:
            self.out[...] = ref[...].astype(f32) + self.rx[k].astype(f32) + self.ry[k].astype(f32)

    def e(self):
        total = self.out[...]
        self.recv(self.rz, 12)
        for k in range(3):
            total = total + self.rz[k].astype(f32)
        self.out[...] = total


def scatter_buffers(rows, cols):
    return [
        pltpu.VMEM(shape, bf16)
        for shape in ((4, 4, 2, rows, cols), (4, 4, rows, cols)) + ((4, rows, cols),) * 3 + ((3, rows, cols),)
    ]


HD=64
def dg(a,b,ca,cb): return lax.dot_general(a,b,(((ca,),(cb,)),((),())),preferred_element_type=f32)

def log_sigmoid(z):
    return jnp.minimum(z, 0.0) - jnp.log1p(jnp.exp(-jnp.abs(z)))

def prepare_mask(s_v, lens, heat, msk, mrows, srows):
    inv = 1.0 / heat[0]
    n = srows
    rows = []
    for i in range(8):
        row = []
        for f in range(4):
            a = s_v[f, pl.ds(i * n, mrows), :].astype(f32) + s_v[f, pl.ds(i * n + mrows, mrows), :].astype(f32)
            row.append(log_sigmoid(a * inv))
        rows.append(jnp.concatenate(row, axis=1))
    lmt = jnp.concatenate(rows, axis=0).T
    key = lax.broadcasted_iota(jnp.int32, lmt.shape, 0)
    for s in range(msk.shape[0]):
        msk[s] = jnp.where(key < lens[s], lmt, -1e30)

def prepare_columns(v_v, col, cols):
    for i in range(8):
        v = v_v[0, pl.ds(i * 16, 16), :].astype(f32)
        col[pl.ds(i * cols, cols), :] = v.T[:cols, :]

def project(f, s, a_v, x, col, qkv):
    acc = dg(a_v[f, :, :576], x[s * 512:(s + 1) * 512, :], 0, 1)
    lo = 0
    while lo < 576:
        g = 576 * f + lo
        kind = g // 768
        hi = min(576, (kind + 1) * 768 - 576 * f)
        part = acc[lo:hi]
        b = g - kind * 768
        if kind == 0:
            part = (part + col[b:b + hi - lo, 2:3]) * 0.125
        elif kind == 2:
            part = part + col[b:b + hi - lo, 3:4]
        qkv[s, g:g + hi - lo, :] = part.astype(bf16)
        lo = hi


def attend_head(qkv, msk, ctx, ptbuf, slot, s, h):
    q = qkv[s, pl.ds(h * HD, HD), :]
    k = qkv[s, pl.ds(768 + h * HD, HD), :]
    v = qkv[s, pl.ds(1536 + h * HD, HD), :]
    st = dg(k, q, 0, 0) + msk[s]
    e = jnp.exp(st - jnp.max(st, axis=0, keepdims=True))
    p = (e * (1.0 / jnp.sum(e, axis=0, keepdims=True))).astype(bf16)
    ptbuf[slot] = p
    ctx[s, pl.ds(h * HD, HD), :] = dg(v, p, 1, 0).astype(bf16)

def attend_all(qkv, msk, ctx, pt, ptbuf, psem, per, hook):
    steps = 24 // per
    out = lambda t: pltpu.make_async_copy(
        ptbuf.at[t % 2], pt.at[pl.ds(t * per, per)], psem.at[t % 2]
    )
    def body(t, carry):
        @pl.when(t >= 2)
        def _():
            out(t - 2).wait()
        s = t // (12 // per)
        for u in range(per):
            h = (t % (12 // per)) * per + u
            attend_head(qkv, msk, ctx, ptbuf.at[t % 2], u, s, h)
        out(t).start()
        hook(t)
        return carry
    lax.fori_loop(0, steps, body, 0)
    for t in (steps - 2, steps - 1):
        out(t).wait()


FORWARD_HEADS = 4
BACKWARD_HEADS = 3


def norm_rows(v):
    mean = jnp.mean(v, axis=-1, keepdims=True)
    c = v - mean
    inv = lax.rsqrt(jnp.mean(c * c, axis=-1, keepdims=True) + 1e-6)
    return c * inv, inv

def norm_rows_back(g, normed, inv, gain):
    e = g * gain
    return inv * (e - jnp.mean(e, axis=-1, keepdims=True) - normed * jnp.mean(e * normed, axis=-1, keepdims=True))

def gather_steps(vec, a0, a1, a2, small, up, down):
    return {
        'first': [(vec.sz, 0), (a0.sz, 0), (small.sz, 0), (a1.sz, 0), (a2.sz, 0), (vec.sp, 0), (a0.sp, 0), (small.sp, 0), (a1.sp, 0), (a2.sp, 0), (vec.z, 1), (vec.z, 2), (vec.z, 3), (vec.o, 0), (vec.d, 0), (a0.d, 0), (a0.z, 1), (small.d, 0), (a0.z, 2), (a1.d, 0), (a0.z, 3), (a0.o, 0), (a2.d, 0), (vec.d, 1), (vec.d, 2), (vec.d, 3), (vec.b, 0), (small.z, 1), (small.z, 2), (a0.d, 1), (small.z, 3), (small.o, 0), (a0.d, 2), (a1.z, 1), (a1.z, 2), (a0.d, 3), (a0.b, 0), (a1.z, 3), (a1.o, 0), (vec.h, 0), (small.d, 1), (a2.z, 1), (small.d, 2), (vec.r, 0), (small.d, 3), (small.b, 0), (a2.z, 2), (a0.h, 0), (a2.z, 3), (up.sz, 0), (up.sp, 0), (a2.o, 0), (a1.d, 1), (a1.d, 2), (a0.r, 0), (a1.d, 3), (a1.b, 0), (a2.d, 1), (small.h, 0), (a2.d, 2), (a2.d, 3), (a2.b, 0), (small.r, 0), (up.z, 1), (up.d, 0), (a1.h, 0), (a2.h, 0), (up.z, 2), (a1.r, 0), (a2.r, 0)],
        'P3': [(up.d, 1)],
        'P5': [(up.z, 3), (up.o, 0)],
        'P6': [(down.sz, 0)],
        0: [(up.d, 2), (down.z, 1)],
        1: [(up.d, 3), (up.b, 0)],
        2: [(down.sp, 0), (down.z, 2)],
        3: [(down.z, 3), (down.o, 0)],
        4: [(up.h, 0), (down.d, 1)],
        5: [(down.d, 0)],
        'UP': [(up.r, 0)],
        'O0': [(down.d, 2)],
        'F01': [(down.d, 3), (down.b, 0)],
        'F11': [(down.h, 0)],
        'LAST': [(down.r, 0)],
    }


def front_kernel(triple, final, expand, bup_in, contract, scales, offsets, gate, jitter, heat, lens, x, cot,
                 wa, qkv_o, ctx_o, pt, out, act, gp, hlow, gslow, gflow, gf, gctx, sums, gbup,
                 a_v, u_v, d_v, s_v, v_v, usrc, wout, col, msk, ptbuf, qkv, ctx, x_s, cot_s, slope, act_s, n1_s, inv_s, vec, bup,
                 gsl_s, gf_s, gfl_s, ssem, rsem, lsem, psem, isem, osem):
    me = partners()
    i, f = me[0], me[1]
    cp = pltpu.make_async_copy
    xc = cp(x, x_s, isem.at[0]); xc.start()
    cc = cp(cot, cot_s, isem.at[1]); cc.start()
    rows = pl.ds(pl.multiple_of(96 * i, 96), 96)
    a_v[f, rows, :576] = triple[...]
    a_v[f, rows, 576:640] = final[:, :64]
    usrc[:, :768] = expand[...]
    usrc[:, 768:] = final[:, 64:]
    at = lambda o, n: pl.ds(pl.multiple_of(o, 16), n)
    s_v[f, at(128 * i, 64), :] = gate[...]
    s_v[f, at(128 * i + 64, 64), :] = jitter[...]
    vectors = jnp.concatenate([scales[...].astype(f32), offsets[...].astype(f32)], axis=0)
    bias = bup_in[...].astype(f32)
    v_v[f, at(16 * i, 16), :] = jnp.concatenate(
        [jnp.concatenate([vectors, jnp.zeros((8, 32), f32)], axis=1)]
        + [bias, jnp.zeros((2, 128), f32)], axis=0
    ).astype(bf16)
    enter_barrier(me)
    attn_v = a_v
    a0, a1, a2 = [Gather(me, attn_v, ssem.at[n], rsem.at[n], 32, 96, 32 * n) for n in range(3)]
    small = Gather(me, s_v, ssem.at[6], rsem.at[6], 128, 128)
    vectors = Gather(me, v_v, ssem.at[5], rsem.at[5], 16, 16)
    up = Gather(me, u_v, ssem.at[3], rsem.at[3], 96, 96, 0, usrc, lsem.at[0])
    down = Gather(me, d_v, ssem.at[4], rsem.at[4], 96, 96, 0, contract, lsem.at[1])
    steps = gather_steps(vectors, a0, a1, a2, small, up, down)
    after = lambda name: run_steps(steps.get(name, ()))
    after("first")
    wac = cp(attn_v, wa, osem.at[0]); wac.start()
    prepare_columns(v_v, col, 96)
    xc.wait()
    for ff in range(4):
        for s in range(2):
            project(ff, s, a_v, x_s, col, qkv)
            after("P%d" % (2 * ff + s))
    after("W")
    prepare_mask(s_v, lens, heat, msk, 64, 128)
    for n in range(8):
        vec[:, 96 * n : 96 * n + 96] = v_v[0, 16 * n : 16 * n + 16, :].astype(f32)[0:8, :96]
    for ff in range(4):
        tail = v_v[ff, 0:16, :].astype(f32)
        for r in range(6):
            bup[:, 768 * ff + 128 * r : 768 * ff + 128 * r + 128] = tail[8 + r : 9 + r]
    def hook(t):
        for n in range(24 // FORWARD_HEADS):
            if steps.get(n):
                pl.when(t == n)(functools.partial(run_steps, steps[n]))
    qc = [cp(qkv.at[s], qkv_o.at[s], osem.at[1 + s]) for s in range(2)]
    for c in qc: c.start()
    attend_all(qkv, msk, ctx, pt, ptbuf, psem, FORWARD_HEADS, hook)
    oc = cp(ctx, ctx_o, osem.at[3]); oc.start()
    after("UP")
    for ff in range(4):
        wout[:, 192 * ff:192 * ff + 64] = a_v[ff, :, 576:640]
        wout[:, 192 * ff + 64:192 * ff + 192] = u_v[ff, :, 768:896]
    ac = [cp(act_s.at[s], act.at[pl.ds(512 * s, 512)], osem.at[4 + s]) for s in range(2)]
    hc = [cp(x_s.at[pl.ds(512 * s, 512)], hlow.at[pl.ds(512 * s, 512)], osem.at[6 + s]) for s in range(2)]
    for s in range(2):
        sl = pl.ds(512 * s, 512)
        first = x_s[sl].astype(f32) + dg(ctx[s], wout[...], 0, 0) + vec[4:5]
        n1, inv1 = norm_rows(first)
        n1_s[s] = n1
        inv_s[s] = inv1
        hl = (n1 * vec[0:1] + vec[6:7]).astype(bf16)
        x_s[sl] = hl
        hc[s].start()
        after("O%d" % s)
        for ff in range(4):
            pre = dg(x_s[sl], u_v[ff, :, :768], 1, 0) + bup[:, 768 * ff:768 * ff + 768]
            phi = 0.5 * (1.0 + lax.erf(pre * 0.7071067811865476))
            slope[s, ff] = (phi + pre * (jnp.exp(-0.5 * pre * pre) * 0.3989422804014327)).astype(SLOPE)
            act_s[s, :, 768 * ff:768 * ff + 768] = (pre * phi).astype(bf16)
            after("F%d%d" % (s, ff))
        ac[s].start()
    after("LAST")
    wac.wait()
    for c in qc: c.wait()
    outs = lambda s, only=range(6): [[
        lambda: cp(cot_s.at[pl.ds(512 * s, 512)], out.at[pl.ds(512 * s, 512)], osem.at[8]),
        lambda: cp(act_s.at[s], gp.at[pl.ds(512 * s, 512)], osem.at[9]),
        lambda: cp(gsl_s, gslow.at[pl.ds(512 * s, 512)], osem.at[10]),
        lambda: cp(gfl_s, gflow.at[pl.ds(512 * s, 512)], osem.at[11]),
        lambda: cp(gf_s, gf.at[pl.ds(512 * s, 512)], osem.at[12]),
        lambda: cp(qkv.at[s, pl.ds(0, 768)], gctx.at[s], osem.at[13]),
    ][n]() for n in only]
    cc.wait()
    total = None
    for s in range(2):
        sl = pl.ds(512 * s, 512)
        n1, inv1 = n1_s[s], inv_s[s]
        acc = n1 * vec[0:1] + vec[6:7] + vec[5:6]
        for ff in range(4):
            acc = acc + dg(act_s[s, :, 768 * ff:768 * ff + 768], d_v[ff], 1, 1)
        n2, inv2 = norm_rows(acc)
        g = cot_s[sl].astype(f32)
        gs = norm_rows_back(g, n2, inv2, vec[1:2])
        rs = lambda v: jnp.sum(v, axis=0, keepdims=True)
        s_gain2, s_cot, s_gs = rs(g * n2), rs(g), rs(gs)
        cot_s[sl] = (n2 * vec[1:2] + vec[7:8]).astype(bf16)
        if s:
            for c in outs(0, (0, 1, 5)): c.wait()
        for c in outs(s, (0,)): c.start()
        if s:
            for c in outs(s - 1, (2, 3, 4)): c.wait()
        gsl = gs.astype(bf16)
        gsl_s[...] = gsl
        for c in outs(s, (2,)): c.start()
        ac[s].wait()
        gh = gs
        for ff in range(4):
            p = (dg(gsl, d_v[ff], 1, 0) * slope[s, ff].astype(f32)).astype(bf16)
            act_s[s, :, 768 * ff:768 * ff + 768] = p
            cols = pl.ds(768 * ff, 768)
            cp(act_s.at[s, :, cols], gp.at[pl.ds(512 * s, 512), cols], osem.at[9]).start()
            b = rs(p.astype(f32))
            cols = slice(768 * ff, 768 * ff + 768)
            gbup[:, cols] = gbup[:, cols] + b if s else b
            gh = gh + dg(p, u_v[ff, :, :768], 1, 1)
        gfirst = norm_rows_back(gh, n1, inv1, vec[0:1])
        gf_s[...] = gfirst
        gfl = gfirst.astype(bf16)
        gfl_s[...] = gfl
        if s == 0:
            oc.wait()
        qkv[s, 0:768, :] = dg(wout[...], gfl, 1, 1).astype(bf16)
        part = jnp.concatenate([rs(gh * n1), s_gain2, jnp.zeros((2, 768), f32), rs(gfirst), s_gs, rs(gh), s_cot], axis=0)
        total = part if total is None else total + part
        for c in outs(s, (3, 4, 5)): c.start()
    sums[...] = total
    for c in outs(1): c.wait()
    for c in hc: c.wait()
    for g in (a0, a1, a2, small, up, down, vectors):
        g.finish()


def front_call(*ops):
    any_ = pl.BlockSpec(memory_space=pl.ANY)
    vm = pl.BlockSpec(memory_space=pltpu.VMEM)
    sm = pl.BlockSpec(memory_space=pltpu.SMEM)
    sd = jax.ShapeDtypeStruct
    dma = pltpu.SemaphoreType.DMA
    V = pltpu.VMEM
    tok = sd((1024, 768), bf16)
    wide = sd((1024, 3072), bf16)
    return pl.pallas_call(
        front_kernel,
        out_shape=(
            sd((4, 768, 640), bf16), sd((2, 2304, 512), bf16), sd((2, 768, 512), bf16),
            sd((24, 512, 512), bf16), tok, wide, wide, tok, tok, tok, sd((1024, 768), f32), sd((2, 768, 512), bf16),
            sd((8, 768), f32), sd((1, 3072), f32),
        ),
        in_specs=[vm, vm, vm, vm, any_, vm, vm, vm, vm, sm, sm, any_, any_],
        out_specs=(any_,) * 12 + (vm, vm),
        scratch_shapes=[
            V((4, 768, 640), bf16), V((4, 768, 896), bf16), V((4, 768, 768), bf16), V((4, 1024, 128), bf16), V((4, 128, 128), bf16), V((96, 896), bf16), V((768, 768), bf16),
            V((768, 16), f32), V((2, 512, 512), f32), V((2, FORWARD_HEADS, 512, 512), bf16), V((2, 2304, 512), bf16), V((2, 768, 512), bf16),
            V((1024, 768), bf16), V((1024, 768), bf16), V((2, 4, 512, 768), SLOPE), V((2, 512, 3072), bf16), V((2, 512, 768), f32),
            V((2, 512, 1), f32), V((8, 768), f32), V((1, 3072), f32), V((512, 768), bf16), V((512, 768), f32), V((512, 768), bf16),
            dma((7, 2)), dma((7, 9)), dma((2,)), dma((2,)), dma((4,)), dma((14,)),
        ],
        compiler_params=pltpu.CompilerParams(collective_id=0, has_side_effects=True, vmem_limit_bytes=63 << 20),
        name="gather_attend_feed_forward",
    )(*ops)


SLOPE = f32


def attend_head_back(qkv, gctx, p_ref, dproj, gm, s, h):
    q = qkv[s, pl.ds(h * HD, HD), :]
    k = qkv[s, pl.ds(768 + h * HD, HD), :]
    v = qkv[s, pl.ds(1536 + h * HD, HD), :]
    go = gctx[s, pl.ds(h * HD, HD), :]
    p = p_ref[...]
    dp = dg(v, go, 0, 0)
    pf = p.astype(f32)
    drow = jnp.sum(pf * dp, axis=0, keepdims=True)
    ds = pf * (dp - drow)
    dsl = ds.astype(bf16)
    dproj[s, pl.ds(1536 + h * HD, HD), :] = dg(go, p, 1, 1).astype(bf16)
    dproj[s, pl.ds(768 + h * HD, HD), :] = dg(q, dsl, 1, 1).astype(bf16)
    dproj[s, pl.ds(h * HD, HD), :] = (dg(k, dsl, 1, 0) * 0.125).astype(bf16)
    return ds

def attend_all_back(qkv, gctx, pt, ptbuf, psem, dproj, gm, per, hook):
    steps = 24 // per
    gm[...] = jnp.zeros(gm.shape, f32)
    load = lambda t: pltpu.make_async_copy(
        pt.at[pl.ds(t * per, per)], ptbuf.at[t % 2], psem.at[t % 2]
    )
    def body(t, carry):
        load(t).wait()
        s = t // (12 // per)
        tot = None
        for u in range(per):
            h = (t % (12 // per)) * per + u
            ds = attend_head_back(qkv, gctx, ptbuf.at[t % 2, u], dproj, gm, s, h)
            tot = ds if tot is None else tot + ds
        gm[...] += tot
        @pl.when(t + 2 < steps)
        def _():
            load(t + 2).start()
        hook(t)
        return carry
    lax.fori_loop(0, steps, body, 0)


ORDER = (1, 2, 3, 0)


def small_rows(part, gm, sums, gbup):
    table = gm[...].T
    zero = jnp.zeros((8, 32), f32)
    for f in range(4):
        bias = jnp.concatenate(
            [gbup[:, 768 * f + 128 * r : 768 * f + 128 * r + 128] for r in range(6)] + [jnp.zeros((2, 128), f32)], axis=0
        )
        for i in range(8):
            ref = part.at[f, i // 2, i % 2]
            for j in range(4):
                at = 64 * i + 16 * j
                ref[96:112, 128 * j : 128 * j + 128] = table[at : at + 16, 128 * f : 128 * f + 128].astype(bf16)
            rows = jnp.concatenate([sums[:, 96 * i : 96 * i + 96], zero], axis=1)
            ref[96:112, 512:640] = jnp.concatenate([rows, bias], axis=0).astype(bf16)


def backward_kernel(wfull, qkv_h, pt, gctx_h, ctx_h, act, gp, hlow, gslow, x, gfl_h, gf, sums_in, gbup, gin, oup, odown, oattn,
                    upart, urc, urq, urx, ury, urz, dpart, drc, drq, drx, dry, drz, apart, arc, arq, arx, ary, arz, gm, sums,
                    lhs, chunk, qkv, gctx, ctx, gfl, dproj, ptbuf, gbuf, ssem, rsem, lsem, csem, isem, psem, gsem):
    me = partners()
    cp = pltpu.make_async_copy
    at = [(me[1] + k) % 4 for k in range(4)]
    def chunk_copy(n):
        src = (act, gp)[n // 4].at[:, pl.ds(pl.multiple_of(768 * at[ORDER[n % 4]], 768), 768)]
        return cp(src, chunk.at[n % 2], csem.at[n % 2])
    l0 = cp(gslow, lhs.at[0], lsem.at[0]); l1 = cp(hlow, lhs.at[1], lsem.at[1]); l2 = cp(x, lhs.at[0], lsem.at[0])
    l0.start(); chunk_copy(0).start()
    ins = [cp(a, b, isem.at[n]) for n, (a, b) in enumerate(((ctx_h, ctx), (gfl_h, gfl), (qkv_h, qkv), (gctx_h, gctx)))]
    up = Scatter(me, upart, (urc, urq, urx, ury, urz), oup, ssem.at[0], rsem.at[0])
    down = Scatter(me, dpart, (drc, drq, drx, dry, drz), odown, ssem.at[1], rsem.at[1])
    attn = Scatter(me, apart, (arc, arq, arx, ary, arz), oattn, ssem.at[2], rsem.at[2])
    before, loop, dots = steps_between(attn, up, down)
    l0.wait()
    for n in range(8):
        g, k = (down, up)[n // 4], ORDER[n % 4]
        if n == 4:
            l2.start()
            for c in ins: c.wait()
            dwo = (dg(ctx[0], gfl[0:512], 1, 0) + dg(ctx[1], gfl[512:1024], 1, 0)).astype(bf16)
            for f in range(4):
                attn.part[f, :, :, 0:96, 576:] = dwo[:, 192 * f:192 * f + 64].reshape(4, 2, 96, 64)
                up.part[f, :, :, :, 768:] = dwo[:, 192 * f + 64:192 * f + 192].reshape(4, 2, 96, 128)
            l1.wait()
        chunk_copy(n).wait()
        if n == 0:
            chunk_copy(1).start(); l1.start()
            for c in ins: c.start()
            for t in range(2): cp(pt.at[pl.ds(t * BACKWARD_HEADS, BACKWARD_HEADS)], ptbuf.at[t], psem.at[t]).start()
        g.part[at[k], :, :, :, 0:768] = dg(lhs[n // 4], chunk[n % 2], 0, 0).astype(bf16).reshape(4, 2, 96, 768)
        if n < 6: chunk_copy(n + 2).start()
        if n == 0:
            enter_barrier(me)
        g.c_(k)
        run_steps(before.get(n, ()))
    def hook(t):
        for at_t in sorted(loop):
            pl.when(t == at_t)(functools.partial(run_steps, loop[at_t]))
    attend_all_back(qkv, gctx, pt, ptbuf, psem, dproj, gm, BACKWARD_HEADS, hook)
    ones = jnp.ones((8, 512), bf16)
    sums[...] = sums_in[...]
    sums[2:3] = (dg(ones, dproj[0, 0:768], 1, 1) + dg(ones, dproj[1, 0:768], 1, 1))[0:1]
    sums[3:4] = (dg(ones, dproj[0, 1536:2304], 1, 1) + dg(ones, dproj[1, 1536:2304], 1, 1))[0:1]
    small_rows(attn.part, gm, sums, gbup)
    l2.wait()
    for n, k in enumerate(ORDER):
        r = pl.ds(pl.multiple_of(576 * at[k], 576), 576)
        dw = dg(lhs[0, 0:512], dproj[0, r, :], 0, 1) + dg(lhs[0, 512:1024], dproj[1, r, :], 0, 1)
        attn.part[at[k], :, :, 0:96, :576] = dw.astype(bf16).reshape(4, 2, 96, 576)
        attn.c_(k)
        run_steps(dots.get(n, ()))
    aw = [cp(wfull.at[f], chunk.at[f % 2, pl.ds(0, 768), pl.ds(0, 640)], csem.at[f % 2]) for f in range(4)]
    aw[0].start(); aw[1].start()
    gi = [cp(gf.at[pl.ds(512 * s, 512)], gbuf.at[s], gsem.at[s]) for s in range(2)]
    for c in gi: c.start()
    for f in range(4):
        aw[f].wait()
        if f == 0:
            for c in gi: c.wait()
        for s in range(2):
            gbuf[s] = gbuf[s] + dg(dproj[s, 576 * f:576 * f + 576], chunk[f % 2, 0:768, :576], 0, 1)
            run_steps(dots.get(4 + 2 * f + s, ()))
        if f < 2: aw[f + 2].start()
    go = [cp(gbuf.at[s], gin.at[pl.ds(512 * s, 512)], gsem.at[s]) for s in range(2)]
    for c in go: c.start()
    run_steps(dots.get(12, ()))
    for c in go: c.wait()
    for g in (attn, up, down):
        g.finish()


def steps_between(attn, up, down):
    before = {
        2: [(down.q, 1)],
        3: [(down.q, 2)],
        4: [(down.q, 3), (down.q, 0), (down.t, 1)],
        5: [(down.t, 2)],
        6: [(up.q, 1)],
        7: [(up.q, 2), (down.t, 3)],
    }
    loop = {
        0: [(down.t, 0), (up.q, 3), (up.q, 0)],
        1: [(down.w, 2)],
        2: [(down.w, 1)],
        3: [(up.t, 1), (up.t, 2)],
        5: [(down.w, 0)],
        6: [(up.t, 3), (down.w, 3)],
        7: [(up.t, 0)],
    }
    dots = {
        0: [(down.e,)],
        1: [(up.w, 2)],
        2: [(attn.q, 1), (up.w, 1)],
        3: [(attn.q, 2), (up.w, 0)],
        5: [(attn.q, 3), (up.w, 3)],
        7: [(attn.t, 1)],
        10: [(attn.t, 2)],
        12: [(attn.t, 3), (attn.q, 0), (attn.w, 1), (up.e,), (attn.w, 3), (attn.w, 2), (attn.t, 0), (attn.w, 0), (attn.e,)],
    }
    return before, loop, dots


def run_steps(todo):
    for step, *arg in todo:
        step(*arg)


def backward_call(*ops):
    any_ = pl.BlockSpec(memory_space=pl.ANY); vm = pl.BlockSpec(memory_space=pltpu.VMEM)
    sd = jax.ShapeDtypeStruct
    dma = pltpu.SemaphoreType.DMA
    V = pltpu.VMEM
    return pl.pallas_call(backward_kernel,
        out_shape=(sd((1024, 768), f32), sd((96, 896), f32), sd((96, 768), f32), sd((112, 640), f32)),
        in_specs=[any_] * 12 + [vm] * 2, out_specs=(any_, vm, vm, vm),
        scratch_shapes=scatter_buffers(96, 896) + scatter_buffers(96, 768) + scatter_buffers(112, 640)
            + [V((512, 512), f32), V((8, 768), f32)]
            + [V((2, 1024, 768), bf16), V((2, 1024, 768), bf16), V((2, 2304, 512), bf16), V((2, 768, 512), bf16), V((2, 768, 512), bf16), V((1024, 768), bf16),
            V((2, 2304, 512), bf16), V((2, BACKWARD_HEADS, 512, 512), bf16), V((2, 512, 768), f32), dma((3, 3)), dma((3, 13)), dma((2,)), dma((2,)), dma((4,)), dma((2,)), dma((2,))],
        compiler_params=pltpu.CompilerParams(collective_id=1, has_side_effects=True, vmem_limit_bytes=63 << 20), name="attend_back_and_reduce")(*ops)


def hand_out_kernel(gin, res, gup, gdown, attn_h, gate_h, jitter_h, heat, gin_o, res_o, qkv, out, up, down, bias, gains, shifts, logits,
                    gbuf, rbuf, ubuf, dbuf, attn, gate, jitter, sem):
    cp = pltpu.make_async_copy
    n = 4
    rows = gin.shape[0] // n
    moves = [(a.at[pl.ds(r * rows, rows)], b.at[pl.ds(r * rows, rows)], c.at[pl.ds(r * rows, rows)])
             for r in range(n) for a, b, c in ((gin, gbuf, gin_o), (res, rbuf, res_o))]
    moves += [(gdown, dbuf, down), (gup, ubuf, None)]
    small = [cp(a, b, sem.at[m]) for m, (a, b) in enumerate(((attn_h, attn), (gate_h, gate), (jitter_h, jitter)))]
    ins = [cp(a, b, sem.at[3 + m]) for m, (a, b, c) in enumerate(moves)]
    outs = [cp(b, c, sem.at[13 + m]) for m, (a, b, c) in enumerate(moves[:-1])]
    for c in small + ins: c.start()
    for c in small: c.wait()
    qkv[...] = attn[:96, :576]
    inv = 1.0 / heat[0]
    table = jnp.concatenate([attn[96:112, 128 * j:128 * j + 128] for j in range(4)], axis=0)
    mixed = (gate[...].astype(f32) + jitter[...].astype(f32)) * inv
    logits[...] = table * (inv / (1.0 + jnp.exp(mixed)))
    gains[...] = attn[96:98, 512:608]
    shifts[...] = attn[98:104, 512:608]
    bias[...] = attn[104:110, 512:640]
    for a, b in zip(ins, outs):
        a.wait()
        b.start()
    ins[-1].wait()
    up[...] = ubuf[:, :768]
    out[:, :64] = attn[:96, 576:]
    out[:, 64:] = ubuf[:, 768:]
    for c in outs: c.wait()


def hand_out_call(gin, res, gup, gdown, attn, gate, jitter, heat):
    any_ = pl.BlockSpec(memory_space=pl.ANY); vm = pl.BlockSpec(memory_space=pltpu.VMEM); sm = pl.BlockSpec(memory_space=pltpu.SMEM)
    sd = lambda *s: jax.ShapeDtypeStruct(s, f32)
    V = pltpu.VMEM
    return pl.pallas_call(hand_out_kernel,
        out_shape=(sd(1024, 768), jax.ShapeDtypeStruct((1024, 768), bf16), sd(96, 576), sd(96, 192), sd(96, 768), sd(96, 768), sd(6, 128), sd(2, 96), sd(6, 96), sd(64, 128)),
        in_specs=[any_] * 7 + [sm], out_specs=(any_, any_, vm, vm, vm, any_) + (vm,) * 4,
        scratch_shapes=[V((1024, 768), f32), V((1024, 768), bf16), V((96, 896), f32), V((96, 768), f32), V((112, 640), f32), V((64, 128), bf16), V((64, 128), bf16), pltpu.SemaphoreType.DMA((23,))],
        compiler_params=pltpu.CompilerParams(vmem_limit_bytes=63 << 20), name="hand_out")(gin, res, gup, gdown, attn, gate, jitter, heat)


def own_device(
    layer_activations,
    token_counts_each,
    attention_triple_matrix,
    attention_final_matrix,
    feedfwd_expand_matrix,
    feedfwd_expand_offset,
    feedfwd_contract_matrix,
    layernorm_scales,
    offset_vectors,
    learned_gate_scores,
    fixed_jitter_matrix,
    relaxation_heat,
    loss_grad_result,
):
    x = layer_activations.reshape(1024, D)
    cot = loss_grad_result.reshape(1024, D)
    (
        attn_full, qkv, ctx, probs, result, act, grad_pre, hidden_low, grad_second_low, grad_first_low, grad_first, grad_ctx,
        sums, grad_bias,
    ) = front_call(
        attention_triple_matrix, attention_final_matrix, feedfwd_expand_matrix, feedfwd_expand_offset.reshape(6, 128),
        feedfwd_contract_matrix.T, layernorm_scales, offset_vectors, learned_gate_scores, fixed_jitter_matrix, relaxation_heat,
        token_counts_each, x, cot,
    )
    grad_inputs, up, down, attn = backward_call(
        attn_full, qkv, probs, grad_ctx, ctx, act, grad_pre, hidden_low, grad_second_low, x, grad_first_low, grad_first,
        sums, grad_bias,
    )
    grad_inputs, result, g_qkv, g_out, g_up, g_down, g_bias, g_gains, g_shifts, g_logits = hand_out_call(
        grad_inputs, result, up, down, attn, learned_gate_scores, fixed_jitter_matrix, relaxation_heat
    )
    return (
        result.reshape(layer_activations.shape),
        grad_inputs.reshape(layer_activations.shape),
        g_qkv,
        g_out,
        g_up,
        g_bias.reshape(-1),
        g_down.T,
        g_gains,
        g_shifts,
        g_logits,
    )


def solution(mesh):
    in_specs = (
        P(AXES, None, None),
        P(AXES),
        P("dp", "ffn"),
        P("dp", "ffn"),
        P("dp", "ffn"),
        P("ffn"),
        P("ffn", "dp"),
        P(None, "dp"),
        P(None, "dp"),
        P("dp", "ffn"),
        P("dp", "ffn"),
        P(),
        P(AXES, None, None),
    )
    out_specs = (
        P(AXES, None, None),
        P(AXES, None, None),
        P("dp", "ffn"),
        P("dp", "ffn"),
        P("dp", "ffn"),
        P("ffn"),
        P("ffn", "dp"),
        P(None, "dp"),
        P(None, "dp"),
        P("dp", "ffn"),
    )
    own = (mesh.shape["dp"], mesh.shape["ffn"]) == (8, 4)
    return jax.shard_map(
        own_device if own else general_device, mesh=mesh, in_specs=in_specs, out_specs=out_specs, check_vma=False
    )
```
